32 devices in a mesh: seq: 8 (over y, x, core), fsdp: 4 (over z).
Axes of the slice: x: 2, y: 2, z: 4, core: 2. Of those that a mesh axis runs over, the one named last changes fastest.
Arguments:
- tokens: bfloat16 [4, 1024, 2048], P('fsdp', 'seq'), may hold values from -6 to 6
- cotangent: bfloat16 [4, 1024, 2048], P('fsdp', 'seq'), may hold values from -6 to 6
- lengths: int32 [4], replicated, may hold values from 256 to 1024, as said below
- routes: int32 [4, 1024, 8], P('fsdp', 'seq'), may hold values from 0 to 63, all different within a row; in each aligned block of 128 rows (0 to 127, 128 to 255, ..., all dimensions but the last counted through in order) at most 24 rows name the same one
- norm_gains: bfloat16 [4, 2048], P(None, ('seq', 'fsdp')), may hold values from 0.5 to 1.5
- qkv_weight: bfloat16 [2048, 6144], P(('seq', 'fsdp')), may hold values from -0.125 to 0.125
- proj_weight: bfloat16 [2048, 2048], P(('seq', 'fsdp')), may hold values from -2 to 2
- router_weight: bfloat16 [2048, 64], P(('seq', 'fsdp')), may hold values from -0.15625 to 0.15625
- expert_up: bfloat16 [64, 2048, 2048], P(('seq', 'fsdp')), may hold values from -0.125 to 0.125
- expert_down: bfloat16 [64, 1024, 2048], P(('seq', 'fsdp')), may hold values from -6 to 6
Outputs:
- layer_out: bfloat16 [4, 1024, 2048], P('fsdp', 'seq')
- input_grad: bfloat16 [4, 1024, 2048], P('fsdp', 'seq')
- gains_grad: float32 [4, 2048], P(None, ('seq', 'fsdp'))
- qkv_grad: float32 [2048, 6144], P(('seq', 'fsdp'))
- proj_grad: float32 [2048, 2048], P(('seq', 'fsdp'))
- router_grad: float32 [2048, 64], P(('seq', 'fsdp'))
- up_grad: float32 [64, 2048, 2048], P(('seq', 'fsdp'))
- down_grad: float32 [64, 1024, 2048], P(('seq', 'fsdp'))
- balance_loss: float32 [1], replicated
The draws below stay inside these ranges and needn't reach their ends.
Inputs may be any that keep to these rules, and one draw needn't show every extreme that they name: `lengths`: valid tokens of each slot; some slot in every draw has all 1024. Each token names 8 different experts; within each aligned block of 128 positions of a slot (the rows of one device) no expert is named by more than 24 routes.
All inputs are finite; a program needn't handle non-finite values.
Results may differ from the reference program's by a relative error of at most 0.02.
Values may be sent and summed in bfloat16 or wider, within the bound.
A program may use at most 320 MiB of HBM per device.

```python
import math
import jax
import jax.numpy as jnp
import numpy as np
from jax import lax

D = 2048
HEADS = 16
HEAD_DIM = 128
EXPERTS = 64
FF = 1024
TOP = 8
SHARD = 128
SLOT_LEN = 1024
SLOTS = 4
SPLIT = 1
PFF = 1024
PIECES = 64
MOST = 24
QBLOCK = 512
N_SEQ = 8


def draw_lengths(key, part):
    base_lengths = jax.random.randint(jax.random.fold_in(key, 11), (SLOTS,), SLOT_LEN // 4, SLOT_LEN + 1)
    chosen = jax.random.randint(jax.random.fold_in(key, 12), (), 0, SLOTS)
    return jnp.where(jnp.arange(SLOTS) == chosen, SLOT_LEN, base_lengths).astype(jnp.int32)


def steps_of(stream_key, dims, split, low, largest):
    level = 1.0
    for dim, parts in split:
        steps = jax.random.uniform(jax.random.fold_in(jax.random.fold_in(stream_key, 6), dim), (parts,), jnp.float32, low / len(split), largest / len(split))
        level = level * jnp.repeat(jnp.exp(steps), dims[dim] // parts).reshape((-1,) + (1,) * (len(dims) - 1 - dim))
    return level


def shared_out(key, own, number, rows, number_of, top, reach, skew):
    sequence = jax.random.permutation(key, number_of)
    packed, usual = portions_of(number_of, rows * top, reach, skew, True), portions_of(number_of, rows * top, reach, skew, False)
    places = jnp.arange(number_of)

    def named(tallies, offset_by):
        used = int((tallies > 0).sum())
        fixed = max(1, used // 4)
        shifted = fixed + (places - fixed + offset_by * (used - fixed)) % max(1, number_of - fixed)
        return jnp.zeros((number_of,), jnp.int32).at[sequence[jnp.where(places < fixed, places, shifted)]].set(jnp.asarray(tallies, jnp.int32))

    tallies = jnp.where(number % 4 == 0, named(packed, number // 4), named(usual, number - number // 4 - 1))
    mixed = jax.random.permutation(jax.random.fold_in(own, 3), number_of)
    donor, receiver = mixed[0:number_of // 2 * 2:2], mixed[1:number_of // 2 * 2:2]
    slack = jnp.minimum(tallies[donor] - 1, reach - tallies[receiver]) // 2
    slack = jnp.where((donor == sequence[0]) | (receiver == sequence[0]) | (tallies[receiver] == 0), 0, jnp.maximum(slack, 0))
    shifted = jax.random.randint(jax.random.fold_in(own, 4), (number_of // 2,), 0, 1 << 20) % (slack + 1)
    tallies = tallies.at[donor].add(-shifted).at[receiver].add(shifted)
    items = jnp.searchsorted(jnp.cumsum(tallies), jnp.arange(rows * top), side="right").astype(jnp.int32)
    grid = items.reshape(top, rows).T
    grid = grid[jax.random.permutation(jax.random.fold_in(own, 1), rows)]
    offset_by = jax.random.randint(jax.random.fold_in(own, 2), (rows, 1), 0, top)
    return jnp.take_along_axis(grid, (jnp.arange(top)[None, :] + offset_by) % top, axis=1)


def portions_of(amount, total, bound, skew, full):
    loads = [(1 << 20) // math.isqrt(rank ** skew) + 1 for rank in range(1, amount + 1)]
    largest = bound if full else min(bound, max(-(-total // amount), total * loads[0] // sum(loads)))
    least = 1 if total - largest >= amount - 1 else 0
    given, rest = [largest] + [least] * (amount - 1), total - largest - least * (amount - 1)
    while rest > 0:
        free = [i for i in range(1, amount) if given[i] < largest] or [i for i in range(1, amount) if given[i] < bound]
        mass, budget = sum([loads[i] for i in free]), rest
        for i in free:
            addition = min(bound - given[i], max(1, budget * loads[i] // mass), rest)
            given[i] = given[i] + addition
            rest = rest - addition
    return np.array(given)


def noise(key, shape, deviation, most, shards=(), held_as=jnp.bfloat16):
    level = steps_of(key, shape, shards, -0.22, 0.18) if shards else 1.0
    result = jax.random.normal(key, shape, jnp.float32) * deviation * level
    return jnp.minimum(jnp.maximum(result, -most), most).astype(held_as)


def setup_inputs(seed: int = 0) -> dict:
    seeds = jax.random.split(jax.random.key(seed), 11)
    tokens = noise(seeds[0], (SLOTS, SLOT_LEN, D), 1.0, 6.0, ((0, 4), (1, 8)))
    cotangent = noise(seeds[1], (SLOTS, SLOT_LEN, D), 1.0, 6.0, ((0, 4), (1, 8)))
    lengths = draw_lengths(jax.random.fold_in(seeds[10], 71), 0)
    routes_keys = jax.random.split(jax.random.fold_in(seeds[3], 1), SLOTS * SLOT_LEN // SHARD)
    routes_turns = jax.random.permutation(jax.random.fold_in(seeds[3], 3), SLOTS * SLOT_LEN // SHARD)
    routes = jax.vmap(lambda own, number: shared_out(jax.random.fold_in(seeds[3], 2), own, number, SHARD, EXPERTS, TOP, MOST, 1))(routes_keys, routes_turns).reshape((SLOTS, SLOT_LEN, TOP))
    norm_gains = jnp.clip(1.0 + 0.1 * jax.random.normal(seeds[4], (4, D), jnp.float32), 0.5, 1.5).astype(jnp.bfloat16)
    qkv_weight = noise(seeds[5], (D, 3 * D), D ** -0.5, 0.125, ((0, 32),))
    proj_weight = noise(seeds[6], (D, D), (max(1, D // 256)) ** -0.5, 2.0, ((0, 32),))
    router_weight = noise(seeds[7], (D, EXPERTS), (0.5 / D ** 0.5), 0.15625, ((0, 32),))
    expert_up = noise(seeds[8], (PIECES, D, 2 * PFF), D ** -0.5, 0.125, ((0, 32),))
    expert_down = noise(seeds[9], (PIECES, PFF, D), (32.0 / FF ** 0.5), 6.0, ((0, 32),))
    return dict(tokens=tokens, cotangent=cotangent, lengths=lengths, routes=routes, norm_gains=norm_gains, qkv_weight=qkv_weight, proj_weight=proj_weight, router_weight=router_weight, expert_up=expert_up, expert_down=expert_down)


epsilon = 1e-06
rope_base = 10000.0

@jax.custom_vjp
def low(v):
    return lax.optimization_barrier(v.astype(jnp.bfloat16)).astype(jnp.float32)

@jax.custom_vjp
def low_back(v):
    return v

def low_keep(v):
    return (low(v), None)

def low_pass(kept, grad):
    return (grad,)

def back_keep(v):
    return (v, None)

def back_low(kept, grad):
    return (low(grad),)
low.defvjp(low_keep, low_pass)
low_back.defvjp(back_keep, back_low)

def rms_scale(values, gain):
    return values * lax.rsqrt(lax.optimization_barrier(jnp.mean(values * values, axis=-1, keepdims=True)) + epsilon) * gain

def rotate(values, positions):
    half_dim = values.shape[-1] // 2
    frequency = rope_base ** (-jnp.arange(half_dim, dtype=jnp.float32) * 2.0 / values.shape[-1])
    angles = positions.astype(jnp.float32)[:, None] * frequency[None, :]
    cosine = jnp.cos(angles)[:, None, :]
    sine_part = jnp.sin(angles)[:, None, :]
    first_half = values[..., :half_dim]
    second_half = values[..., half_dim:]
    return jnp.concatenate([first_half * cosine - second_half * sine_part, second_half * cosine + first_half * sine_part], axis=-1)

def front(raw, gain_query, gain_key, positions, head_count):
    model_width = raw.shape[1] // 3
    rows_here = raw.shape[0]
    query_part = rms_scale(raw[:, :model_width], gain_query).reshape(rows_here, head_count, -1)
    key_part = rms_scale(raw[:, model_width:2 * model_width], gain_key).reshape(rows_here, head_count, -1)
    value_part = raw[:, 2 * model_width:].reshape(rows_here, head_count, -1)
    return (rotate(query_part, positions), rotate(key_part, positions), value_part)

def forward(tokens, norm_gains, qkv_weight, proj_weight, router_weight, expert_up, expert_down, lengths, routes):
    up_table = expert_up.reshape(EXPERTS, SPLIT, D, 2 * PFF)
    down_table = expert_down.reshape(EXPERTS, SPLIT, PFF, D)
    positions = jnp.arange(SLOT_LEN, dtype=jnp.int32)
    scaling = HEAD_DIM ** (-0.5)
    highest = lax.Precision.HIGHEST

    def expert_block(inputs):
        block_rows, block_routes, block_gates = inputs
        flat_routes = block_routes.reshape(-1)
        flat_match = (flat_routes[:, None] == jnp.arange(EXPERTS, dtype=jnp.int32)[None, :]).astype(jnp.int32)
        earlier = jnp.cumsum(flat_match, axis=0) - flat_match
        slot_index = (flat_routes * MOST + lax.optimization_barrier(jnp.sum(earlier * flat_match, axis=1))).astype(jnp.int32)
        owner_row = jnp.arange(SHARD * TOP, dtype=jnp.int32) // TOP
        fill_table = jnp.full((EXPERTS * MOST,), SHARD, dtype=jnp.int32).at[slot_index].set(owner_row)
        padded_rows = jnp.concatenate([block_rows, jnp.zeros((1, D), jnp.float32)], axis=0)
        slot_rows = padded_rows[fill_table].reshape(EXPERTS, 1, MOST, D)
        copies = low_back(jnp.broadcast_to(slot_rows, (EXPERTS, SPLIT, MOST, D)))
        hidden = low_back(jnp.einsum('epmd,epdf->epmf', copies, up_table, precision=highest))
        activation = low(jax.nn.silu(hidden[..., :PFF]) * hidden[..., PFF:])
        pieces = low_back(low(jnp.einsum('epmf,epfd->epmd', activation, down_table, precision=highest)))
        combined = lax.optimization_barrier(jnp.sum(pieces, axis=1)).reshape(EXPERTS * MOST, D)
        route_out = combined[slot_index].reshape(SHARD, TOP, D)
        return lax.optimization_barrier(jnp.sum(block_gates[:, :, None] * route_out, axis=1))

    def one_slot(inputs):
        slot_tokens, slot_length, slot_routes = inputs
        key_valid = positions < slot_length
        row_valid = key_valid.astype(jnp.float32)
        normed_one = low(rms_scale(slot_tokens, norm_gains[0]))
        qkv_raw = low_back(jnp.dot(normed_one, qkv_weight, precision=highest))
        rotated_query, rotated_key, value_heads = front(qkv_raw, norm_gains[1], norm_gains[2], positions, HEADS)
        queries = low_back(low(rotated_query))
        keys_all = low_back(low(rotated_key))
        values_all = low_back(low(value_heads))

        def attend_block(query_block):
            raw_scores = low_back(jnp.einsum('qhd,khd->hqk', query_block, keys_all, precision=highest))
            scores = jnp.where(key_valid[None, None, :], raw_scores * scaling, -1e+30)
            weights = low(jax.nn.softmax(scores, axis=-1))
            return jnp.einsum('hqk,khd->qhd', weights, values_all, precision=highest)
        blocked = queries.reshape(SLOT_LEN // QBLOCK, QBLOCK, HEADS, HEAD_DIM)
        attended = lax.map(jax.checkpoint(attend_block), blocked).reshape(SLOT_LEN, D)
        attended = low_back(low(attended))
        resid_mid = slot_tokens + low_back(jnp.dot(attended, proj_weight, precision=highest))
        normed_two = low(rms_scale(resid_mid, norm_gains[3]))
        router_probs = jax.nn.softmax(jnp.dot(normed_two, router_weight, precision=highest), axis=-1)
        prob_sum = lax.optimization_barrier(jnp.sum(router_probs * row_valid[:, None], axis=0))
        gate_values = jnp.take_along_axis(router_probs, slot_routes, axis=1)
        mixed = lax.map(jax.checkpoint(expert_block), (normed_two.reshape(N_SEQ, SHARD, D), slot_routes.reshape(N_SEQ, SHARD, TOP), gate_values.reshape(N_SEQ, SHARD, TOP)))
        return (resid_mid + mixed.reshape(SLOT_LEN, D), prob_sum)
    return lax.map(jax.checkpoint(one_slot), (tokens, lengths, routes))

def reference(tokens, cotangent, lengths, routes, norm_gains, qkv_weight, proj_weight, router_weight, expert_up, expert_down):
    positions = jnp.arange(SLOT_LEN, dtype=jnp.int32)
    valid = (positions[None, :] < lengths[:, None]).astype(jnp.float32)
    valid_total = jnp.sum(valid)
    route_match = (routes[..., None] == jnp.arange(EXPERTS, dtype=jnp.int32)).astype(jnp.float32)
    counts = lax.optimization_barrier(jnp.sum(route_match * valid[:, :, None, None], axis=(0, 1, 2)))
    fraction = counts / (TOP * valid_total)

    def objective(tokens_in, gains_in, qkv_in, proj_in, router_in, up_in, down_in):
        outputs, prob_sums = forward(tokens_in, gains_in, qkv_in, proj_in, router_in, up_in, down_in, lengths, routes)
        loss_value = EXPERTS * jnp.sum(fraction * lax.optimization_barrier(jnp.sum(prob_sums, axis=0)) / valid_total)
        return (outputs, loss_value.reshape(1))
    primal_values = (tokens.astype(jnp.float32), norm_gains.astype(jnp.float32), qkv_weight.astype(jnp.float32), proj_weight.astype(jnp.float32), router_weight.astype(jnp.float32), expert_up.astype(jnp.float32), expert_down.astype(jnp.float32))
    results, pullback = jax.vjp(objective, *primal_values)
    outputs, loss_value = results
    grads = pullback((cotangent.astype(jnp.float32) * valid[:, :, None], jnp.ones((1,), jnp.float32)))
    return (outputs.astype(jnp.bfloat16), grads[0].astype(jnp.bfloat16), grads[1], grads[2], grads[3], grads[4], grads[5], grads[6], loss_value)
```

```python
import functools

import jax
import jax.numpy as jnp
from jax import lax
from jax.experimental import pallas as pl
from jax.experimental.pallas import tpu as pltpu
from jax.sharding import PartitionSpec as P

HEADS = 16
FF = 1024

epsilon = 1e-06
rope_base = 10000.0
MESH = pl.DeviceIdType.MESH
BF = jnp.bfloat16
F32 = jnp.float32


def dot(a, b, ca, cb):
    return lax.dot_general(a, b, (((ca,), (cb,)), ((), ())), preferred_element_type=F32)


def push_kernel(n_seq, n_fsdp, scope, gather, src, dst, send_sem, recv_sem, own_sem):
    me_s, me_f = lax.axis_index("seq"), lax.axis_index("fsdp")
    n = n_seq * n_fsdp if scope == "all" else n_seq
    me = me_s * n_fsdp + me_f if scope == "all" else me_s

    def where(index):
        if scope == "all":
            return (index // n_fsdp, index % n_fsdp)
        return (index, me_f)

    barrier = pltpu.get_barrier_semaphore()

    def greet(i, carry):
        pl.semaphore_signal(barrier, inc=1, device_id=where((me + i) % n), device_id_type=MESH)
        return carry

    lax.fori_loop(1, n, greet, 0)
    own = pltpu.make_async_copy(src if gather else src.at[me], dst.at[me], own_sem)
    own.start()
    pl.semaphore_wait(barrier, n - 1)

    def copy_to(other):
        return pltpu.make_async_remote_copy(
            src_ref=src if gather else src.at[other],
            dst_ref=dst.at[me],
            send_sem=send_sem.at[other],
            recv_sem=recv_sem.at[me],
            device_id=where(other),
            device_id_type=MESH,
        )

    def copy_from(other):
        return pltpu.make_async_remote_copy(
            src_ref=src if gather else src.at[other],
            dst_ref=dst.at[other],
            send_sem=send_sem.at[other],
            recv_sem=recv_sem.at[other],
            device_id=where(other),
            device_id_type=MESH,
        )

    def send(i, carry):
        copy_to((me + i) % n).start()
        return carry

    lax.fori_loop(1, n, send, 0)

    def finish(i, carry):
        other = (me + i) % n
        copy_from(other).wait_recv()
        copy_to(other).wait_send()
        return carry

    lax.fori_loop(1, n, finish, 0)
    own.wait()


def push(block, n_seq, n_fsdp, scope, gather, collective_id):
    n = n_seq * n_fsdp if scope == "all" else n_seq
    shape = (n,) + (block.shape if gather else block.shape[1:])
    return pl.pallas_call(
        functools.partial(push_kernel, n_seq, n_fsdp, scope, gather),
        out_shape=jax.ShapeDtypeStruct(shape, block.dtype),
        in_specs=[pl.BlockSpec(memory_space=pltpu.VMEM)],
        out_specs=pl.BlockSpec(memory_space=pltpu.VMEM),
        scratch_shapes=[
            pltpu.SemaphoreType.DMA((n,)),
            pltpu.SemaphoreType.DMA((n,)),
            pltpu.SemaphoreType.DMA,
        ],
        compiler_params=pltpu.CompilerParams(collective_id=collective_id, has_side_effects=True),
        name="push_" + scope,
    )(block)


def rows_of(flat, multiple):
    size = flat.shape[0]
    whole = -(-size // (multiple * 128)) * multiple * 128
    return jnp.pad(flat, (0, whole - size)).reshape(-1, 128)


def softmax_columns(k, q, length, scaling):
    scores = dot(k, q, 1, 1) * scaling
    key = lax.broadcasted_iota(jnp.int32, scores.shape, 0)
    scores = jnp.where(key < length, scores, -1e30)
    weights = jnp.exp(scores - jnp.max(scores, axis=0, keepdims=True))
    return weights / jnp.sum(weights, axis=0, keepdims=True)


def attend_kernel(scaling, length, q_ref, k_ref, v_ref, o_ref):
    probs = softmax_columns(k_ref[...], q_ref[...], length[0], scaling).astype(BF)
    o_ref[...] = dot(v_ref[...], probs, 0, 0).T.astype(BF)


def attend(query, key, value, length, block):
    slot_len, width = query.shape
    hd = 128
    return pl.pallas_call(
        functools.partial(attend_kernel, hd ** (-0.5)),
        out_shape=jax.ShapeDtypeStruct(query.shape, BF),
        grid_spec=pltpu.PrefetchScalarGridSpec(
            num_scalar_prefetch=1,
            grid=(width // hd, slot_len // block),
            in_specs=[
                pl.BlockSpec((block, hd), lambda h, i, n: (i, h)),
                pl.BlockSpec((slot_len, hd), lambda h, i, n: (0, h)),
                pl.BlockSpec((slot_len, hd), lambda h, i, n: (0, h)),
            ],
            out_specs=pl.BlockSpec((block, hd), lambda h, i, n: (i, h)),
        ),
        name="attend",
    )(length, query, key, value)


def attend_back_kernel(
    scaling, length, q_ref, k_ref, v_ref, g_ref, dq_ref, dk_ref, dv_ref, dk_sum, dv_sum
):
    step = pl.program_id(1)

    @pl.when(step == 0)
    def _():
        dk_sum[...] = jnp.zeros_like(dk_sum)
        dv_sum[...] = jnp.zeros_like(dv_sum)

    q, k, v, g = q_ref[...], k_ref[...], v_ref[...], g_ref[...]
    probs = softmax_columns(k, q, length[0], scaling)
    dv_sum[...] += dot(probs.astype(BF), g, 1, 0)
    weights_grad = dot(v, g, 1, 1)
    inner = jnp.sum(probs * weights_grad, axis=0, keepdims=True)
    score_grad = (probs * (weights_grad - inner) * scaling).astype(BF)
    dk_sum[...] += dot(score_grad, q, 1, 0)
    dq_ref[...] = dot(k, score_grad, 0, 0).T.astype(BF)

    @pl.when(step == pl.num_programs(1) - 1)
    def _():
        dk_ref[...] = dk_sum[...].astype(BF)
        dv_ref[...] = dv_sum[...].astype(BF)


def attend_back(query, key, value, grad, length, block):
    slot_len, width = query.shape
    hd = 128
    rows = pl.BlockSpec((block, hd), lambda h, i, n: (i, h))
    full = pl.BlockSpec((slot_len, hd), lambda h, i, n: (0, h))
    return pl.pallas_call(
        functools.partial(attend_back_kernel, hd ** (-0.5)),
        out_shape=[jax.ShapeDtypeStruct(query.shape, BF)] * 3,
        grid_spec=pltpu.PrefetchScalarGridSpec(
            num_scalar_prefetch=1,
            grid=(width // hd, slot_len // block),
            in_specs=[rows, full, full, rows],
            out_specs=[rows, full, full],
            scratch_shapes=[pltpu.VMEM((slot_len, hd), F32), pltpu.VMEM((slot_len, hd), F32)],
        ),
        name="attend_back",
    )(length, query, key, value, grad)


def rope_tables(positions, head_dim):
    half = head_dim // 2
    frequency = rope_base ** (-jnp.arange(half, dtype=F32) * 2.0 / head_dim)
    angles = positions.astype(F32)[:, None] * frequency[None, :]
    return jnp.cos(angles)[:, None, :], jnp.sin(angles)[:, None, :]


def rotate(values, cosine, sine):
    half = values.shape[-1] // 2
    a, b = values[..., :half], values[..., half:]
    return jnp.concatenate([a * cosine - b * sine, b * cosine + a * sine], axis=-1)


def rotate_back(values, cosine, sine):
    return rotate(values, cosine, -sine)


def places(block_routes, experts, capacity):
    count = block_routes.shape[0]
    match = (block_routes[:, :, None] == experts[None, None, :]).astype(F32).sum(axis=1)
    lower = jnp.tril(jnp.ones((count, count), BF), -1)
    rank = dot(lower, match.astype(BF), 1, 0)
    place = jnp.arange(capacity, dtype=F32)
    return match[:, :, None] * (rank[:, :, None] == place[None, None, :]).astype(F32)


def local(
    tokens,
    cotangent,
    lengths,
    routes,
    norm_gains,
    qkv_weight,
    proj_weight,
    router_weight,
    expert_up,
    expert_down,
):
    n_seq, n_fsdp = lax.axis_size("seq"), lax.axis_size("fsdp")
    n_dev = n_seq * n_fsdp
    me_s, me_f = lax.axis_index("seq"), lax.axis_index("fsdp")
    shard_len, width = tokens.shape[1], tokens.shape[2]
    slot_len = shard_len * n_seq
    experts = router_weight.shape[1]
    top_count = routes.shape[2]
    capacity = 3 * shard_len * top_count // (2 * experts)
    piece_ff = expert_down.shape[1]
    pieces_dev = expert_up.shape[0]
    split = FF // piece_ff
    head_dim = width // HEADS
    head_width = width // n_seq
    heads_dev = HEADS // n_seq
    owned = qkv_weight.shape[0]
    block = min(512, slot_len)
    length = lax.dynamic_slice_in_dim(lengths, me_f, 1)
    valid_total = jnp.sum(lengths).astype(F32).reshape(1)
    positions = me_s * shard_len + jnp.arange(shard_len, dtype=jnp.int32)
    row_valid = (positions < length[0]).astype(F32)
    local_routes = routes[0]
    push_all = functools.partial(push, n_seq=n_seq, n_fsdp=n_fsdp, scope="all")
    push_seq = functools.partial(push, n_seq=n_seq, n_fsdp=n_fsdp, scope="seq")

    gain_size, router_size = norm_gains.size, router_weight.size
    pieces = [norm_gains.reshape(-1), router_weight.reshape(-1), local_routes.astype(BF).reshape(-1)]
    small = push_all(rows_of(jnp.concatenate(pieces), 16), gather=True, collective_id=0)
    small = small.reshape(n_dev, -1)
    gains = small[:, :gain_size].reshape(n_dev, 4, owned).swapaxes(0, 1).reshape(4, width).astype(F32)
    router = small[:, gain_size : gain_size + router_size].reshape(width, experts)
    all_routes = small[:, gain_size + router_size :][:, : shard_len * top_count]
    all_routes = all_routes.reshape(n_seq, n_fsdp, shard_len, top_count).astype(jnp.int32)

    slot_tokens = lax.all_gather(tokens[0], "seq", axis=0, tiled=True)
    qkv_parts = qkv_weight.reshape(owned, 3, n_seq, head_width)
    qkv_parts = lax.all_to_all(qkv_parts, "seq", split_axis=2, concat_axis=0, tiled=True)
    qkv_parts = qkv_parts.reshape(n_seq, owned, 3 * head_width)
    qkv_local = lax.all_gather(qkv_parts, "fsdp", axis=1).reshape(width, 3 * head_width)
    full_proj = lax.all_gather(proj_weight, ("seq", "fsdp"), axis=0, tiled=True)
    masked_low = jnp.where(row_valid[:, None] > 0, cotangent[0], jnp.zeros((), BF))
    plane_masked = lax.all_gather(masked_low, "fsdp", axis=0, tiled=True)

    plane_routes = lax.dynamic_index_in_dim(all_routes, me_s, 0, keepdims=False)
    piece_ids = (jnp.arange(n_seq)[:, None] * n_fsdp + me_f) * pieces_dev + jnp.arange(pieces_dev)
    plane_experts = (piece_ids // split).reshape(-1).astype(jnp.int32)
    plane_hot = jax.vmap(lambda r: places(r, plane_experts, capacity))(plane_routes)
    block_row = jnp.arange(n_fsdp * shard_len, dtype=F32).reshape(n_fsdp, shard_len)
    plane_index = jnp.einsum("ft,ftec->efc", block_row, plane_hot, precision=lax.Precision.HIGHEST)
    plane_index = plane_index.astype(jnp.int32).reshape(n_seq, pieces_dev, n_fsdp, capacity)
    gather_hot = plane_hot.reshape(n_fsdp, shard_len, n_seq, pieces_dev, capacity).astype(BF)

    def dispatch(plane_rows, piece):
        index = plane_index[:, piece].reshape(-1)
        rows = plane_rows[index].reshape(n_seq, n_fsdp * capacity, width)
        return lax.all_to_all(rows, "seq", split_axis=0, concat_axis=0, tiled=True).reshape(-1, width)

    def combine(pieces_rows):
        total = 0.0
        for piece, rows in enumerate(pieces_rows):
            back = lax.all_to_all(
                rows.reshape(n_seq, n_fsdp * capacity, width), "seq", split_axis=0, concat_axis=0, tiled=True
            )
            back = back.reshape(n_seq, n_fsdp, capacity, width)
            total = total + jnp.einsum(
                "ftsc,sfcd->ftd", gather_hot[:, :, :, piece], back, preferred_element_type=F32
            )
        parts = lax.all_to_all(total.astype(BF), "fsdp", split_axis=0, concat_axis=0, tiled=True)
        return jnp.sum(parts.astype(F32), axis=0)

    def rms(values):
        return lax.rsqrt(jnp.mean(values * values, axis=-1, keepdims=True) + epsilon)

    slot_f32 = slot_tokens.astype(F32)
    normed_one = (slot_f32 * rms(slot_f32) * gains[0]).astype(BF)
    raw = jnp.dot(normed_one, qkv_local, preferred_element_type=F32)
    raw_query, raw_key, raw_value = jnp.split(raw, 3, axis=1)

    def seq_sums(first, second, collective_id):
        sums = jnp.stack([jnp.sum(first, axis=-1), jnp.sum(second, axis=-1)])
        every = push_seq(sums.reshape(-1, 128), gather=True, collective_id=collective_id)
        total = jnp.sum(every, axis=0).reshape(2, slot_len)
        return total[0][:, None], total[1][:, None]

    query_square, key_square = seq_sums(raw_query * raw_query, raw_key * raw_key, 1)
    query_rms = lax.rsqrt(query_square / width + epsilon)
    key_rms = lax.rsqrt(key_square / width + epsilon)
    own_gains = lax.dynamic_slice_in_dim(gains, me_s * head_width, head_width, 1)
    cosine, sine = rope_tables(jnp.arange(slot_len, dtype=jnp.int32), head_dim)

    def heads(values):
        return values.reshape(slot_len, heads_dev, head_dim)

    query = rotate(heads(raw_query * query_rms * own_gains[1]), cosine, sine)
    key = rotate(heads(raw_key * key_rms * own_gains[2]), cosine, sine)
    query = query.astype(BF).reshape(slot_len, head_width)
    key = key.astype(BF).reshape(slot_len, head_width)
    value = raw_value.astype(BF)
    attended = attend(query, key, value, length, block)
    attended_tok = lax.all_to_all(attended, "seq", split_axis=0, concat_axis=1, tiled=True)

    resid_in = tokens[0].astype(F32)
    resid_mid = resid_in + jnp.dot(attended_tok, full_proj, preferred_element_type=F32)
    mid_rms = rms(resid_mid)
    normed_two = (resid_mid * mid_rms * gains[3]).astype(BF)
    plane_rows = lax.all_gather(normed_two, "fsdp", axis=0, tiled=True)
    router_probs = jax.nn.softmax(jnp.dot(normed_two, router, preferred_element_type=F32), axis=-1)

    own_hot = places(local_routes, jnp.arange(experts, dtype=jnp.int32), capacity)
    gate_slot = jnp.sum(own_hot * router_probs[:, :, None], axis=0)
    gate_send = jnp.broadcast_to(gate_slot[:, None], (experts, split, capacity))
    gate_send = gate_send.reshape(n_dev, pieces_dev * capacity)
    gate_pad = -pieces_dev * capacity % 1024
    gate_send = jnp.pad(gate_send, ((0, 0), (0, gate_pad))).reshape(n_dev, -1, 128)
    gate_recv = push_all(gate_send, gather=False, collective_id=2)
    gate_recv = gate_recv.reshape(n_dev, -1)[:, : pieces_dev * capacity]
    gate_recv = gate_recv.reshape(n_dev, pieces_dev, capacity)

    outs, backs, gate_backs, up_grads, down_grads = [], [], [], [], []
    for piece in range(pieces_dev):
        gate_rows = gate_recv[:, piece].reshape(-1, 1)
        cot_rows = dispatch(plane_masked, piece)
        rows = dispatch(plane_rows, piece)
        up, down = expert_up[piece], expert_down[piece]
        hidden = jnp.dot(rows, up, preferred_element_type=F32)
        gate_pre, up_pre = hidden[:, :piece_ff], hidden[:, piece_ff:]
        sigmoid = jax.nn.sigmoid(gate_pre)
        activation = (gate_pre * sigmoid * up_pre).astype(BF)
        piece_out = jnp.dot(activation, down, preferred_element_type=F32).astype(BF).astype(F32)
        outs.append((piece_out * gate_rows).astype(BF))
        cot_f32 = cot_rows.astype(F32)
        gate_backs.append(jnp.sum(piece_out * cot_f32, axis=-1).reshape(n_dev, capacity))
        out_grad = (cot_f32 * gate_rows).astype(BF)
        act_grad = dot(out_grad, down, 1, 1)
        down_grads.append(dot(activation, out_grad, 0, 0))
        gate_grad = act_grad * up_pre * sigmoid * (1.0 + gate_pre * (1.0 - sigmoid))
        up_part = act_grad * gate_pre * sigmoid
        hidden_grad = jnp.concatenate([gate_grad, up_part], axis=-1).astype(BF)
        up_grads.append(dot(rows, hidden_grad, 0, 0))
        backs.append(dot(hidden_grad, up, 1, 1).astype(BF))
    up_grad = jnp.stack(up_grads)
    down_grad = jnp.stack(down_grads)
    normed_two_grad = combine(backs)
    layer_out = (resid_mid + combine(outs)).astype(BF)[None]

    counts = jnp.sum(
        (all_routes[..., None] == jnp.arange(experts, dtype=jnp.int32))
        * (
            jnp.arange(slot_len, dtype=jnp.int32).reshape(n_seq, 1, shard_len)
            < lengths[None, :, None]
        )[..., None, None].astype(F32),
        axis=(0, 1, 2, 3),
    )
    fraction = counts / (top_count * valid_total)
    back_send = jnp.stack(gate_backs, axis=1).reshape(n_dev, pieces_dev * capacity)
    back_send = jnp.pad(back_send, ((0, 0), (0, gate_pad))).reshape(n_dev, -1, 128)
    back_recv = push_all(back_send, gather=False, collective_id=3).reshape(n_dev, -1)
    slot_gates_grad = back_recv[:, : pieces_dev * capacity].reshape(experts, split, capacity).sum(axis=1)
    probs_grad = (
        jnp.sum(own_hot * slot_gates_grad[None], axis=2)
        + (experts * fraction / valid_total)[None, :] * row_valid[:, None]
    )
    logits_grad = router_probs * (
        probs_grad - jnp.sum(router_probs * probs_grad, axis=-1, keepdims=True)
    )
    router_term = lax.dot_general(
        normed_two.astype(F32), logits_grad, (((0,), (0,)), ((), ())), precision=lax.Precision.HIGHEST
    )
    normed_two_grad = normed_two_grad + lax.dot_general(
        logits_grad, router.astype(F32), (((1,), (1,)), ((), ())), precision=lax.Precision.HIGHEST
    )

    def rms_back(values, scale, gain, grad):
        weighted = gain * grad
        mean = jnp.mean(weighted * values, axis=-1, keepdims=True)
        return scale * weighted - values * (scale * scale * scale) * mean, jnp.sum(
            grad * values * scale, axis=0
        )

    mid_part, gain_three = rms_back(resid_mid, mid_rms, gains[3], normed_two_grad)
    mid_grad = masked_low.astype(F32) + mid_part
    branch_grad = mid_grad.astype(BF)
    slot_branch = lax.all_gather(branch_grad, "seq", axis=0, tiled=True)
    attended_grad = dot(branch_grad, full_proj, 1, 1).astype(BF)
    heads_grad = lax.all_to_all(attended_grad, "seq", split_axis=1, concat_axis=0, tiled=True)
    query_grad, key_grad, value_grad = attend_back(query, key, value, heads_grad, length, block)

    query_in = rotate_back(heads(query_grad.astype(F32)), cosine, sine).reshape(slot_len, head_width)
    key_in = rotate_back(heads(key_grad.astype(F32)), cosine, sine).reshape(slot_len, head_width)
    query_weighted, key_weighted = query_in * own_gains[1], key_in * own_gains[2]
    query_dot, key_dot = seq_sums(query_weighted * raw_query, key_weighted * raw_key, 4)
    raw_query_grad = query_rms * query_weighted - raw_query * (query_rms**3) * (query_dot / width)
    raw_key_grad = key_rms * key_weighted - raw_key * (key_rms**3) * (key_dot / width)
    gain_one = jnp.sum(query_in * raw_query * query_rms, axis=0)
    gain_two = jnp.sum(key_in * raw_key * key_rms, axis=0)
    raw_grad = jnp.concatenate(
        [raw_query_grad.astype(BF), raw_key_grad.astype(BF), value_grad], axis=1
    )
    one_part = dot(raw_grad, qkv_local, 1, 1).astype(BF)
    one_grad = lax.psum_scatter(one_part, "seq", scatter_dimension=0, tiled=True).astype(F32)
    input_part, gain_zero = rms_back(resid_in, rms(resid_in), gains[0], one_grad)
    input_grad = (mid_grad + input_part).astype(BF)[None]

    qkv_part = dot(normed_one, raw_grad, 0, 0).astype(BF)
    qkv_part = qkv_part.reshape(n_seq, n_fsdp, owned, 3 * head_width)
    qkv_part = lax.psum_scatter(qkv_part, "fsdp", scatter_dimension=1, tiled=True)
    qkv_part = qkv_part.reshape(n_seq, owned, 3, head_width)
    qkv_part = lax.all_to_all(qkv_part, "seq", split_axis=0, concat_axis=0, tiled=True)
    qkv_grad = qkv_part.transpose(1, 2, 0, 3).reshape(owned, 3 * width).astype(F32)
    proj_part = dot(attended, slot_branch, 0, 0).astype(BF)
    proj_grad = lax.psum_scatter(proj_part, "fsdp", scatter_dimension=0, tiled=True).astype(F32)

    prob_part = jnp.sum(router_probs * row_valid[:, None], axis=0)
    heads_gain = jnp.stack([gain_one, gain_two]).reshape(2, n_fsdp, owned).swapaxes(0, 1)
    same_seq = (jnp.arange(n_seq) == me_s).astype(F32)[:, None, None, None]
    heads_gain = (same_seq * heads_gain[None]).reshape(n_dev, 2 * owned)
    last = jnp.concatenate(
        [
            router_term.reshape(n_dev, owned * experts),
            gain_zero.reshape(n_dev, owned),
            gain_three.reshape(n_dev, owned),
            heads_gain,
            jnp.broadcast_to(prob_part[None], (n_dev, experts)),
        ],
        axis=1,
    )
    last_size = last.shape[1]
    last = jnp.pad(last, ((0, 0), (0, -last_size % 1024))).reshape(n_dev, -1, 128)
    last = push_all(last, gather=False, collective_id=5)
    last = jnp.sum(last, axis=0).reshape(-1)
    cut = owned * experts
    router_grad = last[:cut].reshape(owned, experts)
    gains_grad = jnp.stack(
        [
            last[cut : cut + owned],
            last[cut + 2 * owned : cut + 3 * owned],
            last[cut + 3 * owned : cut + 4 * owned],
            last[cut + owned : cut + 2 * owned],
        ]
    )
    prob_total = last[cut + 4 * owned : cut + 4 * owned + experts]
    loss_value = (experts * jnp.sum(fraction * prob_total / valid_total)).reshape(1)
    return (
        layer_out,
        input_grad,
        gains_grad,
        qkv_grad,
        proj_grad,
        router_grad,
        up_grad,
        down_grad,
        loss_value,
    )


def solution(mesh):
    rows = P(("seq", "fsdp"), None)
    return jax.shard_map(
        local,
        mesh=mesh,
        in_specs=(
            P("fsdp", "seq", None),
            P("fsdp", "seq", None),
            P(),
            P("fsdp", "seq", None),
            P(None, ("seq", "fsdp")),
            rows,
            rows,
            rows,
            P(("seq", "fsdp"), None, None),
            P(("seq", "fsdp"), None, None),
        ),
        out_specs=(
            P("fsdp", "seq", None),
            P("fsdp", "seq", None),
            P(None, ("seq", "fsdp")),
            rows,
            rows,
            rows,
            P(("seq", "fsdp"), None, None),
            P(("seq", "fsdp"), None, None),
            P(),
        ),
        check_vma=False,
    )
```

```python
import functools

import jax
import jax.numpy as jnp
from jax import lax
from jax.experimental import pallas as pl
from jax.experimental.pallas import tpu as pltpu
from jax.sharding import PartitionSpec as P

HEADS = 16
FF = 1024

epsilon = 1e-06
rope_base = 10000.0
MESH = pl.DeviceIdType.MESH
BF = jnp.bfloat16
F32 = jnp.float32


def dot(a, b, ca, cb):
    return lax.dot_general(a, b, (((ca,), (cb,)), ((), ())), preferred_element_type=F32)


def push_kernel(n_seq, n_fsdp, scope, gather, src, dst, send_sem, recv_sem, own_sem):
    me_s, me_f = lax.axis_index("seq"), lax.axis_index("fsdp")
    n = n_seq * n_fsdp if scope == "all" else n_seq
    me = me_s * n_fsdp + me_f if scope == "all" else me_s

    def where(index):
        if scope == "all":
            return (index // n_fsdp, index % n_fsdp)
        return (index, me_f)

    barrier = pltpu.get_barrier_semaphore()

    def greet(i, carry):
        pl.semaphore_signal(barrier, inc=1, device_id=where((me + i) % n), device_id_type=MESH)
        return carry

    lax.fori_loop(1, n, greet, 0)
    own = pltpu.make_async_copy(src if gather else src.at[me], dst.at[me], own_sem)
    own.start()
    pl.semaphore_wait(barrier, n - 1)

    def copy_to(other):
        return pltpu.make_async_remote_copy(
            src_ref=src if gather else src.at[other],
            dst_ref=dst.at[me],
            send_sem=send_sem.at[other],
            recv_sem=recv_sem.at[me],
            device_id=where(other),
            device_id_type=MESH,
        )

    def copy_from(other):
        return pltpu.make_async_remote_copy(
            src_ref=src if gather else src.at[other],
            dst_ref=dst.at[other],
            send_sem=send_sem.at[other],
            recv_sem=recv_sem.at[other],
            device_id=where(other),
            device_id_type=MESH,
        )

    def send(i, carry):
        copy_to((me + i) % n).start()
        return carry

    lax.fori_loop(1, n, send, 0)

    def finish(i, carry):
        other = (me + i) % n
        copy_from(other).wait_recv()
        copy_to(other).wait_send()
        return carry

    lax.fori_loop(1, n, finish, 0)
    own.wait()


def push(block, n_seq, n_fsdp, scope, gather, collective_id):
    n = n_seq * n_fsdp if scope == "all" else n_seq
    shape = (n,) + (block.shape if gather else block.shape[1:])
    return pl.pallas_call(
        functools.partial(push_kernel, n_seq, n_fsdp, scope, gather),
        out_shape=jax.ShapeDtypeStruct(shape, block.dtype),
        in_specs=[pl.BlockSpec(memory_space=pltpu.VMEM)],
        out_specs=pl.BlockSpec(memory_space=pltpu.VMEM),
        scratch_shapes=[
            pltpu.SemaphoreType.DMA((n,)),
            pltpu.SemaphoreType.DMA((n,)),
            pltpu.SemaphoreType.DMA,
        ],
        compiler_params=pltpu.CompilerParams(collective_id=collective_id, has_side_effects=True),
        name="push_" + scope,
    )(block)


def rows_of(flat, multiple):
    size = flat.shape[0]
    whole = -(-size // (multiple * 128)) * multiple * 128
    return jnp.pad(flat, (0, whole - size)).reshape(-1, 128)


def remote(src, dst, send_sem, recv_sem, device):
    return pltpu.make_async_remote_copy(
        src_ref=src,
        dst_ref=dst,
        send_sem=send_sem,
        recv_sem=recv_sem,
        device_id=device,
        device_id_type=MESH,
    )


def greet_all(n_seq, n_fsdp):
    me_s, me_f = lax.axis_index("seq"), lax.axis_index("fsdp")
    n = n_seq * n_fsdp
    me = me_s * n_fsdp + me_f
    barrier = pltpu.get_barrier_semaphore()

    def greet(i, carry):
        other = (me + i) % n
        pl.semaphore_signal(
            barrier, inc=1, device_id=(other // n_fsdp, other % n_fsdp), device_id_type=MESH
        )
        return carry

    lax.fori_loop(1, n, greet, 0)
    pl.semaphore_wait(barrier, n - 1)


def greet_lines(n_seq, n_fsdp):
    me_s, me_f = lax.axis_index("seq"), lax.axis_index("fsdp")
    barrier = pltpu.get_barrier_semaphore()
    for i in range(1, n_seq):
        pl.semaphore_signal(
            barrier, inc=1, device_id=((me_s + i) % n_seq, me_f), device_id_type=MESH
        )
    for i in range(1, n_fsdp):
        pl.semaphore_signal(
            barrier, inc=1, device_id=(me_s, (me_f + i) % n_fsdp), device_id_type=MESH
        )
    pl.semaphore_wait(barrier, n_seq + n_fsdp - 2)


class Exchange:
    def __init__(self, n_seq, n_fsdp, src, dst, sems):
        self.n, self.n_fsdp, self.src, self.dst = n_seq * n_fsdp, n_fsdp, src, dst
        self.send_sem, self.recv_sem, self.own_sem = sems
        self.me = lax.axis_index("seq") * n_fsdp + lax.axis_index("fsdp")

    def copy(self, i, place):
        other = (self.me + i) % self.n
        return remote(
            self.src.at[other],
            self.dst.at[self.me if place is None else place],
            self.send_sem.at[i],
            self.recv_sem.at[self.me if place is None else place],
            (other // self.n_fsdp, other % self.n_fsdp),
        )

    def own(self):
        return pltpu.make_async_copy(
            self.src.at[self.me], self.dst.at[self.me], self.own_sem
        )

    def start(self):
        self.own().start()

        def one(i, carry):
            self.copy(i, None).start()
            return carry

        lax.fori_loop(1, self.n, one, 0)

    def finish(self):
        def one(i, carry):
            self.copy(i, None).wait_send()
            self.copy(i, (self.me + i) % self.n).wait_recv()
            return carry

        lax.fori_loop(1, self.n, one, 0)
        self.own().wait()


def exchange_sems(n):
    return [
        pltpu.SemaphoreType.DMA((n,)),
        pltpu.SemaphoreType.DMA((n,)),
        pltpu.SemaphoreType.DMA,
    ]


def line_step(n_fsdp, step, arrived, forward):
    me_f = lax.axis_index("fsdp")

    @pl.when(me_f - step >= 0)
    def _():
        arrived(me_f - step)

        @pl.when(me_f + 1 < n_fsdp)
        def _():
            forward(me_f - step, 0, me_f + 1)

    @pl.when(me_f + step < n_fsdp)
    def _():
        arrived(me_f + step)

        @pl.when(me_f >= 1)
        def _():
            forward(me_f + step, 1, me_f - 1)


def line_sent(n_fsdp, step, sent):
    me_f = lax.axis_index("fsdp")

    @pl.when((me_f - step >= 0) & (me_f + 1 < n_fsdp))
    def _():
        sent(me_f - step, 0, me_f + 1)

    @pl.when((me_f + step < n_fsdp) & (me_f >= 1))
    def _():
        sent(me_f + step, 1, me_f - 1)


def flipped(index, bit):
    return index + bit * (1 - 2 * ((index // bit) % 2))


class SeqGather:
    def __init__(self, order, own, block, send_sem, recv_sem):
        self.order, self.own, self.block = order, own, block
        self.send_sem, self.recv_sem = send_sem, recv_sem
        self.me_s, self.me_f = lax.axis_index("seq"), lax.axis_index("fsdp")

    def held(self, stage):
        indices = [self.me_s]
        for bit in self.order[:stage]:
            indices = indices + [flipped(i, bit) for i in indices]
        return indices

    def copies(self, stage):
        partner = flipped(self.me_s, self.order[stage])
        result = []
        for count, index in enumerate(self.held(stage)):
            src = self.own if count == 0 else self.block(index)
            sem = self.send_sem.at[(1 << stage) - 1 + count]
            result.append(
                remote(src, self.block(index), sem, self.recv_sem.at[index], (partner, self.me_f))
            )
        return result

    def start(self, stage):
        for copy in self.copies(stage):
            copy.start()

    def wait(self, stage):
        for index in self.held(stage):
            index = flipped(index, self.order[stage])
            remote(
                self.block(index),
                self.block(index),
                self.send_sem.at[0],
                self.recv_sem.at[index],
                (self.me_s, self.me_f),
            ).wait_recv()

    def sent(self):
        for stage in range(len(self.order)):
            for copy in self.copies(stage):
                copy.wait_send()


def gather_orders(n_seq):
    bits = [1 << b for b in range(n_seq.bit_length() - 1)]
    return bits[1:] + bits[:1], bits[:0:-1] + bits[:1]


def first_kernel(
    n_seq,
    n_fsdp,
    small,
    tokens,
    qkv,
    small_all,
    slot,
    qkv_all,
    own_sem,
    small_send,
    small_recv,
    qkv_send,
    qkv_recv,
    line_send,
    line_recv,
    token_send,
    token_recv,
):
    me_s, me_f = lax.axis_index("seq"), lax.axis_index("fsdp")
    n = n_seq * n_fsdp
    me = me_s * n_fsdp + me_f
    head_width = qkv_all.shape[3] // 3
    width = head_width * n_seq
    half = tokens.shape[0] // 2
    orders = gather_orders(n_seq)
    stages = len(orders[0])

    def columns(owner, part):
        start = pl.multiple_of(part * width + owner * head_width, 128)
        return qkv.at[:, pl.ds(start, head_width)]

    def column_place(source, part):
        return qkv_all.at[source, me_f, :, pl.ds(part * head_width, head_width)]

    own = [
        pltpu.make_async_copy(small, small_all.at[me], own_sem.at[0]),
        pltpu.make_async_copy(tokens, slot.at[me_s], own_sem.at[1]),
    ] + [
        pltpu.make_async_copy(columns(me_s, part), column_place(me_s, part), own_sem.at[2 + part])
        for part in range(3)
    ]
    for copy in own:
        copy.start()
    greet_all(n_seq, n_fsdp)

    def column_copy(i, part):
        other = (me_s + i) % n_seq
        return remote(
            columns(other, part),
            column_place(me_s, part),
            qkv_send.at[i, part],
            qkv_recv.at[me_s, part],
            (other, me_f),
        )

    for i in range(1, n_seq):
        for part in range(3):
            column_copy(i, part).start()
    for copy in own:
        copy.wait()

    def line_copy(part, step, block, way, to):
        place = qkv_all.at[part, block]
        return remote(
            place, place, line_send.at[part, way, step], line_recv.at[part, block], (me_s, to)
        )

    def line_first(part):
        @pl.when(me_f + 1 < n_fsdp)
        def _():
            line_copy(part, 0, me_f, 0, me_f + 1).start()

        @pl.when(me_f >= 1)
        def _():
            line_copy(part, 0, me_f, 1, me_f - 1).start()

    def column_arrived(i, carry):
        source = (me_s + i) % n_seq

        @pl.when(i > 0)
        def _():
            for part in range(3):
                remote(
                    columns(source, part),
                    column_place(source, part),
                    qkv_send.at[i, part],
                    qkv_recv.at[source, part],
                    (source, me_f),
                ).wait_recv()

        line_first(source)
        return carry

    lax.fori_loop(0, n_seq, column_arrived, 0)

    flows = []
    for side in range(2):
        rows = pl.ds(side * half, half)
        flows.append(
            SeqGather(
                orders[side],
                tokens.at[rows],
                lambda index, rows=rows: slot.at[index, rows],
                token_send.at[side],
                token_recv.at[side],
            )
        )

    def point(stage):
        for flow in flows:
            if 0 < stage <= stages:
                flow.wait(stage - 1)
            if stage < stages:
                flow.start(stage)

    def small_copy(i):
        other = (me + i) % n
        return remote(
            small,
            small_all.at[me],
            small_send.at[i],
            small_recv.at[me],
            (other // n_fsdp, other % n_fsdp),
        )

    def small_start(i, carry):
        small_copy(i).start()
        return carry

    point(0)
    lax.fori_loop(1, n, small_start, 0)
    count = 1
    for step in range(1, n_fsdp):

        def column_next(i, carry, step=step):
            part = (me_s + i) % n_seq
            line_step(
                n_fsdp,
                step,
                lambda block: line_copy(part, 0, block, 0, me_f).wait_recv(),
                lambda block, way, to: line_copy(part, step, block, way, to).start(),
            )
            return carry

        for part in range(2):
            lax.fori_loop(part * n_seq // 2, (part + 1) * n_seq // 2, column_next, 0)
            point(count)
            count += 1
    while count <= stages:
        point(count)
        count += 1
    for flow in flows:
        flow.sent()

    def column_sent(i, carry):
        for part in range(3):
            column_copy(i, part).wait_send()
        return carry

    lax.fori_loop(1, n_seq, column_sent, 0)

    def small_wait(i, carry):
        other = (me + i) % n
        small_copy(i).wait_send()
        remote(
            small,
            small_all.at[other],
            small_send.at[i],
            small_recv.at[other],
            (other // n_fsdp, other % n_fsdp),
        ).wait_recv()
        return carry

    lax.fori_loop(1, n, small_wait, 0)

    def line_done(part, carry):
        for step in range(n_fsdp):
            line_sent(
                n_fsdp,
                step,
                lambda block, way, to: line_copy(part, step, block, way, to).wait_send(),
            )
        return carry

    lax.fori_loop(0, n_seq, line_done, 0)


def first_gather(small, tokens, qkv, n_seq, n_fsdp, collective_id):
    owned = qkv.shape[0]
    head_width = qkv.shape[1] // (3 * n_seq)
    n = n_seq * n_fsdp
    vmem = pl.BlockSpec(memory_space=pltpu.VMEM)
    any_space = pl.BlockSpec(memory_space=pl.ANY)
    dma = pltpu.SemaphoreType.DMA
    return pl.pallas_call(
        functools.partial(first_kernel, n_seq, n_fsdp),
        out_shape=[
            jax.ShapeDtypeStruct((n,) + small.shape, BF),
            jax.ShapeDtypeStruct((n_seq,) + tokens.shape, BF),
            jax.ShapeDtypeStruct((n_seq, n_fsdp, owned, 3 * head_width), BF),
        ],
        in_specs=[vmem] * 3,
        out_specs=[vmem, any_space, any_space],
        scratch_shapes=[
            dma((5,)),
            dma((n,)),
            dma((n,)),
            dma((n_seq, 3)),
            dma((n_seq, 3)),
            dma((n_seq, 2, n_fsdp)),
            dma((n_seq, n_fsdp)),
            dma((2, n_seq - 1)),
            dma((2, n_seq)),
        ],
        compiler_params=pltpu.CompilerParams(collective_id=collective_id, has_side_effects=True),
        name="first_gather",
    )(small, tokens, qkv)


def greet_seq(n_seq):
    me_s, me_f = lax.axis_index("seq"), lax.axis_index("fsdp")
    barrier = pltpu.get_barrier_semaphore()
    for i in range(1, n_seq):
        pl.semaphore_signal(
            barrier, inc=1, device_id=((me_s + i) % n_seq, me_f), device_id_type=MESH
        )
    pl.semaphore_wait(barrier, n_seq - 1)


class TermSum:
    def __init__(
        self, n_seq, n_fsdp, terms, seq_terms, fsdp_terms, seq_send, seq_recv, fsdp_send, fsdp_recv
    ):
        self.n_seq, self.n_fsdp, self.terms = n_seq, n_fsdp, terms
        self.seq_terms, self.fsdp_terms = seq_terms, fsdp_terms
        self.seq_send, self.seq_recv = seq_send, seq_recv
        self.fsdp_send, self.fsdp_recv = fsdp_send, fsdp_recv
        self.me_s, self.me_f = lax.axis_index("seq"), lax.axis_index("fsdp")

    def part(self, owner):
        columns = self.seq_terms.shape[2]
        return self.terms.at[:, pl.ds(pl.multiple_of(owner * columns, 128), columns)]

    def seq_copy(self, i, place):
        other = (self.me_s + i) % self.n_seq
        return remote(
            self.part(other),
            self.seq_terms.at[place],
            self.seq_send.at[i],
            self.seq_recv.at[place],
            (other, self.me_f),
        )

    def fsdp_copy(self, i, place):
        other = (self.me_f + i) % self.n_fsdp
        return remote(
            self.seq_terms.at[self.me_s],
            self.fsdp_terms.at[place],
            self.fsdp_send.at[i],
            self.fsdp_recv.at[place],
            (self.me_s, other),
        )

    def start_seq(self):
        for i in range(1, self.n_seq):
            self.seq_copy(i, self.me_s).start()

    def over_seq(self):
        result = self.part(self.me_s)[...]
        for i in range(1, self.n_seq):
            place = (self.me_s + i) % self.n_seq
            self.seq_copy(i, place).wait_recv()
            result = result + self.seq_terms[place]
        for i in range(1, self.n_seq):
            self.seq_copy(i, self.me_s).wait_send()
        return result

    def start_fsdp(self, more):
        self.seq_terms[self.me_s] = more + (self.over_seq() if self.terms is not None else 0.0)
        for i in range(1, self.n_fsdp):
            self.fsdp_copy(i, self.me_f).start()

    def finish(self):
        result = self.seq_terms[self.me_s]
        for i in range(1, self.n_fsdp):
            place = (self.me_f + i) % self.n_fsdp
            self.fsdp_copy(i, place).wait_recv()
            result = result + self.fsdp_terms[place]
        for i in range(1, self.n_fsdp):
            self.fsdp_copy(i, self.me_f).wait_send()
        return result


def term_scratch(n_seq, n_fsdp, shape):
    dma = pltpu.SemaphoreType.DMA
    return [
        pltpu.VMEM((n_seq,) + shape, F32),
        pltpu.VMEM((n_fsdp,) + shape, F32),
        dma((n_seq,)),
        dma((n_seq,)),
        dma((n_fsdp,)),
        dma((n_fsdp,)),
    ]


def gather_kernel(n_seq, n_fsdp, x, terms, out, total, own_sem, send_sem, recv_sem, *scratch):
    me_s = lax.axis_index("seq")
    half = x.shape[0] // 2
    own = pltpu.make_async_copy(x, out.at[me_s], own_sem)
    own.start()
    term_sum = TermSum(n_seq, n_fsdp, terms, scratch[0], None, *scratch[1:], None, None)
    greet_seq(n_seq)
    flows = []
    for side, order in enumerate(gather_orders(n_seq)):
        rows = pl.ds(side * half, half)
        flows.append(
            SeqGather(
                order,
                x.at[rows],
                lambda index, rows=rows: out.at[index, rows],
                send_sem.at[side],
                recv_sem.at[side],
            )
        )
    for stage in range(len(flows[0].order)):
        for flow in flows:
            flow.start(stage)
        if stage == 0:
            term_sum.start_seq()
        if stage == 1:
            total[...] = term_sum.over_seq()
        for flow in flows:
            flow.wait(stage)
    for flow in flows:
        flow.sent()
    own.wait()


def gather_seq(x, terms, n_seq, n_fsdp, collective_id):
    vmem = pl.BlockSpec(memory_space=pltpu.VMEM)
    dma = pltpu.SemaphoreType.DMA
    part = (terms.shape[0], terms.shape[1] // n_seq)
    return pl.pallas_call(
        functools.partial(gather_kernel, n_seq, n_fsdp),
        out_shape=[
            jax.ShapeDtypeStruct((n_seq,) + x.shape, x.dtype),
            jax.ShapeDtypeStruct(part, terms.dtype),
        ],
        in_specs=[vmem] * 2,
        out_specs=[vmem] * 2,
        scratch_shapes=[
            dma,
            dma((2, n_seq - 1)),
            dma((2, n_seq)),
            pltpu.VMEM((n_seq,) + part, F32),
            dma((n_seq,)),
            dma((n_seq,)),
        ],
        compiler_params=pltpu.CompilerParams(collective_id=collective_id, has_side_effects=True),
        cost_estimate=pl.CostEstimate(flops=0, bytes_accessed=1 << 26, transcendentals=0),
        name="gather_seq",
    )(x, terms)


class SeqReduce:
    def __init__(self, n_seq, a, w, w_dim, sums, got, send_sem, recv_sem):
        self.a, self.w, self.w_dim, self.sums, self.got = a, w, w_dim, sums, got
        self.send_sem, self.recv_sem = send_sem, recv_sem
        self.me_s, self.me_f = lax.axis_index("seq"), lax.axis_index("fsdp")
        self.orders = [order[-1:] + order[-2::-1] for order in gather_orders(n_seq)]
        self.stages = len(self.orders[0])
        self.half = sums.shape[1] // 2
        self.width = sums.shape[2]

    def combined(self, index, bits):
        indices = [index]
        for bit in bits:
            indices = indices + [flipped(i, bit) for i in indices]
        return indices

    def product(self, index):
        def some(columns):
            w = self.w[:, columns] if self.w_dim == 0 else self.w[columns, :]
            self.sums[index, :, columns] = dot(self.a[index], w, 1, self.w_dim).astype(BF)

        chunked(self.width, 512, some)

    def copy(self, stage, side, count, index):
        order = self.orders[side]
        slot = sum(1 << (self.stages - 1 - s) for s in range(stage)) + count
        rows = pl.ds(side * self.half, self.half)
        return remote(
            self.sums.at[index, rows],
            self.got.at[slot, rows],
            self.send_sem.at[side, slot],
            self.recv_sem.at[side, slot],
            (flipped(self.me_s, order[stage]), self.me_f),
        )

    def leaving(self, stage, side):
        order = self.orders[side]
        return self.combined(flipped(self.me_s, order[stage]), order[stage + 1 :])

    def start(self, stage):
        if stage == 0:
            for count, index in enumerate(self.leaving(0, 0)):
                self.product(index)
                for side in range(2):
                    self.copy(0, side, self.twin(count) if side == 1 else count, index).start()
            for index in self.combined(self.me_s, self.orders[0][1:]):
                self.product(index)
        else:
            for side in range(2):
                for count, index in enumerate(self.leaving(stage, side)):
                    self.copy(stage, side, count, index).start()

    def twin(self, count):
        first, second = self.orders[0][1:], self.orders[1][1:]
        place = 0
        for position, bit in enumerate(first):
            if (count >> position) & 1:
                place += 1 << second.index(bit)
        return place

    def finish(self, stage, last=None):
        for side in range(2):
            order = self.orders[side]
            rows = pl.ds(side * self.half, self.half)
            for count, index in enumerate(self.combined(self.me_s, order[stage + 1 :])):
                copy = self.copy(stage, side, count, index)
                copy.wait_recv()
                slot = sum(1 << (self.stages - 1 - s) for s in range(stage)) + count

                def some(columns):
                    total = self.sums[index, rows, columns].astype(F32)
                    total = total + self.got[slot, rows, columns].astype(F32)
                    if last is None:
                        self.sums[index, rows, columns] = total.astype(BF)
                    else:
                        last[rows, columns] = total

                chunked(self.width, 1024, some)

    def events(self, last):
        def leave(count, index):
            self.product(index)
            for side in range(2):
                self.copy(0, side, self.twin(count) if side == 1 else count, index).start()

        result = [
            (1, functools.partial(leave, count, index))
            for count, index in enumerate(self.leaving(0, 0))
        ]
        for index in self.combined(self.me_s, self.orders[0][1:]):
            result.append((1, functools.partial(self.product, index)))
        result.append((1, functools.partial(self.finish, 0, last if self.stages == 1 else None)))
        for stage in range(1, self.stages):
            result.append((0, functools.partial(self.start, stage)))
            result.append(
                (7, functools.partial(self.finish, stage, last if stage == self.stages - 1 else None))
            )
        return result

    def sent(self):
        for stage in range(self.stages):
            for side in range(2):
                for count, index in enumerate(self.leaving(stage, side)):
                    self.copy(stage, side, count, index).wait_send()


def reduce_scratch(n_seq, rows, width):
    dma = pltpu.SemaphoreType.DMA
    return [
        pltpu.VMEM((n_seq, rows, width), BF),
        pltpu.VMEM((n_seq - 1, rows, width), BF),
        dma((2, n_seq - 1)),
        dma((2, n_seq - 1)),
    ]


def reduce_kernel(n_seq, w_dim, a, w, out, *scratch):
    greet_seq(n_seq)
    reduce = SeqReduce(n_seq, a, w, w_dim, *scratch)
    for stage in range(reduce.stages):
        reduce.start(stage)
        reduce.finish(stage, out if stage == reduce.stages - 1 else None)
    reduce.sent()


def product_reduced(a, w, w_dim, n_seq, collective_id):
    rows = a.shape[0] // n_seq
    width = w.shape[1 - w_dim]
    return pl.pallas_call(
        functools.partial(reduce_kernel, n_seq, w_dim),
        out_shape=jax.ShapeDtypeStruct((rows, width), F32),
        in_specs=[pl.BlockSpec(memory_space=pltpu.VMEM)] * 2,
        out_specs=pl.BlockSpec(memory_space=pltpu.VMEM),
        scratch_shapes=reduce_scratch(n_seq, rows, width),
        compiler_params=pltpu.CompilerParams(
            collective_id=collective_id, has_side_effects=True, vmem_limit_bytes=40 << 20
        ),
        name="product_reduced",
    )(a.reshape(n_seq, rows, -1), w)


def last_kernel(
    n_seq,
    n_fsdp,
    a,
    w,
    part,
    x,
    mid,
    gains,
    terms_in,
    heads,
    input_out,
    qkv_out,
    total,
    *scratch,
):
    up, down, done, got, up_send, up_recv, down_send, down_recv, done_send, done_recv = scratch[:10]
    one, terms, seq_terms, fsdp_terms, seq_send, seq_recv, fsdp_send, fsdp_recv = scratch[10:18]
    me_s, me_f = lax.axis_index("seq"), lax.axis_index("fsdp")
    head_width = part.shape[3] // 3
    width = n_seq * head_width
    greet_lines(n_seq, n_fsdp)
    reduce = SeqReduce(n_seq, a, w, 1, *scratch[18:])
    term_sum = TermSum(
        n_seq,
        n_fsdp,
        terms,
        seq_terms,
        fsdp_terms,
        seq_send,
        seq_recv,
        fsdp_send,
        fsdp_recv,
    )

    def input_rows():
        tile = 32
        terms[...] = terms_in[...]

        def some(i, carry):
            rows = pl.ds(pl.multiple_of(i * tile, tile), tile)
            values = x[rows, :].astype(F32)
            scale = lax.rsqrt(jnp.mean(values * values, axis=-1, keepdims=True) + epsilon)
            grad = one[rows, :]
            weighted = grad * gains[0:1, :]
            mean = jnp.mean(weighted * values, axis=-1, keepdims=True)
            result = scale * weighted - values * (scale * scale * scale * mean)
            input_out[rows, :] = (mid[rows, :] + result).astype(BF)
            terms[0:1, :] += jnp.sum(grad * values * scale, axis=0, keepdims=True)
            return carry

        lax.fori_loop(0, x.shape[0] // tile, some, 0)
        term_sum.start_seq()

    def line_copy(src, way, s, block):
        buffer, send, recv = (up, up_send, up_recv) if way == 0 else (down, down_send, down_recv)
        to = me_f + 1 if way == 0 else me_f - 1
        place = buffer.at[block, s]
        return remote(
            place if src is None else src, place, send.at[block, s], recv.at[block, s], (me_s, to)
        )

    def done_copy(i):
        s = (me_s + i) % n_seq
        return remote(done.at[s], got.at[me_s], done_send.at[i], done_recv.at[me_s], (s, me_f))

    def stream(way, number):
        buffer = up if way == 0 else down
        behind = me_f if way == 0 else n_fsdp - 1 - me_f
        turn, i = number // n_seq, number % n_seq
        s = (me_s + i) % n_seq
        block = n_fsdp - 1 - turn if way == 0 else turn
        ahead = n_fsdp - 1 - behind
        on_time = (number >= 0) & (turn < ahead)
        finishes_up = (me_f == n_fsdp - 1) | ((n_fsdp - 1 > 2 * me_f) & (me_f > 0))

        @pl.when(on_time & (behind == 0))
        def _():
            line_copy(part.at[s, block], way, s, block).start()

        @pl.when(on_time & (behind > 0))
        def _():
            line_copy(None, way, s, block).wait_recv()
            total = buffer[block, s].astype(F32) + part[s, block].astype(F32)
            buffer[block, s] = total.astype(BF)
            line_copy(None, way, s, block).start()

        @pl.when((number >= 0) & (turn == ahead) & (behind > 0))
        def _():
            line_copy(None, way, s, me_f).wait_recv()
            done[s] = (done[s].astype(F32) + buffer[me_f, s].astype(F32)).astype(BF)

            @pl.when(finishes_up if way == 0 else jnp.logical_not(finishes_up))
            def _():
                @pl.when(i > 0)
                def _():
                    done_copy(i).start()

    lag = 2
    slots = n_seq * (n_fsdp - 1) + lag * (n_fsdp - 1)

    def run(first, last):
        def slot(number, carry):
            stream(0, number - lag * me_f)
            stream(1, number - lag * (n_fsdp - 1 - me_f))
            return carry

        lax.fori_loop(first, last, slot, 0)

    def begin(i, carry):
        done[i] = part[i, me_f]
        return carry

    lax.fori_loop(0, n_seq, begin, 0)
    reached = 0
    for number, event in enumerate(
        reduce.events(one)
        + [(0, input_rows), (3, functools.partial(term_sum.start_fsdp, heads[...]))]
    ):
        run(reached, min(slots, reached + event[0]))
        reached = min(slots, reached + event[0])
        event[1]()
    run(reached, slots)

    def place(s, rows):
        for third in range(3):
            columns = pl.ds(pl.multiple_of(third * width + s * head_width, 128), head_width)
            qkv_out[:, columns] = rows[:, third * head_width : (third + 1) * head_width].astype(F32)

    place(me_s, done[me_s])

    def arrived(i, carry):
        s = (me_s + i) % n_seq
        remote(done.at[s], got.at[s], done_send.at[i], done_recv.at[s], (s, me_f)).wait_recv()
        place(s, got[s])
        return carry

    lax.fori_loop(1, n_seq, arrived, 0)

    def all_sent(i, carry):
        s = (me_s + i) % n_seq

        @pl.when(i > 0)
        def _():
            done_copy(i).wait_send()

        for j in range(n_fsdp - 1):

            @pl.when(me_f + j < n_fsdp - 1)
            def _():
                line_copy(None, 0, s, n_fsdp - 1 - j).wait_send()

            @pl.when(j < me_f)
            def _():
                line_copy(None, 1, s, j).wait_send()

        return carry

    lax.fori_loop(0, n_seq, all_sent, 0)
    reduce.sent()
    total[...] = term_sum.finish()


def last_reduce(a, w, part, x, mid, gains, terms, heads, n_seq, n_fsdp, collective_id):
    rows, width = a.shape[0] // n_seq, w.shape[0]
    owned, columns = part.shape[2:]
    vmem = pl.BlockSpec(memory_space=pltpu.VMEM)
    dma = pltpu.SemaphoreType.DMA
    return pl.pallas_call(
        functools.partial(last_kernel, n_seq, n_fsdp),
        out_shape=[
            jax.ShapeDtypeStruct((rows, width), BF),
            jax.ShapeDtypeStruct((owned, n_seq * columns), F32),
            jax.ShapeDtypeStruct(heads.shape, F32),
        ],
        in_specs=[vmem] * 8,
        out_specs=[vmem] * 3,
        scratch_shapes=[
            pltpu.VMEM((n_fsdp, n_seq, owned, columns), BF),
            pltpu.VMEM((n_fsdp, n_seq, owned, columns), BF),
            pltpu.VMEM((n_seq, owned, columns), BF),
            pltpu.VMEM((n_seq, owned, columns), BF),
            dma((n_fsdp, n_seq)),
            dma((n_fsdp, n_seq)),
            dma((n_fsdp, n_seq)),
            dma((n_fsdp, n_seq)),
            dma((n_seq,)),
            dma((n_seq,)),
            pltpu.VMEM((rows, width), F32),
            pltpu.VMEM(terms.shape, F32),
        ]
        + term_scratch(n_seq, n_fsdp, heads.shape)
        + reduce_scratch(n_seq, rows, width),
        compiler_params=pltpu.CompilerParams(
            collective_id=collective_id, has_side_effects=True, vmem_limit_bytes=50 << 20
        ),
        cost_estimate=pl.CostEstimate(flops=0, bytes_accessed=1 << 27, transcendentals=0),
        name="last_reduce",
    )(a.reshape(n_seq, rows, -1), w, part, x, mid, gains, terms, heads)


def chunked(total, size, body):
    def step(i, carry):
        body(pl.ds(pl.multiple_of(i * size, size), size))
        return carry

    lax.fori_loop(0, total // size, step, 0)


def dispatch_kernel(n_seq, n_fsdp, pieces, x, hot, gates, masked, gates_out, masked_out, *refs):
    outs = refs[:pieces]
    (
        gathered,
        send,
        own_sem,
        line_send,
        line_recv,
        row_send,
        row_recv,
        masked_rows,
        masked_sem,
    ) = refs[pieces : pieces + 9]
    gate_exchange = Exchange(n_seq, n_fsdp, gates, gates_out, refs[pieces + 9 :])
    me_s, me_f = lax.axis_index("seq"), lax.axis_index("fsdp")
    width = x.shape[1]
    capacity = outs[0].shape[2]
    greet_all(n_seq, n_fsdp)

    def line_copy(step, block, way, to):
        src = x if step == 0 else gathered.at[block]
        return remote(
            src, gathered.at[block], line_send.at[way, step], line_recv.at[block], (me_s, to)
        )

    def row_copy(block, i, piece):
        other = (me_s + i) % n_seq
        return remote(
            send.at[block, other, piece],
            outs[piece].at[me_s, block],
            row_send.at[block, i, piece],
            row_recv.at[me_s, block, piece],
            (other, me_f),
        )

    def own_copy(block, piece):
        return pltpu.make_async_copy(
            send.at[block, me_s, piece], outs[piece].at[me_s, block], own_sem.at[block, piece]
        )

    def scatter(block, rows):
        def some(columns):
            picked = dot(hot[block], rows[:, columns], 1, 0).astype(BF)
            send[block, :, :, :, columns] = picked.reshape(n_seq, pieces, capacity, -1)

        chunked(width, 512, some)
        for i in range(1, n_seq):
            for piece in range(pieces):
                row_copy(block, i, piece).start()
        for piece in range(pieces):
            own_copy(block, piece).start()

    def masked_copy(block):
        return pltpu.make_async_copy(
            masked_rows.at[block % 2], masked_out.at[:, :, block], masked_sem.at[block % 2]
        )

    def lay_masked(block):
        if block >= 2:
            masked_copy(block - 2).wait()

        def some(columns):
            picked = dot(hot[block], masked[block, :, columns], 1, 0).astype(BF)
            masked_rows[block % 2, :, :, :, columns] = picked.reshape(n_seq, pieces, capacity, -1)

        chunked(width, 512, some)
        masked_copy(block).start()

    @pl.when(me_f + 1 < n_fsdp)
    def _():
        line_copy(0, me_f, 0, me_f + 1).start()

    @pl.when(me_f >= 1)
    def _():
        line_copy(0, me_f, 1, me_f - 1).start()

    scatter(me_f, x)
    gate_exchange.start()
    lay_masked(0)
    for step in range(1, n_fsdp):
        line_step(
            n_fsdp,
            step,
            lambda block: line_copy(1, block, 0, me_f).wait_recv(),
            lambda block, way, to: line_copy(step, block, way, to).start(),
        )

        @pl.when(me_f - step >= 0)
        def _():
            scatter(me_f - step, gathered.at[me_f - step])

        @pl.when(me_f + step < n_fsdp)
        def _():
            scatter(me_f + step, gathered.at[me_f + step])

        lay_masked(step)

    for step in range(n_fsdp):
        line_sent(
            n_fsdp, step, lambda block, way, to: line_copy(step, block, way, to).wait_send()
        )
    for block in range(n_fsdp):
        for piece in range(pieces):
            own_copy(block, piece).wait()
            for i in range(1, n_seq):
                source = (me_s + i) % n_seq
                row_copy(block, i, piece).wait_send()
                remote(
                    send.at[block, source, piece],
                    outs[piece].at[source, block],
                    row_send.at[block, i, piece],
                    row_recv.at[source, block, piece],
                    (source, me_f),
                ).wait_recv()
    gate_exchange.finish()
    for block in range(max(0, n_fsdp - 2), n_fsdp):
        masked_copy(block).wait()


def dispatch_rows(x, hot, gates, masked, n_seq, n_fsdp, pieces, capacity, collective_id):
    rows, width = x.shape
    vmem = pl.BlockSpec(memory_space=pltpu.VMEM)
    dma = pltpu.SemaphoreType.DMA
    return pl.pallas_call(
        functools.partial(dispatch_kernel, n_seq, n_fsdp, pieces),
        out_shape=[
            jax.ShapeDtypeStruct(gates.shape, F32),
            jax.ShapeDtypeStruct((n_seq, pieces, n_fsdp, capacity, width), BF),
        ]
        + [jax.ShapeDtypeStruct((n_seq, n_fsdp, capacity, width), BF)] * pieces,
        in_specs=[vmem] * 4,
        out_specs=[vmem] + [pl.BlockSpec(memory_space=pl.ANY)] * (pieces + 1),
        scratch_shapes=[
            pltpu.VMEM((n_fsdp, rows, width), BF),
            pltpu.VMEM((n_fsdp, n_seq, pieces, capacity, width), BF),
            dma((n_fsdp, pieces)),
            dma((2, n_fsdp)),
            dma((n_fsdp,)),
            dma((n_fsdp, n_seq, pieces)),
            dma((n_seq, n_fsdp, pieces)),
            pltpu.VMEM((2, n_seq, pieces, capacity, width), BF),
            dma((2,)),
        ]
        + exchange_sems(n_seq * n_fsdp),
        compiler_params=pltpu.CompilerParams(
            collective_id=collective_id, has_side_effects=True, vmem_limit_bytes=40 << 20
        ),
        name="dispatch_rows",
    )(x, hot, gates, masked)


def return_kernel(n_seq, n_fsdp, pieces, hot, gates, *refs):
    rows = refs[:pieces]
    out, gates_out, got, parts, sums, own_sem, row_send, row_recv, part_send, part_recv = refs[
        pieces : pieces + 10
    ]
    gate_exchange = Exchange(n_seq, n_fsdp, gates, gates_out, refs[pieces + 10 :])
    me_s, me_f = lax.axis_index("seq"), lax.axis_index("fsdp")
    width = out.shape[1]
    capacity = rows[0].shape[2]
    greet_all(n_seq, n_fsdp)

    def row_copy(j, i, piece):
        other, block = (me_s + i) % n_seq, (me_f + j) % n_fsdp
        return remote(
            rows[piece].at[other, block],
            got.at[block, me_s, piece],
            row_send.at[j % n_fsdp, i, piece],
            row_recv.at[block, me_s, piece],
            (other, me_f),
        )

    def own_copy(j, piece):
        block = (me_f + j) % n_fsdp
        return pltpu.make_async_copy(
            rows[piece].at[me_s, block], got.at[block, me_s, piece], own_sem.at[j % n_fsdp, piece]
        )

    def part_copy(j):
        block = (me_f + j) % n_fsdp
        return remote(
            parts.at[block], sums.at[me_f], part_send.at[j], part_recv.at[me_f], (me_s, block)
        )

    for j in range(1, n_fsdp + 1):
        for piece in range(pieces):
            for i in range(1, n_seq):
                row_copy(j, i, piece).start()
            own_copy(j, piece).start()
    gate_exchange.start()
    for j in range(1, n_fsdp + 1):
        block = (me_f + j) % n_fsdp
        for piece in range(pieces):
            own_copy(j, piece).wait()
            for i in range(1, n_seq):
                source = (me_s + i) % n_seq
                remote(
                    rows[piece].at[source, block],
                    got.at[block, source, piece],
                    row_send.at[0, i, piece],
                    row_recv.at[block, source, piece],
                    (source, me_f),
                ).wait_recv()

        def some(columns):
            arrived = got[block, :, :, :, columns].reshape(n_seq * pieces * capacity, -1)
            total = dot(hot[block], arrived, 1, 0)
            if j < n_fsdp:
                parts[block, :, columns] = total.astype(BF)
            else:
                out[:, columns] = total

        chunked(width, 512, some)
        if j < n_fsdp:
            part_copy(j).start()
    for j in range(1, n_fsdp):
        source = (me_f + n_fsdp - j) % n_fsdp
        remote(
            parts.at[source], sums.at[source], part_send.at[j], part_recv.at[source], (me_s, source)
        ).wait_recv()

    def add(columns):
        total = out[:, columns]
        for j in range(1, n_fsdp):
            total = total + sums[(me_f + j) % n_fsdp, :, columns].astype(F32)
        out[:, columns] = total

    chunked(width, 512, add)
    for j in range(1, n_fsdp):
        part_copy(j).wait_send()
    for j in range(1, n_fsdp + 1):
        for piece in range(pieces):
            for i in range(1, n_seq):
                row_copy(j, i, piece).wait_send()
    gate_exchange.finish()


def return_rows(piece_rows, hot, gates, n_seq, n_fsdp, collective_id):
    pieces = len(piece_rows)
    capacity, width = piece_rows[0].shape[2:]
    count = hot.shape[1]
    vmem = pl.BlockSpec(memory_space=pltpu.VMEM)
    dma = pltpu.SemaphoreType.DMA
    return pl.pallas_call(
        functools.partial(return_kernel, n_seq, n_fsdp, pieces),
        out_shape=[
            jax.ShapeDtypeStruct((count, width), F32),
            jax.ShapeDtypeStruct(gates.shape, F32),
        ],
        in_specs=[vmem, vmem] + [pl.BlockSpec(memory_space=pl.ANY)] * pieces,
        out_specs=[vmem, vmem],
        scratch_shapes=[
            pltpu.VMEM((n_fsdp, n_seq, pieces, capacity, width), BF),
            pltpu.VMEM((n_fsdp, count, width), BF),
            pltpu.VMEM((n_fsdp, count, width), BF),
            dma((n_fsdp, pieces)),
            dma((n_fsdp, n_seq, pieces)),
            dma((n_fsdp, n_seq, pieces)),
            dma((n_fsdp,)),
            dma((n_fsdp,)),
        ]
        + exchange_sems(n_seq * n_fsdp),
        compiler_params=pltpu.CompilerParams(
            collective_id=collective_id, has_side_effects=True, vmem_limit_bytes=40 << 20
        ),
        name="return_rows",
    )(hot, gates, *piece_rows)


def weight_grad_kernel(a, b, *refs):
    refs[-1][0] = dot(a[...], b[0], 0, 0)


def weight_grad(a, b, whole, piece, pieces, part):
    rows, m = a.shape
    parts, _, n = b.shape
    tile = min(256, m)
    more = [] if whole is None else [whole]
    return pl.pallas_call(
        weight_grad_kernel,
        out_shape=jax.ShapeDtypeStruct((pieces, m, n * parts), F32),
        grid=(m // tile,),
        in_specs=[
            pl.BlockSpec((rows, tile), lambda i: (0, i)),
            pl.BlockSpec((1, rows, n), lambda i: (part, 0, 0)),
        ]
        + [pl.BlockSpec(memory_space=pl.ANY)] * len(more),
        out_specs=pl.BlockSpec((1, tile, n), lambda i: (piece, i, part)),
        input_output_aliases={2: 0} if more else {},
        cost_estimate=pl.CostEstimate(
            flops=2 * rows * m * n,
            bytes_accessed=2 * rows * (m + n) + 4 * m * n,
            transcendentals=0,
        ),
        name="weight_grad",
    )(a, b, *more)


def seq_tile(n_seq, rows_each):
    tile = n_seq
    while tile > 1 and (tile * rows_each > 1024 or n_seq % tile):
        tile -= 1
    return tile


def expert_forward_kernel(x, gates, w_gate, w_up, w_down, *refs):
    hidden, activation, out, scaled, total = refs[-5:]
    step = pl.program_id(1)
    gate = dot(x[...], w_gate[0], 1, 0)
    up = dot(x[...], w_up[0], 1, 0)
    hidden[0] = gate
    hidden[1] = up
    act = (gate * jax.nn.sigmoid(gate) * up).astype(BF)
    activation[...] = act
    product = dot(act, w_down[0], 1, 0)

    @pl.when(step == 0)
    def _():
        total[...] = product

    @pl.when(step > 0)
    def _():
        total[...] += product

    @pl.when(step == pl.num_programs(1) - 1)
    def _():
        low = total[...].astype(BF)
        out[...] = low
        scaled[...] = (low.astype(F32) * gates[...]).astype(BF).reshape(scaled.shape)


def expert_forward(x, gates, w_up, w_down, whole, piece, n_seq, n_fsdp):
    rows, width = x.shape
    pieces, ff = w_down.shape[:2]
    capacity = rows // (n_seq * n_fsdp)
    tile = min(256, ff)
    steps = ff // tile
    spans = seq_tile(n_seq, n_fsdp * capacity)
    count = spans * n_fsdp * capacity
    more = [] if whole is None else [whole]
    fixed = lambda r, i: (r, 0)
    return pl.pallas_call(
        expert_forward_kernel,
        out_shape=[
            jax.ShapeDtypeStruct((2, rows, ff), F32),
            jax.ShapeDtypeStruct((rows, ff), BF),
            jax.ShapeDtypeStruct((rows, width), BF),
            jax.ShapeDtypeStruct((n_seq, pieces, n_fsdp, capacity, width), BF),
        ],
        grid=(rows // count, steps),
        in_specs=[
            pl.BlockSpec((count, width), fixed),
            pl.BlockSpec((count, 1), fixed),
            pl.BlockSpec((1, width, tile), lambda r, i: (piece, 0, i)),
            pl.BlockSpec((1, width, tile), lambda r, i: (piece, 0, steps + i)),
            pl.BlockSpec((1, tile, width), lambda r, i: (piece, i, 0)),
        ]
        + [pl.BlockSpec(memory_space=pl.ANY)] * len(more),
        out_specs=[
            pl.BlockSpec((2, count, tile), lambda r, i: (0, r, i)),
            pl.BlockSpec((count, tile), lambda r, i: (r, i)),
            pl.BlockSpec((count, width), fixed),
            pl.BlockSpec((spans, 1, n_fsdp, capacity, width), lambda r, i: (r, piece, 0, 0, 0)),
        ],
        scratch_shapes=[pltpu.VMEM((count, width), F32)],
        input_output_aliases={5: 3} if more else {},
        compiler_params=pltpu.CompilerParams(vmem_limit_bytes=56 << 20),
        cost_estimate=pl.CostEstimate(
            flops=6 * rows * width * ff, bytes_accessed=6 * width * ff, transcendentals=rows * ff
        ),
        name="expert_forward",
    )(x, gates, w_up, w_up, w_down, *more)


def expert_backward_kernel(masked, gates, piece_out, hidden, w_down, out, grad, inner, partial):
    @pl.when(pl.program_id(1) == 0)
    def _():
        partial[...] = jnp.zeros_like(partial)

        def some(columns):
            low = masked[:, 0, :, :, columns].reshape(grad.shape[0], -1).astype(F32)
            grad[:, columns] = (low * gates[...]).astype(BF)
            product = low * piece_out[:, columns].astype(F32)
            for i in range(product.shape[1] // 128):
                partial[...] += product[:, i * 128 : (i + 1) * 128]

        chunked(grad.shape[1], 512, some)
        sums = jnp.sum(partial[...].T, axis=0, keepdims=True)
        inner[...] = jnp.broadcast_to(sums, inner.shape)

    act_grad = dot(grad[...], w_down[0], 1, 1)
    gate, up = hidden[0], hidden[1]
    sigmoid = jax.nn.sigmoid(gate)
    out[0] = (act_grad * up * sigmoid * (1.0 + gate * (1.0 - sigmoid))).astype(BF)
    out[1] = (act_grad * gate * sigmoid).astype(BF)


def expert_backward(masked, gates, piece_out, hidden, w_down, piece):
    rows, width = piece_out.shape
    ff = w_down.shape[1]
    n_seq, _, n_fsdp, capacity, _ = masked.shape
    tile = min(256, ff)
    spans = seq_tile(n_seq, n_fsdp * capacity)
    count = spans * n_fsdp * capacity
    part = pl.BlockSpec((2, count, tile), lambda r, i: (0, r, i))
    fixed = lambda r, i: (r, 0)
    return pl.pallas_call(
        expert_backward_kernel,
        out_shape=[
            jax.ShapeDtypeStruct((2, rows, ff), BF),
            jax.ShapeDtypeStruct((rows, width), BF),
            jax.ShapeDtypeStruct((8, rows), F32),
        ],
        grid=(rows // count, ff // tile),
        in_specs=[
            pl.BlockSpec((spans, 1, n_fsdp, capacity, width), lambda r, i: (r, piece, 0, 0, 0)),
            pl.BlockSpec((count, 1), fixed),
            pl.BlockSpec((count, width), fixed),
            part,
            pl.BlockSpec((1, tile, width), lambda r, i: (piece, i, 0)),
        ],
        out_specs=[
            part,
            pl.BlockSpec((count, width), fixed),
            pl.BlockSpec((8, count), lambda r, i: (0, r)),
        ],
        scratch_shapes=[pltpu.VMEM((count, 128), F32)],
        compiler_params=pltpu.CompilerParams(vmem_limit_bytes=48 << 20),
        cost_estimate=pl.CostEstimate(
            flops=2 * rows * width * ff, bytes_accessed=12 * rows * ff, transcendentals=rows * ff
        ),
        name="expert_backward",
    )(masked, gates, piece_out, hidden, w_down)


def expert_input_kernel(grad, w_up, out):
    ff = grad.shape[2]
    total = dot(grad[0], w_up[0, :, :ff], 1, 1) + dot(grad[1], w_up[0, :, ff:], 1, 1)
    out[...] = total.astype(BF)


def expert_input(grad, w_up, piece):
    rows, ff = grad.shape[1:]
    width = w_up.shape[1]
    tile = min(256, width)
    return pl.pallas_call(
        expert_input_kernel,
        out_shape=jax.ShapeDtypeStruct((rows, width), BF),
        grid=(width // tile,),
        in_specs=[
            pl.BlockSpec((2, rows, ff), lambda i: (0, 0, 0)),
            pl.BlockSpec((1, tile, 2 * ff), lambda i: (piece, i, 0)),
        ],
        out_specs=pl.BlockSpec((rows, tile), lambda i: (0, i)),
        cost_estimate=pl.CostEstimate(
            flops=4 * rows * width * ff, bytes_accessed=4 * width * ff, transcendentals=0
        ),
        name="expert_input",
    )(grad, w_up)


class SeqShare:
    def __init__(self, n_seq, own, every, send_sem, recv_sem):
        self.n_seq, self.own, self.every = n_seq, own, every
        self.send_sem, self.recv_sem = send_sem, recv_sem
        self.me_s, self.me_f = lax.axis_index("seq"), lax.axis_index("fsdp")

    def copy(self, i, place):
        other = (self.me_s + i) % self.n_seq
        return remote(
            self.own,
            self.every.at[place],
            self.send_sem.at[i],
            self.recv_sem.at[place],
            (other, self.me_f),
        )

    def total(self):
        for i in range(1, self.n_seq):
            self.copy(i, self.me_s).start()
        total = self.own[...]
        for i in range(1, self.n_seq):
            place = (self.me_s + i) % self.n_seq
            self.copy(i, place).wait_recv()
            total = total + self.every[place]
        for i in range(1, self.n_seq):
            self.copy(i, self.me_s).wait_send()
        return total


def share_scratch(n_seq, shape):
    dma = pltpu.SemaphoreType.DMA
    return [pltpu.VMEM(shape, F32), pltpu.VMEM((n_seq,) + shape, F32), dma((n_seq,)), dma((n_seq,))]


def row_sums(values):
    ones = jnp.ones((8, values.shape[1]), F32)
    return lax.dot_general(
        ones,
        values,
        (((1,), (1,)), ((), ())),
        preferred_element_type=F32,
        precision=lax.Precision.HIGHEST,
    )


def front_kernel(n_seq, x, gain, w, normed, raw, totals, *scratch):
    greet_seq(n_seq)
    share = SeqShare(n_seq, *scratch)
    head_width = w.shape[1] // 3
    tile = 256

    def some(i, carry):
        rows = pl.ds(pl.multiple_of(i * tile, tile), tile)
        values = x[rows, :].astype(F32)
        scale = lax.rsqrt(jnp.mean(values * values, axis=-1, keepdims=True) + epsilon)
        low = (values * scale * gain[0:1, :]).astype(BF)
        normed[rows, :] = low
        result = dot(low, w[...], 1, 0)
        raw[rows, :] = result
        for part in range(2):
            piece = result[:, part * head_width : (part + 1) * head_width]
            share.own[part : part + 1, rows] = row_sums(piece * piece)[0:1]
        return carry

    share.own[...] = jnp.zeros_like(share.own)
    lax.fori_loop(0, x.shape[0] // tile, some, 0)
    totals[...] = share.total()


def front(x, gains, w, n_seq, collective_id):
    rows, width = x.shape
    vmem = pl.BlockSpec(memory_space=pltpu.VMEM)
    return pl.pallas_call(
        functools.partial(front_kernel, n_seq),
        out_shape=[
            jax.ShapeDtypeStruct((rows, width), BF),
            jax.ShapeDtypeStruct((rows, w.shape[1]), F32),
            jax.ShapeDtypeStruct((8, rows), F32),
        ],
        in_specs=[vmem] * 3,
        out_specs=[vmem] * 3,
        scratch_shapes=share_scratch(n_seq, (8, rows)),
        compiler_params=pltpu.CompilerParams(
            collective_id=collective_id, has_side_effects=True, vmem_limit_bytes=40 << 20
        ),
        name="front",
    )(x, gains, w)


def column_rms(sums, part, width):
    return lax.rsqrt(sums.T[:, part : part + 1] / width + epsilon)


def turned(values, cosine, sine):
    return values * cosine + pltpu.roll(values, values.shape[1] // 2, 1) * sine


def softmax_columns(k, q, length, scaling):
    scores = dot(k, q, 1, 1) * scaling
    key = lax.broadcasted_iota(jnp.int32, scores.shape, 0)
    scores = jnp.where(key < length, scores, -1e30)
    weights = jnp.exp(scores - jnp.max(scores, axis=0, keepdims=True))
    return weights / jnp.sum(weights, axis=0, keepdims=True)


def attend_kernel(
    width,
    length,
    raw_q,
    raw_k,
    raw_v,
    q_sums,
    k_sums,
    gain,
    q_cos,
    q_sin,
    k_cos,
    k_sin,
    o_ref,
    q_ref,
    k_ref,
    v_ref,
):
    scaling = raw_q.shape[1] ** (-0.5)

    @pl.when(pl.program_id(1) == 0)
    def _():
        key = raw_k[...] * column_rms(k_sums[...], 1, width) * gain[2:3, :]
        k_ref[...] = turned(key, k_cos[...], k_sin[...]).astype(BF)
        v_ref[...] = raw_v[...].astype(BF)

    query = raw_q[...] * column_rms(q_sums[...], 0, width) * gain[1:2, :]
    query = turned(query, q_cos[...], q_sin[...]).astype(BF)
    q_ref[...] = query
    probs = softmax_columns(k_ref[...], query, length[0], scaling).astype(BF)
    o_ref[...] = dot(v_ref[...], probs, 0, 0).T.astype(BF)


def attend(raw, totals, gains, cosine, sine, length, block, width):
    slot_len, head_width = raw.shape[0], raw.shape[1] // 3
    hd = cosine.shape[1]
    heads = head_width // hd
    rows = lambda shift: pl.BlockSpec((block, hd), lambda h, i, n: (i, shift + h))
    full = lambda shift: pl.BlockSpec((slot_len, hd), lambda h, i, n: (0, shift + h))
    table = pl.BlockSpec((block, hd), lambda h, i, n: (i, 0))
    whole_table = pl.BlockSpec((slot_len, hd), lambda h, i, n: (0, 0))
    return pl.pallas_call(
        functools.partial(attend_kernel, width),
        out_shape=[jax.ShapeDtypeStruct((slot_len, head_width), BF)] * 4,
        grid_spec=pltpu.PrefetchScalarGridSpec(
            num_scalar_prefetch=1,
            grid=(heads, slot_len // block),
            in_specs=[
                rows(0),
                full(heads),
                full(2 * heads),
                pl.BlockSpec((8, block), lambda h, i, n: (0, i)),
                pl.BlockSpec((8, slot_len), lambda h, i, n: (0, 0)),
                pl.BlockSpec((4, hd), lambda h, i, n: (0, h)),
                table,
                table,
                whole_table,
                whole_table,
            ],
            out_specs=[rows(0), rows(0), full(0), full(0)],
        ),
        cost_estimate=pl.CostEstimate(
            flops=4 * heads * slot_len * slot_len * hd, bytes_accessed=1 << 23, transcendentals=0
        ),
        name="attend",
    )(length, raw, raw, raw, totals, totals, gains, cosine, sine, cosine, sine)


def attend_back_kernel(
    width,
    length,
    q_ref,
    k_ref,
    v_ref,
    g_ref,
    raw_q,
    raw_k,
    q_sums,
    k_sums,
    gain,
    q_cos,
    q_sin,
    k_cos,
    k_sin,
    dq_ref,
    dk_ref,
    dv_ref,
    dots,
    gain_out,
    dk_sum,
    dv_sum,
):
    head, step = pl.program_id(0), pl.program_id(1)
    last = step == pl.num_programs(1) - 1
    block, hd = q_ref.shape
    scaling = hd ** (-0.5)

    @pl.when(step == 0)
    def _():
        dk_sum[...] = jnp.zeros_like(dk_sum)
        dv_sum[...] = jnp.zeros_like(dv_sum)
        gain_out[...] = jnp.zeros_like(gain_out)

        @pl.when(head == 0)
        def _():
            dots[...] = jnp.zeros_like(dots)

    q, k, v, g = q_ref[...], k_ref[...], v_ref[...], g_ref[...]
    probs = softmax_columns(k, q, length[0], scaling)
    dv_sum[...] += dot(probs.astype(BF), g, 1, 0)
    weights_grad = dot(v, g, 1, 1)
    inner = jnp.sum(probs * weights_grad, axis=0, keepdims=True)
    score_grad = (probs * (weights_grad - inner) * scaling).astype(BF)
    dk_sum[...] += dot(score_grad, q, 1, 0)
    query_grad = dot(k, score_grad, 0, 0).T.astype(BF).astype(F32)
    query_in = turned(query_grad, q_cos[...], -q_sin[...])
    dq_ref[...] = query_in
    product = query_in * raw_q[...]
    rows = pl.ds(pl.multiple_of(step * block, block), block)
    dots[0:1, rows] += row_sums(product * gain[1:2, :])[0:1]
    gain_out[0:1, :] += jnp.sum(
        product * column_rms(q_sums[...], 0, width), axis=0, keepdims=True
    )

    @pl.when(last)
    def _():
        key_in = turned(dk_sum[...].astype(BF).astype(F32), k_cos[...], -k_sin[...])
        dk_ref[...] = key_in
        dv_ref[...] = dv_sum[...].astype(BF)
        product = key_in * raw_k[...]
        dots[1:2, :] += row_sums(product * gain[2:3, :])[0:1]
        gain_out[1:2, :] = jnp.sum(
            product * column_rms(k_sums[...], 1, width), axis=0, keepdims=True
        )


def attend_back(query, key, value, grad, raw, totals, gains, cosine, sine, length, block, width):
    slot_len, head_width = query.shape
    hd = cosine.shape[1]
    heads = head_width // hd
    rows = pl.BlockSpec((block, hd), lambda h, i, n: (i, h))
    full = lambda shift: pl.BlockSpec((slot_len, hd), lambda h, i, n: (0, shift + h))
    table = pl.BlockSpec((block, hd), lambda h, i, n: (i, 0))
    whole_table = pl.BlockSpec((slot_len, hd), lambda h, i, n: (0, 0))
    return pl.pallas_call(
        functools.partial(attend_back_kernel, width),
        out_shape=[
            jax.ShapeDtypeStruct(query.shape, F32),
            jax.ShapeDtypeStruct(query.shape, F32),
            jax.ShapeDtypeStruct(query.shape, BF),
            jax.ShapeDtypeStruct((8, slot_len), F32),
            jax.ShapeDtypeStruct((8, head_width), F32),
        ],
        grid_spec=pltpu.PrefetchScalarGridSpec(
            num_scalar_prefetch=1,
            grid=(heads, slot_len // block),
            in_specs=[
                rows,
                full(0),
                full(0),
                rows,
                rows,
                full(heads),
                pl.BlockSpec((8, block), lambda h, i, n: (0, i)),
                pl.BlockSpec((8, slot_len), lambda h, i, n: (0, 0)),
                pl.BlockSpec((4, hd), lambda h, i, n: (0, h)),
                table,
                table,
                whole_table,
                whole_table,
            ],
            out_specs=[
                rows,
                full(0),
                full(0),
                pl.BlockSpec((8, slot_len), lambda h, i, n: (0, 0)),
                pl.BlockSpec((8, hd), lambda h, i, n: (0, h)),
            ],
            scratch_shapes=[pltpu.VMEM((slot_len, hd), F32), pltpu.VMEM((slot_len, hd), F32)],
        ),
        cost_estimate=pl.CostEstimate(
            flops=20 * heads * slot_len * slot_len * hd, bytes_accessed=1 << 24, transcendentals=0
        ),
        name="attend_back",
    )(
        length,
        query,
        key,
        value,
        grad,
        raw,
        raw,
        totals,
        totals,
        gains,
        cosine,
        sine,
        cosine,
        sine,
    )


def raw_back_kernel(
    n_seq, n_fsdp, width, dq, dk, dv, raw, totals, gain, dots, terms, out, terms_out, *scratch
):
    greet_lines(n_seq, n_fsdp)
    share = SeqShare(n_seq, *scratch[:4])
    term_sum = TermSum(n_seq, n_fsdp, None, *scratch[4:6], None, None, *scratch[6:])
    term_sum.start_fsdp(terms[...])
    head_width = dq.shape[1]
    share.own[...] = dots[...]
    share.own[...] = share.total()
    tile = 256

    def some(i, carry):
        rows = pl.ds(pl.multiple_of(i * tile, tile), tile)
        inner = share.own[:, rows].T / width
        for part, grad in enumerate((dq, dk)):
            columns = slice(part * head_width, (part + 1) * head_width)
            scale = column_rms(totals[:, rows], part, width)
            weighted = grad[rows, :] * gain[part + 1 : part + 2, :]
            cube = scale * scale * scale
            result = scale * weighted - raw[rows, columns] * (cube * inner[:, part : part + 1])
            out[rows, columns] = result.astype(BF)
        out[rows, 2 * head_width :] = dv[rows, :]
        return carry

    lax.fori_loop(0, dq.shape[0] // tile, some, 0)
    terms_out[...] = term_sum.finish()


def raw_back(dq, dk, dv, raw, totals, gains, dots, terms, n_seq, n_fsdp, width, collective_id):
    vmem = pl.BlockSpec(memory_space=pltpu.VMEM)
    dma = pltpu.SemaphoreType.DMA
    return pl.pallas_call(
        functools.partial(raw_back_kernel, n_seq, n_fsdp, width),
        out_shape=[
            jax.ShapeDtypeStruct(raw.shape, BF),
            jax.ShapeDtypeStruct(terms.shape, F32),
        ],
        in_specs=[vmem] * 8,
        out_specs=[vmem] * 2,
        scratch_shapes=share_scratch(n_seq, dots.shape)
        + [
            pltpu.VMEM((n_seq,) + terms.shape, F32),
            pltpu.VMEM((n_fsdp,) + terms.shape, F32),
            dma((n_fsdp,)),
            dma((n_fsdp,)),
        ],
        compiler_params=pltpu.CompilerParams(
            collective_id=collective_id, has_side_effects=True, vmem_limit_bytes=40 << 20
        ),
        name="raw_back",
    )(dq, dk, dv, raw, totals, gains, dots, terms)


def rope_tables(positions, head_dim):
    half = head_dim // 2
    frequency = rope_base ** (-jnp.arange(half, dtype=F32) * 2.0 / head_dim)
    angles = positions.astype(F32)[:, None] * frequency[None, :]
    cosine, sine = jnp.cos(angles), jnp.sin(angles)
    return jnp.concatenate([cosine, cosine], axis=1), jnp.concatenate([-sine, sine], axis=1)


def places(block_routes, experts, capacity):
    count = block_routes.shape[0]
    match = (block_routes[:, :, None] == experts[None, None, :]).astype(F32).sum(axis=1)
    lower = jnp.tril(jnp.ones((count, count), BF), -1)
    rank = dot(lower, match.astype(BF), 1, 0)
    place = jnp.arange(capacity, dtype=F32)
    return match[:, :, None] * (rank[:, :, None] == place[None, None, :]).astype(F32)


def local(
    tokens,
    cotangent,
    lengths,
    routes,
    norm_gains,
    qkv_weight,
    proj_weight,
    router_weight,
    expert_up,
    expert_down,
):
    n_seq, n_fsdp = lax.axis_size("seq"), lax.axis_size("fsdp")
    n_dev = n_seq * n_fsdp
    me_s, me_f = lax.axis_index("seq"), lax.axis_index("fsdp")
    shard_len, width = tokens.shape[1], tokens.shape[2]
    slot_len = shard_len * n_seq
    experts = router_weight.shape[1]
    top_count = routes.shape[2]
    capacity = 3 * shard_len * top_count // (2 * experts)
    piece_ff = expert_down.shape[1]
    pieces_dev = expert_up.shape[0]
    split = FF // piece_ff
    head_dim = width // HEADS
    head_width = width // n_seq
    heads_dev = HEADS // n_seq
    owned = qkv_weight.shape[0]
    block = min(512, slot_len)
    length = lax.dynamic_slice_in_dim(lengths, me_f, 1)
    valid_total = jnp.sum(lengths).astype(F32).reshape(1)
    positions = me_s * shard_len + jnp.arange(shard_len, dtype=jnp.int32)
    row_valid = (positions < length[0]).astype(F32)
    local_routes = routes[0]
    push_all = functools.partial(push, n_seq=n_seq, n_fsdp=n_fsdp, scope="all")
    push_seq = functools.partial(push, n_seq=n_seq, n_fsdp=n_fsdp, scope="seq")

    gain_size, router_size = norm_gains.size, router_weight.size
    pieces = [norm_gains.reshape(-1), router_weight.reshape(-1), local_routes.astype(BF).reshape(-1)]
    small, slot_tokens, qkv_local = first_gather(
        rows_of(jnp.concatenate(pieces), 16),
        tokens[0],
        qkv_weight,
        n_seq,
        n_fsdp,
        collective_id=0,
    )
    slot_tokens = slot_tokens.reshape(slot_len, width)
    qkv_local = qkv_local.reshape(width, 3 * head_width)
    small = small.reshape(n_dev, -1)
    gains = small[:, :gain_size].reshape(n_dev, 4, owned).swapaxes(0, 1).reshape(4, width).astype(F32)
    router = small[:, gain_size : gain_size + router_size].reshape(width, experts)
    all_routes = small[:, gain_size + router_size :][:, : shard_len * top_count]
    all_routes = all_routes.reshape(n_seq, n_fsdp, shard_len, top_count).astype(jnp.int32)

    masked_low = jnp.where(row_valid[:, None] > 0, cotangent[0], jnp.zeros((), BF))
    proj_later = lax.optimization_barrier((proj_weight, slot_tokens))[0]
    proj_rows = lax.all_gather(proj_later, "fsdp", axis=0, tiled=True)

    plane_routes = lax.dynamic_index_in_dim(all_routes, me_s, 0, keepdims=False)
    piece_ids = (jnp.arange(n_seq)[:, None] * n_fsdp + me_f) * pieces_dev + jnp.arange(pieces_dev)
    plane_experts = (piece_ids // split).reshape(-1).astype(jnp.int32)
    plane_hot = jax.vmap(lambda r: places(r, plane_experts, capacity))(plane_routes)
    to_rows = plane_hot.reshape(n_fsdp, shard_len, -1).astype(BF)
    to_places = to_rows.swapaxes(1, 2)

    def exchange(rows):
        return lax.all_to_all(rows, "seq", split_axis=0, concat_axis=0, tiled=True)

    normed_one, raw, totals = front(slot_tokens, gains, qkv_local, n_seq, collective_id=1)
    masked_later = lax.optimization_barrier((masked_low, raw))[0]
    plane_masked = lax.all_gather(masked_later, "fsdp", axis=0)

    def combine(pieces_back):
        total = 0.0
        for piece in range(pieces_dev):
            back = pieces_back[:, piece]
            hot = to_rows.reshape(n_fsdp, shard_len, n_seq, pieces_dev, capacity)[:, :, :, piece]
            total = total + jnp.einsum("ftsc,sfcd->ftd", hot, back, preferred_element_type=F32)
        return total.astype(BF)

    def rms(values):
        return lax.rsqrt(jnp.mean(values * values, axis=-1, keepdims=True) + epsilon)

    own_gains = lax.dynamic_slice_in_dim(gains, me_s * head_width, head_width, 1)
    cosine, sine = rope_tables(jnp.arange(slot_len, dtype=jnp.int32), head_dim)
    attended, query, key, value = attend(
        raw, totals, own_gains, cosine, sine, length, block, width
    )

    resid_in = tokens[0].astype(F32)
    resid_mid = resid_in + product_reduced(attended, proj_rows, 0, n_seq, collective_id=8)
    mid_rms = rms(resid_mid)
    normed_two = (resid_mid * mid_rms * gains[3]).astype(BF)
    router_probs = jax.nn.softmax(jnp.dot(normed_two, router, preferred_element_type=F32), axis=-1)

    own_hot = places(local_routes, jnp.arange(experts, dtype=jnp.int32), capacity)
    gate_slot = jnp.sum(own_hot * router_probs[:, :, None], axis=0)
    gate_send = jnp.broadcast_to(gate_slot[:, None], (experts, split, capacity))
    gate_send = gate_send.reshape(n_dev, pieces_dev * capacity)
    gate_pad = -pieces_dev * capacity % 1024
    gate_send = jnp.pad(gate_send, ((0, 0), (0, gate_pad))).reshape(n_dev, -1, 128)
    gate_recv, cot_rows, *piece_rows = dispatch_rows(
        normed_two,
        to_places,
        gate_send,
        plane_masked,
        n_seq,
        n_fsdp,
        pieces_dev,
        capacity,
        collective_id=6,
    )
    cot_all = exchange(cot_rows)
    gate_recv = gate_recv.reshape(n_dev, -1)[:, : pieces_dev * capacity]
    gate_recv = gate_recv.reshape(n_dev, pieces_dev, capacity)

    forward = []
    outs = None
    for piece in range(pieces_dev):
        gate_rows = gate_recv[:, piece].reshape(-1, 1)
        rows = piece_rows[piece].reshape(-1, width)
        result = expert_forward(rows, gate_rows, expert_up, expert_down, outs, piece, n_seq, n_fsdp)
        outs = result[-1]
        forward.append((gate_rows, rows) + tuple(result[:-1]))
    outs_back = exchange(outs)
    cot_all, forward = lax.optimization_barrier((cot_all, forward))
    backs, gate_backs = [], []
    up_grad = down_grad = None
    for piece in range(pieces_dev):
        gate_rows, rows, hidden, activation, piece_out = forward[piece]
        hidden_grad, out_grad, gate_back = expert_backward(
            cot_all, gate_rows, piece_out, hidden, expert_down, piece
        )
        gate_backs.append(gate_back[0].reshape(n_dev, capacity))
        backs.append(expert_input(hidden_grad, expert_up, piece))
        down_grad = weight_grad(activation, out_grad[None], down_grad, piece, pieces_dev, 0)
        for part in range(2):
            up_grad = weight_grad(rows, hidden_grad, up_grad, piece, pieces_dev, part)
    back_send = jnp.stack(gate_backs, axis=1).reshape(n_dev, pieces_dev * capacity)
    back_send = jnp.pad(back_send, ((0, 0), (0, gate_pad))).reshape(n_dev, -1, 128)
    backs, outs_back, up_grad, down_grad = lax.optimization_barrier(
        (backs, outs_back, up_grad, down_grad)
    )
    backs = [rows.reshape(n_seq, n_fsdp, capacity, width) for rows in backs]
    normed_two_grad, back_recv = return_rows(
        backs, to_rows, back_send, n_seq, n_fsdp, collective_id=7
    )
    outs_back = lax.optimization_barrier((outs_back, normed_two_grad))[0]
    outs_sums = combine(outs_back)

    seen = (all_routes[..., None] == jnp.arange(experts, dtype=jnp.int32)).astype(BF)
    live = jnp.arange(slot_len, dtype=jnp.int32).reshape(n_seq, 1, shard_len) < lengths[None, :, None]
    live = jnp.broadcast_to(live[..., None], all_routes.shape).astype(BF)
    counts = dot(live.reshape(1, -1), seen.reshape(-1, experts), 1, 0)[0]
    fraction = counts / (top_count * valid_total)
    back_recv = back_recv.reshape(n_dev, -1)
    slot_gates_grad = back_recv[:, : pieces_dev * capacity].reshape(experts, split, capacity).sum(axis=1)
    probs_grad = (
        jnp.sum(own_hot * slot_gates_grad[None], axis=2)
        + (experts * fraction / valid_total)[None, :] * row_valid[:, None]
    )
    logits_grad = router_probs * (
        probs_grad - jnp.sum(router_probs * probs_grad, axis=-1, keepdims=True)
    )
    router_term = lax.dot_general(
        logits_grad, normed_two.astype(F32), (((0,), (0,)), ((), ())), precision=lax.Precision.HIGHEST
    )
    normed_two_grad = normed_two_grad + lax.dot_general(
        logits_grad, router.astype(F32), (((1,), (1,)), ((), ())), precision=lax.Precision.HIGHEST
    )

    def rms_back(values, scale, gain, grad):
        weighted = gain * grad
        mean = jnp.mean(weighted * values, axis=-1, keepdims=True)
        return scale * weighted - values * (scale * scale * scale) * mean, jnp.sum(
            grad * values * scale, axis=0
        )

    mid_part, gain_three = rms_back(resid_mid, mid_rms, gains[3], normed_two_grad)
    mid_grad = masked_low.astype(F32) + mid_part
    branch_grad = mid_grad.astype(BF)
    branch_later, outs_sums = lax.optimization_barrier((branch_grad, outs_sums))
    outs_parts = lax.all_to_all(outs_sums, "fsdp", split_axis=0, concat_axis=0, tiled=True)
    slot_branch, router_parts = gather_seq(
        branch_later, router_term, n_seq, n_fsdp, collective_id=9
    )
    slot_branch = slot_branch.reshape(slot_len, width)
    heads_grad = dot(slot_branch, proj_rows, 1, 1).astype(BF)
    query_in, key_in, value_grad, dots, heads_gain = attend_back(
        query,
        key,
        value,
        heads_grad,
        raw,
        totals,
        own_gains,
        cosine,
        sine,
        length,
        block,
        width,
    )
    raw_grad, router_parts = raw_back(
        query_in,
        key_in,
        value_grad,
        raw,
        totals,
        own_gains,
        dots,
        router_parts,
        n_seq,
        n_fsdp,
        width,
        collective_id=4,
    )
    raw_grad, outs_parts = lax.optimization_barrier((raw_grad, outs_parts))
    layer_out = (resid_mid + jnp.sum(outs_parts.astype(F32), axis=0)).astype(BF)[None]

    qkv_part = dot(normed_one, raw_grad, 0, 0).astype(BF)
    qkv_part = qkv_part.reshape(n_seq, n_fsdp, owned, 3 * head_width)
    prob_part = jnp.sum(router_probs * row_valid[:, None], axis=0)
    prob_row = jnp.tile(jnp.pad(prob_part, (0, head_width - experts)), n_seq)
    terms = jnp.pad(jnp.stack([gain_three, prob_row]), ((1, 5), (0, 0)))
    heads_terms = jnp.pad(heads_gain[:2], ((3, 3), (0, 0)))
    input_grad, qkv_grad, last = last_reduce(
        raw_grad,
        qkv_local,
        qkv_part,
        tokens[0],
        mid_grad,
        gains,
        terms,
        heads_terms,
        n_seq,
        n_fsdp,
        collective_id=10,
    )
    input_grad = input_grad[None]

    proj_part = dot(attended, slot_branch, 0, 0).astype(BF)
    proj_grad = lax.psum_scatter(proj_part, "fsdp", scatter_dimension=0, tiled=True).astype(F32)

    router_grad = lax.dynamic_slice_in_dim(router_parts, me_f * owned, owned, 1).T
    prob_total = last[2, :experts]
    last = lax.dynamic_slice_in_dim(last, me_f * owned, owned, 1)
    gains_grad = jnp.stack([last[0], last[3], last[4], last[1]])
    loss_value = (experts * jnp.sum(fraction * prob_total / valid_total)).reshape(1)
    return (
        layer_out,
        input_grad,
        gains_grad,
        qkv_grad,
        proj_grad,
        router_grad,
        up_grad,
        down_grad,
        loss_value,
    )


def solution(mesh):
    rows = P(("seq", "fsdp"), None)
    return jax.shard_map(
        local,
        mesh=mesh,
        in_specs=(
            P("fsdp", "seq", None),
            P("fsdp", "seq", None),
            P(),
            P("fsdp", "seq", None),
            P(None, ("seq", "fsdp")),
            rows,
            rows,
            rows,
            P(("seq", "fsdp"), None, None),
            P(("seq", "fsdp"), None, None),
        ),
        out_specs=(
            P("fsdp", "seq", None),
            P("fsdp", "seq", None),
            P(None, ("seq", "fsdp")),
            rows,
            rows,
            rows,
            P(("seq", "fsdp"), None, None),
            P(("seq", "fsdp"), None, None),
            P(),
        ),
        check_vma=False,
    )
```

```python
import functools

import jax
import jax.numpy as jnp
from jax import lax
from jax.experimental import pallas as pl
from jax.experimental.pallas import tpu as pltpu
from jax.sharding import PartitionSpec as P

HEADS = 16
FF = 1024

epsilon = 1e-06
rope_base = 10000.0
MESH = pl.DeviceIdType.MESH
BF = jnp.bfloat16
F32 = jnp.float32


def dot(a, b, ca, cb):
    return lax.dot_general(a, b, (((ca,), (cb,)), ((), ())), preferred_element_type=F32)


def push_kernel(n_seq, n_fsdp, scope, gather, src, dst, send_sem, recv_sem, own_sem):
    me_s, me_f = lax.axis_index("seq"), lax.axis_index("fsdp")
    n = n_seq * n_fsdp if scope == "all" else n_seq
    me = me_s * n_fsdp + me_f if scope == "all" else me_s

    def where(index):
        if scope == "all":
            return (index // n_fsdp, index % n_fsdp)
        return (index, me_f)

    barrier = pltpu.get_barrier_semaphore()

    def greet(i, carry):
        pl.semaphore_signal(barrier, inc=1, device_id=where((me + i) % n), device_id_type=MESH)
        return carry

    lax.fori_loop(1, n, greet, 0)
    own = pltpu.make_async_copy(src if gather else src.at[me], dst.at[me], own_sem)
    own.start()
    pl.semaphore_wait(barrier, n - 1)

    def copy_to(other):
        return pltpu.make_async_remote_copy(
            src_ref=src if gather else src.at[other],
            dst_ref=dst.at[me],
            send_sem=send_sem.at[other],
            recv_sem=recv_sem.at[me],
            device_id=where(other),
            device_id_type=MESH,
        )

    def copy_from(other):
        return pltpu.make_async_remote_copy(
            src_ref=src if gather else src.at[other],
            dst_ref=dst.at[other],
            send_sem=send_sem.at[other],
            recv_sem=recv_sem.at[other],
            device_id=where(other),
            device_id_type=MESH,
        )

    def send(i, carry):
        copy_to((me + i) % n).start()
        return carry

    lax.fori_loop(1, n, send, 0)

    def finish(i, carry):
        other = (me + i) % n
        copy_from(other).wait_recv()
        copy_to(other).wait_send()
        return carry

    lax.fori_loop(1, n, finish, 0)
    own.wait()


def push(block, n_seq, n_fsdp, scope, gather, collective_id):
    n = n_seq * n_fsdp if scope == "all" else n_seq
    shape = (n,) + (block.shape if gather else block.shape[1:])
    return pl.pallas_call(
        functools.partial(push_kernel, n_seq, n_fsdp, scope, gather),
        out_shape=jax.ShapeDtypeStruct(shape, block.dtype),
        in_specs=[pl.BlockSpec(memory_space=pltpu.VMEM)],
        out_specs=pl.BlockSpec(memory_space=pltpu.VMEM),
        scratch_shapes=[
            pltpu.SemaphoreType.DMA((n,)),
            pltpu.SemaphoreType.DMA((n,)),
            pltpu.SemaphoreType.DMA,
        ],
        compiler_params=pltpu.CompilerParams(collective_id=collective_id, has_side_effects=True),
        name="push_" + scope,
    )(block)


def rows_of(flat, multiple):
    size = flat.shape[0]
    whole = -(-size // (multiple * 128)) * multiple * 128
    return jnp.pad(flat, (0, whole - size)).reshape(-1, 128)


def remote(src, dst, send_sem, recv_sem, device):
    return pltpu.make_async_remote_copy(
        src_ref=src,
        dst_ref=dst,
        send_sem=send_sem,
        recv_sem=recv_sem,
        device_id=device,
        device_id_type=MESH,
    )


def greet_all(n_seq, n_fsdp):
    me_s, me_f = lax.axis_index("seq"), lax.axis_index("fsdp")
    n = n_seq * n_fsdp
    me = me_s * n_fsdp + me_f
    barrier = pltpu.get_barrier_semaphore()

    def greet(i, carry):
        other = (me + i) % n
        pl.semaphore_signal(
            barrier, inc=1, device_id=(other // n_fsdp, other % n_fsdp), device_id_type=MESH
        )
        return carry

    lax.fori_loop(1, n, greet, 0)
    pl.semaphore_wait(barrier, n - 1)


def greet_lines(n_seq, n_fsdp):
    me_s, me_f = lax.axis_index("seq"), lax.axis_index("fsdp")
    barrier = pltpu.get_barrier_semaphore()
    for i in range(1, n_seq):
        pl.semaphore_signal(
            barrier, inc=1, device_id=((me_s + i) % n_seq, me_f), device_id_type=MESH
        )
    for i in range(1, n_fsdp):
        pl.semaphore_signal(
            barrier, inc=1, device_id=(me_s, (me_f + i) % n_fsdp), device_id_type=MESH
        )
    pl.semaphore_wait(barrier, n_seq + n_fsdp - 2)


class Exchange:
    def __init__(self, n_seq, n_fsdp, src, dst, sems):
        self.n, self.n_fsdp, self.src, self.dst = n_seq * n_fsdp, n_fsdp, src, dst
        self.send_sem, self.recv_sem, self.own_sem = sems
        self.me = lax.axis_index("seq") * n_fsdp + lax.axis_index("fsdp")

    def copy(self, i, place):
        other = (self.me + i) % self.n
        return remote(
            self.src.at[other],
            self.dst.at[self.me if place is None else place],
            self.send_sem.at[i],
            self.recv_sem.at[self.me if place is None else place],
            (other // self.n_fsdp, other % self.n_fsdp),
        )

    def own(self):
        return pltpu.make_async_copy(
            self.src.at[self.me], self.dst.at[self.me], self.own_sem
        )

    def start(self):
        self.own().start()

        def one(i, carry):
            self.copy(i, None).start()
            return carry

        lax.fori_loop(1, self.n, one, 0)

    def finish(self):
        def one(i, carry):
            self.copy(i, None).wait_send()
            self.copy(i, (self.me + i) % self.n).wait_recv()
            return carry

        lax.fori_loop(1, self.n, one, 0)
        self.own().wait()


def exchange_sems(n):
    return [
        pltpu.SemaphoreType.DMA((n,)),
        pltpu.SemaphoreType.DMA((n,)),
        pltpu.SemaphoreType.DMA,
    ]


def line_step(n_fsdp, step, arrived, forward):
    me_f = lax.axis_index("fsdp")

    @pl.when(me_f - step >= 0)
    def _():
        arrived(me_f - step)

        @pl.when(me_f + 1 < n_fsdp)
        def _():
            forward(me_f - step, 0, me_f + 1)

    @pl.when(me_f + step < n_fsdp)
    def _():
        arrived(me_f + step)

        @pl.when(me_f >= 1)
        def _():
            forward(me_f + step, 1, me_f - 1)


def line_sent(n_fsdp, step, sent):
    me_f = lax.axis_index("fsdp")

    @pl.when((me_f - step >= 0) & (me_f + 1 < n_fsdp))
    def _():
        sent(me_f - step, 0, me_f + 1)

    @pl.when((me_f + step < n_fsdp) & (me_f >= 1))
    def _():
        sent(me_f + step, 1, me_f - 1)


def flipped(index, bit):
    return index + bit * (1 - 2 * ((index // bit) % 2))


class SeqGather:
    def __init__(self, order, own, block, send_sem, recv_sem):
        self.order, self.own, self.block = order, own, block
        self.send_sem, self.recv_sem = send_sem, recv_sem
        self.me_s, self.me_f = lax.axis_index("seq"), lax.axis_index("fsdp")

    def held(self, stage):
        indices = [self.me_s]
        for bit in self.order[:stage]:
            indices = indices + [flipped(i, bit) for i in indices]
        return indices

    def copies(self, stage):
        partner = flipped(self.me_s, self.order[stage])
        result = []
        for count, index in enumerate(self.held(stage)):
            src = self.own if count == 0 else self.block(index)
            sem = self.send_sem.at[(1 << stage) - 1 + count]
            result.append(
                remote(src, self.block(index), sem, self.recv_sem.at[index], (partner, self.me_f))
            )
        return result

    def start(self, stage):
        for copy in self.copies(stage):
            copy.start()

    def wait(self, stage):
        for index in self.held(stage):
            index = flipped(index, self.order[stage])
            remote(
                self.block(index),
                self.block(index),
                self.send_sem.at[0],
                self.recv_sem.at[index],
                (self.me_s, self.me_f),
            ).wait_recv()

    def sent(self):
        for stage in range(len(self.order)):
            for copy in self.copies(stage):
                copy.wait_send()


def gather_orders(n_seq):
    bits = [1 << b for b in range(n_seq.bit_length() - 1)]
    return bits[1:] + bits[:1], bits[:0:-1] + bits[:1]


def block_places(routes, ids, capacity):
    count = routes.shape[1]
    match = jnp.zeros((ids.shape[0], count), F32)
    for k in range(routes.shape[0]):
        match = match + (routes[k : k + 1, :] == ids).astype(F32)
    row = lax.broadcasted_iota(jnp.int32, (count, count), 0)
    column = lax.broadcasted_iota(jnp.int32, (count, count), 1)
    rank = dot(match.astype(BF), (row < column).astype(BF), 1, 0)
    place = lax.broadcasted_iota(jnp.int32, (ids.shape[0], capacity, count), 1).astype(F32)
    hot = match[:, None, :] * (rank[:, None, :] == place).astype(F32)
    return hot.reshape(ids.shape[0] * capacity, count)


def first_kernel(
    n_seq,
    n_fsdp,
    pieces,
    split,
    capacity,
    owned,
    top,
    small,
    tokens,
    qkv,
    masked,
    small_all,
    gains,
    slot,
    qkv_all,
    masked_all,
    to_places,
    to_rows,
    send,
    own_sem,
    small_send,
    small_recv,
    qkv_send,
    qkv_recv,
    line_send,
    line_recv,
    token_send,
    token_recv,
    row_send,
    row_recv,
    row_own,
):
    me_s, me_f = lax.axis_index("seq"), lax.axis_index("fsdp")
    n = n_seq * n_fsdp
    me = me_s * n_fsdp + me_f
    head_width = qkv_all.shape[3] // 3
    width = head_width * n_seq
    half = tokens.shape[0] // 2
    orders = gather_orders(n_seq)
    stages = len(orders[0])

    def columns(owner, part):
        start = pl.multiple_of(part * width + owner * head_width, 128)
        return qkv.at[:, pl.ds(start, head_width)]

    def column_place(source, part):
        return qkv_all.at[source, me_f, :, pl.ds(part * head_width, head_width)]

    own = [
        pltpu.make_async_copy(small, small_all.at[me], own_sem.at[0]),
        pltpu.make_async_copy(tokens, slot.at[me_s], own_sem.at[1]),
    ] + [
        pltpu.make_async_copy(columns(me_s, part), column_place(me_s, part), own_sem.at[2 + part])
        for part in range(3)
    ]
    for copy in own:
        copy.start()
    greet_all(n_seq, n_fsdp)

    def small_copy(i):
        other = (me + i) % n
        return remote(
            small,
            small_all.at[me],
            small_send.at[i],
            small_recv.at[me],
            (other // n_fsdp, other % n_fsdp),
        )

    def small_arrived(other):
        return remote(
            small,
            small_all.at[other],
            small_send.at[0],
            small_recv.at[other],
            (other // n_fsdp, other % n_fsdp),
        )

    def small_start(i, carry):
        small_copy(i).start()
        return carry

    lax.fori_loop(1, n, small_start, 0)

    def column_copy(i, part):
        other = (me_s + i) % n_seq
        return remote(
            columns(other, part),
            column_place(me_s, part),
            qkv_send.at[i, part],
            qkv_recv.at[me_s, part],
            (other, me_f),
        )

    for i in range(1, n_seq):
        for part in range(3):
            column_copy(i, part).start()

    flows = []
    for side in range(2):
        rows = pl.ds(side * half, half)
        flows.append(
            SeqGather(
                orders[side],
                tokens.at[rows],
                lambda index, rows=rows: slot.at[index, rows],
                token_send.at[side],
                token_recv.at[side],
            )
        )

    def point(stage):
        for flow in flows:
            if 0 < stage <= stages:
                flow.wait(stage - 1)
            if stage < stages:
                flow.start(stage)

    point(0)
    for copy in own:
        copy.wait()

    piece = lax.broadcasted_iota(jnp.int32, (n_seq * pieces, 1), 0)
    piece = ((piece // pieces) * n_fsdp + me_f) * pieces + piece % pieces
    ids = piece // split

    def row_copy(i, place):
        other = (me_s + i) % n_seq
        return remote(
            send.at[other], masked_all.at[place, :, me_f], row_send.at[i], row_recv.at[place], (other, me_f)
        )

    def own_row():
        return pltpu.make_async_copy(send.at[me_s], masked_all.at[me_s, :, me_f], row_own)

    def table(block):
        routes = small_all[me_s * n_fsdp + block, 8 : 8 + top, :].astype(F32).astype(jnp.int32)
        hot = block_places(routes, ids, capacity)
        to_places[block] = hot.astype(BF)
        to_rows[block] = hot.T.astype(BF)

    def scatter():
        def some(lanes):
            picked = dot(to_places[me_f], masked[:, lanes], 1, 0).astype(BF)
            send[:, :, :, lanes] = picked.reshape(n_seq, pieces, capacity, -1)

        chunked(width, 512, some)
        for i in range(1, n_seq):
            row_copy(i, me_s).start()
        own_row().start()

    def line_copy(part, step, block, way, to):
        place = qkv_all.at[part, block]
        return remote(
            place, place, line_send.at[part, way, step], line_recv.at[part, block], (me_s, to)
        )

    def line_first(part):
        @pl.when(me_f + 1 < n_fsdp)
        def _():
            line_copy(part, 0, me_f, 0, me_f + 1).start()

        @pl.when(me_f >= 1)
        def _():
            line_copy(part, 0, me_f, 1, me_f - 1).start()

    def column_arrived(i, carry):
        source = (me_s + i) % n_seq

        @pl.when(i > 0)
        def _():
            for part in range(3):
                remote(
                    columns(source, part),
                    column_place(source, part),
                    qkv_send.at[i, part],
                    qkv_recv.at[source, part],
                    (source, me_f),
                ).wait_recv()

        line_first(source)
        return carry

    lax.fori_loop(0, n_seq, column_arrived, 0)

    def column_step(step):
        def column_next(i, carry):
            part = (me_s + i) % n_seq
            line_step(
                n_fsdp,
                step,
                lambda block: line_copy(part, 0, block, 0, me_f).wait_recv(),
                lambda block, way, to: line_copy(part, step, block, way, to).start(),
            )
            return carry

        lax.fori_loop(0, n_seq, column_next, 0)

    point(1)
    table(me_f)
    for stage in range(2, stages + 1):
        point(stage)
    scatter()
    for step in range(1, n_fsdp):
        column_step(step)
    for i in range(1, n_fsdp):
        block = (me_f + i) % n_fsdp
        small_arrived(me_s * n_fsdp + block).wait_recv()
        table(block)
    for flow in flows:
        flow.sent()

    def small_wait(i, carry):
        other = (me + i) % n
        small_copy(i).wait_send()

        @pl.when(other // n_fsdp != me_s)
        def _():
            small_arrived(other).wait_recv()

        return carry

    lax.fori_loop(1, n, small_wait, 0)

    lane = lax.broadcasted_iota(jnp.int32, (8, 128), 1)
    each = 128 // owned
    for j in range(width // 128):
        total = jnp.zeros((8, 128), F32)
        for k in range(each):
            some = jnp.where(lane < owned, small_all[j * each + k, :8, :].astype(F32), 0.0)
            total = total + (pltpu.roll(some, k * owned, 1) if k else some)
        gains[:, j * 128 : (j + 1) * 128] = total

    def column_sent(i, carry):
        for part in range(3):
            column_copy(i, part).wait_send()
        return carry

    lax.fori_loop(1, n_seq, column_sent, 0)

    def line_done(part, carry):
        for step in range(n_fsdp):
            line_sent(
                n_fsdp,
                step,
                lambda block, way, to: line_copy(part, step, block, way, to).wait_send(),
            )
        return carry

    lax.fori_loop(0, n_seq, line_done, 0)
    own_row().wait()
    for i in range(1, n_seq):
        row_copy(i, me_s).wait_send()
        row_copy(i, (me_s + i) % n_seq).wait_recv()


def first_gather(
    small, tokens, qkv, masked, n_seq, n_fsdp, pieces, split, capacity, top, collective_id
):
    owned = qkv.shape[0]
    rows, width = tokens.shape
    head_width = width // n_seq
    n = n_seq * n_fsdp
    places_all = n_seq * pieces * capacity
    vmem = pl.BlockSpec(memory_space=pltpu.VMEM)
    any_space = pl.BlockSpec(memory_space=pl.ANY)
    dma = pltpu.SemaphoreType.DMA
    return pl.pallas_call(
        functools.partial(first_kernel, n_seq, n_fsdp, pieces, split, capacity, owned, top),
        out_shape=[
            jax.ShapeDtypeStruct((n,) + small.shape, BF),
            jax.ShapeDtypeStruct((8, width), F32),
            jax.ShapeDtypeStruct((n_seq,) + tokens.shape, BF),
            jax.ShapeDtypeStruct((n_seq, n_fsdp, owned, 3 * head_width), BF),
            jax.ShapeDtypeStruct((n_seq, pieces, n_fsdp, capacity, width), BF),
            jax.ShapeDtypeStruct((n_fsdp, places_all, rows), BF),
            jax.ShapeDtypeStruct((n_fsdp, rows, places_all), BF),
        ],
        in_specs=[vmem] * 4,
        out_specs=[vmem, vmem, any_space, any_space, any_space, vmem, vmem],
        scratch_shapes=[
            pltpu.VMEM((n_seq, pieces, capacity, width), BF),
            dma((5,)),
            dma((n,)),
            dma((n,)),
            dma((n_seq, 3)),
            dma((n_seq, 3)),
            dma((n_seq, 2, n_fsdp)),
            dma((n_seq, n_fsdp)),
            dma((2, n_seq - 1)),
            dma((2, n_seq)),
            dma((n_seq,)),
            dma((n_seq,)),
            dma,
        ],
        compiler_params=pltpu.CompilerParams(
            collective_id=collective_id, has_side_effects=True, vmem_limit_bytes=40 << 20
        ),
        name="first_gather",
    )(small, tokens, qkv, masked)


def greet_seq(n_seq):
    me_s, me_f = lax.axis_index("seq"), lax.axis_index("fsdp")
    barrier = pltpu.get_barrier_semaphore()
    for i in range(1, n_seq):
        pl.semaphore_signal(
            barrier, inc=1, device_id=((me_s + i) % n_seq, me_f), device_id_type=MESH
        )
    pl.semaphore_wait(barrier, n_seq - 1)


class TermSum:
    def __init__(
        self, n_seq, n_fsdp, terms, seq_terms, fsdp_terms, seq_send, seq_recv, fsdp_send, fsdp_recv
    ):
        self.n_seq, self.n_fsdp, self.terms = n_seq, n_fsdp, terms
        self.seq_terms, self.fsdp_terms = seq_terms, fsdp_terms
        self.seq_send, self.seq_recv = seq_send, seq_recv
        self.fsdp_send, self.fsdp_recv = fsdp_send, fsdp_recv
        self.me_s, self.me_f = lax.axis_index("seq"), lax.axis_index("fsdp")

    def part(self, owner):
        columns = self.seq_terms.shape[2]
        return self.terms.at[:, pl.ds(pl.multiple_of(owner * columns, 128), columns)]

    def seq_copy(self, i, place):
        other = (self.me_s + i) % self.n_seq
        return remote(
            self.part(other),
            self.seq_terms.at[place],
            self.seq_send.at[i],
            self.seq_recv.at[place],
            (other, self.me_f),
        )

    def fsdp_copy(self, i, place):
        other = (self.me_f + i) % self.n_fsdp
        return remote(
            self.seq_terms.at[self.me_s],
            self.fsdp_terms.at[place],
            self.fsdp_send.at[i],
            self.fsdp_recv.at[place],
            (self.me_s, other),
        )

    def start_seq(self):
        for i in range(1, self.n_seq):
            self.seq_copy(i, self.me_s).start()

    def over_seq(self):
        result = self.part(self.me_s)[...]
        for i in range(1, self.n_seq):
            place = (self.me_s + i) % self.n_seq
            self.seq_copy(i, place).wait_recv()
            result = result + self.seq_terms[place]
        for i in range(1, self.n_seq):
            self.seq_copy(i, self.me_s).wait_send()
        return result

    def start_fsdp(self, more):
        self.seq_terms[self.me_s] = more + (self.over_seq() if self.terms is not None else 0.0)
        for i in range(1, self.n_fsdp):
            self.fsdp_copy(i, self.me_f).start()

    def finish(self):
        result = self.seq_terms[self.me_s]
        for i in range(1, self.n_fsdp):
            place = (self.me_f + i) % self.n_fsdp
            self.fsdp_copy(i, place).wait_recv()
            result = result + self.fsdp_terms[place]
        for i in range(1, self.n_fsdp):
            self.fsdp_copy(i, self.me_f).wait_send()
        return result


def term_scratch(n_seq, n_fsdp, shape):
    dma = pltpu.SemaphoreType.DMA
    return [
        pltpu.VMEM((n_seq,) + shape, F32),
        pltpu.VMEM((n_fsdp,) + shape, F32),
        dma((n_seq,)),
        dma((n_seq,)),
        dma((n_fsdp,)),
        dma((n_fsdp,)),
    ]


def gather_kernel(n_seq, n_fsdp, x, terms, out, total, own_sem, send_sem, recv_sem, *scratch):
    me_s = lax.axis_index("seq")
    half = x.shape[0] // 2
    own = pltpu.make_async_copy(x, out.at[me_s], own_sem)
    own.start()
    term_sum = TermSum(n_seq, n_fsdp, terms, scratch[0], None, *scratch[1:], None, None)
    greet_seq(n_seq)
    flows = []
    for side, order in enumerate(gather_orders(n_seq)):
        rows = pl.ds(side * half, half)
        flows.append(
            SeqGather(
                order,
                x.at[rows],
                lambda index, rows=rows: out.at[index, rows],
                send_sem.at[side],
                recv_sem.at[side],
            )
        )
    for stage in range(len(flows[0].order)):
        for flow in flows:
            flow.start(stage)
        if stage == 0:
            term_sum.start_seq()
        if stage == 1:
            total[...] = term_sum.over_seq()
        for flow in flows:
            flow.wait(stage)
    for flow in flows:
        flow.sent()
    own.wait()


def gather_seq(x, terms, n_seq, n_fsdp, collective_id):
    vmem = pl.BlockSpec(memory_space=pltpu.VMEM)
    dma = pltpu.SemaphoreType.DMA
    part = (terms.shape[0], terms.shape[1] // n_seq)
    return pl.pallas_call(
        functools.partial(gather_kernel, n_seq, n_fsdp),
        out_shape=[
            jax.ShapeDtypeStruct((n_seq,) + x.shape, x.dtype),
            jax.ShapeDtypeStruct(part, terms.dtype),
        ],
        in_specs=[vmem] * 2,
        out_specs=[vmem] * 2,
        scratch_shapes=[
            dma,
            dma((2, n_seq - 1)),
            dma((2, n_seq)),
            pltpu.VMEM((n_seq,) + part, F32),
            dma((n_seq,)),
            dma((n_seq,)),
        ],
        compiler_params=pltpu.CompilerParams(collective_id=collective_id, has_side_effects=True),
        cost_estimate=pl.CostEstimate(flops=0, bytes_accessed=1 << 26, transcendentals=0),
        name="gather_seq",
    )(x, terms)


class SeqReduce:
    def __init__(self, n_seq, a, w, w_dim, sums, got, send_sem, recv_sem):
        self.a, self.w, self.w_dim, self.sums, self.got = a, w, w_dim, sums, got
        self.send_sem, self.recv_sem = send_sem, recv_sem
        self.me_s, self.me_f = lax.axis_index("seq"), lax.axis_index("fsdp")
        self.orders = [order[-1:] + order[-2::-1] for order in gather_orders(n_seq)]
        self.stages = len(self.orders[0])
        self.half = sums.shape[1] // 2
        self.width = sums.shape[2]

    def combined(self, index, bits):
        indices = [index]
        for bit in bits:
            indices = indices + [flipped(i, bit) for i in indices]
        return indices

    def product(self, index):
        def some(columns):
            w = self.w[:, columns] if self.w_dim == 0 else self.w[columns, :]
            self.sums[index, :, columns] = dot(self.a[index], w, 1, self.w_dim).astype(BF)

        chunked(self.width, 512, some)

    def copy(self, stage, side, count, index):
        order = self.orders[side]
        slot = sum(1 << (self.stages - 1 - s) for s in range(stage)) + count
        rows = pl.ds(side * self.half, self.half)
        return remote(
            self.sums.at[index, rows],
            self.got.at[slot, rows],
            self.send_sem.at[side, slot],
            self.recv_sem.at[side, slot],
            (flipped(self.me_s, order[stage]), self.me_f),
        )

    def leaving(self, stage, side):
        order = self.orders[side]
        return self.combined(flipped(self.me_s, order[stage]), order[stage + 1 :])

    def start(self, stage):
        if stage == 0:
            for count, index in enumerate(self.leaving(0, 0)):
                self.product(index)
                for side in range(2):
                    self.copy(0, side, self.twin(count) if side == 1 else count, index).start()
            for index in self.combined(self.me_s, self.orders[0][1:]):
                self.product(index)
        else:
            for side in range(2):
                for count, index in enumerate(self.leaving(stage, side)):
                    self.copy(stage, side, count, index).start()

    def twin(self, count):
        first, second = self.orders[0][1:], self.orders[1][1:]
        place = 0
        for position, bit in enumerate(first):
            if (count >> position) & 1:
                place += 1 << second.index(bit)
        return place

    def finish(self, stage, last=None):
        for side in range(2):
            order = self.orders[side]
            rows = pl.ds(side * self.half, self.half)
            for count, index in enumerate(self.combined(self.me_s, order[stage + 1 :])):
                copy = self.copy(stage, side, count, index)
                copy.wait_recv()
                slot = sum(1 << (self.stages - 1 - s) for s in range(stage)) + count

                def some(columns):
                    total = self.sums[index, rows, columns].astype(F32)
                    total = total + self.got[slot, rows, columns].astype(F32)
                    if last is None:
                        self.sums[index, rows, columns] = total.astype(BF)
                    else:
                        last[rows, columns] = total

                chunked(self.width, 1024, some)

    def events(self, last):
        def leave(count, index):
            self.product(index)
            for side in range(2):
                self.copy(0, side, self.twin(count) if side == 1 else count, index).start()

        result = [
            (1, functools.partial(leave, count, index))
            for count, index in enumerate(self.leaving(0, 0))
        ]
        for index in self.combined(self.me_s, self.orders[0][1:]):
            result.append((1, functools.partial(self.product, index)))
        result.append((1, functools.partial(self.finish, 0, last if self.stages == 1 else None)))
        for stage in range(1, self.stages):
            result.append((0, functools.partial(self.start, stage)))
            result.append(
                (7, functools.partial(self.finish, stage, last if stage == self.stages - 1 else None))
            )
        return result

    def sent(self):
        for stage in range(self.stages):
            for side in range(2):
                for count, index in enumerate(self.leaving(stage, side)):
                    self.copy(stage, side, count, index).wait_send()


def reduce_scratch(n_seq, rows, width):
    dma = pltpu.SemaphoreType.DMA
    return [
        pltpu.VMEM((n_seq, rows, width), BF),
        pltpu.VMEM((n_seq - 1, rows, width), BF),
        dma((2, n_seq - 1)),
        dma((2, n_seq - 1)),
    ]


def reduce_kernel(n_seq, w_dim, a, w, out, *scratch):
    greet_seq(n_seq)
    reduce = SeqReduce(n_seq, a, w, w_dim, *scratch)
    for stage in range(reduce.stages):
        reduce.start(stage)
        reduce.finish(stage, out if stage == reduce.stages - 1 else None)
    reduce.sent()


def product_reduced(a, w, w_dim, n_seq, collective_id):
    rows = a.shape[0] // n_seq
    width = w.shape[1 - w_dim]
    return pl.pallas_call(
        functools.partial(reduce_kernel, n_seq, w_dim),
        out_shape=jax.ShapeDtypeStruct((rows, width), F32),
        in_specs=[pl.BlockSpec(memory_space=pltpu.VMEM)] * 2,
        out_specs=pl.BlockSpec(memory_space=pltpu.VMEM),
        scratch_shapes=reduce_scratch(n_seq, rows, width),
        compiler_params=pltpu.CompilerParams(
            collective_id=collective_id, has_side_effects=True, vmem_limit_bytes=40 << 20
        ),
        name="product_reduced",
    )(a.reshape(n_seq, rows, -1), w)


def last_kernel(
    n_seq,
    n_fsdp,
    a,
    w,
    part,
    x,
    mid,
    gains,
    terms_in,
    heads,
    input_out,
    qkv_out,
    total,
    *scratch,
):
    up, down, done, got, up_send, up_recv, down_send, down_recv, done_send, done_recv = scratch[:10]
    one, terms, seq_terms, fsdp_terms, seq_send, seq_recv, fsdp_send, fsdp_recv = scratch[10:18]
    me_s, me_f = lax.axis_index("seq"), lax.axis_index("fsdp")
    head_width = part.shape[3] // 3
    width = n_seq * head_width
    greet_lines(n_seq, n_fsdp)
    reduce = SeqReduce(n_seq, a, w, 1, *scratch[18:])
    term_sum = TermSum(
        n_seq,
        n_fsdp,
        terms,
        seq_terms,
        fsdp_terms,
        seq_send,
        seq_recv,
        fsdp_send,
        fsdp_recv,
    )

    def input_rows():
        tile = 32
        terms[...] = terms_in[...]

        def some(i, carry):
            rows = pl.ds(pl.multiple_of(i * tile, tile), tile)
            values = x[rows, :].astype(F32)
            scale = lax.rsqrt(jnp.mean(values * values, axis=-1, keepdims=True) + epsilon)
            grad = one[rows, :]
            weighted = grad * gains[0:1, :]
            mean = jnp.mean(weighted * values, axis=-1, keepdims=True)
            result = scale * weighted - values * (scale * scale * scale * mean)
            input_out[rows, :] = (mid[rows, :] + result).astype(BF)
            terms[0:1, :] += jnp.sum(grad * values * scale, axis=0, keepdims=True)
            return carry

        lax.fori_loop(0, x.shape[0] // tile, some, 0)
        term_sum.start_seq()

    def line_copy(src, way, s, block):
        buffer, send, recv = (up, up_send, up_recv) if way == 0 else (down, down_send, down_recv)
        to = me_f + 1 if way == 0 else me_f - 1
        place = buffer.at[block, s]
        return remote(
            place if src is None else src, place, send.at[block, s], recv.at[block, s], (me_s, to)
        )

    def done_copy(i):
        s = (me_s + i) % n_seq
        return remote(done.at[s], got.at[me_s], done_send.at[i], done_recv.at[me_s], (s, me_f))

    def stream(way, number):
        buffer = up if way == 0 else down
        behind = me_f if way == 0 else n_fsdp - 1 - me_f
        turn, i = number // n_seq, number % n_seq
        s = (me_s + i) % n_seq
        block = n_fsdp - 1 - turn if way == 0 else turn
        ahead = n_fsdp - 1 - behind
        on_time = (number >= 0) & (turn < ahead)
        finishes_up = (me_f == n_fsdp - 1) | ((n_fsdp - 1 > 2 * me_f) & (me_f > 0))

        @pl.when(on_time & (behind == 0))
        def _():
            line_copy(part.at[s, block], way, s, block).start()

        @pl.when(on_time & (behind > 0))
        def _():
            line_copy(None, way, s, block).wait_recv()
            total = buffer[block, s].astype(F32) + part[s, block].astype(F32)
            buffer[block, s] = total.astype(BF)
            line_copy(None, way, s, block).start()

        @pl.when((number >= 0) & (turn == ahead) & (behind > 0))
        def _():
            line_copy(None, way, s, me_f).wait_recv()
            done[s] = (done[s].astype(F32) + buffer[me_f, s].astype(F32)).astype(BF)

            @pl.when(finishes_up if way == 0 else jnp.logical_not(finishes_up))
            def _():
                @pl.when(i > 0)
                def _():
                    done_copy(i).start()

    lag = 2
    slots = n_seq * (n_fsdp - 1) + lag * (n_fsdp - 1)

    def run(first, last):
        def slot(number, carry):
            stream(0, number - lag * me_f)
            stream(1, number - lag * (n_fsdp - 1 - me_f))
            return carry

        lax.fori_loop(first, last, slot, 0)

    def begin(i, carry):
        done[i] = part[i, me_f]
        return carry

    lax.fori_loop(0, n_seq, begin, 0)
    reached = 0
    for number, event in enumerate(
        reduce.events(one)
        + [(0, input_rows), (3, functools.partial(term_sum.start_fsdp, heads[...]))]
    ):
        run(reached, min(slots, reached + event[0]))
        reached = min(slots, reached + event[0])
        event[1]()
    run(reached, slots)

    def place(s, rows):
        for third in range(3):
            columns = pl.ds(pl.multiple_of(third * width + s * head_width, 128), head_width)
            qkv_out[:, columns] = rows[:, third * head_width : (third + 1) * head_width].astype(F32)

    place(me_s, done[me_s])

    def arrived(i, carry):
        s = (me_s + i) % n_seq
        remote(done.at[s], got.at[s], done_send.at[i], done_recv.at[s], (s, me_f)).wait_recv()
        place(s, got[s])
        return carry

    lax.fori_loop(1, n_seq, arrived, 0)

    def all_sent(i, carry):
        s = (me_s + i) % n_seq

        @pl.when(i > 0)
        def _():
            done_copy(i).wait_send()

        for j in range(n_fsdp - 1):

            @pl.when(me_f + j < n_fsdp - 1)
            def _():
                line_copy(None, 0, s, n_fsdp - 1 - j).wait_send()

            @pl.when(j < me_f)
            def _():
                line_copy(None, 1, s, j).wait_send()

        return carry

    lax.fori_loop(0, n_seq, all_sent, 0)
    reduce.sent()
    total[...] = term_sum.finish()


def last_reduce(a, w, part, x, mid, gains, terms, heads, n_seq, n_fsdp, collective_id):
    rows, width = a.shape[0] // n_seq, w.shape[0]
    owned, columns = part.shape[2:]
    vmem = pl.BlockSpec(memory_space=pltpu.VMEM)
    dma = pltpu.SemaphoreType.DMA
    return pl.pallas_call(
        functools.partial(last_kernel, n_seq, n_fsdp),
        out_shape=[
            jax.ShapeDtypeStruct((rows, width), BF),
            jax.ShapeDtypeStruct((owned, n_seq * columns), F32),
            jax.ShapeDtypeStruct(heads.shape, F32),
        ],
        in_specs=[vmem] * 8,
        out_specs=[vmem] * 3,
        scratch_shapes=[
            pltpu.VMEM((n_fsdp, n_seq, owned, columns), BF),
            pltpu.VMEM((n_fsdp, n_seq, owned, columns), BF),
            pltpu.VMEM((n_seq, owned, columns), BF),
            pltpu.VMEM((n_seq, owned, columns), BF),
            dma((n_fsdp, n_seq)),
            dma((n_fsdp, n_seq)),
            dma((n_fsdp, n_seq)),
            dma((n_fsdp, n_seq)),
            dma((n_seq,)),
            dma((n_seq,)),
            pltpu.VMEM((rows, width), F32),
            pltpu.VMEM(terms.shape, F32),
        ]
        + term_scratch(n_seq, n_fsdp, heads.shape)
        + reduce_scratch(n_seq, rows, width),
        compiler_params=pltpu.CompilerParams(
            collective_id=collective_id, has_side_effects=True, vmem_limit_bytes=50 << 20
        ),
        cost_estimate=pl.CostEstimate(flops=0, bytes_accessed=1 << 27, transcendentals=0),
        name="last_reduce",
    )(a.reshape(n_seq, rows, -1), w, part, x, mid, gains, terms, heads)


def chunked(total, size, body):
    def step(i, carry):
        body(pl.ds(pl.multiple_of(i * size, size), size))
        return carry

    lax.fori_loop(0, total // size, step, 0)


def dispatch_kernel(n_seq, n_fsdp, pieces, x, hot, gates, masked, before, w_up, w_down, *refs):
    masked_all, columns_out, scaled = refs[:3]
    outs, hiddens, acts, results = (refs[3 + k * pieces : 3 + (k + 1) * pieces] for k in range(4))
    rest = refs[3 + 4 * pieces :]
    gates_out, gathered, send, total = rest[:4]
    own_sem, line_send, line_recv, row_send, row_recv, own_two, send_two, recv_two = rest[4:12]
    gate_exchange = Exchange(n_seq, n_fsdp, gates, gates_out, rest[12:])
    me_s, me_f = lax.axis_index("seq"), lax.axis_index("fsdp")
    width = x.shape[1]
    capacity = outs[0].shape[2]
    greet_all(n_seq, n_fsdp)

    def line_copy(step, block, way, to):
        src = x if step == 0 else gathered.at[block]
        return remote(
            src, gathered.at[block], line_send.at[way, step], line_recv.at[block], (me_s, to)
        )

    def row_copy(block, i, piece, place):
        other = (me_s + i) % n_seq
        return remote(
            send.at[block, other, piece],
            outs[piece].at[place, block],
            row_send.at[block, i, piece],
            row_recv.at[place, block, piece],
            (other, me_f),
        )

    def own_copy(block, piece):
        return pltpu.make_async_copy(
            send.at[block, me_s, piece], outs[piece].at[me_s, block], own_sem.at[block, piece]
        )

    def masked_copy(block, i, place):
        other = (me_s + i) % n_seq
        return remote(
            send.at[block, other],
            masked_all.at[place, :, block],
            send_two.at[block, i],
            recv_two.at[place, block],
            (other, me_f),
        )

    def own_masked(block):
        return pltpu.make_async_copy(
            send.at[block, me_s], masked_all.at[me_s, :, block], own_two.at[block]
        )

    def pick(block, rows):
        def some(columns):
            picked = dot(hot[block], rows[:, columns], 1, 0).astype(BF)
            send[block, :, :, :, columns] = picked.reshape(n_seq, pieces, capacity, -1)

        chunked(width, 512, some)

    def scatter(block, rows):
        pick(block, rows)
        for i in range(1, n_seq):
            for piece in range(pieces):
                row_copy(block, i, piece, me_s).start()
        for piece in range(pieces):
            own_copy(block, piece).start()

    def scatter_masked(block):
        for piece in range(pieces):
            own_copy(block, piece).wait()
            for i in range(1, n_seq):
                row_copy(block, i, piece, me_s).wait_send()
        pick(block, masked.at[block])
        for i in range(1, n_seq):
            masked_copy(block, i, me_s).start()
        own_masked(block).start()

    def around(step, act):
        @pl.when(me_f - step >= 0)
        def _():
            act(me_f - step)

        @pl.when(me_f + step < n_fsdp)
        def _():
            act(me_f + step)

    @pl.when(me_f + 1 < n_fsdp)
    def _():
        line_copy(0, me_f, 0, me_f + 1).start()

    @pl.when(me_f >= 1)
    def _():
        line_copy(0, me_f, 1, me_f - 1).start()

    scatter(me_f, x)
    gate_exchange.start()
    for step in range(1, n_fsdp):
        line_step(
            n_fsdp,
            step,
            lambda block: line_copy(1, block, 0, me_f).wait_recv(),
            lambda block, way, to: line_copy(step, block, way, to).start(),
        )
        around(step, lambda block: scatter(block, gathered.at[block]))
    for step in range(1, n_fsdp):
        around(step, scatter_masked)
    for step in range(n_fsdp):
        line_sent(
            n_fsdp, step, lambda block, way, to: line_copy(step, block, way, to).wait_send()
        )

    gate_exchange.finish()
    n = n_seq * n_fsdp
    for piece in range(pieces):
        lanes = lax.broadcasted_iota(jnp.int32, (n, capacity, 128), 2)
        place = lax.broadcasted_iota(jnp.int32, (n, capacity, 128), 1)
        values = jnp.broadcast_to(gates_out[:, piece : piece + 1, :], (n, capacity, 128))
        column = jnp.sum(jnp.where(lanes == place, values, 0.0), axis=2, keepdims=True)
        columns_out[piece] = column.reshape(n * capacity, 1)

    for piece in range(pieces):
        own_copy(me_f, piece).wait()
        for i in range(1, n_seq):
            row_copy(me_f, i, piece, me_s).wait_send()
    for piece in range(pieces):
        for block in range(n_fsdp):
            for i in range(1, n_seq):
                row_copy(block, i, piece, (me_s + i) % n_seq).wait_recv()

    ff = w_down.shape[1]
    tile = min(256, ff)
    steps = ff // tile
    spans = seq_tile(n_seq, n_fsdp * capacity, 3072 // n_fsdp)
    count = spans * n_fsdp * capacity
    for piece in range(pieces):

        def body(rows, w_gate, w_value, w_back, hidden, act, result, scaled_rows):
            step = pl.program_id(1)
            low = rows[...].reshape(count, width)
            gate = dot(low, w_gate[0], 1, 0)
            up = dot(low, w_value[0], 1, 0)
            hidden[0] = gate
            hidden[1] = up
            act[...] = (gate * jax.nn.sigmoid(gate) * up).astype(BF)
            product = dot(act[...], w_back[0], 1, 0)

            @pl.when(step == 0)
            def _():
                total[...] = product

            @pl.when(step > 0)
            def _():
                total[...] += product

            @pl.when(step == steps - 1)
            def _():
                start = pl.multiple_of(pl.program_id(0) * count, 8)
                column = columns_out[piece, pl.ds(start, count), :]
                result[...] = total[...].astype(BF)
                gated = (result[...].astype(F32) * column).astype(BF)
                scaled_rows[...] = gated.reshape(scaled_rows.shape)

        pltpu.emit_pipeline(
            body,
            grid=(n * capacity // count, steps),
            in_specs=[
                pl.BlockSpec((spans, n_fsdp, capacity, width), lambda r, i: (r, 0, 0, 0)),
                pl.BlockSpec((1, width, tile), lambda r, i: (piece, 0, i)),
                pl.BlockSpec((1, width, tile), lambda r, i: (piece, 0, steps + i)),
                pl.BlockSpec((1, tile, width), lambda r, i: (piece, i, 0)),
            ],
            out_specs=[
                pl.BlockSpec((2, count, tile), lambda r, i: (0, r, i)),
                pl.BlockSpec((count, tile), lambda r, i: (r, i)),
                pl.BlockSpec((count, width), lambda r, i: (r, 0)),
                pl.BlockSpec((spans, 1, n_fsdp, capacity, width), lambda r, i: (r, piece, 0, 0, 0)),
            ],
        )(
            outs[piece],
            w_up,
            w_up,
            w_down,
            hiddens[piece],
            acts[piece],
            results[piece],
            scaled,
        )

    for step in range(1, n_fsdp):
        around(step, lambda block: own_masked(block).wait())
    for step in range(1, n_fsdp):
        for i in range(1, n_seq):

            def done(block):
                masked_copy(block, i, me_s).wait_send()
                masked_copy(block, i, (me_s + i) % n_seq).wait_recv()

            around(step, done)


def dispatch_rows(
    x, hot, gates, masked, before, w_up, w_down, n_seq, n_fsdp, capacity, collective_id
):
    count, width = x.shape
    pieces, ff = w_down.shape[:2]
    rows = n_seq * n_fsdp * capacity
    tile_rows = seq_tile(n_seq, n_fsdp * capacity, 3072 // n_fsdp) * n_fsdp * capacity
    vmem = pl.BlockSpec(memory_space=pltpu.VMEM)
    any_space = pl.BlockSpec(memory_space=pl.ANY)
    dma = pltpu.SemaphoreType.DMA
    return pl.pallas_call(
        functools.partial(dispatch_kernel, n_seq, n_fsdp, pieces),
        out_shape=[
            jax.ShapeDtypeStruct(before.shape, BF),
            jax.ShapeDtypeStruct((pieces, rows, 1), F32),
            jax.ShapeDtypeStruct(before.shape, BF),
        ]
        + [jax.ShapeDtypeStruct((n_seq, n_fsdp, capacity, width), BF)] * pieces
        + [jax.ShapeDtypeStruct((2, rows, ff), F32)] * pieces
        + [jax.ShapeDtypeStruct((rows, ff), BF)] * pieces
        + [jax.ShapeDtypeStruct((rows, width), BF)] * pieces,
        in_specs=[vmem] * 4 + [any_space] * 3,
        out_specs=[any_space, vmem] + [any_space] * (1 + 4 * pieces),
        scratch_shapes=[
            pltpu.VMEM(gates.shape, F32),
            pltpu.VMEM((n_fsdp, count, width), BF),
            pltpu.VMEM((n_fsdp, n_seq, pieces, capacity, width), BF),
            pltpu.VMEM((tile_rows, width), F32),
            dma((n_fsdp, pieces)),
            dma((2, n_fsdp)),
            dma((n_fsdp,)),
            dma((n_fsdp, n_seq, pieces)),
            dma((n_seq, n_fsdp, pieces)),
            dma((n_fsdp,)),
            dma((n_fsdp, n_seq)),
            dma((n_seq, n_fsdp)),
        ]
        + exchange_sems(n_seq * n_fsdp),
        input_output_aliases={4: 0},
        compiler_params=pltpu.CompilerParams(
            collective_id=collective_id, has_side_effects=True, vmem_limit_bytes=60 << 20
        ),
        name="dispatch_rows",
    )(x, hot, gates, masked, before, w_up, w_down)


def return_kernel(n_seq, n_fsdp, pieces, hot, gates, *refs):
    rows = refs[:pieces]
    out, gates_out, got, parts, sums, own_sem, row_send, row_recv, part_send, part_recv = refs[
        pieces : pieces + 10
    ]
    gate_exchange = Exchange(n_seq, n_fsdp, gates, gates_out, refs[pieces + 10 :])
    me_s, me_f = lax.axis_index("seq"), lax.axis_index("fsdp")
    width = out.shape[1]
    capacity = rows[0].shape[2]
    greet_all(n_seq, n_fsdp)

    def row_copy(j, i, piece):
        other, block = (me_s + i) % n_seq, (me_f + j) % n_fsdp
        return remote(
            rows[piece].at[other, block],
            got.at[block, me_s, piece],
            row_send.at[j % n_fsdp, i, piece],
            row_recv.at[block, me_s, piece],
            (other, me_f),
        )

    def own_copy(j, piece):
        block = (me_f + j) % n_fsdp
        return pltpu.make_async_copy(
            rows[piece].at[me_s, block], got.at[block, me_s, piece], own_sem.at[j % n_fsdp, piece]
        )

    def part_copy(j):
        block = (me_f + j) % n_fsdp
        return remote(
            parts.at[block], sums.at[me_f], part_send.at[j], part_recv.at[me_f], (me_s, block)
        )

    for j in range(1, n_fsdp + 1):
        for piece in range(pieces):
            for i in range(1, n_seq):
                row_copy(j, i, piece).start()
            own_copy(j, piece).start()
    gate_exchange.start()
    for j in range(1, n_fsdp + 1):
        block = (me_f + j) % n_fsdp
        for piece in range(pieces):
            own_copy(j, piece).wait()
            for i in range(1, n_seq):
                source = (me_s + i) % n_seq
                remote(
                    rows[piece].at[source, block],
                    got.at[block, source, piece],
                    row_send.at[0, i, piece],
                    row_recv.at[block, source, piece],
                    (source, me_f),
                ).wait_recv()

        def some(columns):
            arrived = got[block, :, :, :, columns].reshape(n_seq * pieces * capacity, -1)
            total = dot(hot[block], arrived, 1, 0)
            if j < n_fsdp:
                parts[block, :, columns] = total.astype(BF)
            else:
                out[:, columns] = total

        chunked(width, 512, some)
        if j < n_fsdp:
            part_copy(j).start()
    for j in range(1, n_fsdp):
        source = (me_f + n_fsdp - j) % n_fsdp
        remote(
            parts.at[source], sums.at[source], part_send.at[j], part_recv.at[source], (me_s, source)
        ).wait_recv()

    def add(columns):
        total = out[:, columns]
        for j in range(1, n_fsdp):
            total = total + sums[(me_f + j) % n_fsdp, :, columns].astype(F32)
        out[:, columns] = total

    chunked(width, 512, add)
    for j in range(1, n_fsdp):
        part_copy(j).wait_send()
    for j in range(1, n_fsdp + 1):
        for piece in range(pieces):
            for i in range(1, n_seq):
                row_copy(j, i, piece).wait_send()
    gate_exchange.finish()


def return_rows(piece_rows, hot, gates, n_seq, n_fsdp, collective_id):
    pieces = len(piece_rows)
    capacity, width = piece_rows[0].shape[2:]
    count = hot.shape[1]
    vmem = pl.BlockSpec(memory_space=pltpu.VMEM)
    dma = pltpu.SemaphoreType.DMA
    return pl.pallas_call(
        functools.partial(return_kernel, n_seq, n_fsdp, pieces),
        out_shape=[
            jax.ShapeDtypeStruct((count, width), F32),
            jax.ShapeDtypeStruct(gates.shape, F32),
        ],
        in_specs=[vmem, vmem] + [pl.BlockSpec(memory_space=pl.ANY)] * pieces,
        out_specs=[vmem, vmem],
        scratch_shapes=[
            pltpu.VMEM((n_fsdp, n_seq, pieces, capacity, width), BF),
            pltpu.VMEM((n_fsdp, count, width), BF),
            pltpu.VMEM((n_fsdp, count, width), BF),
            dma((n_fsdp, pieces)),
            dma((n_fsdp, n_seq, pieces)),
            dma((n_fsdp, n_seq, pieces)),
            dma((n_fsdp,)),
            dma((n_fsdp,)),
        ]
        + exchange_sems(n_seq * n_fsdp),
        compiler_params=pltpu.CompilerParams(
            collective_id=collective_id, has_side_effects=True, vmem_limit_bytes=40 << 20
        ),
        name="return_rows",
    )(hot, gates, *piece_rows)


def weight_grad_kernel(a, b, *refs):
    parts, _, n = b.shape
    for part in range(parts):
        refs[-1][0, :, part * n : (part + 1) * n] = dot(a[...], b[part], 0, 0)


def weight_grad(a, b, whole, piece, pieces):
    rows, m = a.shape
    parts, _, n = b.shape
    tile = min(256, m)
    more = [] if whole is None else [whole]
    return pl.pallas_call(
        weight_grad_kernel,
        out_shape=jax.ShapeDtypeStruct((pieces, m, n * parts), F32),
        grid=(m // tile,),
        in_specs=[
            pl.BlockSpec((rows, tile), lambda i: (0, i)),
            pl.BlockSpec((parts, rows, n), lambda i: (0, 0, 0)),
        ]
        + [pl.BlockSpec(memory_space=pl.ANY)] * len(more),
        out_specs=pl.BlockSpec((1, tile, n * parts), lambda i: (piece, i, 0)),
        input_output_aliases={2: 0} if more else {},
        cost_estimate=pl.CostEstimate(
            flops=2 * rows * m * n * parts,
            bytes_accessed=4 * m * n * parts,
            transcendentals=0,
        ),
        name="weight_grad",
    )(a, b, *more)


def seq_tile(n_seq, rows_each, most=1024):
    tile = n_seq
    while tile > 1 and (tile * rows_each > most or n_seq % tile):
        tile -= 1
    return tile


def expert_backward_kernel(masked, gates, piece_out, hidden, w_down, out, grad, inner, partial):
    @pl.when(pl.program_id(1) == 0)
    def _():
        partial[...] = jnp.zeros_like(partial)

        def some(columns):
            low = masked[:, 0, :, :, columns].reshape(grad.shape[0], -1).astype(F32)
            grad[:, columns] = (low * gates[...]).astype(BF)
            product = low * piece_out[:, columns].astype(F32)
            for i in range(product.shape[1] // 128):
                partial[...] += product[:, i * 128 : (i + 1) * 128]

        chunked(grad.shape[1], 512, some)
        sums = jnp.sum(partial[...].T, axis=0, keepdims=True)
        inner[...] = jnp.broadcast_to(sums, inner.shape)

    act_grad = dot(grad[...], w_down[0], 1, 1)
    gate, up = hidden[0], hidden[1]
    sigmoid = jax.nn.sigmoid(gate)
    out[0] = (act_grad * up * sigmoid * (1.0 + gate * (1.0 - sigmoid))).astype(BF)
    out[1] = (act_grad * gate * sigmoid).astype(BF)


def expert_backward(masked, gates, piece_out, hidden, w_down, piece):
    rows, width = piece_out.shape
    ff = w_down.shape[1]
    n_seq, _, n_fsdp, capacity, _ = masked.shape
    tile = min(256, ff)
    spans = seq_tile(n_seq, n_fsdp * capacity)
    count = spans * n_fsdp * capacity
    part = pl.BlockSpec((2, count, tile), lambda r, i: (0, r, i))
    fixed = lambda r, i: (r, 0)
    return pl.pallas_call(
        expert_backward_kernel,
        out_shape=[
            jax.ShapeDtypeStruct((2, rows, ff), BF),
            jax.ShapeDtypeStruct((rows, width), BF),
            jax.ShapeDtypeStruct((8, rows), F32),
        ],
        grid=(rows // count, ff // tile),
        in_specs=[
            pl.BlockSpec((spans, 1, n_fsdp, capacity, width), lambda r, i: (r, piece, 0, 0, 0)),
            pl.BlockSpec((count, 1), fixed),
            pl.BlockSpec((count, width), fixed),
            part,
            pl.BlockSpec((1, tile, width), lambda r, i: (piece, i, 0)),
        ],
        out_specs=[
            part,
            pl.BlockSpec((count, width), fixed),
            pl.BlockSpec((8, count), lambda r, i: (0, r)),
        ],
        scratch_shapes=[pltpu.VMEM((count, 128), F32)],
        compiler_params=pltpu.CompilerParams(vmem_limit_bytes=48 << 20),
        cost_estimate=pl.CostEstimate(
            flops=2 * rows * width * ff, bytes_accessed=12 * rows * ff, transcendentals=rows * ff
        ),
        name="expert_backward",
    )(masked, gates, piece_out, hidden, w_down)


def expert_input_kernel(grad, w_up, out):
    ff = grad.shape[2]
    total = dot(grad[0], w_up[0, :, :ff], 1, 1) + dot(grad[1], w_up[0, :, ff:], 1, 1)
    out[...] = total.astype(BF)


def expert_input(grad, w_up, piece):
    rows, ff = grad.shape[1:]
    width = w_up.shape[1]
    tile = min(256, width)
    return pl.pallas_call(
        expert_input_kernel,
        out_shape=jax.ShapeDtypeStruct((rows, width), BF),
        grid=(width // tile,),
        in_specs=[
            pl.BlockSpec((2, rows, ff), lambda i: (0, 0, 0)),
            pl.BlockSpec((1, tile, 2 * ff), lambda i: (piece, i, 0)),
        ],
        out_specs=pl.BlockSpec((rows, tile), lambda i: (0, i)),
        cost_estimate=pl.CostEstimate(
            flops=4 * rows * width * ff, bytes_accessed=4 * width * ff, transcendentals=0
        ),
        name="expert_input",
    )(grad, w_up)


class SeqShare:
    def __init__(self, n_seq, own, every, send_sem, recv_sem):
        self.n_seq, self.own, self.every = n_seq, own, every
        self.send_sem, self.recv_sem = send_sem, recv_sem
        self.me_s, self.me_f = lax.axis_index("seq"), lax.axis_index("fsdp")

    def copy(self, i, place):
        other = (self.me_s + i) % self.n_seq
        return remote(
            self.own,
            self.every.at[place],
            self.send_sem.at[i],
            self.recv_sem.at[place],
            (other, self.me_f),
        )

    def total(self):
        for i in range(1, self.n_seq):
            self.copy(i, self.me_s).start()
        total = self.own[...]
        for i in range(1, self.n_seq):
            place = (self.me_s + i) % self.n_seq
            self.copy(i, place).wait_recv()
            total = total + self.every[place]
        for i in range(1, self.n_seq):
            self.copy(i, self.me_s).wait_send()
        return total


def share_scratch(n_seq, shape):
    dma = pltpu.SemaphoreType.DMA
    return [pltpu.VMEM(shape, F32), pltpu.VMEM((n_seq,) + shape, F32), dma((n_seq,)), dma((n_seq,))]


def row_sums(values):
    ones = jnp.ones((8, values.shape[1]), F32)
    return lax.dot_general(
        ones,
        values,
        (((1,), (1,)), ((), ())),
        preferred_element_type=F32,
        precision=lax.Precision.HIGHEST,
    )


def front_kernel(n_seq, x, gain, w, normed, raw, totals, *scratch):
    greet_seq(n_seq)
    share = SeqShare(n_seq, *scratch)
    head_width = w.shape[1] // 3
    tile = 256

    def some(i, carry):
        rows = pl.ds(pl.multiple_of(i * tile, tile), tile)
        values = x[rows, :].astype(F32)
        scale = lax.rsqrt(jnp.mean(values * values, axis=-1, keepdims=True) + epsilon)
        low = (values * scale * gain[0:1, :]).astype(BF)
        normed[rows, :] = low
        result = dot(low, w[...], 1, 0)
        raw[rows, :] = result
        for part in range(2):
            piece = result[:, part * head_width : (part + 1) * head_width]
            share.own[part : part + 1, rows] = row_sums(piece * piece)[0:1]
        return carry

    share.own[...] = jnp.zeros_like(share.own)
    lax.fori_loop(0, x.shape[0] // tile, some, 0)
    totals[...] = share.total()


def front(x, gains, w, n_seq, collective_id):
    rows, width = x.shape
    vmem = pl.BlockSpec(memory_space=pltpu.VMEM)
    return pl.pallas_call(
        functools.partial(front_kernel, n_seq),
        out_shape=[
            jax.ShapeDtypeStruct((rows, width), BF),
            jax.ShapeDtypeStruct((rows, w.shape[1]), F32),
            jax.ShapeDtypeStruct((8, rows), F32),
        ],
        in_specs=[vmem] * 3,
        out_specs=[vmem] * 3,
        scratch_shapes=share_scratch(n_seq, (8, rows)),
        compiler_params=pltpu.CompilerParams(
            collective_id=collective_id, has_side_effects=True, vmem_limit_bytes=40 << 20
        ),
        name="front",
    )(x, gains, w)


def column_rms(sums, part, width):
    return lax.rsqrt(sums.T[:, part : part + 1] / width + epsilon)


def turned(values, cosine, sine):
    return values * cosine + pltpu.roll(values, values.shape[1] // 2, 1) * sine


def softmax_columns(k, q, length, scaling):
    scores = dot(k, q, 1, 1) * scaling
    key = lax.broadcasted_iota(jnp.int32, scores.shape, 0)
    scores = jnp.where(key < length, scores, -1e30)
    weights = jnp.exp(scores - jnp.max(scores, axis=0, keepdims=True))
    return weights / jnp.sum(weights, axis=0, keepdims=True)


def attend_kernel(
    width,
    length,
    raw_q,
    raw_k,
    raw_v,
    q_sums,
    k_sums,
    gain,
    q_cos,
    q_sin,
    k_cos,
    k_sin,
    o_ref,
    q_ref,
    k_ref,
    v_ref,
):
    scaling = raw_q.shape[1] ** (-0.5)

    @pl.when(pl.program_id(1) == 0)
    def _():
        key = raw_k[...] * column_rms(k_sums[...], 1, width) * gain[2:3, :]
        k_ref[...] = turned(key, k_cos[...], k_sin[...]).astype(BF)
        v_ref[...] = raw_v[...].astype(BF)

    query = raw_q[...] * column_rms(q_sums[...], 0, width) * gain[1:2, :]
    query = turned(query, q_cos[...], q_sin[...]).astype(BF)
    q_ref[...] = query
    probs = softmax_columns(k_ref[...], query, length[0], scaling).astype(BF)
    o_ref[...] = dot(v_ref[...], probs, 0, 0).T.astype(BF)


def attend(raw, totals, gains, cosine, sine, length, block, width):
    slot_len, head_width = raw.shape[0], raw.shape[1] // 3
    hd = cosine.shape[1]
    heads = head_width // hd
    rows = lambda shift: pl.BlockSpec((block, hd), lambda h, i, n: (i, shift + h))
    full = lambda shift: pl.BlockSpec((slot_len, hd), lambda h, i, n: (0, shift + h))
    table = pl.BlockSpec((block, hd), lambda h, i, n: (i, 0))
    whole_table = pl.BlockSpec((slot_len, hd), lambda h, i, n: (0, 0))
    return pl.pallas_call(
        functools.partial(attend_kernel, width),
        out_shape=[jax.ShapeDtypeStruct((slot_len, head_width), BF)] * 4,
        grid_spec=pltpu.PrefetchScalarGridSpec(
            num_scalar_prefetch=1,
            grid=(heads, slot_len // block),
            in_specs=[
                rows(0),
                full(heads),
                full(2 * heads),
                pl.BlockSpec((8, block), lambda h, i, n: (0, i)),
                pl.BlockSpec((8, slot_len), lambda h, i, n: (0, 0)),
                pl.BlockSpec((8, hd), lambda h, i, n: (0, h)),
                table,
                table,
                whole_table,
                whole_table,
            ],
            out_specs=[rows(0), rows(0), full(0), full(0)],
        ),
        cost_estimate=pl.CostEstimate(
            flops=4 * heads * slot_len * slot_len * hd, bytes_accessed=1 << 23, transcendentals=0
        ),
        name="attend",
    )(length, raw, raw, raw, totals, totals, gains, cosine, sine, cosine, sine)


def attend_back_kernel(
    width,
    length,
    q_ref,
    k_ref,
    v_ref,
    g_ref,
    raw_q,
    raw_k,
    q_sums,
    k_sums,
    gain,
    q_cos,
    q_sin,
    k_cos,
    k_sin,
    dq_ref,
    dk_ref,
    dv_ref,
    dots,
    gain_out,
    dk_sum,
    dv_sum,
):
    head, step = pl.program_id(0), pl.program_id(1)
    last = step == pl.num_programs(1) - 1
    block, hd = q_ref.shape
    scaling = hd ** (-0.5)

    @pl.when(step == 0)
    def _():
        dk_sum[...] = jnp.zeros_like(dk_sum)
        dv_sum[...] = jnp.zeros_like(dv_sum)
        gain_out[...] = jnp.zeros_like(gain_out)

        @pl.when(head == 0)
        def _():
            dots[...] = jnp.zeros_like(dots)

    q, k, v, g = q_ref[...], k_ref[...], v_ref[...], g_ref[...]
    probs = softmax_columns(k, q, length[0], scaling)
    dv_sum[...] += dot(probs.astype(BF), g, 1, 0)
    weights_grad = dot(v, g, 1, 1)
    inner = jnp.sum(probs * weights_grad, axis=0, keepdims=True)
    score_grad = (probs * (weights_grad - inner) * scaling).astype(BF)
    dk_sum[...] += dot(score_grad, q, 1, 0)
    query_grad = dot(k, score_grad, 0, 0).T.astype(BF).astype(F32)
    query_in = turned(query_grad, q_cos[...], -q_sin[...])
    dq_ref[...] = query_in
    product = query_in * raw_q[...]
    rows = pl.ds(pl.multiple_of(step * block, block), block)
    dots[0:1, rows] += row_sums(product * gain[1:2, :])[0:1]
    gain_out[0:1, :] += jnp.sum(
        product * column_rms(q_sums[...], 0, width), axis=0, keepdims=True
    )

    @pl.when(last)
    def _():
        key_in = turned(dk_sum[...].astype(BF).astype(F32), k_cos[...], -k_sin[...])
        dk_ref[...] = key_in
        dv_ref[...] = dv_sum[...].astype(BF)
        product = key_in * raw_k[...]
        dots[1:2, :] += row_sums(product * gain[2:3, :])[0:1]
        gain_out[1:2, :] = jnp.sum(
            product * column_rms(k_sums[...], 1, width), axis=0, keepdims=True
        )


def attend_back(query, key, value, grad, raw, totals, gains, cosine, sine, length, block, width):
    slot_len, head_width = query.shape
    hd = cosine.shape[1]
    heads = head_width // hd
    rows = pl.BlockSpec((block, hd), lambda h, i, n: (i, h))
    full = lambda shift: pl.BlockSpec((slot_len, hd), lambda h, i, n: (0, shift + h))
    table = pl.BlockSpec((block, hd), lambda h, i, n: (i, 0))
    whole_table = pl.BlockSpec((slot_len, hd), lambda h, i, n: (0, 0))
    return pl.pallas_call(
        functools.partial(attend_back_kernel, width),
        out_shape=[
            jax.ShapeDtypeStruct(query.shape, F32),
            jax.ShapeDtypeStruct(query.shape, F32),
            jax.ShapeDtypeStruct(query.shape, BF),
            jax.ShapeDtypeStruct((8, slot_len), F32),
            jax.ShapeDtypeStruct((8, head_width), F32),
        ],
        grid_spec=pltpu.PrefetchScalarGridSpec(
            num_scalar_prefetch=1,
            grid=(heads, slot_len // block),
            in_specs=[
                rows,
                full(0),
                full(0),
                rows,
                rows,
                full(heads),
                pl.BlockSpec((8, block), lambda h, i, n: (0, i)),
                pl.BlockSpec((8, slot_len), lambda h, i, n: (0, 0)),
                pl.BlockSpec((8, hd), lambda h, i, n: (0, h)),
                table,
                table,
                whole_table,
                whole_table,
            ],
            out_specs=[
                rows,
                full(0),
                full(0),
                pl.BlockSpec((8, slot_len), lambda h, i, n: (0, 0)),
                pl.BlockSpec((8, hd), lambda h, i, n: (0, h)),
            ],
            scratch_shapes=[pltpu.VMEM((slot_len, hd), F32), pltpu.VMEM((slot_len, hd), F32)],
        ),
        cost_estimate=pl.CostEstimate(
            flops=20 * heads * slot_len * slot_len * hd, bytes_accessed=1 << 24, transcendentals=0
        ),
        name="attend_back",
    )(
        length,
        query,
        key,
        value,
        grad,
        raw,
        raw,
        totals,
        totals,
        gains,
        cosine,
        sine,
        cosine,
        sine,
    )


def raw_back_kernel(
    n_seq, n_fsdp, width, dq, dk, dv, raw, totals, gain, dots, terms, out, terms_out, *scratch
):
    greet_lines(n_seq, n_fsdp)
    share = SeqShare(n_seq, *scratch[:4])
    term_sum = TermSum(n_seq, n_fsdp, None, *scratch[4:6], None, None, *scratch[6:])
    term_sum.start_fsdp(terms[...])
    head_width = dq.shape[1]
    share.own[...] = dots[...]
    share.own[...] = share.total()
    tile = 256

    def some(i, carry):
        rows = pl.ds(pl.multiple_of(i * tile, tile), tile)
        inner = share.own[:, rows].T / width
        for part, grad in enumerate((dq, dk)):
            columns = slice(part * head_width, (part + 1) * head_width)
            scale = column_rms(totals[:, rows], part, width)
            weighted = grad[rows, :] * gain[part + 1 : part + 2, :]
            cube = scale * scale * scale
            result = scale * weighted - raw[rows, columns] * (cube * inner[:, part : part + 1])
            out[rows, columns] = result.astype(BF)
        out[rows, 2 * head_width :] = dv[rows, :]
        return carry

    lax.fori_loop(0, dq.shape[0] // tile, some, 0)
    terms_out[...] = term_sum.finish()


def raw_back(dq, dk, dv, raw, totals, gains, dots, terms, n_seq, n_fsdp, width, collective_id):
    vmem = pl.BlockSpec(memory_space=pltpu.VMEM)
    dma = pltpu.SemaphoreType.DMA
    return pl.pallas_call(
        functools.partial(raw_back_kernel, n_seq, n_fsdp, width),
        out_shape=[
            jax.ShapeDtypeStruct(raw.shape, BF),
            jax.ShapeDtypeStruct(terms.shape, F32),
        ],
        in_specs=[vmem] * 8,
        out_specs=[vmem] * 2,
        scratch_shapes=share_scratch(n_seq, dots.shape)
        + [
            pltpu.VMEM((n_seq,) + terms.shape, F32),
            pltpu.VMEM((n_fsdp,) + terms.shape, F32),
            dma((n_fsdp,)),
            dma((n_fsdp,)),
        ],
        compiler_params=pltpu.CompilerParams(
            collective_id=collective_id, has_side_effects=True, vmem_limit_bytes=40 << 20
        ),
        name="raw_back",
    )(dq, dk, dv, raw, totals, gains, dots, terms)


def rope_tables(positions, head_dim):
    half = head_dim // 2
    frequency = rope_base ** (-jnp.arange(half, dtype=F32) * 2.0 / head_dim)
    angles = positions.astype(F32)[:, None] * frequency[None, :]
    cosine, sine = jnp.cos(angles), jnp.sin(angles)
    return jnp.concatenate([cosine, cosine], axis=1), jnp.concatenate([-sine, sine], axis=1)


def places(block_routes, experts, capacity):
    count = block_routes.shape[0]
    match = (block_routes[:, :, None] == experts[None, None, :]).astype(F32).sum(axis=1)
    lower = jnp.tril(jnp.ones((count, count), BF), -1)
    rank = dot(lower, match.astype(BF), 1, 0)
    place = jnp.arange(capacity, dtype=F32)
    return match[:, :, None] * (rank[:, :, None] == place[None, None, :]).astype(F32)


def local(
    tokens,
    cotangent,
    lengths,
    routes,
    norm_gains,
    qkv_weight,
    proj_weight,
    router_weight,
    expert_up,
    expert_down,
):
    n_seq, n_fsdp = lax.axis_size("seq"), lax.axis_size("fsdp")
    n_dev = n_seq * n_fsdp
    me_s, me_f = lax.axis_index("seq"), lax.axis_index("fsdp")
    shard_len, width = tokens.shape[1], tokens.shape[2]
    slot_len = shard_len * n_seq
    experts = router_weight.shape[1]
    top_count = routes.shape[2]
    capacity = 3 * shard_len * top_count // (2 * experts)
    piece_ff = expert_down.shape[1]
    pieces_dev = expert_up.shape[0]
    split = FF // piece_ff
    head_dim = width // HEADS
    head_width = width // n_seq
    heads_dev = HEADS // n_seq
    owned = qkv_weight.shape[0]
    block = min(512, slot_len)
    length = lax.dynamic_slice_in_dim(lengths, me_f, 1)
    valid_total = jnp.sum(lengths).astype(F32).reshape(1)
    positions = me_s * shard_len + jnp.arange(shard_len, dtype=jnp.int32)
    row_valid = (positions < length[0]).astype(F32)
    local_routes = routes[0]
    push_all = functools.partial(push, n_seq=n_seq, n_fsdp=n_fsdp, scope="all")
    push_seq = functools.partial(push, n_seq=n_seq, n_fsdp=n_fsdp, scope="seq")

    masked_low = jnp.where(row_valid[:, None] > 0, cotangent[0], jnp.zeros((), BF))
    own_small = jnp.concatenate(
        [
            jnp.pad(norm_gains, ((0, 4), (0, 128 - owned))),
            local_routes.T.astype(BF),
            rows_of(router_weight.reshape(-1), 16),
        ]
    )
    small, gains, slot_tokens, qkv_local, cot_all, to_places, to_rows = first_gather(
        own_small,
        tokens[0],
        qkv_weight,
        masked_low,
        n_seq,
        n_fsdp,
        pieces_dev,
        split,
        capacity,
        top_count,
        collective_id=0,
    )
    slot_tokens = slot_tokens.reshape(slot_len, width)
    qkv_local = qkv_local.reshape(width, 3 * head_width)
    router = small[:, 8 + top_count :].reshape(n_dev, -1)[:, : owned * experts]
    router = router.reshape(width, experts)
    all_routes = small[:, 8 : 8 + top_count].swapaxes(1, 2)
    all_routes = all_routes.reshape(n_seq, n_fsdp, shard_len, top_count).astype(jnp.int32)
    proj_later = lax.optimization_barrier((proj_weight, slot_tokens))[0]
    proj_rows = lax.all_gather(proj_later, "fsdp", axis=0, tiled=True)

    def exchange(rows):
        return lax.all_to_all(rows, "seq", split_axis=0, concat_axis=0, tiled=True)

    normed_one, raw, totals = front(slot_tokens, gains, qkv_local, n_seq, collective_id=1)

    masked_later = lax.optimization_barrier((masked_low, raw))[0]
    plane_masked = lax.all_gather(masked_later, "fsdp", axis=0)

    def combine(pieces_back):
        total = 0.0
        for piece in range(pieces_dev):
            back = pieces_back[:, piece]
            hot = to_rows.reshape(n_fsdp, shard_len, n_seq, pieces_dev, capacity)[:, :, :, piece]
            total = total + jnp.einsum("ftsc,sfcd->ftd", hot, back, preferred_element_type=F32)
        return total.astype(BF)

    def rms(values):
        return lax.rsqrt(jnp.mean(values * values, axis=-1, keepdims=True) + epsilon)

    own_gains = lax.dynamic_slice_in_dim(gains, me_s * head_width, head_width, 1)
    cosine, sine = rope_tables(jnp.arange(slot_len, dtype=jnp.int32), head_dim)
    attended, query, key, value = attend(
        raw, totals, own_gains, cosine, sine, length, block, width
    )

    resid_in = tokens[0].astype(F32)
    resid_mid = resid_in + product_reduced(attended, proj_rows, 0, n_seq, collective_id=8)
    mid_rms = rms(resid_mid)
    normed_two = (resid_mid * mid_rms * gains[3]).astype(BF)
    router_probs = jax.nn.softmax(jnp.dot(normed_two, router, preferred_element_type=F32), axis=-1)

    own_hot = places(local_routes, jnp.arange(experts, dtype=jnp.int32), capacity)
    gate_slot = jnp.sum(own_hot * router_probs[:, :, None], axis=0)
    gate_send = jnp.broadcast_to(gate_slot[:, None], (experts, split, capacity))
    gate_send = gate_send.reshape(n_dev, pieces_dev, capacity)
    gate_send = jnp.pad(gate_send, ((0, 0), (0, -pieces_dev % 8), (0, 128 - capacity)))
    cot_all, gate_columns, outs, *experts_forward = dispatch_rows(
        normed_two,
        to_places,
        gate_send,
        plane_masked,
        cot_all,
        expert_up,
        expert_down,
        n_seq,
        n_fsdp,
        capacity,
        collective_id=6,
    )
    outs_back = exchange(outs)
    backs, gate_backs = [], []
    up_grad = down_grad = None
    for piece in range(pieces_dev):
        rows, hidden, activation, piece_out = experts_forward[piece::pieces_dev]
        rows = rows.reshape(-1, width)
        hidden_grad, out_grad, gate_back = expert_backward(
            cot_all, gate_columns[piece], piece_out, hidden, expert_down, piece
        )
        gate_backs.append(gate_back[0].reshape(n_dev, capacity))
        backs.append(expert_input(hidden_grad, expert_up, piece))
        down_grad = weight_grad(activation, out_grad[None], down_grad, piece, pieces_dev)
        up_grad = weight_grad(rows, hidden_grad, up_grad, piece, pieces_dev)
    back_send = jnp.stack(gate_backs, axis=1).reshape(n_dev, pieces_dev * capacity)
    gate_pad = -pieces_dev * capacity % 1024
    back_send = jnp.pad(back_send, ((0, 0), (0, gate_pad))).reshape(n_dev, -1, 128)
    backs, outs_back, up_grad, down_grad = lax.optimization_barrier(
        (backs, outs_back, up_grad, down_grad)
    )
    backs = [rows.reshape(n_seq, n_fsdp, capacity, width) for rows in backs]
    normed_two_grad, back_recv = return_rows(
        backs, to_rows, back_send, n_seq, n_fsdp, collective_id=7
    )
    outs_back = lax.optimization_barrier((outs_back, normed_two_grad))[0]
    outs_sums = combine(outs_back)

    seen = (all_routes[..., None] == jnp.arange(experts, dtype=jnp.int32)).astype(BF)
    live = jnp.arange(slot_len, dtype=jnp.int32).reshape(n_seq, 1, shard_len) < lengths[None, :, None]
    live = jnp.broadcast_to(live[..., None], all_routes.shape).astype(BF)
    counts = dot(live.reshape(1, -1), seen.reshape(-1, experts), 1, 0)[0]
    fraction = counts / (top_count * valid_total)
    back_recv = back_recv.reshape(n_dev, -1)
    slot_gates_grad = back_recv[:, : pieces_dev * capacity].reshape(experts, split, capacity).sum(axis=1)
    probs_grad = (
        jnp.sum(own_hot * slot_gates_grad[None], axis=2)
        + (experts * fraction / valid_total)[None, :] * row_valid[:, None]
    )
    logits_grad = router_probs * (
        probs_grad - jnp.sum(router_probs * probs_grad, axis=-1, keepdims=True)
    )
    router_term = lax.dot_general(
        logits_grad, normed_two.astype(F32), (((0,), (0,)), ((), ())), precision=lax.Precision.HIGHEST
    )
    normed_two_grad = normed_two_grad + lax.dot_general(
        logits_grad, router.astype(F32), (((1,), (1,)), ((), ())), precision=lax.Precision.HIGHEST
    )

    def rms_back(values, scale, gain, grad):
        weighted = gain * grad
        mean = jnp.mean(weighted * values, axis=-1, keepdims=True)
        return scale * weighted - values * (scale * scale * scale) * mean, jnp.sum(
            grad * values * scale, axis=0
        )

    mid_part, gain_three = rms_back(resid_mid, mid_rms, gains[3], normed_two_grad)
    mid_grad = masked_low.astype(F32) + mid_part
    branch_grad = mid_grad.astype(BF)
    branch_later, outs_sums = lax.optimization_barrier((branch_grad, outs_sums))
    outs_parts = lax.all_to_all(outs_sums, "fsdp", split_axis=0, concat_axis=0, tiled=True)
    slot_branch, router_parts = gather_seq(
        branch_later, router_term, n_seq, n_fsdp, collective_id=9
    )
    slot_branch = slot_branch.reshape(slot_len, width)
    heads_grad = dot(slot_branch, proj_rows, 1, 1).astype(BF)
    query_in, key_in, value_grad, dots, heads_gain = attend_back(
        query,
        key,
        value,
        heads_grad,
        raw,
        totals,
        own_gains,
        cosine,
        sine,
        length,
        block,
        width,
    )
    raw_grad, router_parts = raw_back(
        query_in,
        key_in,
        value_grad,
        raw,
        totals,
        own_gains,
        dots,
        router_parts,
        n_seq,
        n_fsdp,
        width,
        collective_id=4,
    )
    raw_grad, outs_parts = lax.optimization_barrier((raw_grad, outs_parts))
    layer_out = (resid_mid + jnp.sum(outs_parts.astype(F32), axis=0)).astype(BF)[None]

    qkv_part = dot(normed_one, raw_grad, 0, 0).astype(BF)
    qkv_part = qkv_part.reshape(n_seq, n_fsdp, owned, 3 * head_width)
    prob_part = jnp.sum(router_probs * row_valid[:, None], axis=0)
    prob_row = jnp.tile(jnp.pad(prob_part, (0, head_width - experts)), n_seq)
    terms = jnp.pad(jnp.stack([gain_three, prob_row]), ((1, 5), (0, 0)))
    heads_terms = jnp.pad(heads_gain[:2], ((3, 3), (0, 0)))
    input_grad, qkv_grad, last = last_reduce(
        raw_grad,
        qkv_local,
        qkv_part,
        tokens[0],
        mid_grad,
        gains,
        terms,
        heads_terms,
        n_seq,
        n_fsdp,
        collective_id=10,
    )
    input_grad = input_grad[None]

    proj_part = dot(attended, slot_branch, 0, 0).astype(BF)
    proj_grad = lax.psum_scatter(proj_part, "fsdp", scatter_dimension=0, tiled=True).astype(F32)

    router_grad = lax.dynamic_slice_in_dim(router_parts, me_f * owned, owned, 1).T
    prob_total = last[2, :experts]
    last = lax.dynamic_slice_in_dim(last, me_f * owned, owned, 1)
    gains_grad = jnp.stack([last[0], last[3], last[4], last[1]])
    loss_value = (experts * jnp.sum(fraction * prob_total / valid_total)).reshape(1)
    return (
        layer_out,
        input_grad,
        gains_grad,
        qkv_grad,
        proj_grad,
        router_grad,
        up_grad,
        down_grad,
        loss_value,
    )


def solution(mesh):
    rows = P(("seq", "fsdp"), None)
    return jax.shard_map(
        local,
        mesh=mesh,
        in_specs=(
            P("fsdp", "seq", None),
            P("fsdp", "seq", None),
            P(),
            P("fsdp", "seq", None),
            P(None, ("seq", "fsdp")),
            rows,
            rows,
            rows,
            P(("seq", "fsdp"), None, None),
            P(("seq", "fsdp"), None, None),
        ),
        out_specs=(
            P("fsdp", "seq", None),
            P("fsdp", "seq", None),
            P(None, ("seq", "fsdp")),
            rows,
            rows,
            rows,
            P(("seq", "fsdp"), None, None),
            P(("seq", "fsdp"), None, None),
            P(),
        ),
        check_vma=False,
    )
```

```python
import functools

import jax
import jax.numpy as jnp
from jax import lax
from jax.experimental import pallas as pl
from jax.experimental.pallas import tpu as pltpu
from jax.sharding import PartitionSpec as P

HEADS = 16
FF = 1024

epsilon = 1e-06
rope_base = 10000.0
MESH = pl.DeviceIdType.MESH
BF = jnp.bfloat16
F32 = jnp.float32


def dot(a, b, ca, cb):
    return lax.dot_general(a, b, (((ca,), (cb,)), ((), ())), preferred_element_type=F32)


def push_kernel(n_seq, n_fsdp, scope, gather, src, dst, send_sem, recv_sem, own_sem):
    me_s, me_f = lax.axis_index("seq"), lax.axis_index("fsdp")
    n = n_seq * n_fsdp if scope == "all" else n_seq
    me = me_s * n_fsdp + me_f if scope == "all" else me_s

    def where(index):
        if scope == "all":
            return (index // n_fsdp, index % n_fsdp)
        return (index, me_f)

    barrier = pltpu.get_barrier_semaphore()

    def greet(i, carry):
        pl.semaphore_signal(barrier, inc=1, device_id=where((me + i) % n), device_id_type=MESH)
        return carry

    lax.fori_loop(1, n, greet, 0)
    own = pltpu.make_async_copy(src if gather else src.at[me], dst.at[me], own_sem)
    own.start()
    pl.semaphore_wait(barrier, n - 1)

    def copy_to(other):
        return pltpu.make_async_remote_copy(
            src_ref=src if gather else src.at[other],
            dst_ref=dst.at[me],
            send_sem=send_sem.at[other],
            recv_sem=recv_sem.at[me],
            device_id=where(other),
            device_id_type=MESH,
        )

    def copy_from(other):
        return pltpu.make_async_remote_copy(
            src_ref=src if gather else src.at[other],
            dst_ref=dst.at[other],
            send_sem=send_sem.at[other],
            recv_sem=recv_sem.at[other],
            device_id=where(other),
            device_id_type=MESH,
        )

    def send(i, carry):
        copy_to((me + i) % n).start()
        return carry

    lax.fori_loop(1, n, send, 0)

    def finish(i, carry):
        other = (me + i) % n
        copy_from(other).wait_recv()
        copy_to(other).wait_send()
        return carry

    lax.fori_loop(1, n, finish, 0)
    own.wait()


def push(block, n_seq, n_fsdp, scope, gather, collective_id):
    n = n_seq * n_fsdp if scope == "all" else n_seq
    shape = (n,) + (block.shape if gather else block.shape[1:])
    return pl.pallas_call(
        functools.partial(push_kernel, n_seq, n_fsdp, scope, gather),
        out_shape=jax.ShapeDtypeStruct(shape, block.dtype),
        in_specs=[pl.BlockSpec(memory_space=pltpu.VMEM)],
        out_specs=pl.BlockSpec(memory_space=pltpu.VMEM),
        scratch_shapes=[
            pltpu.SemaphoreType.DMA((n,)),
            pltpu.SemaphoreType.DMA((n,)),
            pltpu.SemaphoreType.DMA,
        ],
        compiler_params=pltpu.CompilerParams(collective_id=collective_id, has_side_effects=True),
        name="push_" + scope,
    )(block)


def rows_of(flat, multiple):
    size = flat.shape[0]
    whole = -(-size // (multiple * 128)) * multiple * 128
    return jnp.pad(flat, (0, whole - size)).reshape(-1, 128)


def remote(src, dst, send_sem, recv_sem, device):
    return pltpu.make_async_remote_copy(
        src_ref=src,
        dst_ref=dst,
        send_sem=send_sem,
        recv_sem=recv_sem,
        device_id=device,
        device_id_type=MESH,
    )


def greet_all(n_seq, n_fsdp):
    me_s, me_f = lax.axis_index("seq"), lax.axis_index("fsdp")
    n = n_seq * n_fsdp
    me = me_s * n_fsdp + me_f
    barrier = pltpu.get_barrier_semaphore()

    def greet(i, carry):
        other = (me + i) % n
        pl.semaphore_signal(
            barrier, inc=1, device_id=(other // n_fsdp, other % n_fsdp), device_id_type=MESH
        )
        return carry

    lax.fori_loop(1, n, greet, 0)
    pl.semaphore_wait(barrier, n - 1)


def greet_lines(n_seq, n_fsdp):
    me_s, me_f = lax.axis_index("seq"), lax.axis_index("fsdp")
    barrier = pltpu.get_barrier_semaphore()
    for i in range(1, n_seq):
        pl.semaphore_signal(
            barrier, inc=1, device_id=((me_s + i) % n_seq, me_f), device_id_type=MESH
        )
    for i in range(1, n_fsdp):
        pl.semaphore_signal(
            barrier, inc=1, device_id=(me_s, (me_f + i) % n_fsdp), device_id_type=MESH
        )
    pl.semaphore_wait(barrier, n_seq + n_fsdp - 2)


class Exchange:
    def __init__(self, n_seq, n_fsdp, src, dst, sems):
        self.n, self.n_fsdp, self.src, self.dst = n_seq * n_fsdp, n_fsdp, src, dst
        self.send_sem, self.recv_sem, self.own_sem = sems
        self.me = lax.axis_index("seq") * n_fsdp + lax.axis_index("fsdp")

    def copy(self, i, place):
        other = (self.me + i) % self.n
        return remote(
            self.src.at[other],
            self.dst.at[self.me if place is None else place],
            self.send_sem.at[i],
            self.recv_sem.at[self.me if place is None else place],
            (other // self.n_fsdp, other % self.n_fsdp),
        )

    def own(self):
        return pltpu.make_async_copy(
            self.src.at[self.me], self.dst.at[self.me], self.own_sem
        )

    def start(self):
        self.own().start()

        def one(i, carry):
            self.copy(i, None).start()
            return carry

        lax.fori_loop(1, self.n, one, 0)

    def finish(self):
        def one(i, carry):
            self.copy(i, None).wait_send()
            self.copy(i, (self.me + i) % self.n).wait_recv()
            return carry

        lax.fori_loop(1, self.n, one, 0)
        self.own().wait()


def exchange_sems(n):
    return [
        pltpu.SemaphoreType.DMA((n,)),
        pltpu.SemaphoreType.DMA((n,)),
        pltpu.SemaphoreType.DMA,
    ]


def line_step(n_fsdp, step, arrived, forward):
    me_f = lax.axis_index("fsdp")

    @pl.when(me_f - step >= 0)
    def _():
        arrived(me_f - step)

        @pl.when(me_f + 1 < n_fsdp)
        def _():
            forward(me_f - step, 0, me_f + 1)

    @pl.when(me_f + step < n_fsdp)
    def _():
        arrived(me_f + step)

        @pl.when(me_f >= 1)
        def _():
            forward(me_f + step, 1, me_f - 1)


def line_sent(n_fsdp, step, sent):
    me_f = lax.axis_index("fsdp")

    @pl.when((me_f - step >= 0) & (me_f + 1 < n_fsdp))
    def _():
        sent(me_f - step, 0, me_f + 1)

    @pl.when((me_f + step < n_fsdp) & (me_f >= 1))
    def _():
        sent(me_f + step, 1, me_f - 1)


def flipped(index, bit):
    return index + bit * (1 - 2 * ((index // bit) % 2))


class SeqGather:
    def __init__(self, order, own, block, send_sem, recv_sem):
        self.order, self.own, self.block = order, own, block
        self.send_sem, self.recv_sem = send_sem, recv_sem
        self.me_s, self.me_f = lax.axis_index("seq"), lax.axis_index("fsdp")

    def held(self, stage):
        indices = [self.me_s]
        for bit in self.order[:stage]:
            indices = indices + [flipped(i, bit) for i in indices]
        return indices

    def copies(self, stage):
        partner = flipped(self.me_s, self.order[stage])
        result = []
        for count, index in enumerate(self.held(stage)):
            src = self.own if count == 0 else self.block(index)
            sem = self.send_sem.at[(1 << stage) - 1 + count]
            result.append(
                remote(src, self.block(index), sem, self.recv_sem.at[index], (partner, self.me_f))
            )
        return result

    def start(self, stage):
        for copy in self.copies(stage):
            copy.start()

    def wait(self, stage):
        for index in self.held(stage):
            index = flipped(index, self.order[stage])
            remote(
                self.block(index),
                self.block(index),
                self.send_sem.at[0],
                self.recv_sem.at[index],
                (self.me_s, self.me_f),
            ).wait_recv()

    def sent(self):
        for stage in range(len(self.order)):
            for copy in self.copies(stage):
                copy.wait_send()


def gather_orders(n_seq):
    bits = [1 << b for b in range(n_seq.bit_length() - 1)]
    return bits[1:] + bits[:1], bits[:0:-1] + bits[:1]


def block_places(routes, ids, capacity):
    count = routes.shape[1]
    match = jnp.zeros((ids.shape[0], count), F32)
    for k in range(routes.shape[0]):
        match = match + (routes[k : k + 1, :] == ids).astype(F32)
    row = lax.broadcasted_iota(jnp.int32, (count, count), 0)
    column = lax.broadcasted_iota(jnp.int32, (count, count), 1)
    rank = dot(match.astype(BF), (row < column).astype(BF), 1, 0)
    place = lax.broadcasted_iota(jnp.int32, (ids.shape[0], capacity, count), 1).astype(F32)
    hot = match[:, None, :] * (rank[:, None, :] == place).astype(F32)
    return hot.reshape(ids.shape[0] * capacity, count)


def first_kernel(
    n_seq,
    n_fsdp,
    pieces,
    split,
    capacity,
    owned,
    top,
    small,
    tokens,
    qkv,
    masked,
    lengths,
    small_all,
    gains,
    slot,
    qkv_all,
    masked_all,
    to_places,
    to_rows,
    counts,
    send,
    own_sem,
    small_send,
    small_recv,
    qkv_send,
    qkv_recv,
    line_send,
    line_recv,
    token_send,
    token_recv,
    row_send,
    row_recv,
    row_own,
):
    me_s, me_f = lax.axis_index("seq"), lax.axis_index("fsdp")
    n = n_seq * n_fsdp
    me = me_s * n_fsdp + me_f
    head_width = qkv_all.shape[3] // 3
    width = head_width * n_seq
    half = tokens.shape[0] // 2
    orders = gather_orders(n_seq)
    stages = len(orders[0])

    def columns(owner, part):
        start = pl.multiple_of(part * width + owner * head_width, 128)
        return qkv.at[:, pl.ds(start, head_width)]

    def column_place(source, part):
        return qkv_all.at[source, me_f, :, pl.ds(part * head_width, head_width)]

    own = [
        pltpu.make_async_copy(small, small_all.at[me], own_sem.at[0]),
        pltpu.make_async_copy(tokens, slot.at[me_s], own_sem.at[1]),
    ] + [
        pltpu.make_async_copy(columns(me_s, part), column_place(me_s, part), own_sem.at[2 + part])
        for part in range(3)
    ]
    for copy in own:
        copy.start()
    greet_all(n_seq, n_fsdp)

    def small_copy(i):
        other = (me + i) % n
        return remote(
            small,
            small_all.at[me],
            small_send.at[i],
            small_recv.at[me],
            (other // n_fsdp, other % n_fsdp),
        )

    def small_arrived(other):
        return remote(
            small,
            small_all.at[other],
            small_send.at[0],
            small_recv.at[other],
            (other // n_fsdp, other % n_fsdp),
        )

    def small_start(i, carry):
        small_copy(i).start()
        return carry

    lax.fori_loop(1, n, small_start, 0)

    def column_copy(i, part):
        other = (me_s + i) % n_seq
        return remote(
            columns(other, part),
            column_place(me_s, part),
            qkv_send.at[i, part],
            qkv_recv.at[me_s, part],
            (other, me_f),
        )

    for i in range(1, n_seq):
        for part in range(3):
            column_copy(i, part).start()

    flows = []
    for side in range(2):
        rows = pl.ds(side * half, half)
        flows.append(
            SeqGather(
                orders[side],
                tokens.at[rows],
                lambda index, rows=rows: slot.at[index, rows],
                token_send.at[side],
                token_recv.at[side],
            )
        )

    def point(stage):
        for flow in flows:
            if 0 < stage <= stages:
                flow.wait(stage - 1)
            if stage < stages:
                flow.start(stage)

    point(0)
    for copy in own:
        copy.wait()

    piece = lax.broadcasted_iota(jnp.int32, (n_seq * pieces, 1), 0)
    piece = ((piece // pieces) * n_fsdp + me_f) * pieces + piece % pieces
    ids = piece // split

    def row_copy(i, place):
        other = (me_s + i) % n_seq
        return remote(
            send.at[other], masked_all.at[place, :, me_f], row_send.at[i], row_recv.at[place], (other, me_f)
        )

    def own_row():
        return pltpu.make_async_copy(send.at[me_s], masked_all.at[me_s, :, me_f], row_own)

    def table(block):
        routes = small_all[me_s * n_fsdp + block, 8 : 8 + top, :].astype(F32).astype(jnp.int32)
        hot = block_places(routes, ids, capacity)
        to_places[block] = hot.astype(BF)
        to_rows[block] = hot.T.astype(BF)

    def scatter():
        def some(lanes):
            picked = dot(to_places[me_f], masked[:, lanes], 1, 0).astype(BF)
            send[:, :, :, lanes] = picked.reshape(n_seq, pieces, capacity, -1)

        chunked(width, 512, some)
        for i in range(1, n_seq):
            row_copy(i, me_s).start()
        own_row().start()

    def line_copy(part, step, block, way, to):
        place = qkv_all.at[part, block]
        return remote(
            place, place, line_send.at[part, way, step], line_recv.at[part, block], (me_s, to)
        )

    def line_first(part):
        @pl.when(me_f + 1 < n_fsdp)
        def _():
            line_copy(part, 0, me_f, 0, me_f + 1).start()

        @pl.when(me_f >= 1)
        def _():
            line_copy(part, 0, me_f, 1, me_f - 1).start()

    def column_arrived(i, carry):
        source = (me_s + i) % n_seq

        @pl.when(i > 0)
        def _():
            for part in range(3):
                remote(
                    columns(source, part),
                    column_place(source, part),
                    qkv_send.at[i, part],
                    qkv_recv.at[source, part],
                    (source, me_f),
                ).wait_recv()

        line_first(source)
        return carry

    lax.fori_loop(0, n_seq, column_arrived, 0)

    def column_step(step):
        def column_next(i, carry):
            part = (me_s + i) % n_seq
            line_step(
                n_fsdp,
                step,
                lambda block: line_copy(part, 0, block, 0, me_f).wait_recv(),
                lambda block, way, to: line_copy(part, step, block, way, to).start(),
            )
            return carry

        lax.fori_loop(0, n_seq, column_next, 0)

    point(1)
    table(me_f)
    for stage in range(2, stages + 1):
        point(stage)
    scatter()
    column_step(1)
    for i in range(1, n_fsdp):
        block = (me_f + i) % n_fsdp
        small_arrived(me_s * n_fsdp + block).wait_recv()
        table(block)
    for flow in flows:
        flow.sent()

    def small_wait(i, carry):
        other = (me + i) % n
        small_copy(i).wait_send()

        @pl.when(other // n_fsdp != me_s)
        def _():
            small_arrived(other).wait_recv()

        return carry

    lax.fori_loop(1, n, small_wait, 0)

    lane = lax.broadcasted_iota(jnp.int32, (8, 128), 1)
    each = 128 // owned
    for j in range(width // 128):
        total = jnp.zeros((8, 128), F32)
        for k in range(each):
            some = jnp.where(lane < owned, small_all[j * each + k, :8, :].astype(F32), 0.0)
            total = total + (pltpu.roll(some, k * owned, 1) if k else some)
        gains[:, j * 128 : (j + 1) * 128] = total

    all_ids = lax.broadcasted_iota(jnp.int32, (counts.shape[1], 1), 0)
    position = lax.broadcasted_iota(jnp.int32, (1, tokens.shape[0]), 1)

    def seen(device, sums):
        routes = small_all[device, 8 : 8 + top, :].astype(F32).astype(jnp.int32)
        match = jnp.zeros(sums.shape, F32)
        for k in range(top):
            match = match + (routes[k : k + 1, :] == all_ids).astype(F32)
        first = (device // n_fsdp) * tokens.shape[0]
        live = (position + first < lengths[device % n_fsdp]).astype(F32)
        return sums + match * live

    sums = jnp.zeros((counts.shape[1], tokens.shape[0]), F32)
    sums = lax.fori_loop(0, n, seen, sums)
    counts[...] = jnp.broadcast_to(jnp.sum(sums.T, axis=0, keepdims=True), counts.shape)

    for step in range(2, n_fsdp):
        column_step(step)

    def column_sent(i, carry):
        for part in range(3):
            column_copy(i, part).wait_send()
        return carry

    lax.fori_loop(1, n_seq, column_sent, 0)

    def line_done(part, carry):
        for step in range(n_fsdp):
            line_sent(
                n_fsdp,
                step,
                lambda block, way, to: line_copy(part, step, block, way, to).wait_send(),
            )
        return carry

    lax.fori_loop(0, n_seq, line_done, 0)
    own_row().wait()
    for i in range(1, n_seq):
        row_copy(i, me_s).wait_send()
        row_copy(i, (me_s + i) % n_seq).wait_recv()


def first_gather(
    small,
    tokens,
    qkv,
    masked,
    lengths,
    n_seq,
    n_fsdp,
    pieces,
    split,
    capacity,
    top,
    experts,
    collective_id,
):
    owned = qkv.shape[0]
    rows, width = tokens.shape
    head_width = width // n_seq
    n = n_seq * n_fsdp
    places_all = n_seq * pieces * capacity
    vmem = pl.BlockSpec(memory_space=pltpu.VMEM)
    any_space = pl.BlockSpec(memory_space=pl.ANY)
    dma = pltpu.SemaphoreType.DMA
    return pl.pallas_call(
        functools.partial(first_kernel, n_seq, n_fsdp, pieces, split, capacity, owned, top),
        out_shape=[
            jax.ShapeDtypeStruct((n,) + small.shape, BF),
            jax.ShapeDtypeStruct((8, width), F32),
            jax.ShapeDtypeStruct((n_seq,) + tokens.shape, BF),
            jax.ShapeDtypeStruct((n_seq, n_fsdp, owned, 3 * head_width), BF),
            jax.ShapeDtypeStruct((n_seq, pieces, n_fsdp, capacity, width), BF),
            jax.ShapeDtypeStruct((n_fsdp, places_all, rows), BF),
            jax.ShapeDtypeStruct((n_fsdp, rows, places_all), BF),
            jax.ShapeDtypeStruct((8, experts), F32),
        ],
        in_specs=[vmem] * 4 + [pl.BlockSpec(memory_space=pltpu.SMEM)],
        out_specs=[vmem, vmem, any_space, any_space, any_space, vmem, vmem, vmem],
        scratch_shapes=[
            pltpu.VMEM((n_seq, pieces, capacity, width), BF),
            dma((5,)),
            dma((n,)),
            dma((n,)),
            dma((n_seq, 3)),
            dma((n_seq, 3)),
            dma((n_seq, 2, n_fsdp)),
            dma((n_seq, n_fsdp)),
            dma((2, n_seq - 1)),
            dma((2, n_seq)),
            dma((n_seq,)),
            dma((n_seq,)),
            dma,
        ],
        compiler_params=pltpu.CompilerParams(
            collective_id=collective_id, has_side_effects=True, vmem_limit_bytes=40 << 20
        ),
        name="first_gather",
    )(small, tokens, qkv, masked, lengths)


def greet_seq(n_seq):
    me_s, me_f = lax.axis_index("seq"), lax.axis_index("fsdp")
    barrier = pltpu.get_barrier_semaphore()
    for i in range(1, n_seq):
        pl.semaphore_signal(
            barrier, inc=1, device_id=((me_s + i) % n_seq, me_f), device_id_type=MESH
        )
    pl.semaphore_wait(barrier, n_seq - 1)


class TermSum:
    def __init__(
        self, n_seq, n_fsdp, terms, seq_terms, fsdp_terms, seq_send, seq_recv, fsdp_send, fsdp_recv
    ):
        self.n_seq, self.n_fsdp, self.terms = n_seq, n_fsdp, terms
        self.seq_terms, self.fsdp_terms = seq_terms, fsdp_terms
        self.seq_send, self.seq_recv = seq_send, seq_recv
        self.fsdp_send, self.fsdp_recv = fsdp_send, fsdp_recv
        self.me_s, self.me_f = lax.axis_index("seq"), lax.axis_index("fsdp")

    def part(self, owner):
        columns = self.seq_terms.shape[2]
        return self.terms.at[:, pl.ds(pl.multiple_of(owner * columns, 128), columns)]

    def seq_copy(self, i, place):
        other = (self.me_s + i) % self.n_seq
        return remote(
            self.part(other),
            self.seq_terms.at[place],
            self.seq_send.at[i],
            self.seq_recv.at[place],
            (other, self.me_f),
        )

    def fsdp_copy(self, i, place):
        other = (self.me_f + i) % self.n_fsdp
        return remote(
            self.seq_terms.at[self.me_s],
            self.fsdp_terms.at[place],
            self.fsdp_send.at[i],
            self.fsdp_recv.at[place],
            (self.me_s, other),
        )

    def start_seq(self):
        for i in range(1, self.n_seq):
            self.seq_copy(i, self.me_s).start()

    def over_seq(self):
        result = self.part(self.me_s)[...]
        for i in range(1, self.n_seq):
            place = (self.me_s + i) % self.n_seq
            self.seq_copy(i, place).wait_recv()
            result = result + self.seq_terms[place]
        for i in range(1, self.n_seq):
            self.seq_copy(i, self.me_s).wait_send()
        return result

    def start_fsdp(self, more):
        self.seq_terms[self.me_s] = more + (self.over_seq() if self.terms is not None else 0.0)
        for i in range(1, self.n_fsdp):
            self.fsdp_copy(i, self.me_f).start()

    def finish(self):
        result = self.seq_terms[self.me_s]
        for i in range(1, self.n_fsdp):
            place = (self.me_f + i) % self.n_fsdp
            self.fsdp_copy(i, place).wait_recv()
            result = result + self.fsdp_terms[place]
        for i in range(1, self.n_fsdp):
            self.fsdp_copy(i, self.me_f).wait_send()
        return result


def term_scratch(n_seq, n_fsdp, shape):
    dma = pltpu.SemaphoreType.DMA
    return [
        pltpu.VMEM((n_seq,) + shape, F32),
        pltpu.VMEM((n_fsdp,) + shape, F32),
        dma((n_seq,)),
        dma((n_seq,)),
        dma((n_fsdp,)),
        dma((n_fsdp,)),
    ]


def gather_kernel(n_seq, n_fsdp, x, terms, out, total, own_sem, send_sem, recv_sem, *scratch):
    me_s = lax.axis_index("seq")
    half = x.shape[0] // 2
    own = pltpu.make_async_copy(x, out.at[me_s], own_sem)
    own.start()
    term_sum = TermSum(n_seq, n_fsdp, terms, scratch[0], None, *scratch[1:], None, None)
    greet_seq(n_seq)
    flows = []
    for side, order in enumerate(gather_orders(n_seq)):
        rows = pl.ds(side * half, half)
        flows.append(
            SeqGather(
                order,
                x.at[rows],
                lambda index, rows=rows: out.at[index, rows],
                send_sem.at[side],
                recv_sem.at[side],
            )
        )
    for stage in range(len(flows[0].order)):
        for flow in flows:
            flow.start(stage)
        if stage == 0:
            term_sum.start_seq()
        if stage == 1:
            total[...] = term_sum.over_seq()
        for flow in flows:
            flow.wait(stage)
    for flow in flows:
        flow.sent()
    own.wait()


def gather_seq(x, terms, n_seq, n_fsdp, collective_id):
    vmem = pl.BlockSpec(memory_space=pltpu.VMEM)
    dma = pltpu.SemaphoreType.DMA
    part = (terms.shape[0], terms.shape[1] // n_seq)
    return pl.pallas_call(
        functools.partial(gather_kernel, n_seq, n_fsdp),
        out_shape=[
            jax.ShapeDtypeStruct((n_seq,) + x.shape, x.dtype),
            jax.ShapeDtypeStruct(part, terms.dtype),
        ],
        in_specs=[vmem] * 2,
        out_specs=[vmem] * 2,
        scratch_shapes=[
            dma,
            dma((2, n_seq - 1)),
            dma((2, n_seq)),
            pltpu.VMEM((n_seq,) + part, F32),
            dma((n_seq,)),
            dma((n_seq,)),
        ],
        compiler_params=pltpu.CompilerParams(collective_id=collective_id, has_side_effects=True),
        cost_estimate=pl.CostEstimate(flops=0, bytes_accessed=1 << 26, transcendentals=0),
        name="gather_seq",
    )(x, terms)


class SeqReduce:
    def __init__(self, n_seq, a, w, w_dim, sums, got, send_sem, recv_sem):
        self.a, self.w, self.w_dim, self.sums, self.got = a, w, w_dim, sums, got
        self.send_sem, self.recv_sem = send_sem, recv_sem
        self.me_s, self.me_f = lax.axis_index("seq"), lax.axis_index("fsdp")
        self.orders = [order[-1:] + order[-2::-1] for order in gather_orders(n_seq)]
        self.stages = len(self.orders[0])
        self.half = sums.shape[1] // 2
        self.width = sums.shape[2]

    def combined(self, index, bits):
        indices = [index]
        for bit in bits:
            indices = indices + [flipped(i, bit) for i in indices]
        return indices

    def product(self, index):
        def some(columns):
            w = self.w[:, columns] if self.w_dim == 0 else self.w[columns, :]
            self.sums[index, :, columns] = dot(self.a[index], w, 1, self.w_dim).astype(BF)

        chunked(self.width, 512, some)

    def copy(self, stage, side, count, index):
        order = self.orders[side]
        slot = sum(1 << (self.stages - 1 - s) for s in range(stage)) + count
        rows = pl.ds(side * self.half, self.half)
        return remote(
            self.sums.at[index, rows],
            self.got.at[slot, rows],
            self.send_sem.at[side, slot],
            self.recv_sem.at[side, slot],
            (flipped(self.me_s, order[stage]), self.me_f),
        )

    def leaving(self, stage, side):
        order = self.orders[side]
        return self.combined(flipped(self.me_s, order[stage]), order[stage + 1 :])

    def start(self, stage):
        if stage == 0:
            for count, index in enumerate(self.leaving(0, 0)):
                self.product(index)
                for side in range(2):
                    self.copy(0, side, self.twin(count) if side == 1 else count, index).start()
            for index in self.combined(self.me_s, self.orders[0][1:]):
                self.product(index)
        else:
            for side in range(2):
                for count, index in enumerate(self.leaving(stage, side)):
                    self.copy(stage, side, count, index).start()

    def twin(self, count):
        first, second = self.orders[0][1:], self.orders[1][1:]
        place = 0
        for position, bit in enumerate(first):
            if (count >> position) & 1:
                place += 1 << second.index(bit)
        return place

    def finish(self, stage, last=None):
        for side in range(2):
            order = self.orders[side]
            rows = pl.ds(side * self.half, self.half)
            for count, index in enumerate(self.combined(self.me_s, order[stage + 1 :])):
                copy = self.copy(stage, side, count, index)
                copy.wait_recv()
                slot = sum(1 << (self.stages - 1 - s) for s in range(stage)) + count

                def some(columns):
                    total = self.sums[index, rows, columns].astype(F32)
                    total = total + self.got[slot, rows, columns].astype(F32)
                    if last is None:
                        self.sums[index, rows, columns] = total.astype(BF)
                    else:
                        last[rows, columns] = total

                chunked(self.width, 1024, some)

    def events(self, last):
        def leave(count, index):
            self.product(index)
            for side in range(2):
                self.copy(0, side, self.twin(count) if side == 1 else count, index).start()

        result = [
            (1, functools.partial(leave, count, index))
            for count, index in enumerate(self.leaving(0, 0))
        ]
        for index in self.combined(self.me_s, self.orders[0][1:]):
            result.append((1, functools.partial(self.product, index)))
        result.append((1, functools.partial(self.finish, 0, last if self.stages == 1 else None)))
        for stage in range(1, self.stages):
            result.append((0, functools.partial(self.start, stage)))
            result.append(
                (7, functools.partial(self.finish, stage, last if stage == self.stages - 1 else None))
            )
        return result

    def sent(self):
        for stage in range(self.stages):
            for side in range(2):
                for count, index in enumerate(self.leaving(stage, side)):
                    self.copy(stage, side, count, index).wait_send()


def reduce_scratch(n_seq, rows, width):
    dma = pltpu.SemaphoreType.DMA
    return [
        pltpu.VMEM((n_seq, rows, width), BF),
        pltpu.VMEM((n_seq - 1, rows, width), BF),
        dma((2, n_seq - 1)),
        dma((2, n_seq - 1)),
    ]


def reduce_kernel(n_seq, w_dim, a, w, out, *scratch):
    greet_seq(n_seq)
    reduce = SeqReduce(n_seq, a, w, w_dim, *scratch)
    for stage in range(reduce.stages):
        reduce.start(stage)
        reduce.finish(stage, out if stage == reduce.stages - 1 else None)
    reduce.sent()


def product_reduced(a, w, w_dim, n_seq, collective_id):
    rows = a.shape[0] // n_seq
    width = w.shape[1 - w_dim]
    return pl.pallas_call(
        functools.partial(reduce_kernel, n_seq, w_dim),
        out_shape=jax.ShapeDtypeStruct((rows, width), F32),
        in_specs=[pl.BlockSpec(memory_space=pltpu.VMEM)] * 2,
        out_specs=pl.BlockSpec(memory_space=pltpu.VMEM),
        scratch_shapes=reduce_scratch(n_seq, rows, width),
        compiler_params=pltpu.CompilerParams(
            collective_id=collective_id, has_side_effects=True, vmem_limit_bytes=40 << 20
        ),
        name="product_reduced",
    )(a.reshape(n_seq, rows, -1), w)


def last_kernel(
    n_seq,
    n_fsdp,
    a,
    w,
    normed,
    x,
    mid,
    gains,
    terms_in,
    heads,
    resid,
    ready,
    input_out,
    qkv_out,
    total,
    layer_out,
    *scratch,
):
    up, down, done, got, up_send, up_recv, down_send, down_recv, done_send, done_recv = scratch[:10]
    one, part, terms, seq_terms, fsdp_terms, seq_send, seq_recv, fsdp_send, fsdp_recv = scratch[10:19]
    me_s, me_f = lax.axis_index("seq"), lax.axis_index("fsdp")
    head_width = a.shape[2] // 3
    width = n_seq * head_width
    greet_lines(n_seq, n_fsdp)
    reduce = SeqReduce(n_seq, a, w, 1, *scratch[19:])
    term_sum = TermSum(
        n_seq,
        n_fsdp,
        terms,
        seq_terms,
        fsdp_terms,
        seq_send,
        seq_recv,
        fsdp_send,
        fsdp_recv,
    )

    def input_rows():
        tile = 32
        terms[...] = terms_in[...]

        def some(i, carry):
            rows = pl.ds(pl.multiple_of(i * tile, tile), tile)
            values = x[rows, :].astype(F32)
            scale = lax.rsqrt(jnp.mean(values * values, axis=-1, keepdims=True) + epsilon)
            grad = one[rows, :]
            weighted = grad * gains[0:1, :]
            mean = jnp.mean(weighted * values, axis=-1, keepdims=True)
            result = scale * weighted - values * (scale * scale * scale * mean)
            input_out[rows, :] = (mid[rows, :] + result).astype(BF)
            terms[0:1, :] += jnp.sum(grad * values * scale, axis=0, keepdims=True)
            layer = resid[rows, :]
            for block in range(n_fsdp):
                layer = layer + ready[block, rows, :].astype(F32)
            layer_out[rows, :] = layer.astype(BF)
            return carry

        lax.fori_loop(0, x.shape[0] // tile, some, 0)
        term_sum.start_seq()

    def line_copy(src, way, s, block):
        buffer, send, recv = (up, up_send, up_recv) if way == 0 else (down, down_send, down_recv)
        to = me_f + 1 if way == 0 else me_f - 1
        place = buffer.at[block, s]
        return remote(
            place if src is None else src, place, send.at[block, s], recv.at[block, s], (me_s, to)
        )

    def done_copy(i):
        s = (me_s + i) % n_seq
        return remote(done.at[s], got.at[me_s], done_send.at[i], done_recv.at[me_s], (s, me_f))

    def stream(way, number):
        buffer = up if way == 0 else down
        behind = me_f if way == 0 else n_fsdp - 1 - me_f
        turn, i = number // n_seq, number % n_seq
        s = (me_s + i) % n_seq
        block = n_fsdp - 1 - turn if way == 0 else turn
        ahead = n_fsdp - 1 - behind
        on_time = (number >= 0) & (turn < ahead)
        finishes_up = (me_f == n_fsdp - 1) | ((n_fsdp - 1 > 2 * me_f) & (me_f > 0))

        @pl.when(on_time & (behind == 0))
        def _():
            line_copy(part.at[s, block], way, s, block).start()

        @pl.when(on_time & (behind > 0))
        def _():
            line_copy(None, way, s, block).wait_recv()
            total = buffer[block, s].astype(F32) + part[s, block].astype(F32)
            buffer[block, s] = total.astype(BF)
            line_copy(None, way, s, block).start()

        @pl.when((number >= 0) & (turn == ahead) & (behind > 0))
        def _():
            line_copy(None, way, s, me_f).wait_recv()
            done[s] = (done[s].astype(F32) + buffer[me_f, s].astype(F32)).astype(BF)

            @pl.when(finishes_up if way == 0 else jnp.logical_not(finishes_up))
            def _():
                @pl.when(i > 0)
                def _():
                    done_copy(i).start()

    lag = 2
    slots = n_seq * (n_fsdp - 1) + lag * (n_fsdp - 1)

    owned = part.shape[2]
    stripe = n_fsdp * owned

    def make(s):
        lanes = pl.ds(pl.multiple_of(s * stripe, 128), stripe)
        every = a[...].reshape(-1, a.shape[2])
        product = dot(normed[:, lanes], every, 0, 0).astype(BF)
        for block in range(n_fsdp):
            part[s, block] = product[block * owned : (block + 1) * owned]
        done[s] = part[s, me_f]

    def run(first, last):
        def slot(number, carry):
            @pl.when(number < n_seq)
            def _():
                make((me_s + number) % n_seq)

            stream(0, number - lag * me_f)
            stream(1, number - lag * (n_fsdp - 1 - me_f))
            return carry

        lax.fori_loop(first, last, slot, 0)

    reached = 0
    for number, event in enumerate(
        reduce.events(one)
        + [(0, input_rows), (3, functools.partial(term_sum.start_fsdp, heads[...]))]
    ):
        run(reached, min(slots, reached + event[0]))
        reached = min(slots, reached + event[0])
        event[1]()
    run(reached, slots)

    def place(s, rows):
        for third in range(3):
            columns = pl.ds(pl.multiple_of(third * width + s * head_width, 128), head_width)
            qkv_out[:, columns] = rows[:, third * head_width : (third + 1) * head_width].astype(F32)

    place(me_s, done[me_s])

    def arrived(i, carry):
        s = (me_s + i) % n_seq
        remote(done.at[s], got.at[s], done_send.at[i], done_recv.at[s], (s, me_f)).wait_recv()
        place(s, got[s])
        return carry

    lax.fori_loop(1, n_seq, arrived, 0)

    def all_sent(i, carry):
        s = (me_s + i) % n_seq

        @pl.when(i > 0)
        def _():
            done_copy(i).wait_send()

        for j in range(n_fsdp - 1):

            @pl.when(me_f + j < n_fsdp - 1)
            def _():
                line_copy(None, 0, s, n_fsdp - 1 - j).wait_send()

            @pl.when(j < me_f)
            def _():
                line_copy(None, 1, s, j).wait_send()

        return carry

    lax.fori_loop(0, n_seq, all_sent, 0)
    reduce.sent()
    total[...] = term_sum.finish()


def last_reduce(
    a, w, normed, x, mid, gains, terms, heads, resid, ready, n_seq, n_fsdp, collective_id
):
    rows, width = a.shape[0] // n_seq, w.shape[0]
    columns = a.shape[1]
    owned = width // (n_seq * n_fsdp)
    vmem = pl.BlockSpec(memory_space=pltpu.VMEM)
    dma = pltpu.SemaphoreType.DMA
    return pl.pallas_call(
        functools.partial(last_kernel, n_seq, n_fsdp),
        out_shape=[
            jax.ShapeDtypeStruct((rows, width), BF),
            jax.ShapeDtypeStruct((owned, n_seq * columns), F32),
            jax.ShapeDtypeStruct(heads.shape, F32),
            jax.ShapeDtypeStruct((rows, width), BF),
        ],
        in_specs=[vmem] * 10,
        out_specs=[vmem] * 4,
        scratch_shapes=[
            pltpu.VMEM((n_fsdp, n_seq, owned, columns), BF),
            pltpu.VMEM((n_fsdp, n_seq, owned, columns), BF),
            pltpu.VMEM((n_seq, owned, columns), BF),
            pltpu.VMEM((n_seq, owned, columns), BF),
            dma((n_fsdp, n_seq)),
            dma((n_fsdp, n_seq)),
            dma((n_fsdp, n_seq)),
            dma((n_fsdp, n_seq)),
            dma((n_seq,)),
            dma((n_seq,)),
            pltpu.VMEM((rows, width), F32),
            pltpu.VMEM((n_seq, n_fsdp, owned, columns), BF),
            pltpu.VMEM(terms.shape, F32),
        ]
        + term_scratch(n_seq, n_fsdp, heads.shape)
        + reduce_scratch(n_seq, rows, width),
        compiler_params=pltpu.CompilerParams(
            collective_id=collective_id, has_side_effects=True, vmem_limit_bytes=60 << 20
        ),
        cost_estimate=pl.CostEstimate(flops=0, bytes_accessed=1 << 27, transcendentals=0),
        name="last_reduce",
    )(a.reshape(n_seq, rows, -1), w, normed, x, mid, gains, terms, heads, resid, ready)


def chunked(total, size, body):
    def step(i, carry):
        body(pl.ds(pl.multiple_of(i * size, size), size))
        return carry

    lax.fori_loop(0, total // size, step, 0)


def dispatch_kernel(n_seq, n_fsdp, pieces, x, hot, gates, masked, before, w_up, w_down, *refs):
    masked_all, columns_out, scaled = refs[:3]
    outs, hiddens, acts, results = (refs[3 + k * pieces : 3 + (k + 1) * pieces] for k in range(4))
    rest = refs[3 + 4 * pieces :]
    gates_out, gathered, send, total = rest[:4]
    own_sem, line_send, line_recv, row_send, row_recv, own_two, send_two, recv_two = rest[4:12]
    gate_exchange = Exchange(n_seq, n_fsdp, gates, gates_out, rest[12:])
    me_s, me_f = lax.axis_index("seq"), lax.axis_index("fsdp")
    width = x.shape[1]
    capacity = outs[0].shape[2]
    greet_all(n_seq, n_fsdp)

    def line_copy(step, block, way, to):
        src = x if step == 0 else gathered.at[block]
        return remote(
            src, gathered.at[block], line_send.at[way, step], line_recv.at[block], (me_s, to)
        )

    def row_copy(block, i, piece, place):
        other = (me_s + i) % n_seq
        return remote(
            send.at[block, other, piece],
            outs[piece].at[place, block],
            row_send.at[block, i, piece],
            row_recv.at[place, block, piece],
            (other, me_f),
        )

    def own_copy(block, piece):
        return pltpu.make_async_copy(
            send.at[block, me_s, piece], outs[piece].at[me_s, block], own_sem.at[block, piece]
        )

    def masked_copy(block, i, place):
        other = (me_s + i) % n_seq
        return remote(
            send.at[block, other],
            masked_all.at[place, :, block],
            send_two.at[block, i],
            recv_two.at[place, block],
            (other, me_f),
        )

    def own_masked(block):
        return pltpu.make_async_copy(
            send.at[block, me_s], masked_all.at[me_s, :, block], own_two.at[block]
        )

    def pick(block, rows):
        def some(columns):
            picked = dot(hot[block], rows[:, columns], 1, 0).astype(BF)
            send[block, :, :, :, columns] = picked.reshape(n_seq, pieces, capacity, -1)

        chunked(width, 512, some)

    def scatter(block, rows):
        pick(block, rows)
        for i in range(1, n_seq):
            for piece in range(pieces):
                row_copy(block, i, piece, me_s).start()
        for piece in range(pieces):
            own_copy(block, piece).start()

    def scatter_masked(block):
        for piece in range(pieces):
            own_copy(block, piece).wait()
            for i in range(1, n_seq):
                row_copy(block, i, piece, me_s).wait_send()
        pick(block, masked.at[block])
        for i in range(1, n_seq):
            masked_copy(block, i, me_s).start()
        own_masked(block).start()

    def around(step, act):
        @pl.when(me_f - step >= 0)
        def _():
            act(me_f - step)

        @pl.when(me_f + step < n_fsdp)
        def _():
            act(me_f + step)

    @pl.when(me_f + 1 < n_fsdp)
    def _():
        line_copy(0, me_f, 0, me_f + 1).start()

    @pl.when(me_f >= 1)
    def _():
        line_copy(0, me_f, 1, me_f - 1).start()

    scatter(me_f, x)
    gate_exchange.start()
    for step in range(1, n_fsdp):
        line_step(
            n_fsdp,
            step,
            lambda block: line_copy(1, block, 0, me_f).wait_recv(),
            lambda block, way, to: line_copy(step, block, way, to).start(),
        )
        around(step, lambda block: scatter(block, gathered.at[block]))
    for step in range(1, n_fsdp):
        around(step, scatter_masked)
    for step in range(n_fsdp):
        line_sent(
            n_fsdp, step, lambda block, way, to: line_copy(step, block, way, to).wait_send()
        )

    gate_exchange.finish()
    n = n_seq * n_fsdp
    for piece in range(pieces):
        lanes = lax.broadcasted_iota(jnp.int32, (n, capacity, 128), 2)
        place = lax.broadcasted_iota(jnp.int32, (n, capacity, 128), 1)
        values = jnp.broadcast_to(gates_out[:, piece : piece + 1, :], (n, capacity, 128))
        column = jnp.sum(jnp.where(lanes == place, values, 0.0), axis=2, keepdims=True)
        columns_out[piece] = column.reshape(n * capacity, 1)

    for piece in range(pieces):
        own_copy(me_f, piece).wait()
        for i in range(1, n_seq):
            row_copy(me_f, i, piece, me_s).wait_send()
    for piece in range(pieces):
        for block in range(n_fsdp):
            for i in range(1, n_seq):
                row_copy(block, i, piece, (me_s + i) % n_seq).wait_recv()

    ff = w_down.shape[1]
    tile = min(256, ff)
    steps = ff // tile
    spans = seq_tile(n_seq, n_fsdp * capacity, 3072 // n_fsdp)
    count = spans * n_fsdp * capacity
    for piece in range(pieces):

        def body(rows, w_gate, w_value, w_back, hidden, act, result, scaled_rows):
            step = pl.program_id(1)
            low = rows[...].reshape(count, width)
            gate = dot(low, w_gate[0], 1, 0)
            up = dot(low, w_value[0], 1, 0)
            hidden[0] = gate
            hidden[1] = up
            act[...] = (gate * jax.nn.sigmoid(gate) * up).astype(BF)
            product = dot(act[...], w_back[0], 1, 0)

            @pl.when(step == 0)
            def _():
                total[...] = product

            @pl.when(step > 0)
            def _():
                total[...] += product

            @pl.when(step == steps - 1)
            def _():
                start = pl.multiple_of(pl.program_id(0) * count, 8)
                column = columns_out[piece, pl.ds(start, count), :]
                result[...] = total[...].astype(BF)
                gated = (result[...].astype(F32) * column).astype(BF)
                scaled_rows[...] = gated.reshape(scaled_rows.shape)

        pltpu.emit_pipeline(
            body,
            grid=(n * capacity // count, steps),
            in_specs=[
                pl.BlockSpec((spans, n_fsdp, capacity, width), lambda r, i: (r, 0, 0, 0)),
                pl.BlockSpec((1, width, tile), lambda r, i: (piece, 0, i)),
                pl.BlockSpec((1, width, tile), lambda r, i: (piece, 0, steps + i)),
                pl.BlockSpec((1, tile, width), lambda r, i: (piece, i, 0)),
            ],
            out_specs=[
                pl.BlockSpec((2, count, tile), lambda r, i: (0, r, i)),
                pl.BlockSpec((count, tile), lambda r, i: (r, i)),
                pl.BlockSpec((count, width), lambda r, i: (r, 0)),
                pl.BlockSpec((spans, 1, n_fsdp, capacity, width), lambda r, i: (r, piece, 0, 0, 0)),
            ],
        )(
            outs[piece],
            w_up,
            w_up,
            w_down,
            hiddens[piece],
            acts[piece],
            results[piece],
            scaled,
        )

    for step in range(1, n_fsdp):
        around(step, lambda block: own_masked(block).wait())
    for step in range(1, n_fsdp):
        for i in range(1, n_seq):

            def done(block):
                masked_copy(block, i, me_s).wait_send()
                masked_copy(block, i, (me_s + i) % n_seq).wait_recv()

            around(step, done)


def dispatch_rows(
    x, hot, gates, masked, before, w_up, w_down, n_seq, n_fsdp, capacity, collective_id
):
    count, width = x.shape
    pieces, ff = w_down.shape[:2]
    rows = n_seq * n_fsdp * capacity
    tile_rows = seq_tile(n_seq, n_fsdp * capacity, 3072 // n_fsdp) * n_fsdp * capacity
    vmem = pl.BlockSpec(memory_space=pltpu.VMEM)
    any_space = pl.BlockSpec(memory_space=pl.ANY)
    dma = pltpu.SemaphoreType.DMA
    return pl.pallas_call(
        functools.partial(dispatch_kernel, n_seq, n_fsdp, pieces),
        out_shape=[
            jax.ShapeDtypeStruct(before.shape, BF),
            jax.ShapeDtypeStruct((pieces, rows, 1), F32),
            jax.ShapeDtypeStruct(before.shape, BF),
        ]
        + [jax.ShapeDtypeStruct((n_seq, n_fsdp, capacity, width), BF)] * pieces
        + [jax.ShapeDtypeStruct((2, rows, ff), F32)] * pieces
        + [jax.ShapeDtypeStruct((rows, ff), BF)] * pieces
        + [jax.ShapeDtypeStruct((rows, width), BF)] * pieces,
        in_specs=[vmem] * 4 + [any_space] * 3,
        out_specs=[any_space, vmem] + [any_space] * (1 + 4 * pieces),
        scratch_shapes=[
            pltpu.VMEM(gates.shape, F32),
            pltpu.VMEM((n_fsdp, count, width), BF),
            pltpu.VMEM((n_fsdp, n_seq, pieces, capacity, width), BF),
            pltpu.VMEM((tile_rows, width), F32),
            dma((n_fsdp, pieces)),
            dma((2, n_fsdp)),
            dma((n_fsdp,)),
            dma((n_fsdp, n_seq, pieces)),
            dma((n_seq, n_fsdp, pieces)),
            dma((n_fsdp,)),
            dma((n_fsdp, n_seq)),
            dma((n_seq, n_fsdp)),
        ]
        + exchange_sems(n_seq * n_fsdp),
        input_output_aliases={4: 0},
        compiler_params=pltpu.CompilerParams(
            collective_id=collective_id, has_side_effects=True, vmem_limit_bytes=60 << 20
        ),
        name="dispatch_rows",
    )(x, hot, gates, masked, before, w_up, w_down)


def return_kernel(n_seq, n_fsdp, pieces, hot, gates, ready, w_up, *refs):
    grads = refs[:pieces]
    out, gates_out, ready_sums = refs[pieces : pieces + 3]
    rest = refs[pieces + 3 :]
    weights, hidden, rows, got, parts, sums, some_ready = rest[:7]
    w_sem, h_sem, ready_sem, own_sem, row_send, row_recv, part_send, part_recv = rest[7:15]
    gate_exchange = Exchange(n_seq, n_fsdp, gates, gates_out, rest[15:])
    me_s, me_f = lax.axis_index("seq"), lax.axis_index("fsdp")
    width = out.shape[1]
    capacity = rows.shape[3]
    ff = hidden.shape[5]
    tile = min(256, width)
    chunks = width // tile

    def weight_copy(piece, chunk):
        lines = pl.ds(pl.multiple_of(chunk * tile, tile), tile)
        return pltpu.make_async_copy(
            w_up.at[piece, lines], weights.at[piece, lines], w_sem.at[piece, chunk]
        )

    def hidden_copy(piece):
        return pltpu.make_async_copy(grads[piece], hidden.at[piece], h_sem.at[piece])

    def ready_copy(block):
        return pltpu.make_async_copy(
            ready.at[:, :, block], some_ready.at[block % 2], ready_sem.at[block % 2]
        )

    def row_copy(block, i, place):
        other = (me_s + i) % n_seq
        return remote(
            rows.at[block, other],
            got.at[block, place],
            row_send.at[block, i],
            row_recv.at[block, place],
            (other, me_f),
        )

    def own_copy(block):
        return pltpu.make_async_copy(rows.at[block, me_s], got.at[block, me_s], own_sem.at[block])

    def part_copy(j):
        block = (me_f + j) % n_fsdp
        return remote(
            parts.at[block], sums.at[me_f], part_send.at[j], part_recv.at[me_f], (me_s, block)
        )

    for piece in range(pieces):
        hidden_copy(piece).start()

        def begin(chunk, carry):
            weight_copy(piece, chunk).start()
            return carry

        lax.fori_loop(0, chunks, begin, 0)
    for block in range(min(2, n_fsdp)):
        ready_copy(block).start()
    greet_all(n_seq, n_fsdp)
    gate_exchange.start()

    def compute(j):
        block = (me_f + j) % n_fsdp
        for piece in range(pieces):
            if j == 1:
                hidden_copy(piece).wait()
            gate_grad = hidden[piece, 0, :, block].reshape(-1, ff)
            up_grad = hidden[piece, 1, :, block].reshape(-1, ff)

            def some(chunk, carry):
                if j == 1:
                    weight_copy(piece, chunk).wait()
                lines = pl.ds(pl.multiple_of(chunk * tile, tile), tile)
                total = dot(gate_grad, weights[piece, lines, :ff], 1, 1)
                total = total + dot(up_grad, weights[piece, lines, ff:], 1, 1)
                rows[block, :, piece, :, lines] = total.astype(BF).reshape(n_seq, capacity, -1)
                return carry

            lax.fori_loop(0, chunks, some, 0)
        for i in range(1, n_seq):
            row_copy(block, i, me_s).start()
        own_copy(block).start()

    def finish(j):
        block = (me_f + j) % n_fsdp
        own_copy(block).wait()
        for i in range(1, n_seq):
            row_copy(block, i, (me_s + i) % n_seq).wait_recv()

        def some(columns):
            arrived = got[block, :, :, :, columns].reshape(n_seq * pieces * capacity, -1)
            total = dot(hot[block], arrived, 1, 0)
            if j < n_fsdp:
                parts[block, :, columns] = total.astype(BF)
            else:
                out[:, columns] = total

        chunked(width, 512, some)
        if j < n_fsdp:
            part_copy(j).start()

    def sum_ready(block):
        ready_copy(block).wait()

        def some(columns):
            arrived = some_ready[block % 2, :, :, :, columns]
            arrived = arrived.reshape(n_seq * pieces * capacity, -1)
            ready_sums[block, :, columns] = dot(hot[block], arrived, 1, 0).astype(BF)

        chunked(width, 512, some)
        if block + 2 < n_fsdp:
            ready_copy(block + 2).start()

    for j in range(1, n_fsdp + 1):
        compute(j)
        if j >= 3:
            finish(j - 2)
    for block in range(n_fsdp):
        sum_ready(block)
    for j in range(max(1, n_fsdp - 1), n_fsdp + 1):
        finish(j)
    for j in range(1, n_fsdp):
        source = (me_f + n_fsdp - j) % n_fsdp
        remote(
            parts.at[source], sums.at[source], part_send.at[j], part_recv.at[source], (me_s, source)
        ).wait_recv()

    def add(columns):
        total = out[:, columns]
        for j in range(1, n_fsdp):
            total = total + sums[(me_f + j) % n_fsdp, :, columns].astype(F32)
        out[:, columns] = total

    chunked(width, 512, add)
    for j in range(1, n_fsdp):
        part_copy(j).wait_send()
    for block in range(n_fsdp):
        for i in range(1, n_seq):
            row_copy(block, i, me_s).wait_send()
    gate_exchange.finish()


def return_rows(grads, w_up, hot, gates, ready, n_seq, n_fsdp, collective_id):
    pieces, width = w_up.shape[:2]
    ff = w_up.shape[2] // 2
    count = hot.shape[1]
    capacity = ready.shape[3]
    vmem = pl.BlockSpec(memory_space=pltpu.VMEM)
    any_space = pl.BlockSpec(memory_space=pl.ANY)
    dma = pltpu.SemaphoreType.DMA
    return pl.pallas_call(
        functools.partial(return_kernel, n_seq, n_fsdp, pieces),
        out_shape=[
            jax.ShapeDtypeStruct((count, width), F32),
            jax.ShapeDtypeStruct(gates.shape, F32),
            jax.ShapeDtypeStruct((n_fsdp, count, width), BF),
        ],
        in_specs=[vmem, vmem, any_space, any_space] + [any_space] * pieces,
        out_specs=[vmem] * 3,
        scratch_shapes=[
            pltpu.VMEM(w_up.shape, BF),
            pltpu.VMEM((pieces, 2, n_seq, n_fsdp, capacity, ff), BF),
            pltpu.VMEM((n_fsdp, n_seq, pieces, capacity, width), BF),
            pltpu.VMEM((n_fsdp, n_seq, pieces, capacity, width), BF),
            pltpu.VMEM((n_fsdp, count, width), BF),
            pltpu.VMEM((n_fsdp, count, width), BF),
            pltpu.VMEM((2, n_seq, pieces, capacity, width), BF),
            dma((pieces, width // min(256, width))),
            dma((pieces,)),
            dma((2,)),
            dma((n_fsdp,)),
            dma((n_fsdp, n_seq)),
            dma((n_fsdp, n_seq)),
            dma((n_fsdp,)),
            dma((n_fsdp,)),
        ]
        + exchange_sems(n_seq * n_fsdp),
        compiler_params=pltpu.CompilerParams(
            collective_id=collective_id, has_side_effects=True, vmem_limit_bytes=60 << 20
        ),
        name="return_rows",
    )(hot, gates, ready, w_up, *grads)


def weight_grad_kernel(a, b, *refs):
    parts, _, n = b.shape
    for part in range(parts):
        refs[-1][0, :, part * n : (part + 1) * n] = dot(a[...], b[part], 0, 0)


def weight_grad(a, b, whole, piece, pieces):
    rows, m = a.shape
    parts, _, n = b.shape
    tile = min(256, m)
    more = [] if whole is None else [whole]
    return pl.pallas_call(
        weight_grad_kernel,
        out_shape=jax.ShapeDtypeStruct((pieces, m, n * parts), F32),
        grid=(m // tile,),
        in_specs=[
            pl.BlockSpec((rows, tile), lambda i: (0, i)),
            pl.BlockSpec((parts, rows, n), lambda i: (0, 0, 0)),
        ]
        + [pl.BlockSpec(memory_space=pl.ANY)] * len(more),
        out_specs=pl.BlockSpec((1, tile, n * parts), lambda i: (piece, i, 0)),
        input_output_aliases={2: 0} if more else {},
        cost_estimate=pl.CostEstimate(
            flops=2 * rows * m * n * parts,
            bytes_accessed=4 * m * n * parts,
            transcendentals=0,
        ),
        name="weight_grad",
    )(a, b, *more)


def seq_tile(n_seq, rows_each, most=1024):
    tile = n_seq
    while tile > 1 and (tile * rows_each > most or n_seq % tile):
        tile -= 1
    return tile


def expert_backward_kernel(masked, gates, piece_out, hidden, w_down, out, grad, inner, partial):
    @pl.when(pl.program_id(1) == 0)
    def _():
        partial[...] = jnp.zeros_like(partial)

        def some(columns):
            low = masked[:, 0, :, :, columns].reshape(grad.shape[0], -1).astype(F32)
            grad[:, columns] = (low * gates[...]).astype(BF)
            product = low * piece_out[:, columns].astype(F32)
            for i in range(product.shape[1] // 128):
                partial[...] += product[:, i * 128 : (i + 1) * 128]

        chunked(grad.shape[1], 512, some)
        sums = jnp.sum(partial[...].T, axis=0, keepdims=True)
        inner[...] = jnp.broadcast_to(sums, inner.shape)

    act_grad = dot(grad[...], w_down[0], 1, 1)
    gate, up = hidden[0], hidden[1]
    sigmoid = jax.nn.sigmoid(gate)
    out[0] = (act_grad * up * sigmoid * (1.0 + gate * (1.0 - sigmoid))).astype(BF)
    out[1] = (act_grad * gate * sigmoid).astype(BF)


def expert_backward(masked, gates, piece_out, hidden, w_down, piece):
    rows, width = piece_out.shape
    ff = w_down.shape[1]
    n_seq, _, n_fsdp, capacity, _ = masked.shape
    tile = min(256, ff)
    spans = seq_tile(n_seq, n_fsdp * capacity)
    count = spans * n_fsdp * capacity
    part = pl.BlockSpec((2, count, tile), lambda r, i: (0, r, i))
    fixed = lambda r, i: (r, 0)
    return pl.pallas_call(
        expert_backward_kernel,
        out_shape=[
            jax.ShapeDtypeStruct((2, rows, ff), BF),
            jax.ShapeDtypeStruct((rows, width), BF),
            jax.ShapeDtypeStruct((8, rows), F32),
        ],
        grid=(rows // count, ff // tile),
        in_specs=[
            pl.BlockSpec((spans, 1, n_fsdp, capacity, width), lambda r, i: (r, piece, 0, 0, 0)),
            pl.BlockSpec((count, 1), fixed),
            pl.BlockSpec((count, width), fixed),
            part,
            pl.BlockSpec((1, tile, width), lambda r, i: (piece, i, 0)),
        ],
        out_specs=[
            part,
            pl.BlockSpec((count, width), fixed),
            pl.BlockSpec((8, count), lambda r, i: (0, r)),
        ],
        scratch_shapes=[pltpu.VMEM((count, 128), F32)],
        compiler_params=pltpu.CompilerParams(vmem_limit_bytes=48 << 20),
        cost_estimate=pl.CostEstimate(
            flops=2 * rows * width * ff, bytes_accessed=12 * rows * ff, transcendentals=rows * ff
        ),
        name="expert_backward",
    )(masked, gates, piece_out, hidden, w_down)


class SeqShare:
    def __init__(self, n_seq, own, every, send_sem, recv_sem):
        self.n_seq, self.own, self.every = n_seq, own, every
        self.send_sem, self.recv_sem = send_sem, recv_sem
        self.me_s, self.me_f = lax.axis_index("seq"), lax.axis_index("fsdp")

    def copy(self, i, place):
        other = (self.me_s + i) % self.n_seq
        return remote(
            self.own,
            self.every.at[place],
            self.send_sem.at[i],
            self.recv_sem.at[place],
            (other, self.me_f),
        )

    def total(self):
        for i in range(1, self.n_seq):
            self.copy(i, self.me_s).start()
        total = self.own[...]
        for i in range(1, self.n_seq):
            place = (self.me_s + i) % self.n_seq
            self.copy(i, place).wait_recv()
            total = total + self.every[place]
        for i in range(1, self.n_seq):
            self.copy(i, self.me_s).wait_send()
        return total


def share_scratch(n_seq, shape):
    dma = pltpu.SemaphoreType.DMA
    return [pltpu.VMEM(shape, F32), pltpu.VMEM((n_seq,) + shape, F32), dma((n_seq,)), dma((n_seq,))]


def row_sums(values):
    ones = jnp.ones((8, values.shape[1]), F32)
    return lax.dot_general(
        ones,
        values,
        (((1,), (1,)), ((), ())),
        preferred_element_type=F32,
        precision=lax.Precision.HIGHEST,
    )


def front_kernel(n_seq, x, gain, w, normed, raw, totals, *scratch):
    greet_seq(n_seq)
    share = SeqShare(n_seq, *scratch)
    head_width = w.shape[1] // 3
    tile = 256

    def some(i, carry):
        rows = pl.ds(pl.multiple_of(i * tile, tile), tile)
        values = x[rows, :].astype(F32)
        scale = lax.rsqrt(jnp.mean(values * values, axis=-1, keepdims=True) + epsilon)
        low = (values * scale * gain[0:1, :]).astype(BF)
        normed[rows, :] = low
        result = dot(low, w[...], 1, 0)
        raw[rows, :] = result
        for part in range(2):
            piece = result[:, part * head_width : (part + 1) * head_width]
            share.own[part : part + 1, rows] = row_sums(piece * piece)[0:1]
        return carry

    share.own[...] = jnp.zeros_like(share.own)
    lax.fori_loop(0, x.shape[0] // tile, some, 0)
    totals[...] = share.total()


def front(x, gains, w, n_seq, collective_id):
    rows, width = x.shape
    vmem = pl.BlockSpec(memory_space=pltpu.VMEM)
    return pl.pallas_call(
        functools.partial(front_kernel, n_seq),
        out_shape=[
            jax.ShapeDtypeStruct((rows, width), BF),
            jax.ShapeDtypeStruct((rows, w.shape[1]), F32),
            jax.ShapeDtypeStruct((8, rows), F32),
        ],
        in_specs=[vmem] * 3,
        out_specs=[vmem] * 3,
        scratch_shapes=share_scratch(n_seq, (8, rows)),
        compiler_params=pltpu.CompilerParams(
            collective_id=collective_id, has_side_effects=True, vmem_limit_bytes=40 << 20
        ),
        name="front",
    )(x, gains, w)


def column_rms(sums, part, width):
    return lax.rsqrt(sums.T[:, part : part + 1] / width + epsilon)


def turned(values, cosine, sine):
    return values * cosine + pltpu.roll(values, values.shape[1] // 2, 1) * sine


def softmax_columns(k, q, length, scaling):
    scores = dot(k, q, 1, 1) * scaling
    key = lax.broadcasted_iota(jnp.int32, scores.shape, 0)
    scores = jnp.where(key < length, scores, -1e30)
    weights = jnp.exp(scores - jnp.max(scores, axis=0, keepdims=True))
    return weights / jnp.sum(weights, axis=0, keepdims=True)


def attend_kernel(
    width,
    length,
    raw_q,
    raw_k,
    raw_v,
    q_sums,
    k_sums,
    gain,
    q_cos,
    q_sin,
    k_cos,
    k_sin,
    o_ref,
    q_ref,
    k_ref,
    v_ref,
):
    scaling = raw_q.shape[1] ** (-0.5)

    @pl.when(pl.program_id(1) == 0)
    def _():
        key = raw_k[...] * column_rms(k_sums[...], 1, width) * gain[2:3, :]
        k_ref[...] = turned(key, k_cos[...], k_sin[...]).astype(BF)
        v_ref[...] = raw_v[...].astype(BF)

    query = raw_q[...] * column_rms(q_sums[...], 0, width) * gain[1:2, :]
    query = turned(query, q_cos[...], q_sin[...]).astype(BF)
    q_ref[...] = query
    probs = softmax_columns(k_ref[...], query, length[0], scaling).astype(BF)
    o_ref[...] = dot(v_ref[...], probs, 0, 0).T.astype(BF)


def attend(raw, totals, gains, cosine, sine, length, block, width):
    slot_len, head_width = raw.shape[0], raw.shape[1] // 3
    hd = cosine.shape[1]
    heads = head_width // hd
    rows = lambda shift: pl.BlockSpec((block, hd), lambda h, i, n: (i, shift + h))
    full = lambda shift: pl.BlockSpec((slot_len, hd), lambda h, i, n: (0, shift + h))
    table = pl.BlockSpec((block, hd), lambda h, i, n: (i, 0))
    whole_table = pl.BlockSpec((slot_len, hd), lambda h, i, n: (0, 0))
    return pl.pallas_call(
        functools.partial(attend_kernel, width),
        out_shape=[jax.ShapeDtypeStruct((slot_len, head_width), BF)] * 4,
        grid_spec=pltpu.PrefetchScalarGridSpec(
            num_scalar_prefetch=1,
            grid=(heads, slot_len // block),
            in_specs=[
                rows(0),
                full(heads),
                full(2 * heads),
                pl.BlockSpec((8, block), lambda h, i, n: (0, i)),
                pl.BlockSpec((8, slot_len), lambda h, i, n: (0, 0)),
                pl.BlockSpec((8, hd), lambda h, i, n: (0, h)),
                table,
                table,
                whole_table,
                whole_table,
            ],
            out_specs=[rows(0), rows(0), full(0), full(0)],
        ),
        cost_estimate=pl.CostEstimate(
            flops=4 * heads * slot_len * slot_len * hd, bytes_accessed=1 << 23, transcendentals=0
        ),
        name="attend",
    )(length, raw, raw, raw, totals, totals, gains, cosine, sine, cosine, sine)


def attend_back_kernel(
    width,
    length,
    q_ref,
    k_ref,
    v_ref,
    g_ref,
    raw_q,
    raw_k,
    q_sums,
    k_sums,
    gain,
    q_cos,
    q_sin,
    k_cos,
    k_sin,
    dq_ref,
    dk_ref,
    dv_ref,
    dots,
    gain_out,
    dk_sum,
    dv_sum,
):
    head, step = pl.program_id(0), pl.program_id(1)
    last = step == pl.num_programs(1) - 1
    block, hd = q_ref.shape
    scaling = hd ** (-0.5)

    @pl.when(step == 0)
    def _():
        dk_sum[...] = jnp.zeros_like(dk_sum)
        dv_sum[...] = jnp.zeros_like(dv_sum)
        gain_out[...] = jnp.zeros_like(gain_out)

        @pl.when(head == 0)
        def _():
            dots[...] = jnp.zeros_like(dots)

    q, k, v, g = q_ref[...], k_ref[...], v_ref[...], g_ref[...]
    probs = softmax_columns(k, q, length[0], scaling)
    dv_sum[...] += dot(probs.astype(BF), g, 1, 0)
    weights_grad = dot(v, g, 1, 1)
    inner = jnp.sum(probs * weights_grad, axis=0, keepdims=True)
    score_grad = (probs * (weights_grad - inner) * scaling).astype(BF)
    dk_sum[...] += dot(score_grad, q, 1, 0)
    query_grad = dot(k, score_grad, 0, 0).T.astype(BF).astype(F32)
    query_in = turned(query_grad, q_cos[...], -q_sin[...])
    dq_ref[...] = query_in
    product = query_in * raw_q[...]
    rows = pl.ds(pl.multiple_of(step * block, block), block)
    dots[0:1, rows] += row_sums(product * gain[1:2, :])[0:1]
    gain_out[0:1, :] += jnp.sum(
        product * column_rms(q_sums[...], 0, width), axis=0, keepdims=True
    )

    @pl.when(last)
    def _():
        key_in = turned(dk_sum[...].astype(BF).astype(F32), k_cos[...], -k_sin[...])
        dk_ref[...] = key_in
        dv_ref[...] = dv_sum[...].astype(BF)
        product = key_in * raw_k[...]
        dots[1:2, :] += row_sums(product * gain[2:3, :])[0:1]
        gain_out[1:2, :] = jnp.sum(
            product * column_rms(k_sums[...], 1, width), axis=0, keepdims=True
        )


def attend_back(query, key, value, grad, raw, totals, gains, cosine, sine, length, block, width):
    slot_len, head_width = query.shape
    hd = cosine.shape[1]
    heads = head_width // hd
    rows = pl.BlockSpec((block, hd), lambda h, i, n: (i, h))
    full = lambda shift: pl.BlockSpec((slot_len, hd), lambda h, i, n: (0, shift + h))
    table = pl.BlockSpec((block, hd), lambda h, i, n: (i, 0))
    whole_table = pl.BlockSpec((slot_len, hd), lambda h, i, n: (0, 0))
    return pl.pallas_call(
        functools.partial(attend_back_kernel, width),
        out_shape=[
            jax.ShapeDtypeStruct(query.shape, F32),
            jax.ShapeDtypeStruct(query.shape, F32),
            jax.ShapeDtypeStruct(query.shape, BF),
            jax.ShapeDtypeStruct((8, slot_len), F32),
            jax.ShapeDtypeStruct((8, head_width), F32),
        ],
        grid_spec=pltpu.PrefetchScalarGridSpec(
            num_scalar_prefetch=1,
            grid=(heads, slot_len // block),
            in_specs=[
                rows,
                full(0),
                full(0),
                rows,
                rows,
                full(heads),
                pl.BlockSpec((8, block), lambda h, i, n: (0, i)),
                pl.BlockSpec((8, slot_len), lambda h, i, n: (0, 0)),
                pl.BlockSpec((8, hd), lambda h, i, n: (0, h)),
                table,
                table,
                whole_table,
                whole_table,
            ],
            out_specs=[
                rows,
                full(0),
                full(0),
                pl.BlockSpec((8, slot_len), lambda h, i, n: (0, 0)),
                pl.BlockSpec((8, hd), lambda h, i, n: (0, h)),
            ],
            scratch_shapes=[pltpu.VMEM((slot_len, hd), F32), pltpu.VMEM((slot_len, hd), F32)],
        ),
        cost_estimate=pl.CostEstimate(
            flops=20 * heads * slot_len * slot_len * hd, bytes_accessed=1 << 24, transcendentals=0
        ),
        name="attend_back",
    )(
        length,
        query,
        key,
        value,
        grad,
        raw,
        raw,
        totals,
        totals,
        gains,
        cosine,
        sine,
        cosine,
        sine,
    )


def raw_back_kernel(
    n_seq, n_fsdp, width, dq, dk, dv, raw, totals, gain, dots, terms, out, terms_out, *scratch
):
    greet_lines(n_seq, n_fsdp)
    share = SeqShare(n_seq, *scratch[:4])
    term_sum = TermSum(n_seq, n_fsdp, None, *scratch[4:6], None, None, *scratch[6:])
    term_sum.start_fsdp(terms[...])
    head_width = dq.shape[1]
    share.own[...] = dots[...]
    share.own[...] = share.total()
    tile = 256

    def some(i, carry):
        rows = pl.ds(pl.multiple_of(i * tile, tile), tile)
        inner = share.own[:, rows].T / width
        for part, grad in enumerate((dq, dk)):
            columns = slice(part * head_width, (part + 1) * head_width)
            scale = column_rms(totals[:, rows], part, width)
            weighted = grad[rows, :] * gain[part + 1 : part + 2, :]
            cube = scale * scale * scale
            result = scale * weighted - raw[rows, columns] * (cube * inner[:, part : part + 1])
            out[rows, columns] = result.astype(BF)
        out[rows, 2 * head_width :] = dv[rows, :]
        return carry

    lax.fori_loop(0, dq.shape[0] // tile, some, 0)
    terms_out[...] = term_sum.finish()


def raw_back(dq, dk, dv, raw, totals, gains, dots, terms, n_seq, n_fsdp, width, collective_id):
    vmem = pl.BlockSpec(memory_space=pltpu.VMEM)
    dma = pltpu.SemaphoreType.DMA
    return pl.pallas_call(
        functools.partial(raw_back_kernel, n_seq, n_fsdp, width),
        out_shape=[
            jax.ShapeDtypeStruct(raw.shape, BF),
            jax.ShapeDtypeStruct(terms.shape, F32),
        ],
        in_specs=[vmem] * 8,
        out_specs=[vmem] * 2,
        scratch_shapes=share_scratch(n_seq, dots.shape)
        + [
            pltpu.VMEM((n_seq,) + terms.shape, F32),
            pltpu.VMEM((n_fsdp,) + terms.shape, F32),
            dma((n_fsdp,)),
            dma((n_fsdp,)),
        ],
        compiler_params=pltpu.CompilerParams(
            collective_id=collective_id, has_side_effects=True, vmem_limit_bytes=40 << 20
        ),
        name="raw_back",
    )(dq, dk, dv, raw, totals, gains, dots, terms)


def rope_tables(positions, head_dim):
    half = head_dim // 2
    frequency = rope_base ** (-jnp.arange(half, dtype=F32) * 2.0 / head_dim)
    angles = positions.astype(F32)[:, None] * frequency[None, :]
    cosine, sine = jnp.cos(angles), jnp.sin(angles)
    return jnp.concatenate([cosine, cosine], axis=1), jnp.concatenate([-sine, sine], axis=1)


def places(block_routes, experts, capacity):
    count = block_routes.shape[0]
    match = (block_routes[:, :, None] == experts[None, None, :]).astype(F32).sum(axis=1)
    lower = jnp.tril(jnp.ones((count, count), BF), -1)
    rank = dot(lower, match.astype(BF), 1, 0)
    place = jnp.arange(capacity, dtype=F32)
    return match[:, :, None] * (rank[:, :, None] == place[None, None, :]).astype(F32)


def local(
    tokens,
    cotangent,
    lengths,
    routes,
    norm_gains,
    qkv_weight,
    proj_weight,
    router_weight,
    expert_up,
    expert_down,
):
    n_seq, n_fsdp = lax.axis_size("seq"), lax.axis_size("fsdp")
    n_dev = n_seq * n_fsdp
    me_s, me_f = lax.axis_index("seq"), lax.axis_index("fsdp")
    shard_len, width = tokens.shape[1], tokens.shape[2]
    slot_len = shard_len * n_seq
    experts = router_weight.shape[1]
    top_count = routes.shape[2]
    capacity = 3 * shard_len * top_count // (2 * experts)
    piece_ff = expert_down.shape[1]
    pieces_dev = expert_up.shape[0]
    split = FF // piece_ff
    head_dim = width // HEADS
    head_width = width // n_seq
    heads_dev = HEADS // n_seq
    owned = qkv_weight.shape[0]
    block = min(512, slot_len)
    length = lax.dynamic_slice_in_dim(lengths, me_f, 1)
    valid_total = jnp.sum(lengths).astype(F32).reshape(1)
    positions = me_s * shard_len + jnp.arange(shard_len, dtype=jnp.int32)
    row_valid = (positions < length[0]).astype(F32)
    local_routes = routes[0]
    push_all = functools.partial(push, n_seq=n_seq, n_fsdp=n_fsdp, scope="all")
    push_seq = functools.partial(push, n_seq=n_seq, n_fsdp=n_fsdp, scope="seq")

    masked_low = jnp.where(row_valid[:, None] > 0, cotangent[0], jnp.zeros((), BF))
    own_small = jnp.concatenate(
        [
            jnp.pad(norm_gains, ((0, 4), (0, 128 - owned))),
            local_routes.T.astype(BF),
            rows_of(router_weight.reshape(-1), 16),
        ]
    )
    small, gains, slot_tokens, qkv_local, cot_all, to_places, to_rows, counts = first_gather(
        own_small,
        tokens[0],
        qkv_weight,
        masked_low,
        lengths,
        n_seq,
        n_fsdp,
        pieces_dev,
        split,
        capacity,
        top_count,
        experts,
        collective_id=0,
    )
    slot_tokens = slot_tokens.reshape(slot_len, width)
    qkv_local = qkv_local.reshape(width, 3 * head_width)
    router = small[:, 8 + top_count :].reshape(n_dev, -1)[:, : owned * experts]
    router = router.reshape(width, experts)
    proj_later = lax.optimization_barrier((proj_weight, slot_tokens))[0]
    proj_rows = lax.all_gather(proj_later, "fsdp", axis=0, tiled=True)

    def exchange(rows):
        return lax.all_to_all(rows, "seq", split_axis=0, concat_axis=0, tiled=True)

    normed_one, raw, totals = front(slot_tokens, gains, qkv_local, n_seq, collective_id=1)

    masked_later = lax.optimization_barrier((masked_low, raw))[0]
    plane_masked = lax.all_gather(masked_later, "fsdp", axis=0)

    def rms(values):
        return lax.rsqrt(jnp.mean(values * values, axis=-1, keepdims=True) + epsilon)

    own_gains = lax.dynamic_slice_in_dim(gains, me_s * head_width, head_width, 1)
    cosine, sine = rope_tables(jnp.arange(slot_len, dtype=jnp.int32), head_dim)
    attended, query, key, value = attend(
        raw, totals, own_gains, cosine, sine, length, block, width
    )

    resid_in = tokens[0].astype(F32)
    resid_mid = resid_in + product_reduced(attended, proj_rows, 0, n_seq, collective_id=8)
    mid_rms = rms(resid_mid)
    normed_two = (resid_mid * mid_rms * gains[3]).astype(BF)
    router_probs = jax.nn.softmax(jnp.dot(normed_two, router, preferred_element_type=F32), axis=-1)

    own_hot = places(local_routes, jnp.arange(experts, dtype=jnp.int32), capacity)
    gate_slot = jnp.sum(own_hot * router_probs[:, :, None], axis=0)
    gate_send = jnp.broadcast_to(gate_slot[:, None], (experts, split, capacity))
    gate_send = gate_send.reshape(n_dev, pieces_dev, capacity)
    gate_send = jnp.pad(gate_send, ((0, 0), (0, -pieces_dev % 8), (0, 128 - capacity)))
    cot_all, gate_columns, outs, *experts_forward = dispatch_rows(
        normed_two,
        to_places,
        gate_send,
        plane_masked,
        cot_all,
        expert_up,
        expert_down,
        n_seq,
        n_fsdp,
        capacity,
        collective_id=6,
    )
    outs_back = exchange(outs)
    backs, gate_backs = [], []
    up_grad = down_grad = None
    for piece in range(pieces_dev):
        rows, hidden, activation, piece_out = experts_forward[piece::pieces_dev]
        rows = rows.reshape(-1, width)
        hidden_grad, out_grad, gate_back = expert_backward(
            cot_all, gate_columns[piece], piece_out, hidden, expert_down, piece
        )
        gate_backs.append(gate_back[0].reshape(n_dev, capacity))
        backs.append(hidden_grad.reshape(2, n_seq, n_fsdp, capacity, piece_ff))
        down_grad = weight_grad(activation, out_grad[None], down_grad, piece, pieces_dev)
        up_grad = weight_grad(rows, hidden_grad, up_grad, piece, pieces_dev)
    back_send = jnp.stack(gate_backs, axis=1).reshape(n_dev, pieces_dev * capacity)
    gate_pad = -pieces_dev * capacity % 1024
    back_send = jnp.pad(back_send, ((0, 0), (0, gate_pad))).reshape(n_dev, -1, 128)
    backs, outs_back, up_grad, down_grad = lax.optimization_barrier(
        (backs, outs_back, up_grad, down_grad)
    )
    backs, outs_back, up_grad, down_grad = lax.optimization_barrier(
        (backs, outs_back, up_grad, down_grad)
    )
    normed_two_grad, back_recv, outs_sums = return_rows(
        backs, expert_up, to_rows, back_send, outs_back, n_seq, n_fsdp, collective_id=7
    )

    fraction = counts[0] / (top_count * valid_total)
    back_recv = back_recv.reshape(n_dev, -1)
    slot_gates_grad = back_recv[:, : pieces_dev * capacity].reshape(experts, split, capacity).sum(axis=1)
    probs_grad = (
        jnp.sum(own_hot * slot_gates_grad[None], axis=2)
        + (experts * fraction / valid_total)[None, :] * row_valid[:, None]
    )
    logits_grad = router_probs * (
        probs_grad - jnp.sum(router_probs * probs_grad, axis=-1, keepdims=True)
    )
    router_term = lax.dot_general(
        logits_grad, normed_two.astype(F32), (((0,), (0,)), ((), ())), precision=lax.Precision.HIGHEST
    )
    normed_two_grad = normed_two_grad + lax.dot_general(
        logits_grad, router.astype(F32), (((1,), (1,)), ((), ())), precision=lax.Precision.HIGHEST
    )

    def rms_back(values, scale, gain, grad):
        weighted = gain * grad
        mean = jnp.mean(weighted * values, axis=-1, keepdims=True)
        return scale * weighted - values * (scale * scale * scale) * mean, jnp.sum(
            grad * values * scale, axis=0
        )

    mid_part, gain_three = rms_back(resid_mid, mid_rms, gains[3], normed_two_grad)
    mid_grad = masked_low.astype(F32) + mid_part
    branch_grad = mid_grad.astype(BF)
    outs_parts = lax.all_to_all(outs_sums, "fsdp", split_axis=0, concat_axis=0, tiled=True)
    slot_branch, router_parts = gather_seq(
        branch_grad, router_term, n_seq, n_fsdp, collective_id=9
    )
    slot_branch = slot_branch.reshape(slot_len, width)
    heads_grad = dot(slot_branch, proj_rows, 1, 1).astype(BF)
    query_in, key_in, value_grad, dots, heads_gain = attend_back(
        query,
        key,
        value,
        heads_grad,
        raw,
        totals,
        own_gains,
        cosine,
        sine,
        length,
        block,
        width,
    )
    raw_grad, router_parts = raw_back(
        query_in,
        key_in,
        value_grad,
        raw,
        totals,
        own_gains,
        dots,
        router_parts,
        n_seq,
        n_fsdp,
        width,
        collective_id=4,
    )
    raw_grad, outs_parts = lax.optimization_barrier((raw_grad, outs_parts))

    prob_part = jnp.sum(router_probs * row_valid[:, None], axis=0)
    prob_row = jnp.tile(jnp.pad(prob_part, (0, head_width - experts)), n_seq)
    terms = jnp.pad(jnp.stack([gain_three, prob_row]), ((1, 5), (0, 0)))
    heads_terms = jnp.pad(heads_gain[:2], ((3, 3), (0, 0)))
    input_grad, qkv_grad, last, layer_out = last_reduce(
        raw_grad,
        qkv_local,
        normed_one,
        tokens[0],
        mid_grad,
        gains,
        terms,
        heads_terms,
        resid_mid,
        outs_parts,
        n_seq,
        n_fsdp,
        collective_id=10,
    )
    input_grad = input_grad[None]
    layer_out = layer_out[None]

    proj_part = dot(attended, slot_branch, 0, 0).astype(BF)
    proj_grad = lax.psum_scatter(proj_part, "fsdp", scatter_dimension=0, tiled=True).astype(F32)

    router_grad = lax.dynamic_slice_in_dim(router_parts, me_f * owned, owned, 1).T
    prob_total = last[2, :experts]
    last = lax.dynamic_slice_in_dim(last, me_f * owned, owned, 1)
    gains_grad = jnp.stack([last[0], last[3], last[4], last[1]])
    loss_value = (experts * jnp.sum(fraction * prob_total / valid_total)).reshape(1)
    return (
        layer_out,
        input_grad,
        gains_grad,
        qkv_grad,
        proj_grad,
        router_grad,
        up_grad,
        down_grad,
        loss_value,
    )


def solution(mesh):
    rows = P(("seq", "fsdp"), None)
    return jax.shard_map(
        local,
        mesh=mesh,
        in_specs=(
            P("fsdp", "seq", None),
            P("fsdp", "seq", None),
            P(),
            P("fsdp", "seq", None),
            P(None, ("seq", "fsdp")),
            rows,
            rows,
            rows,
            P(("seq", "fsdp"), None, None),
            P(("seq", "fsdp"), None, None),
        ),
        out_specs=(
            P("fsdp", "seq", None),
            P("fsdp", "seq", None),
            P(None, ("seq", "fsdp")),
            rows,
            rows,
            rows,
            P(("seq", "fsdp"), None, None),
            P(("seq", "fsdp"), None, None),
            P(),
        ),
        check_vma=False,
    )
```

```python
import functools

import jax
import jax.numpy as jnp
from jax import lax
from jax.experimental import pallas as pl
from jax.experimental.pallas import tpu as pltpu
from jax.sharding import PartitionSpec as P

HEADS = 16
FF = 1024

epsilon = 1e-06
rope_base = 10000.0
MESH = pl.DeviceIdType.MESH
BF = jnp.bfloat16
F32 = jnp.float32


def dot(a, b, ca, cb):
    return lax.dot_general(a, b, (((ca,), (cb,)), ((), ())), preferred_element_type=F32)


def push_kernel(n_seq, n_fsdp, scope, gather, src, dst, send_sem, recv_sem, own_sem):
    me_s, me_f = lax.axis_index("seq"), lax.axis_index("fsdp")
    n = n_seq * n_fsdp if scope == "all" else n_seq
    me = me_s * n_fsdp + me_f if scope == "all" else me_s

    def where(index):
        if scope == "all":
            return (index // n_fsdp, index % n_fsdp)
        return (index, me_f)

    barrier = pltpu.get_barrier_semaphore()

    def greet(i, carry):
        pl.semaphore_signal(barrier, inc=1, device_id=where((me + i) % n), device_id_type=MESH)
        return carry

    lax.fori_loop(1, n, greet, 0)
    own = pltpu.make_async_copy(src if gather else src.at[me], dst.at[me], own_sem)
    own.start()
    pl.semaphore_wait(barrier, n - 1)

    def copy_to(other):
        return pltpu.make_async_remote_copy(
            src_ref=src if gather else src.at[other],
            dst_ref=dst.at[me],
            send_sem=send_sem.at[other],
            recv_sem=recv_sem.at[me],
            device_id=where(other),
            device_id_type=MESH,
        )

    def copy_from(other):
        return pltpu.make_async_remote_copy(
            src_ref=src if gather else src.at[other],
            dst_ref=dst.at[other],
            send_sem=send_sem.at[other],
            recv_sem=recv_sem.at[other],
            device_id=where(other),
            device_id_type=MESH,
        )

    def send(i, carry):
        copy_to((me + i) % n).start()
        return carry

    lax.fori_loop(1, n, send, 0)

    def finish(i, carry):
        other = (me + i) % n
        copy_from(other).wait_recv()
        copy_to(other).wait_send()
        return carry

    lax.fori_loop(1, n, finish, 0)
    own.wait()


def push(block, n_seq, n_fsdp, scope, gather, collective_id):
    n = n_seq * n_fsdp if scope == "all" else n_seq
    shape = (n,) + (block.shape if gather else block.shape[1:])
    return pl.pallas_call(
        functools.partial(push_kernel, n_seq, n_fsdp, scope, gather),
        out_shape=jax.ShapeDtypeStruct(shape, block.dtype),
        in_specs=[pl.BlockSpec(memory_space=pltpu.VMEM)],
        out_specs=pl.BlockSpec(memory_space=pltpu.VMEM),
        scratch_shapes=[
            pltpu.SemaphoreType.DMA((n,)),
            pltpu.SemaphoreType.DMA((n,)),
            pltpu.SemaphoreType.DMA,
        ],
        compiler_params=pltpu.CompilerParams(collective_id=collective_id, has_side_effects=True),
        name="push_" + scope,
    )(block)


def rows_of(flat, multiple):
    size = flat.shape[0]
    whole = -(-size // (multiple * 128)) * multiple * 128
    return jnp.pad(flat, (0, whole - size)).reshape(-1, 128)


def remote(src, dst, send_sem, recv_sem, device):
    return pltpu.make_async_remote_copy(
        src_ref=src,
        dst_ref=dst,
        send_sem=send_sem,
        recv_sem=recv_sem,
        device_id=device,
        device_id_type=MESH,
    )


def greet_all(n_seq, n_fsdp):
    me_s, me_f = lax.axis_index("seq"), lax.axis_index("fsdp")
    n = n_seq * n_fsdp
    me = me_s * n_fsdp + me_f
    barrier = pltpu.get_barrier_semaphore()

    def greet(i, carry):
        other = (me + i) % n
        pl.semaphore_signal(
            barrier, inc=1, device_id=(other // n_fsdp, other % n_fsdp), device_id_type=MESH
        )
        return carry

    lax.fori_loop(1, n, greet, 0)
    pl.semaphore_wait(barrier, n - 1)


def greet_lines(n_seq, n_fsdp):
    me_s, me_f = lax.axis_index("seq"), lax.axis_index("fsdp")
    barrier = pltpu.get_barrier_semaphore()
    for i in range(1, n_seq):
        pl.semaphore_signal(
            barrier, inc=1, device_id=((me_s + i) % n_seq, me_f), device_id_type=MESH
        )
    for i in range(1, n_fsdp):
        pl.semaphore_signal(
            barrier, inc=1, device_id=(me_s, (me_f + i) % n_fsdp), device_id_type=MESH
        )
    pl.semaphore_wait(barrier, n_seq + n_fsdp - 2)


def loading(body, greet, inputs):
    def kernel(*refs):
        held, sems = refs[-1 - inputs : -1], refs[-1]
        copies = [
            pltpu.make_async_copy(refs[i], held[i], sems.at[i]) for i in range(inputs)
        ]
        for copy in copies:
            copy.start()
        greet()
        for copy in copies:
            copy.wait()
        body(*held, *refs[inputs : -1 - inputs])

    return kernel


def load_scratch(arrays):
    held = [pltpu.VMEM(array.shape, array.dtype) for array in arrays]
    return held + [pltpu.SemaphoreType.DMA((len(arrays),))]


class Exchange:
    def __init__(self, n_seq, n_fsdp, src, dst, sems):
        self.n, self.n_fsdp, self.src, self.dst = n_seq * n_fsdp, n_fsdp, src, dst
        self.send_sem, self.recv_sem, self.own_sem = sems
        self.me = lax.axis_index("seq") * n_fsdp + lax.axis_index("fsdp")

    def copy(self, i, place):
        other = (self.me + i) % self.n
        return remote(
            self.src.at[other],
            self.dst.at[self.me if place is None else place],
            self.send_sem.at[i],
            self.recv_sem.at[self.me if place is None else place],
            (other // self.n_fsdp, other % self.n_fsdp),
        )

    def own(self):
        return pltpu.make_async_copy(
            self.src.at[self.me], self.dst.at[self.me], self.own_sem
        )

    def start(self):
        self.own().start()

        def one(i, carry):
            self.copy(i, None).start()
            return carry

        lax.fori_loop(1, self.n, one, 0)

    def finish(self):
        def one(i, carry):
            self.copy(i, None).wait_send()
            self.copy(i, (self.me + i) % self.n).wait_recv()
            return carry

        lax.fori_loop(1, self.n, one, 0)
        self.own().wait()


def exchange_sems(n):
    return [
        pltpu.SemaphoreType.DMA((n,)),
        pltpu.SemaphoreType.DMA((n,)),
        pltpu.SemaphoreType.DMA,
    ]


def line_step(n_fsdp, step, arrived, forward):
    me_f = lax.axis_index("fsdp")

    @pl.when(me_f - step >= 0)
    def _():
        arrived(me_f - step)

        @pl.when(me_f + 1 < n_fsdp)
        def _():
            forward(me_f - step, 0, me_f + 1)

    @pl.when(me_f + step < n_fsdp)
    def _():
        arrived(me_f + step)

        @pl.when(me_f >= 1)
        def _():
            forward(me_f + step, 1, me_f - 1)


def line_sent(n_fsdp, step, sent):
    me_f = lax.axis_index("fsdp")

    @pl.when((me_f - step >= 0) & (me_f + 1 < n_fsdp))
    def _():
        sent(me_f - step, 0, me_f + 1)

    @pl.when((me_f + step < n_fsdp) & (me_f >= 1))
    def _():
        sent(me_f + step, 1, me_f - 1)


def flipped(index, bit):
    return index + bit * (1 - 2 * ((index // bit) % 2))


class SeqGather:
    def __init__(self, order, own, block, send_sem, recv_sem):
        self.order, self.own, self.block = order, own, block
        self.send_sem, self.recv_sem = send_sem, recv_sem
        self.me_s, self.me_f = lax.axis_index("seq"), lax.axis_index("fsdp")

    def held(self, stage):
        indices = [self.me_s]
        for bit in self.order[:stage]:
            indices = indices + [flipped(i, bit) for i in indices]
        return indices

    def copies(self, stage):
        partner = flipped(self.me_s, self.order[stage])
        result = []
        for count, index in enumerate(self.held(stage)):
            src = self.own if count == 0 else self.block(index)
            sem = self.send_sem.at[(1 << stage) - 1 + count]
            result.append(
                remote(src, self.block(index), sem, self.recv_sem.at[index], (partner, self.me_f))
            )
        return result

    def start(self, stage):
        for copy in self.copies(stage):
            copy.start()

    def wait(self, stage):
        for index in self.held(stage):
            index = flipped(index, self.order[stage])
            remote(
                self.block(index),
                self.block(index),
                self.send_sem.at[0],
                self.recv_sem.at[index],
                (self.me_s, self.me_f),
            ).wait_recv()

    def sent(self):
        for stage in range(len(self.order)):
            for copy in self.copies(stage):
                copy.wait_send()


def gather_orders(n_seq):
    bits = [1 << b for b in range(n_seq.bit_length() - 1)]
    return bits[1:] + bits[:1], bits[:0:-1] + bits[:1]


def block_places(routes, ids, capacity):
    count = routes.shape[1]
    match = jnp.zeros((ids.shape[0], count), F32)
    for k in range(routes.shape[0]):
        match = match + (routes[k : k + 1, :] == ids).astype(F32)
    row = lax.broadcasted_iota(jnp.int32, (count, count), 0)
    column = lax.broadcasted_iota(jnp.int32, (count, count), 1)
    rank = dot(match.astype(BF), (row < column).astype(BF), 1, 0)
    place = lax.broadcasted_iota(jnp.int32, (ids.shape[0], capacity, count), 1).astype(F32)
    hot = match[:, None, :] * (rank[:, None, :] == place).astype(F32)
    return hot.reshape(ids.shape[0] * capacity, count)


def first_kernel(
    n_seq,
    n_fsdp,
    pieces,
    split,
    capacity,
    owned,
    top,
    small,
    tokens,
    qkv,
    masked,
    lengths,
    small_all,
    gains,
    slot,
    qkv_all,
    masked_all,
    to_places,
    to_rows,
    counts,
    send,
    own_sem,
    small_send,
    small_recv,
    qkv_send,
    qkv_recv,
    line_send,
    line_recv,
    token_send,
    token_recv,
    row_send,
    row_recv,
    row_own,
):
    me_s, me_f = lax.axis_index("seq"), lax.axis_index("fsdp")
    n = n_seq * n_fsdp
    me = me_s * n_fsdp + me_f
    head_width = qkv_all.shape[3] // 3
    width = head_width * n_seq
    half = tokens.shape[0] // 2
    orders = gather_orders(n_seq)
    stages = len(orders[0])

    def columns(owner, part):
        start = pl.multiple_of(part * width + owner * head_width, 128)
        return qkv.at[:, pl.ds(start, head_width)]

    def column_place(source, part):
        return qkv_all.at[source, me_f, :, pl.ds(part * head_width, head_width)]

    own = [
        pltpu.make_async_copy(small, small_all.at[me], own_sem.at[0]),
        pltpu.make_async_copy(tokens, slot.at[me_s], own_sem.at[1]),
    ] + [
        pltpu.make_async_copy(columns(me_s, part), column_place(me_s, part), own_sem.at[2 + part])
        for part in range(3)
    ]
    for copy in own:
        copy.start()

    def small_copy(i):
        other = (me + i) % n
        return remote(
            small,
            small_all.at[me],
            small_send.at[i],
            small_recv.at[me],
            (other // n_fsdp, other % n_fsdp),
        )

    def small_arrived(other):
        return remote(
            small,
            small_all.at[other],
            small_send.at[0],
            small_recv.at[other],
            (other // n_fsdp, other % n_fsdp),
        )

    def small_start(i, carry):
        small_copy(i).start()
        return carry

    lax.fori_loop(1, n, small_start, 0)

    def column_copy(i, part):
        other = (me_s + i) % n_seq
        return remote(
            columns(other, part),
            column_place(me_s, part),
            qkv_send.at[i, part],
            qkv_recv.at[me_s, part],
            (other, me_f),
        )

    for i in range(1, n_seq):
        for part in range(3):
            column_copy(i, part).start()

    flows = []
    for side in range(2):
        rows = pl.ds(side * half, half)
        flows.append(
            SeqGather(
                orders[side],
                tokens.at[rows],
                lambda index, rows=rows: slot.at[index, rows],
                token_send.at[side],
                token_recv.at[side],
            )
        )

    def point(stage):
        for flow in flows:
            if 0 < stage <= stages:
                flow.wait(stage - 1)
            if stage < stages:
                flow.start(stage)

    point(0)
    for copy in own:
        copy.wait()

    piece = lax.broadcasted_iota(jnp.int32, (n_seq * pieces, 1), 0)
    piece = ((piece // pieces) * n_fsdp + me_f) * pieces + piece % pieces
    ids = piece // split

    def row_copy(i, place):
        other = (me_s + i) % n_seq
        return remote(
            send.at[other], masked_all.at[place, :, me_f], row_send.at[i], row_recv.at[place], (other, me_f)
        )

    def own_row():
        return pltpu.make_async_copy(send.at[me_s], masked_all.at[me_s, :, me_f], row_own)

    def table(block):
        routes = small_all[me_s * n_fsdp + block, 8 : 8 + top, :].astype(F32).astype(jnp.int32)
        hot = block_places(routes, ids, capacity)
        to_places[block] = hot.astype(BF)
        to_rows[block] = hot.T.astype(BF)

    def scatter():
        def some(lanes):
            picked = dot(to_places[me_f], masked[:, lanes], 1, 0).astype(BF)
            send[:, :, :, lanes] = picked.reshape(n_seq, pieces, capacity, -1)

        chunked(width, 512, some)
        for i in range(1, n_seq):
            row_copy(i, me_s).start()
        own_row().start()

    def line_copy(part, step, block, way, to):
        place = qkv_all.at[part, block]
        return remote(
            place, place, line_send.at[part, way, step], line_recv.at[part, block], (me_s, to)
        )

    def line_first(part):
        @pl.when(me_f + 1 < n_fsdp)
        def _():
            line_copy(part, 0, me_f, 0, me_f + 1).start()

        @pl.when(me_f >= 1)
        def _():
            line_copy(part, 0, me_f, 1, me_f - 1).start()

    def column_arrived(i, carry):
        source = (me_s + i) % n_seq

        @pl.when(i > 0)
        def _():
            for part in range(3):
                remote(
                    columns(source, part),
                    column_place(source, part),
                    qkv_send.at[i, part],
                    qkv_recv.at[source, part],
                    (source, me_f),
                ).wait_recv()

        line_first(source)
        return carry

    lax.fori_loop(0, n_seq, column_arrived, 0)

    def column_step(step):
        def column_next(i, carry):
            part = (me_s + i) % n_seq
            line_step(
                n_fsdp,
                step,
                lambda block: line_copy(part, 0, block, 0, me_f).wait_recv(),
                lambda block, way, to: line_copy(part, step, block, way, to).start(),
            )
            return carry

        lax.fori_loop(0, n_seq, column_next, 0)

    point(1)
    table(me_f)
    for stage in range(2, stages + 1):
        point(stage)
    scatter()
    column_step(1)
    for i in range(1, n_fsdp):
        block = (me_f + i) % n_fsdp
        small_arrived(me_s * n_fsdp + block).wait_recv()
        table(block)
    for flow in flows:
        flow.sent()

    def small_wait(i, carry):
        other = (me + i) % n
        small_copy(i).wait_send()

        @pl.when(other // n_fsdp != me_s)
        def _():
            small_arrived(other).wait_recv()

        return carry

    lax.fori_loop(1, n, small_wait, 0)

    lane = lax.broadcasted_iota(jnp.int32, (8, 128), 1)
    each = 128 // owned
    for j in range(width // 128):
        total = jnp.zeros((8, 128), F32)
        for k in range(each):
            some = jnp.where(lane < owned, small_all[j * each + k, :8, :].astype(F32), 0.0)
            total = total + (pltpu.roll(some, k * owned, 1) if k else some)
        gains[:, j * 128 : (j + 1) * 128] = total

    all_ids = lax.broadcasted_iota(jnp.int32, (counts.shape[1], 1), 0)
    position = lax.broadcasted_iota(jnp.int32, (1, tokens.shape[0]), 1)

    def seen(device, sums):
        routes = small_all[device, 8 : 8 + top, :].astype(F32).astype(jnp.int32)
        match = jnp.zeros(sums.shape, F32)
        for k in range(top):
            match = match + (routes[k : k + 1, :] == all_ids).astype(F32)
        first = (device // n_fsdp) * tokens.shape[0]
        live = (position + first < lengths[device % n_fsdp]).astype(F32)
        return sums + match * live

    sums = jnp.zeros((counts.shape[1], tokens.shape[0]), F32)
    sums = lax.fori_loop(0, n, seen, sums)
    counts[...] = jnp.broadcast_to(jnp.sum(sums.T, axis=0, keepdims=True), counts.shape)

    for step in range(2, n_fsdp):
        column_step(step)

    def column_sent(i, carry):
        for part in range(3):
            column_copy(i, part).wait_send()
        return carry

    lax.fori_loop(1, n_seq, column_sent, 0)

    def line_done(part, carry):
        for step in range(n_fsdp):
            line_sent(
                n_fsdp,
                step,
                lambda block, way, to: line_copy(part, step, block, way, to).wait_send(),
            )
        return carry

    lax.fori_loop(0, n_seq, line_done, 0)
    own_row().wait()
    for i in range(1, n_seq):
        row_copy(i, me_s).wait_send()
        row_copy(i, (me_s + i) % n_seq).wait_recv()


def first_gather(
    small,
    tokens,
    qkv,
    masked,
    lengths,
    n_seq,
    n_fsdp,
    pieces,
    split,
    capacity,
    top,
    experts,
    collective_id,
):
    owned = qkv.shape[0]
    rows, width = tokens.shape
    head_width = width // n_seq
    n = n_seq * n_fsdp
    places_all = n_seq * pieces * capacity
    vmem = pl.BlockSpec(memory_space=pltpu.VMEM)
    any_space = pl.BlockSpec(memory_space=pl.ANY)
    dma = pltpu.SemaphoreType.DMA
    return pl.pallas_call(
        loading(
            functools.partial(first_kernel, n_seq, n_fsdp, pieces, split, capacity, owned, top),
            functools.partial(greet_all, n_seq, n_fsdp),
            4,
        ),
        out_shape=[
            jax.ShapeDtypeStruct((n,) + small.shape, BF),
            jax.ShapeDtypeStruct((8, width), F32),
            jax.ShapeDtypeStruct((n_seq,) + tokens.shape, BF),
            jax.ShapeDtypeStruct((n_seq, n_fsdp, owned, 3 * head_width), BF),
            jax.ShapeDtypeStruct((n_seq, pieces, n_fsdp, capacity, width), BF),
            jax.ShapeDtypeStruct((n_fsdp, places_all, rows), BF),
            jax.ShapeDtypeStruct((n_fsdp, rows, places_all), BF),
            jax.ShapeDtypeStruct((8, experts), F32),
        ],
        in_specs=[pl.BlockSpec(memory_space=pltpu.HBM)] * 4 + [pl.BlockSpec(memory_space=pltpu.SMEM)],
        out_specs=[vmem, vmem, any_space, any_space, any_space, vmem, vmem, vmem],
        scratch_shapes=[
            pltpu.VMEM((n_seq, pieces, capacity, width), BF),
            dma((5,)),
            dma((n,)),
            dma((n,)),
            dma((n_seq, 3)),
            dma((n_seq, 3)),
            dma((n_seq, 2, n_fsdp)),
            dma((n_seq, n_fsdp)),
            dma((2, n_seq - 1)),
            dma((2, n_seq)),
            dma((n_seq,)),
            dma((n_seq,)),
            dma,
        ]
        + load_scratch([small, tokens, qkv, masked]),
        compiler_params=pltpu.CompilerParams(
            collective_id=collective_id, has_side_effects=True, vmem_limit_bytes=62 << 20
        ),
        name="first_gather",
    )(small, tokens, qkv, masked, lengths)


def greet_seq(n_seq):
    me_s, me_f = lax.axis_index("seq"), lax.axis_index("fsdp")
    barrier = pltpu.get_barrier_semaphore()
    for i in range(1, n_seq):
        pl.semaphore_signal(
            barrier, inc=1, device_id=((me_s + i) % n_seq, me_f), device_id_type=MESH
        )
    pl.semaphore_wait(barrier, n_seq - 1)


class TermSum:
    def __init__(
        self, n_seq, n_fsdp, terms, seq_terms, fsdp_terms, seq_send, seq_recv, fsdp_send, fsdp_recv
    ):
        self.n_seq, self.n_fsdp, self.terms = n_seq, n_fsdp, terms
        self.seq_terms, self.fsdp_terms = seq_terms, fsdp_terms
        self.seq_send, self.seq_recv = seq_send, seq_recv
        self.fsdp_send, self.fsdp_recv = fsdp_send, fsdp_recv
        self.me_s, self.me_f = lax.axis_index("seq"), lax.axis_index("fsdp")

    def part(self, owner):
        columns = self.seq_terms.shape[2]
        return self.terms.at[:, pl.ds(pl.multiple_of(owner * columns, 128), columns)]

    def seq_copy(self, i, place):
        other = (self.me_s + i) % self.n_seq
        return remote(
            self.part(other),
            self.seq_terms.at[place],
            self.seq_send.at[i],
            self.seq_recv.at[place],
            (other, self.me_f),
        )

    def fsdp_copy(self, i, place):
        other = (self.me_f + i) % self.n_fsdp
        return remote(
            self.seq_terms.at[self.me_s],
            self.fsdp_terms.at[place],
            self.fsdp_send.at[i],
            self.fsdp_recv.at[place],
            (self.me_s, other),
        )

    def start_seq(self):
        for i in range(1, self.n_seq):
            self.seq_copy(i, self.me_s).start()

    def over_seq(self):
        result = self.part(self.me_s)[...]
        for i in range(1, self.n_seq):
            place = (self.me_s + i) % self.n_seq
            self.seq_copy(i, place).wait_recv()
            result = result + self.seq_terms[place]
        for i in range(1, self.n_seq):
            self.seq_copy(i, self.me_s).wait_send()
        return result

    def start_fsdp(self, more):
        self.seq_terms[self.me_s] = more + (self.over_seq() if self.terms is not None else 0.0)
        for i in range(1, self.n_fsdp):
            self.fsdp_copy(i, self.me_f).start()

    def finish(self):
        result = self.seq_terms[self.me_s]
        for i in range(1, self.n_fsdp):
            place = (self.me_f + i) % self.n_fsdp
            self.fsdp_copy(i, place).wait_recv()
            result = result + self.fsdp_terms[place]
        for i in range(1, self.n_fsdp):
            self.fsdp_copy(i, self.me_f).wait_send()
        return result


def term_scratch(n_seq, n_fsdp, shape):
    dma = pltpu.SemaphoreType.DMA
    return [
        pltpu.VMEM((n_seq,) + shape, F32),
        pltpu.VMEM((n_fsdp,) + shape, F32),
        dma((n_seq,)),
        dma((n_seq,)),
        dma((n_fsdp,)),
        dma((n_fsdp,)),
    ]


def gather_kernel(n_seq, n_fsdp, x, terms, out, total, own_sem, send_sem, recv_sem, *scratch):
    me_s = lax.axis_index("seq")
    half = x.shape[0] // 2
    own = pltpu.make_async_copy(x, out.at[me_s], own_sem)
    own.start()
    term_sum = TermSum(n_seq, n_fsdp, terms, scratch[0], None, *scratch[1:], None, None)
    greet_seq(n_seq)
    flows = []
    for side, order in enumerate(gather_orders(n_seq)):
        rows = pl.ds(side * half, half)
        flows.append(
            SeqGather(
                order,
                x.at[rows],
                lambda index, rows=rows: out.at[index, rows],
                send_sem.at[side],
                recv_sem.at[side],
            )
        )
    for stage in range(len(flows[0].order)):
        for flow in flows:
            flow.start(stage)
        if stage == 0:
            term_sum.start_seq()
        if stage == 1:
            total[...] = term_sum.over_seq()
        for flow in flows:
            flow.wait(stage)
    for flow in flows:
        flow.sent()
    own.wait()


def gather_seq(x, terms, n_seq, n_fsdp, collective_id):
    vmem = pl.BlockSpec(memory_space=pltpu.VMEM)
    dma = pltpu.SemaphoreType.DMA
    part = (terms.shape[0], terms.shape[1] // n_seq)
    return pl.pallas_call(
        functools.partial(gather_kernel, n_seq, n_fsdp),
        out_shape=[
            jax.ShapeDtypeStruct((n_seq,) + x.shape, x.dtype),
            jax.ShapeDtypeStruct(part, terms.dtype),
        ],
        in_specs=[vmem] * 2,
        out_specs=[vmem] * 2,
        scratch_shapes=[
            dma,
            dma((2, n_seq - 1)),
            dma((2, n_seq)),
            pltpu.VMEM((n_seq,) + part, F32),
            dma((n_seq,)),
            dma((n_seq,)),
        ],
        compiler_params=pltpu.CompilerParams(collective_id=collective_id, has_side_effects=True),
        cost_estimate=pl.CostEstimate(flops=0, bytes_accessed=1 << 26, transcendentals=0),
        name="gather_seq",
    )(x, terms)


class SeqReduce:
    def __init__(self, n_seq, a, w, w_dim, sums, got, send_sem, recv_sem):
        self.a, self.w, self.w_dim, self.sums, self.got = a, w, w_dim, sums, got
        self.send_sem, self.recv_sem = send_sem, recv_sem
        self.me_s, self.me_f = lax.axis_index("seq"), lax.axis_index("fsdp")
        self.orders = [order[-1:] + order[-2::-1] for order in gather_orders(n_seq)]
        self.stages = len(self.orders[0])
        self.half = sums.shape[1] // 2
        self.width = sums.shape[2]

    def combined(self, index, bits):
        indices = [index]
        for bit in bits:
            indices = indices + [flipped(i, bit) for i in indices]
        return indices

    def product(self, index):
        def some(columns):
            w = self.w[:, columns] if self.w_dim == 0 else self.w[columns, :]
            self.sums[index, :, columns] = dot(self.a[index], w, 1, self.w_dim).astype(BF)

        chunked(self.width, 512, some)

    def copy(self, stage, side, count, index):
        order = self.orders[side]
        slot = sum(1 << (self.stages - 1 - s) for s in range(stage)) + count
        rows = pl.ds(side * self.half, self.half)
        return remote(
            self.sums.at[index, rows],
            self.got.at[slot, rows],
            self.send_sem.at[side, slot],
            self.recv_sem.at[side, slot],
            (flipped(self.me_s, order[stage]), self.me_f),
        )

    def leaving(self, stage, side):
        order = self.orders[side]
        return self.combined(flipped(self.me_s, order[stage]), order[stage + 1 :])

    def start(self, stage):
        if stage == 0:
            for count, index in enumerate(self.leaving(0, 0)):
                self.product(index)
                for side in range(2):
                    self.copy(0, side, self.twin(count) if side == 1 else count, index).start()
            for index in self.combined(self.me_s, self.orders[0][1:]):
                self.product(index)
        else:
            for side in range(2):
                for count, index in enumerate(self.leaving(stage, side)):
                    self.copy(stage, side, count, index).start()

    def twin(self, count):
        first, second = self.orders[0][1:], self.orders[1][1:]
        place = 0
        for position, bit in enumerate(first):
            if (count >> position) & 1:
                place += 1 << second.index(bit)
        return place

    def finish(self, stage, last=None):
        for side in range(2):
            order = self.orders[side]
            rows = pl.ds(side * self.half, self.half)
            for count, index in enumerate(self.combined(self.me_s, order[stage + 1 :])):
                copy = self.copy(stage, side, count, index)
                copy.wait_recv()
                slot = sum(1 << (self.stages - 1 - s) for s in range(stage)) + count

                def some(columns):
                    total = self.sums[index, rows, columns].astype(F32)
                    total = total + self.got[slot, rows, columns].astype(F32)
                    if last is None:
                        self.sums[index, rows, columns] = total.astype(BF)
                    else:
                        last[rows, columns] = total

                chunked(self.width, 1024, some)

    def events(self, last):
        def leave(count, index):
            self.product(index)
            for side in range(2):
                self.copy(0, side, self.twin(count) if side == 1 else count, index).start()

        result = [
            (1, functools.partial(leave, count, index))
            for count, index in enumerate(self.leaving(0, 0))
        ]
        for index in self.combined(self.me_s, self.orders[0][1:]):
            result.append((1, functools.partial(self.product, index)))
        result.append((1, functools.partial(self.finish, 0, last if self.stages == 1 else None)))
        for stage in range(1, self.stages):
            result.append((0, functools.partial(self.start, stage)))
            result.append(
                (7, functools.partial(self.finish, stage, last if stage == self.stages - 1 else None))
            )
        return result

    def sent(self):
        for stage in range(self.stages):
            for side in range(2):
                for count, index in enumerate(self.leaving(stage, side)):
                    self.copy(stage, side, count, index).wait_send()


def reduce_scratch(n_seq, rows, width):
    dma = pltpu.SemaphoreType.DMA
    return [
        pltpu.VMEM((n_seq, rows, width), BF),
        pltpu.VMEM((n_seq - 1, rows, width), BF),
        dma((2, n_seq - 1)),
        dma((2, n_seq - 1)),
    ]


def reduce_kernel(n_seq, w_dim, a, w, out, *scratch):
    reduce = SeqReduce(n_seq, a, w, w_dim, *scratch)
    for stage in range(reduce.stages):
        reduce.start(stage)
        reduce.finish(stage, out if stage == reduce.stages - 1 else None)
    reduce.sent()


def product_reduced(a, w, w_dim, n_seq, collective_id):
    rows = a.shape[0] // n_seq
    width = w.shape[1 - w_dim]
    a = a.reshape(n_seq, rows, -1)
    return pl.pallas_call(
        loading(
            functools.partial(reduce_kernel, n_seq, w_dim),
            functools.partial(greet_seq, n_seq),
            2,
        ),
        out_shape=jax.ShapeDtypeStruct((rows, width), F32),
        in_specs=[pl.BlockSpec(memory_space=pltpu.HBM)] * 2,
        out_specs=pl.BlockSpec(memory_space=pltpu.VMEM),
        scratch_shapes=reduce_scratch(n_seq, rows, width) + load_scratch([a, w]),
        compiler_params=pltpu.CompilerParams(
            collective_id=collective_id, has_side_effects=True, vmem_limit_bytes=62 << 20
        ),
        name="product_reduced",
    )(a, w)


def last_kernel(
    n_seq,
    n_fsdp,
    a,
    w,
    normed,
    x,
    mid,
    gains,
    terms_in,
    heads,
    resid,
    ready,
    input_out,
    qkv_out,
    total,
    layer_out,
    *scratch,
):
    up, down, done, got, up_send, up_recv, down_send, down_recv, done_send, done_recv = scratch[:10]
    one, part, terms, seq_terms, fsdp_terms, seq_send, seq_recv, fsdp_send, fsdp_recv = scratch[10:19]
    me_s, me_f = lax.axis_index("seq"), lax.axis_index("fsdp")
    head_width = a.shape[2] // 3
    width = n_seq * head_width
    greet_lines(n_seq, n_fsdp)
    reduce = SeqReduce(n_seq, a, w, 1, *scratch[19:])
    term_sum = TermSum(
        n_seq,
        n_fsdp,
        terms,
        seq_terms,
        fsdp_terms,
        seq_send,
        seq_recv,
        fsdp_send,
        fsdp_recv,
    )

    def input_rows():
        tile = 32
        terms[...] = terms_in[...]

        def some(i, carry):
            rows = pl.ds(pl.multiple_of(i * tile, tile), tile)
            values = x[rows, :].astype(F32)
            scale = lax.rsqrt(jnp.mean(values * values, axis=-1, keepdims=True) + epsilon)
            grad = one[rows, :]
            weighted = grad * gains[0:1, :]
            mean = jnp.mean(weighted * values, axis=-1, keepdims=True)
            result = scale * weighted - values * (scale * scale * scale * mean)
            input_out[rows, :] = (mid[rows, :] + result).astype(BF)
            terms[0:1, :] += jnp.sum(grad * values * scale, axis=0, keepdims=True)
            layer = resid[rows, :]
            for block in range(n_fsdp):
                layer = layer + ready[block, rows, :].astype(F32)
            layer_out[rows, :] = layer.astype(BF)
            return carry

        lax.fori_loop(0, x.shape[0] // tile, some, 0)
        term_sum.start_seq()

    def line_copy(src, way, s, block):
        buffer, send, recv = (up, up_send, up_recv) if way == 0 else (down, down_send, down_recv)
        to = me_f + 1 if way == 0 else me_f - 1
        place = buffer.at[block, s]
        return remote(
            place if src is None else src, place, send.at[block, s], recv.at[block, s], (me_s, to)
        )

    def done_copy(i):
        s = (me_s + i) % n_seq
        return remote(done.at[s], got.at[me_s], done_send.at[i], done_recv.at[me_s], (s, me_f))

    def stream(way, number):
        buffer = up if way == 0 else down
        behind = me_f if way == 0 else n_fsdp - 1 - me_f
        turn, i = number // n_seq, number % n_seq
        s = (me_s + i) % n_seq
        block = n_fsdp - 1 - turn if way == 0 else turn
        ahead = n_fsdp - 1 - behind
        on_time = (number >= 0) & (turn < ahead)
        finishes_up = (me_f == n_fsdp - 1) | ((n_fsdp - 1 > 2 * me_f) & (me_f > 0))

        @pl.when(on_time & (behind == 0))
        def _():
            line_copy(part.at[s, block], way, s, block).start()

        @pl.when(on_time & (behind > 0))
        def _():
            line_copy(None, way, s, block).wait_recv()
            total = buffer[block, s].astype(F32) + part[s, block].astype(F32)
            buffer[block, s] = total.astype(BF)
            line_copy(None, way, s, block).start()

        @pl.when((number >= 0) & (turn == ahead) & (behind > 0))
        def _():
            line_copy(None, way, s, me_f).wait_recv()
            done[s] = (done[s].astype(F32) + buffer[me_f, s].astype(F32)).astype(BF)

            @pl.when(finishes_up if way == 0 else jnp.logical_not(finishes_up))
            def _():
                @pl.when(i > 0)
                def _():
                    done_copy(i).start()

    lag = 2
    slots = n_seq * (n_fsdp - 1) + lag * (n_fsdp - 1)

    owned = part.shape[2]
    stripe = n_fsdp * owned

    def make(s):
        lanes = pl.ds(pl.multiple_of(s * stripe, 128), stripe)
        every = a[...].reshape(-1, a.shape[2])
        product = dot(normed[:, lanes], every, 0, 0).astype(BF)
        for block in range(n_fsdp):
            part[s, block] = product[block * owned : (block + 1) * owned]
        done[s] = part[s, me_f]

    def run(first, last):
        def slot(number, carry):
            @pl.when(number < n_seq)
            def _():
                make((me_s + number) % n_seq)

            stream(0, number - lag * me_f)
            stream(1, number - lag * (n_fsdp - 1 - me_f))
            return carry

        lax.fori_loop(first, last, slot, 0)

    reached = 0
    for number, event in enumerate(
        reduce.events(one)
        + [(0, input_rows), (3, functools.partial(term_sum.start_fsdp, heads[...]))]
    ):
        run(reached, min(slots, reached + event[0]))
        reached = min(slots, reached + event[0])
        event[1]()
    run(reached, slots)

    def place(s, rows):
        for third in range(3):
            columns = pl.ds(pl.multiple_of(third * width + s * head_width, 128), head_width)
            qkv_out[:, columns] = rows[:, third * head_width : (third + 1) * head_width].astype(F32)

    place(me_s, done[me_s])

    def arrived(i, carry):
        s = (me_s + i) % n_seq
        remote(done.at[s], got.at[s], done_send.at[i], done_recv.at[s], (s, me_f)).wait_recv()
        place(s, got[s])
        return carry

    lax.fori_loop(1, n_seq, arrived, 0)

    def all_sent(i, carry):
        s = (me_s + i) % n_seq

        @pl.when(i > 0)
        def _():
            done_copy(i).wait_send()

        for j in range(n_fsdp - 1):

            @pl.when(me_f + j < n_fsdp - 1)
            def _():
                line_copy(None, 0, s, n_fsdp - 1 - j).wait_send()

            @pl.when(j < me_f)
            def _():
                line_copy(None, 1, s, j).wait_send()

        return carry

    lax.fori_loop(0, n_seq, all_sent, 0)
    reduce.sent()
    total[...] = term_sum.finish()


def last_reduce(
    a, w, normed, x, mid, gains, terms, heads, resid, ready, n_seq, n_fsdp, collective_id
):
    rows, width = a.shape[0] // n_seq, w.shape[0]
    columns = a.shape[1]
    owned = width // (n_seq * n_fsdp)
    vmem = pl.BlockSpec(memory_space=pltpu.VMEM)
    dma = pltpu.SemaphoreType.DMA
    return pl.pallas_call(
        functools.partial(last_kernel, n_seq, n_fsdp),
        out_shape=[
            jax.ShapeDtypeStruct((rows, width), BF),
            jax.ShapeDtypeStruct((owned, n_seq * columns), F32),
            jax.ShapeDtypeStruct(heads.shape, F32),
            jax.ShapeDtypeStruct((rows, width), BF),
        ],
        in_specs=[vmem] * 10,
        out_specs=[vmem] * 4,
        scratch_shapes=[
            pltpu.VMEM((n_fsdp, n_seq, owned, columns), BF),
            pltpu.VMEM((n_fsdp, n_seq, owned, columns), BF),
            pltpu.VMEM((n_seq, owned, columns), BF),
            pltpu.VMEM((n_seq, owned, columns), BF),
            dma((n_fsdp, n_seq)),
            dma((n_fsdp, n_seq)),
            dma((n_fsdp, n_seq)),
            dma((n_fsdp, n_seq)),
            dma((n_seq,)),
            dma((n_seq,)),
            pltpu.VMEM((rows, width), F32),
            pltpu.VMEM((n_seq, n_fsdp, owned, columns), BF),
            pltpu.VMEM(terms.shape, F32),
        ]
        + term_scratch(n_seq, n_fsdp, heads.shape)
        + reduce_scratch(n_seq, rows, width),
        compiler_params=pltpu.CompilerParams(
            collective_id=collective_id, has_side_effects=True, vmem_limit_bytes=60 << 20
        ),
        cost_estimate=pl.CostEstimate(flops=0, bytes_accessed=1 << 27, transcendentals=0),
        name="last_reduce",
    )(a.reshape(n_seq, rows, -1), w, normed, x, mid, gains, terms, heads, resid, ready)


def chunked(total, size, body):
    def step(i, carry):
        body(pl.ds(pl.multiple_of(i * size, size), size))
        return carry

    lax.fori_loop(0, total // size, step, 0)


def dispatch_kernel(n_seq, n_fsdp, pieces, x, hot, gates, masked, before, w_up, w_down, *refs):
    masked_all, columns_out, scaled = refs[:3]
    outs, hiddens, acts, results = (refs[3 + k * pieces : 3 + (k + 1) * pieces] for k in range(4))
    rest = refs[3 + 4 * pieces :]
    gates_out, gathered, gathered_two, send, total = rest[:5]
    own_sem, line_send, line_recv, row_send, row_recv, own_two, send_two, recv_two = rest[5:13]
    line_send_two, line_recv_two = rest[13:15]
    gate_exchange = Exchange(n_seq, n_fsdp, gates, gates_out, rest[15:])
    me_s, me_f = lax.axis_index("seq"), lax.axis_index("fsdp")
    width = x.shape[1]
    capacity = outs[0].shape[2]
    greet_all(n_seq, n_fsdp)

    def line_copy(step, block, way, to):
        src = x if step == 0 else gathered.at[block]
        return remote(
            src, gathered.at[block], line_send.at[way, step], line_recv.at[block], (me_s, to)
        )

    def line_two(step, block, way, to):
        src = masked if step == 0 else gathered_two.at[block]
        return remote(
            src,
            gathered_two.at[block],
            line_send_two.at[way, step],
            line_recv_two.at[block],
            (me_s, to),
        )

    def row_copy(block, i, piece, place):
        other = (me_s + i) % n_seq
        return remote(
            send.at[block, other, piece],
            outs[piece].at[place, block],
            row_send.at[block, i, piece],
            row_recv.at[place, block, piece],
            (other, me_f),
        )

    def own_copy(block, piece):
        return pltpu.make_async_copy(
            send.at[block, me_s, piece], outs[piece].at[me_s, block], own_sem.at[block, piece]
        )

    def masked_copy(block, i, place):
        other = (me_s + i) % n_seq
        return remote(
            send.at[block, other],
            masked_all.at[place, :, block],
            send_two.at[block, i],
            recv_two.at[place, block],
            (other, me_f),
        )

    def own_masked(block):
        return pltpu.make_async_copy(
            send.at[block, me_s], masked_all.at[me_s, :, block], own_two.at[block]
        )

    def pick(block, rows):
        def some(columns):
            picked = dot(hot[block], rows[:, columns], 1, 0).astype(BF)
            send[block, :, :, :, columns] = picked.reshape(n_seq, pieces, capacity, -1)

        chunked(width, 512, some)

    def scatter(block, rows):
        pick(block, rows)
        for i in range(1, n_seq):
            for piece in range(pieces):
                row_copy(block, i, piece, me_s).start()
        for piece in range(pieces):
            own_copy(block, piece).start()

    def scatter_masked(block):
        for piece in range(pieces):
            own_copy(block, piece).wait()
            for i in range(1, n_seq):
                row_copy(block, i, piece, me_s).wait_send()
        pick(block, gathered_two.at[block])
        for i in range(1, n_seq):
            masked_copy(block, i, me_s).start()
        own_masked(block).start()

    def around(step, act):
        @pl.when(me_f - step >= 0)
        def _():
            act(me_f - step)

        @pl.when(me_f + step < n_fsdp)
        def _():
            act(me_f + step)

    @pl.when(me_f + 1 < n_fsdp)
    def _():
        line_copy(0, me_f, 0, me_f + 1).start()

    @pl.when(me_f >= 1)
    def _():
        line_copy(0, me_f, 1, me_f - 1).start()

    scatter(me_f, x)
    gate_exchange.start()
    for step in range(1, n_fsdp):
        line_step(
            n_fsdp,
            step,
            lambda block: line_copy(1, block, 0, me_f).wait_recv(),
            lambda block, way, to: line_copy(step, block, way, to).start(),
        )
        around(step, lambda block: scatter(block, gathered.at[block]))

    @pl.when(me_f + 1 < n_fsdp)
    def _():
        line_two(0, me_f, 0, me_f + 1).start()

    @pl.when(me_f >= 1)
    def _():
        line_two(0, me_f, 1, me_f - 1).start()

    for step in range(1, n_fsdp):
        line_step(
            n_fsdp,
            step,
            lambda block: line_two(1, block, 0, me_f).wait_recv(),
            lambda block, way, to: line_two(step, block, way, to).start(),
        )
        around(step, scatter_masked)
    for step in range(n_fsdp):
        line_sent(
            n_fsdp, step, lambda block, way, to: line_copy(step, block, way, to).wait_send()
        )
        line_sent(n_fsdp, step, lambda block, way, to: line_two(step, block, way, to).wait_send())

    gate_exchange.finish()
    n = n_seq * n_fsdp
    for piece in range(pieces):
        lanes = lax.broadcasted_iota(jnp.int32, (n, capacity, 128), 2)
        place = lax.broadcasted_iota(jnp.int32, (n, capacity, 128), 1)
        values = jnp.broadcast_to(gates_out[:, piece : piece + 1, :], (n, capacity, 128))
        column = jnp.sum(jnp.where(lanes == place, values, 0.0), axis=2, keepdims=True)
        columns_out[piece] = column.reshape(n * capacity, 1)

    for piece in range(pieces):
        own_copy(me_f, piece).wait()
        for i in range(1, n_seq):
            row_copy(me_f, i, piece, me_s).wait_send()
    for piece in range(pieces):
        for block in range(n_fsdp):
            for i in range(1, n_seq):
                row_copy(block, i, piece, (me_s + i) % n_seq).wait_recv()

    ff = w_down.shape[1]
    tile = min(256, ff)
    steps = ff // tile
    spans = seq_tile(n_seq, n_fsdp * capacity, 3072 // n_fsdp)
    count = spans * n_fsdp * capacity
    for piece in range(pieces):

        def body(rows, w_gate, w_value, w_back, hidden, act, result, scaled_rows):
            step = pl.program_id(1)
            low = rows[...].reshape(count, width)
            gate = dot(low, w_gate[0], 1, 0)
            up = dot(low, w_value[0], 1, 0)
            hidden[0] = gate
            hidden[1] = up
            act[...] = (gate * jax.nn.sigmoid(gate) * up).astype(BF)
            product = dot(act[...], w_back[0], 1, 0)

            @pl.when(step == 0)
            def _():
                total[...] = product

            @pl.when(step > 0)
            def _():
                total[...] += product

            @pl.when(step == steps - 1)
            def _():
                start = pl.multiple_of(pl.program_id(0) * count, 8)
                column = columns_out[piece, pl.ds(start, count), :]
                result[...] = total[...].astype(BF)
                gated = (result[...].astype(F32) * column).astype(BF)
                scaled_rows[...] = gated.reshape(scaled_rows.shape)

        pltpu.emit_pipeline(
            body,
            grid=(n * capacity // count, steps),
            in_specs=[
                pl.BlockSpec((spans, n_fsdp, capacity, width), lambda r, i: (r, 0, 0, 0)),
                pl.BlockSpec((1, width, tile), lambda r, i: (piece, 0, i)),
                pl.BlockSpec((1, width, tile), lambda r, i: (piece, 0, steps + i)),
                pl.BlockSpec((1, tile, width), lambda r, i: (piece, i, 0)),
            ],
            out_specs=[
                pl.BlockSpec((2, count, tile), lambda r, i: (0, r, i)),
                pl.BlockSpec((count, tile), lambda r, i: (r, i)),
                pl.BlockSpec((count, width), lambda r, i: (r, 0)),
                pl.BlockSpec((spans, 1, n_fsdp, capacity, width), lambda r, i: (r, piece, 0, 0, 0)),
            ],
        )(
            outs[piece],
            w_up,
            w_up,
            w_down,
            hiddens[piece],
            acts[piece],
            results[piece],
            scaled,
        )

    for step in range(1, n_fsdp):
        around(step, lambda block: own_masked(block).wait())
    for step in range(1, n_fsdp):
        for i in range(1, n_seq):

            def done(block):
                masked_copy(block, i, me_s).wait_send()
                masked_copy(block, i, (me_s + i) % n_seq).wait_recv()

            around(step, done)


def dispatch_rows(
    x, hot, gates, masked, before, w_up, w_down, n_seq, n_fsdp, capacity, collective_id
):
    count, width = x.shape
    pieces, ff = w_down.shape[:2]
    rows = n_seq * n_fsdp * capacity
    tile_rows = seq_tile(n_seq, n_fsdp * capacity, 3072 // n_fsdp) * n_fsdp * capacity
    vmem = pl.BlockSpec(memory_space=pltpu.VMEM)
    any_space = pl.BlockSpec(memory_space=pl.ANY)
    dma = pltpu.SemaphoreType.DMA
    return pl.pallas_call(
        functools.partial(dispatch_kernel, n_seq, n_fsdp, pieces),
        out_shape=[
            jax.ShapeDtypeStruct(before.shape, BF),
            jax.ShapeDtypeStruct((pieces, rows, 1), F32),
            jax.ShapeDtypeStruct(before.shape, BF),
        ]
        + [jax.ShapeDtypeStruct((n_seq, n_fsdp, capacity, width), BF)] * pieces
        + [jax.ShapeDtypeStruct((2, rows, ff), F32)] * pieces
        + [jax.ShapeDtypeStruct((rows, ff), BF)] * pieces
        + [jax.ShapeDtypeStruct((rows, width), BF)] * pieces,
        in_specs=[vmem] * 4 + [any_space] * 3,
        out_specs=[any_space, vmem] + [any_space] * (1 + 4 * pieces),
        scratch_shapes=[
            pltpu.VMEM(gates.shape, F32),
            pltpu.VMEM((n_fsdp, count, width), BF),
            pltpu.VMEM((n_fsdp, count, width), BF),
            pltpu.VMEM((n_fsdp, n_seq, pieces, capacity, width), BF),
            pltpu.VMEM((tile_rows, width), F32),
            dma((n_fsdp, pieces)),
            dma((2, n_fsdp)),
            dma((n_fsdp,)),
            dma((n_fsdp, n_seq, pieces)),
            dma((n_seq, n_fsdp, pieces)),
            dma((n_fsdp,)),
            dma((n_fsdp, n_seq)),
            dma((n_seq, n_fsdp)),
            dma((2, n_fsdp)),
            dma((n_fsdp,)),
        ]
        + exchange_sems(n_seq * n_fsdp),
        input_output_aliases={4: 0},
        compiler_params=pltpu.CompilerParams(
            collective_id=collective_id, has_side_effects=True, vmem_limit_bytes=60 << 20
        ),
        name="dispatch_rows",
    )(x, hot, gates, masked, before, w_up, w_down)


def return_kernel(n_seq, n_fsdp, pieces, hot, gates, ready, w_up, *refs):
    grads = refs[:pieces]
    out, gates_out, ready_sums = refs[pieces : pieces + 3]
    rest = refs[pieces + 3 :]
    weights, hidden, rows, got, parts, sums, some_ready = rest[:7]
    w_sem, h_sem, ready_sem, own_sem, row_send, row_recv, part_send, part_recv = rest[7:15]
    gate_exchange = Exchange(n_seq, n_fsdp, gates, gates_out, rest[15:])
    me_s, me_f = lax.axis_index("seq"), lax.axis_index("fsdp")
    width = out.shape[1]
    capacity = rows.shape[3]
    ff = hidden.shape[5]
    tile = min(256, width)
    chunks = width // tile

    def weight_copy(piece, chunk):
        lines = pl.ds(pl.multiple_of(chunk * tile, tile), tile)
        return pltpu.make_async_copy(
            w_up.at[piece, lines], weights.at[piece, lines], w_sem.at[piece, chunk]
        )

    def hidden_copy(piece):
        return pltpu.make_async_copy(grads[piece], hidden.at[piece], h_sem.at[piece])

    def ready_copy(block):
        return pltpu.make_async_copy(
            ready.at[:, :, block], some_ready.at[block % 2], ready_sem.at[block % 2]
        )

    def row_copy(block, i, place):
        other = (me_s + i) % n_seq
        return remote(
            rows.at[block, other],
            got.at[block, place],
            row_send.at[block, i],
            row_recv.at[block, place],
            (other, me_f),
        )

    def own_copy(block):
        return pltpu.make_async_copy(rows.at[block, me_s], got.at[block, me_s], own_sem.at[block])

    def part_copy(j):
        block = (me_f + j) % n_fsdp
        return remote(
            parts.at[block], sums.at[me_f], part_send.at[j], part_recv.at[me_f], (me_s, block)
        )

    for piece in range(pieces):
        hidden_copy(piece).start()

        def begin(chunk, carry):
            weight_copy(piece, chunk).start()
            return carry

        lax.fori_loop(0, chunks, begin, 0)
    for block in range(min(2, n_fsdp)):
        ready_copy(block).start()
    greet_all(n_seq, n_fsdp)
    gate_exchange.start()

    def compute(j):
        block = (me_f + j) % n_fsdp
        for piece in range(pieces):
            if j == 1:
                hidden_copy(piece).wait()
            gate_grad = hidden[piece, 0, :, block].reshape(-1, ff)
            up_grad = hidden[piece, 1, :, block].reshape(-1, ff)

            def some(chunk, carry):
                if j == 1:
                    weight_copy(piece, chunk).wait()
                lines = pl.ds(pl.multiple_of(chunk * tile, tile), tile)
                total = dot(gate_grad, weights[piece, lines, :ff], 1, 1)
                total = total + dot(up_grad, weights[piece, lines, ff:], 1, 1)
                rows[block, :, piece, :, lines] = total.astype(BF).reshape(n_seq, capacity, -1)
                return carry

            lax.fori_loop(0, chunks, some, 0)
        for i in range(1, n_seq):
            row_copy(block, i, me_s).start()
        own_copy(block).start()

    def finish(j):
        block = (me_f + j) % n_fsdp
        own_copy(block).wait()
        for i in range(1, n_seq):
            row_copy(block, i, (me_s + i) % n_seq).wait_recv()

        def some(columns):
            arrived = got[block, :, :, :, columns].reshape(n_seq * pieces * capacity, -1)
            total = dot(hot[block], arrived, 1, 0)
            if j < n_fsdp:
                parts[block, :, columns] = total.astype(BF)
            else:
                out[:, columns] = total

        chunked(width, 512, some)
        if j < n_fsdp:
            part_copy(j).start()

    def sum_ready(block):
        ready_copy(block).wait()

        def some(columns):
            arrived = some_ready[block % 2, :, :, :, columns]
            arrived = arrived.reshape(n_seq * pieces * capacity, -1)
            ready_sums[block, :, columns] = dot(hot[block], arrived, 1, 0).astype(BF)

        chunked(width, 512, some)
        if block + 2 < n_fsdp:
            ready_copy(block + 2).start()

    for j in range(1, n_fsdp + 1):
        compute(j)
        if j >= 3:
            finish(j - 2)
    for block in range(n_fsdp):
        sum_ready(block)
    for j in range(max(1, n_fsdp - 1), n_fsdp + 1):
        finish(j)
    for j in range(1, n_fsdp):
        source = (me_f + n_fsdp - j) % n_fsdp
        remote(
            parts.at[source], sums.at[source], part_send.at[j], part_recv.at[source], (me_s, source)
        ).wait_recv()

    def add(columns):
        total = out[:, columns]
        for j in range(1, n_fsdp):
            total = total + sums[(me_f + j) % n_fsdp, :, columns].astype(F32)
        out[:, columns] = total

    chunked(width, 512, add)
    for j in range(1, n_fsdp):
        part_copy(j).wait_send()
    for block in range(n_fsdp):
        for i in range(1, n_seq):
            row_copy(block, i, me_s).wait_send()
    gate_exchange.finish()


def return_rows(grads, w_up, hot, gates, ready, n_seq, n_fsdp, collective_id):
    pieces, width = w_up.shape[:2]
    ff = w_up.shape[2] // 2
    count = hot.shape[1]
    capacity = ready.shape[3]
    vmem = pl.BlockSpec(memory_space=pltpu.VMEM)
    any_space = pl.BlockSpec(memory_space=pl.ANY)
    dma = pltpu.SemaphoreType.DMA
    return pl.pallas_call(
        functools.partial(return_kernel, n_seq, n_fsdp, pieces),
        out_shape=[
            jax.ShapeDtypeStruct((count, width), F32),
            jax.ShapeDtypeStruct(gates.shape, F32),
            jax.ShapeDtypeStruct((n_fsdp, count, width), BF),
        ],
        in_specs=[vmem, vmem, any_space, any_space] + [any_space] * pieces,
        out_specs=[vmem] * 3,
        scratch_shapes=[
            pltpu.VMEM(w_up.shape, BF),
            pltpu.VMEM((pieces, 2, n_seq, n_fsdp, capacity, ff), BF),
            pltpu.VMEM((n_fsdp, n_seq, pieces, capacity, width), BF),
            pltpu.VMEM((n_fsdp, n_seq, pieces, capacity, width), BF),
            pltpu.VMEM((n_fsdp, count, width), BF),
            pltpu.VMEM((n_fsdp, count, width), BF),
            pltpu.VMEM((2, n_seq, pieces, capacity, width), BF),
            dma((pieces, width // min(256, width))),
            dma((pieces,)),
            dma((2,)),
            dma((n_fsdp,)),
            dma((n_fsdp, n_seq)),
            dma((n_fsdp, n_seq)),
            dma((n_fsdp,)),
            dma((n_fsdp,)),
        ]
        + exchange_sems(n_seq * n_fsdp),
        compiler_params=pltpu.CompilerParams(
            collective_id=collective_id, has_side_effects=True, vmem_limit_bytes=60 << 20
        ),
        name="return_rows",
    )(hot, gates, ready, w_up, *grads)


def weight_grad_kernel(a, b, *refs):
    parts, _, n = b.shape
    for part in range(parts):
        refs[-1][0, :, part * n : (part + 1) * n] = dot(a[...], b[part], 0, 0)


def weight_grad(a, b, whole, piece, pieces):
    rows, m = a.shape
    parts, _, n = b.shape
    tile = min(256, m)
    more = [] if whole is None else [whole]
    return pl.pallas_call(
        weight_grad_kernel,
        out_shape=jax.ShapeDtypeStruct((pieces, m, n * parts), F32),
        grid=(m // tile,),
        in_specs=[
            pl.BlockSpec((rows, tile), lambda i: (0, i)),
            pl.BlockSpec((parts, rows, n), lambda i: (0, 0, 0)),
        ]
        + [pl.BlockSpec(memory_space=pl.ANY)] * len(more),
        out_specs=pl.BlockSpec((1, tile, n * parts), lambda i: (piece, i, 0)),
        input_output_aliases={2: 0} if more else {},
        cost_estimate=pl.CostEstimate(
            flops=2 * rows * m * n * parts,
            bytes_accessed=4 * m * n * parts,
            transcendentals=0,
        ),
        name="weight_grad",
    )(a, b, *more)


def seq_tile(n_seq, rows_each, most=1024):
    tile = n_seq
    while tile > 1 and (tile * rows_each > most or n_seq % tile):
        tile -= 1
    return tile


def expert_backward_kernel(masked, gates, piece_out, hidden, w_down, out, grad, inner, partial):
    @pl.when(pl.program_id(1) == 0)
    def _():
        partial[...] = jnp.zeros_like(partial)

        def some(columns):
            low = masked[:, 0, :, :, columns].reshape(grad.shape[0], -1).astype(F32)
            grad[:, columns] = (low * gates[...]).astype(BF)
            product = low * piece_out[:, columns].astype(F32)
            for i in range(product.shape[1] // 128):
                partial[...] += product[:, i * 128 : (i + 1) * 128]

        chunked(grad.shape[1], 512, some)
        sums = jnp.sum(partial[...].T, axis=0, keepdims=True)
        inner[...] = jnp.broadcast_to(sums, inner.shape)

    act_grad = dot(grad[...], w_down[0], 1, 1)
    gate, up = hidden[0], hidden[1]
    sigmoid = jax.nn.sigmoid(gate)
    out[0] = (act_grad * up * sigmoid * (1.0 + gate * (1.0 - sigmoid))).astype(BF)
    out[1] = (act_grad * gate * sigmoid).astype(BF)


def expert_backward(masked, gates, piece_out, hidden, w_down, piece):
    rows, width = piece_out.shape
    ff = w_down.shape[1]
    n_seq, _, n_fsdp, capacity, _ = masked.shape
    tile = min(256, ff)
    spans = seq_tile(n_seq, n_fsdp * capacity)
    count = spans * n_fsdp * capacity
    part = pl.BlockSpec((2, count, tile), lambda r, i: (0, r, i))
    fixed = lambda r, i: (r, 0)
    return pl.pallas_call(
        expert_backward_kernel,
        out_shape=[
            jax.ShapeDtypeStruct((2, rows, ff), BF),
            jax.ShapeDtypeStruct((rows, width), BF),
            jax.ShapeDtypeStruct((8, rows), F32),
        ],
        grid=(rows // count, ff // tile),
        in_specs=[
            pl.BlockSpec((spans, 1, n_fsdp, capacity, width), lambda r, i: (r, piece, 0, 0, 0)),
            pl.BlockSpec((count, 1), fixed),
            pl.BlockSpec((count, width), fixed),
            part,
            pl.BlockSpec((1, tile, width), lambda r, i: (piece, i, 0)),
        ],
        out_specs=[
            part,
            pl.BlockSpec((count, width), fixed),
            pl.BlockSpec((8, count), lambda r, i: (0, r)),
        ],
        scratch_shapes=[pltpu.VMEM((count, 128), F32)],
        compiler_params=pltpu.CompilerParams(vmem_limit_bytes=62 << 20),
        cost_estimate=pl.CostEstimate(
            flops=2 * rows * width * ff, bytes_accessed=12 * rows * ff, transcendentals=rows * ff
        ),
        name="expert_backward",
    )(masked, gates, piece_out, hidden, w_down)


class SeqShare:
    def __init__(self, n_seq, own, every, send_sem, recv_sem):
        self.n_seq, self.own, self.every = n_seq, own, every
        self.send_sem, self.recv_sem = send_sem, recv_sem
        self.me_s, self.me_f = lax.axis_index("seq"), lax.axis_index("fsdp")

    def copy(self, i, place):
        other = (self.me_s + i) % self.n_seq
        return remote(
            self.own,
            self.every.at[place],
            self.send_sem.at[i],
            self.recv_sem.at[place],
            (other, self.me_f),
        )

    def total(self):
        for i in range(1, self.n_seq):
            self.copy(i, self.me_s).start()
        total = self.own[...]
        for i in range(1, self.n_seq):
            place = (self.me_s + i) % self.n_seq
            self.copy(i, place).wait_recv()
            total = total + self.every[place]
        for i in range(1, self.n_seq):
            self.copy(i, self.me_s).wait_send()
        return total


def share_scratch(n_seq, shape):
    dma = pltpu.SemaphoreType.DMA
    return [pltpu.VMEM(shape, F32), pltpu.VMEM((n_seq,) + shape, F32), dma((n_seq,)), dma((n_seq,))]


def row_sums(values):
    ones = jnp.ones((8, values.shape[1]), F32)
    return lax.dot_general(
        ones,
        values,
        (((1,), (1,)), ((), ())),
        preferred_element_type=F32,
        precision=lax.Precision.HIGHEST,
    )


def front_kernel(n_seq, x, gain, w, normed_out, raw_out, totals, normed, raw, sems, *scratch):
    share = SeqShare(n_seq, *scratch)
    head_width = w.shape[1] // 3
    tile = 256

    def some(i, carry):
        rows = pl.ds(pl.multiple_of(i * tile, tile), tile)
        values = x[rows, :].astype(F32)
        scale = lax.rsqrt(jnp.mean(values * values, axis=-1, keepdims=True) + epsilon)
        low = (values * scale * gain[0:1, :]).astype(BF)
        normed[rows, :] = low
        result = dot(low, w[...], 1, 0)
        raw[rows, :] = result
        for copy in away(i):
            copy.start()
        for part in range(2):
            piece = result[:, part * head_width : (part + 1) * head_width]
            share.own[part : part + 1, rows] = row_sums(piece * piece)[0:1]
        return carry

    def away(i):
        rows = pl.ds(pl.multiple_of(i * tile, tile), tile)
        return [
            pltpu.make_async_copy(normed.at[rows], normed_out.at[rows], sems.at[0, i]),
            pltpu.make_async_copy(raw.at[rows], raw_out.at[rows], sems.at[1, i]),
        ]

    def gone(i, carry):
        for copy in away(i):
            copy.wait()
        return carry

    share.own[...] = jnp.zeros_like(share.own)
    lax.fori_loop(0, x.shape[0] // tile, some, 0)
    totals[...] = share.total()
    lax.fori_loop(0, x.shape[0] // tile, gone, 0)


def front(x, gains, w, n_seq, collective_id):
    rows, width = x.shape
    vmem = pl.BlockSpec(memory_space=pltpu.VMEM)
    hbm = pl.BlockSpec(memory_space=pltpu.HBM)
    return pl.pallas_call(
        loading(functools.partial(front_kernel, n_seq), functools.partial(greet_seq, n_seq), 3),
        out_shape=[
            jax.ShapeDtypeStruct((rows, width), BF),
            jax.ShapeDtypeStruct((rows, w.shape[1]), F32),
            jax.ShapeDtypeStruct((8, rows), F32),
        ],
        in_specs=[hbm] * 3,
        out_specs=[hbm, hbm, vmem],
        scratch_shapes=[
            pltpu.VMEM((rows, width), BF),
            pltpu.VMEM((rows, w.shape[1]), F32),
            pltpu.SemaphoreType.DMA((2, rows // 256)),
        ]
        + share_scratch(n_seq, (8, rows))
        + load_scratch([x, gains, w]),
        compiler_params=pltpu.CompilerParams(
            collective_id=collective_id, has_side_effects=True, vmem_limit_bytes=62 << 20
        ),
        name="front",
    )(x, gains, w)


def column_rms(sums, part, width):
    return lax.rsqrt(sums.T[:, part : part + 1] / width + epsilon)


def turned(values, cosine, sine):
    return values * cosine + pltpu.roll(values, values.shape[1] // 2, 1) * sine


def softmax_columns(k, q, length, scaling):
    scores = dot(k, q, 1, 1) * scaling
    key = lax.broadcasted_iota(jnp.int32, scores.shape, 0)
    scores = jnp.where(key < length, scores, -1e30)
    weights = jnp.exp(scores - jnp.max(scores, axis=0, keepdims=True))
    return weights / jnp.sum(weights, axis=0, keepdims=True)


def attend_kernel(
    width,
    length,
    raw_q,
    raw_k,
    raw_v,
    q_sums,
    k_sums,
    gain,
    q_cos,
    q_sin,
    k_cos,
    k_sin,
    o_ref,
    q_ref,
    k_ref,
    v_ref,
):
    scaling = raw_q.shape[1] ** (-0.5)

    @pl.when(pl.program_id(1) == 0)
    def _():
        key = raw_k[...] * column_rms(k_sums[...], 1, width) * gain[2:3, :]
        k_ref[...] = turned(key, k_cos[...], k_sin[...]).astype(BF)
        v_ref[...] = raw_v[...].astype(BF)

    query = raw_q[...] * column_rms(q_sums[...], 0, width) * gain[1:2, :]
    query = turned(query, q_cos[...], q_sin[...]).astype(BF)
    q_ref[...] = query
    probs = softmax_columns(k_ref[...], query, length[0], scaling).astype(BF)
    o_ref[...] = dot(v_ref[...], probs, 0, 0).T.astype(BF)


def attend(raw, totals, gains, cosine, sine, length, block, width):
    slot_len, head_width = raw.shape[0], raw.shape[1] // 3
    hd = cosine.shape[1]
    heads = head_width // hd
    rows = lambda shift: pl.BlockSpec((block, hd), lambda h, i, n: (i, shift + h))
    full = lambda shift: pl.BlockSpec((slot_len, hd), lambda h, i, n: (0, shift + h))
    table = pl.BlockSpec((block, hd), lambda h, i, n: (i, 0))
    whole_table = pl.BlockSpec((slot_len, hd), lambda h, i, n: (0, 0))
    return pl.pallas_call(
        functools.partial(attend_kernel, width),
        out_shape=[jax.ShapeDtypeStruct((slot_len, head_width), BF)] * 4,
        grid_spec=pltpu.PrefetchScalarGridSpec(
            num_scalar_prefetch=1,
            grid=(heads, slot_len // block),
            in_specs=[
                rows(0),
                full(heads),
                full(2 * heads),
                pl.BlockSpec((8, block), lambda h, i, n: (0, i)),
                pl.BlockSpec((8, slot_len), lambda h, i, n: (0, 0)),
                pl.BlockSpec((8, hd), lambda h, i, n: (0, h)),
                table,
                table,
                whole_table,
                whole_table,
            ],
            out_specs=[rows(0), rows(0), full(0), full(0)],
        ),
        cost_estimate=pl.CostEstimate(
            flops=4 * heads * slot_len * slot_len * hd, bytes_accessed=1 << 23, transcendentals=0
        ),
        compiler_params=pltpu.CompilerParams(vmem_limit_bytes=62 << 20),
        name="attend",
    )(length, raw, raw, raw, totals, totals, gains, cosine, sine, cosine, sine)


def attend_back_kernel(
    width,
    length,
    q_ref,
    k_ref,
    v_ref,
    g_ref,
    raw_q,
    raw_k,
    q_sums,
    k_sums,
    gain,
    q_cos,
    q_sin,
    k_cos,
    k_sin,
    dq_ref,
    dk_ref,
    dv_ref,
    dots,
    gain_out,
    dk_sum,
    dv_sum,
):
    head, step = pl.program_id(0), pl.program_id(1)
    last = step == pl.num_programs(1) - 1
    block, hd = q_ref.shape
    scaling = hd ** (-0.5)

    @pl.when(step == 0)
    def _():
        dk_sum[...] = jnp.zeros_like(dk_sum)
        dv_sum[...] = jnp.zeros_like(dv_sum)
        gain_out[...] = jnp.zeros_like(gain_out)

        @pl.when(head == 0)
        def _():
            dots[...] = jnp.zeros_like(dots)

    q, k, v, g = q_ref[...], k_ref[...], v_ref[...], g_ref[...]
    probs = softmax_columns(k, q, length[0], scaling)
    dv_sum[...] += dot(probs.astype(BF), g, 1, 0)
    weights_grad = dot(v, g, 1, 1)
    inner = jnp.sum(probs * weights_grad, axis=0, keepdims=True)
    score_grad = (probs * (weights_grad - inner) * scaling).astype(BF)
    dk_sum[...] += dot(score_grad, q, 1, 0)
    query_grad = dot(k, score_grad, 0, 0).T.astype(BF).astype(F32)
    query_in = turned(query_grad, q_cos[...], -q_sin[...])
    dq_ref[...] = query_in
    product = query_in * raw_q[...]
    rows = pl.ds(pl.multiple_of(step * block, block), block)
    dots[0:1, rows] += row_sums(product * gain[1:2, :])[0:1]
    gain_out[0:1, :] += jnp.sum(
        product * column_rms(q_sums[...], 0, width), axis=0, keepdims=True
    )

    @pl.when(last)
    def _():
        key_in = turned(dk_sum[...].astype(BF).astype(F32), k_cos[...], -k_sin[...])
        dk_ref[...] = key_in
        dv_ref[...] = dv_sum[...].astype(BF)
        product = key_in * raw_k[...]
        dots[1:2, :] += row_sums(product * gain[2:3, :])[0:1]
        gain_out[1:2, :] = jnp.sum(
            product * column_rms(k_sums[...], 1, width), axis=0, keepdims=True
        )


def attend_back(query, key, value, grad, raw, totals, gains, cosine, sine, length, block, width):
    slot_len, head_width = query.shape
    hd = cosine.shape[1]
    heads = head_width // hd
    rows = pl.BlockSpec((block, hd), lambda h, i, n: (i, h))
    full = lambda shift: pl.BlockSpec((slot_len, hd), lambda h, i, n: (0, shift + h))
    table = pl.BlockSpec((block, hd), lambda h, i, n: (i, 0))
    whole_table = pl.BlockSpec((slot_len, hd), lambda h, i, n: (0, 0))
    return pl.pallas_call(
        functools.partial(attend_back_kernel, width),
        out_shape=[
            jax.ShapeDtypeStruct(query.shape, F32),
            jax.ShapeDtypeStruct(query.shape, F32),
            jax.ShapeDtypeStruct(query.shape, BF),
            jax.ShapeDtypeStruct((8, slot_len), F32),
            jax.ShapeDtypeStruct((8, head_width), F32),
        ],
        grid_spec=pltpu.PrefetchScalarGridSpec(
            num_scalar_prefetch=1,
            grid=(heads, slot_len // block),
            in_specs=[
                rows,
                full(0),
                full(0),
                rows,
                rows,
                full(heads),
                pl.BlockSpec((8, block), lambda h, i, n: (0, i)),
                pl.BlockSpec((8, slot_len), lambda h, i, n: (0, 0)),
                pl.BlockSpec((8, hd), lambda h, i, n: (0, h)),
                table,
                table,
                whole_table,
                whole_table,
            ],
            out_specs=[
                rows,
                full(0),
                full(0),
                pl.BlockSpec((8, slot_len), lambda h, i, n: (0, 0)),
                pl.BlockSpec((8, hd), lambda h, i, n: (0, h)),
            ],
            scratch_shapes=[pltpu.VMEM((slot_len, hd), F32), pltpu.VMEM((slot_len, hd), F32)],
        ),
        cost_estimate=pl.CostEstimate(
            flops=20 * heads * slot_len * slot_len * hd, bytes_accessed=1 << 24, transcendentals=0
        ),
        compiler_params=pltpu.CompilerParams(vmem_limit_bytes=62 << 20),
        name="attend_back",
    )(
        length,
        query,
        key,
        value,
        grad,
        raw,
        raw,
        totals,
        totals,
        gains,
        cosine,
        sine,
        cosine,
        sine,
    )


def raw_back_kernel(
    n_seq, n_fsdp, width, dq, dk, dv, raw, totals, gain, dots, terms, out, terms_out, *scratch
):
    share = SeqShare(n_seq, *scratch[:4])
    term_sum = TermSum(n_seq, n_fsdp, None, *scratch[4:6], None, None, *scratch[6:])
    term_sum.start_fsdp(terms[...])
    head_width = dq.shape[1]
    share.own[...] = dots[...]
    share.own[...] = share.total()
    tile = 256

    def some(i, carry):
        rows = pl.ds(pl.multiple_of(i * tile, tile), tile)
        inner = share.own[:, rows].T / width
        for part, grad in enumerate((dq, dk)):
            columns = slice(part * head_width, (part + 1) * head_width)
            scale = column_rms(totals[:, rows], part, width)
            weighted = grad[rows, :] * gain[part + 1 : part + 2, :]
            cube = scale * scale * scale
            result = scale * weighted - raw[rows, columns] * (cube * inner[:, part : part + 1])
            out[rows, columns] = result.astype(BF)
        out[rows, 2 * head_width :] = dv[rows, :]
        return carry

    lax.fori_loop(0, dq.shape[0] // tile, some, 0)
    terms_out[...] = term_sum.finish()


def raw_back(dq, dk, dv, raw, totals, gains, dots, terms, n_seq, n_fsdp, width, collective_id):
    vmem = pl.BlockSpec(memory_space=pltpu.VMEM)
    dma = pltpu.SemaphoreType.DMA
    return pl.pallas_call(
        loading(
            functools.partial(raw_back_kernel, n_seq, n_fsdp, width),
            functools.partial(greet_lines, n_seq, n_fsdp),
            8,
        ),
        out_shape=[
            jax.ShapeDtypeStruct(raw.shape, BF),
            jax.ShapeDtypeStruct(terms.shape, F32),
        ],
        in_specs=[pl.BlockSpec(memory_space=pltpu.HBM)] * 8,
        out_specs=[vmem] * 2,
        scratch_shapes=share_scratch(n_seq, dots.shape)
        + [
            pltpu.VMEM((n_seq,) + terms.shape, F32),
            pltpu.VMEM((n_fsdp,) + terms.shape, F32),
            dma((n_fsdp,)),
            dma((n_fsdp,)),
        ]
        + load_scratch([dq, dk, dv, raw, totals, gains, dots, terms]),
        compiler_params=pltpu.CompilerParams(
            collective_id=collective_id, has_side_effects=True, vmem_limit_bytes=62 << 20
        ),
        name="raw_back",
    )(dq, dk, dv, raw, totals, gains, dots, terms)


def rope_tables(positions, head_dim):
    half = head_dim // 2
    frequency = rope_base ** (-jnp.arange(half, dtype=F32) * 2.0 / head_dim)
    angles = positions.astype(F32)[:, None] * frequency[None, :]
    cosine, sine = jnp.cos(angles), jnp.sin(angles)
    return jnp.concatenate([cosine, cosine], axis=1), jnp.concatenate([-sine, sine], axis=1)


def places(block_routes, experts, capacity):
    count = block_routes.shape[0]
    match = (block_routes[:, :, None] == experts[None, None, :]).astype(F32).sum(axis=1)
    lower = jnp.tril(jnp.ones((count, count), BF), -1)
    rank = dot(lower, match.astype(BF), 1, 0)
    place = jnp.arange(capacity, dtype=F32)
    return match[:, :, None] * (rank[:, :, None] == place[None, None, :]).astype(F32)


def local(
    tokens,
    cotangent,
    lengths,
    routes,
    norm_gains,
    qkv_weight,
    proj_weight,
    router_weight,
    expert_up,
    expert_down,
):
    n_seq, n_fsdp = lax.axis_size("seq"), lax.axis_size("fsdp")
    n_dev = n_seq * n_fsdp
    me_s, me_f = lax.axis_index("seq"), lax.axis_index("fsdp")
    shard_len, width = tokens.shape[1], tokens.shape[2]
    slot_len = shard_len * n_seq
    experts = router_weight.shape[1]
    top_count = routes.shape[2]
    capacity = 3 * shard_len * top_count // (2 * experts)
    piece_ff = expert_down.shape[1]
    pieces_dev = expert_up.shape[0]
    split = FF // piece_ff
    head_dim = width // HEADS
    head_width = width // n_seq
    heads_dev = HEADS // n_seq
    owned = qkv_weight.shape[0]
    block = min(512, slot_len)
    length = lax.dynamic_slice_in_dim(lengths, me_f, 1)
    valid_total = jnp.sum(lengths).astype(F32).reshape(1)
    positions = me_s * shard_len + jnp.arange(shard_len, dtype=jnp.int32)
    row_valid = (positions < length[0]).astype(F32)
    local_routes = routes[0]
    push_all = functools.partial(push, n_seq=n_seq, n_fsdp=n_fsdp, scope="all")
    push_seq = functools.partial(push, n_seq=n_seq, n_fsdp=n_fsdp, scope="seq")

    masked_low = jnp.where(row_valid[:, None] > 0, cotangent[0], jnp.zeros((), BF))
    own_small = jnp.concatenate(
        [
            jnp.pad(norm_gains, ((0, 4), (0, 128 - owned))),
            local_routes.T.astype(BF),
            rows_of(router_weight.reshape(-1), 16),
        ]
    )
    small, gains, slot_tokens, qkv_local, cot_all, to_places, to_rows, counts = first_gather(
        own_small,
        tokens[0],
        qkv_weight,
        masked_low,
        lengths,
        n_seq,
        n_fsdp,
        pieces_dev,
        split,
        capacity,
        top_count,
        experts,
        collective_id=0,
    )
    slot_tokens = slot_tokens.reshape(slot_len, width)
    qkv_local = qkv_local.reshape(width, 3 * head_width)
    router = small[:, 8 + top_count :].reshape(n_dev, -1)[:, : owned * experts]
    router = router.reshape(width, experts)
    proj_later = lax.optimization_barrier((proj_weight, slot_tokens))[0]
    proj_rows = lax.all_gather(proj_later, "fsdp", axis=0, tiled=True)

    def exchange(rows):
        return lax.all_to_all(rows, "seq", split_axis=0, concat_axis=0, tiled=True)

    normed_one, raw, totals = front(slot_tokens, gains, qkv_local, n_seq, collective_id=1)


    def rms(values):
        return lax.rsqrt(jnp.mean(values * values, axis=-1, keepdims=True) + epsilon)

    own_gains = lax.dynamic_slice_in_dim(gains, me_s * head_width, head_width, 1)
    cosine, sine = rope_tables(jnp.arange(slot_len, dtype=jnp.int32), head_dim)
    attended, query, key, value = attend(
        raw, totals, own_gains, cosine, sine, length, block, width
    )

    resid_in = tokens[0].astype(F32)
    resid_mid = resid_in + product_reduced(attended, proj_rows, 0, n_seq, collective_id=8)
    mid_rms = rms(resid_mid)
    normed_two = (resid_mid * mid_rms * gains[3]).astype(BF)
    router_probs = jax.nn.softmax(jnp.dot(normed_two, router, preferred_element_type=F32), axis=-1)

    own_hot = places(local_routes, jnp.arange(experts, dtype=jnp.int32), capacity)
    gate_slot = jnp.sum(own_hot * router_probs[:, :, None], axis=0)
    gate_send = jnp.broadcast_to(gate_slot[:, None], (experts, split, capacity))
    gate_send = gate_send.reshape(n_dev, pieces_dev, capacity)
    gate_send = jnp.pad(gate_send, ((0, 0), (0, -pieces_dev % 8), (0, 128 - capacity)))
    cot_all, gate_columns, outs, *experts_forward = dispatch_rows(
        normed_two,
        to_places,
        gate_send,
        masked_low,
        cot_all,
        expert_up,
        expert_down,
        n_seq,
        n_fsdp,
        capacity,
        collective_id=6,
    )
    outs_back = exchange(outs)
    backs, gate_backs = [], []
    up_grad = down_grad = None
    for piece in range(pieces_dev):
        rows, hidden, activation, piece_out = experts_forward[piece::pieces_dev]
        rows = rows.reshape(-1, width)
        hidden_grad, out_grad, gate_back = expert_backward(
            cot_all, gate_columns[piece], piece_out, hidden, expert_down, piece
        )
        gate_backs.append(gate_back[0].reshape(n_dev, capacity))
        backs.append(hidden_grad.reshape(2, n_seq, n_fsdp, capacity, piece_ff))
        down_grad = weight_grad(activation, out_grad[None], down_grad, piece, pieces_dev)
        up_grad = weight_grad(rows, hidden_grad, up_grad, piece, pieces_dev)
    back_send = jnp.stack(gate_backs, axis=1).reshape(n_dev, pieces_dev * capacity)
    gate_pad = -pieces_dev * capacity % 1024
    back_send = jnp.pad(back_send, ((0, 0), (0, gate_pad))).reshape(n_dev, -1, 128)
    backs, outs_back, up_grad, down_grad = lax.optimization_barrier(
        (backs, outs_back, up_grad, down_grad)
    )
    backs, outs_back, up_grad, down_grad = lax.optimization_barrier(
        (backs, outs_back, up_grad, down_grad)
    )
    normed_two_grad, back_recv, outs_sums = return_rows(
        backs, expert_up, to_rows, back_send, outs_back, n_seq, n_fsdp, collective_id=7
    )

    fraction = counts[0] / (top_count * valid_total)
    back_recv = back_recv.reshape(n_dev, -1)
    slot_gates_grad = back_recv[:, : pieces_dev * capacity].reshape(experts, split, capacity).sum(axis=1)
    probs_grad = (
        jnp.sum(own_hot * slot_gates_grad[None], axis=2)
        + (experts * fraction / valid_total)[None, :] * row_valid[:, None]
    )
    logits_grad = router_probs * (
        probs_grad - jnp.sum(router_probs * probs_grad, axis=-1, keepdims=True)
    )
    router_term = lax.dot_general(
        logits_grad, normed_two.astype(F32), (((0,), (0,)), ((), ())), precision=lax.Precision.HIGHEST
    )
    normed_two_grad = normed_two_grad + lax.dot_general(
        logits_grad, router.astype(F32), (((1,), (1,)), ((), ())), precision=lax.Precision.HIGHEST
    )

    def rms_back(values, scale, gain, grad):
        weighted = gain * grad
        mean = jnp.mean(weighted * values, axis=-1, keepdims=True)
        return scale * weighted - values * (scale * scale * scale) * mean, jnp.sum(
            grad * values * scale, axis=0
        )

    mid_part, gain_three = rms_back(resid_mid, mid_rms, gains[3], normed_two_grad)
    mid_grad = masked_low.astype(F32) + mid_part
    branch_grad = mid_grad.astype(BF)
    outs_parts = lax.all_to_all(outs_sums, "fsdp", split_axis=0, concat_axis=0, tiled=True)
    slot_branch, router_parts = gather_seq(
        branch_grad, router_term, n_seq, n_fsdp, collective_id=9
    )
    slot_branch = slot_branch.reshape(slot_len, width)
    heads_grad = dot(slot_branch, proj_rows, 1, 1).astype(BF)
    query_in, key_in, value_grad, dots, heads_gain = attend_back(
        query,
        key,
        value,
        heads_grad,
        raw,
        totals,
        own_gains,
        cosine,
        sine,
        length,
        block,
        width,
    )
    raw_grad, router_parts = raw_back(
        query_in,
        key_in,
        value_grad,
        raw,
        totals,
        own_gains,
        dots,
        router_parts,
        n_seq,
        n_fsdp,
        width,
        collective_id=4,
    )
    raw_grad, outs_parts = lax.optimization_barrier((raw_grad, outs_parts))

    prob_part = jnp.sum(router_probs * row_valid[:, None], axis=0)
    prob_row = jnp.tile(jnp.pad(prob_part, (0, head_width - experts)), n_seq)
    terms = jnp.pad(jnp.stack([gain_three, prob_row]), ((1, 5), (0, 0)))
    heads_terms = jnp.pad(heads_gain[:2], ((3, 3), (0, 0)))
    input_grad, qkv_grad, last, layer_out = last_reduce(
        raw_grad,
        qkv_local,
        normed_one,
        tokens[0],
        mid_grad,
        gains,
        terms,
        heads_terms,
        resid_mid,
        outs_parts,
        n_seq,
        n_fsdp,
        collective_id=10,
    )
    input_grad = input_grad[None]
    layer_out = layer_out[None]

    proj_part = dot(attended, slot_branch, 0, 0).astype(BF)
    proj_grad = lax.psum_scatter(proj_part, "fsdp", scatter_dimension=0, tiled=True).astype(F32)

    router_grad = lax.dynamic_slice_in_dim(router_parts, me_f * owned, owned, 1).T
    prob_total = last[2, :experts]
    last = lax.dynamic_slice_in_dim(last, me_f * owned, owned, 1)
    gains_grad = jnp.stack([last[0], last[3], last[4], last[1]])
    loss_value = (experts * jnp.sum(fraction * prob_total / valid_total)).reshape(1)
    return (
        layer_out,
        input_grad,
        gains_grad,
        qkv_grad,
        proj_grad,
        router_grad,
        up_grad,
        down_grad,
        loss_value,
    )


def solution(mesh):
    rows = P(("seq", "fsdp"), None)
    return jax.shard_map(
        local,
        mesh=mesh,
        in_specs=(
            P("fsdp", "seq", None),
            P("fsdp", "seq", None),
            P(),
            P("fsdp", "seq", None),
            P(None, ("seq", "fsdp")),
            rows,
            rows,
            rows,
            P(("seq", "fsdp"), None, None),
            P(("seq", "fsdp"), None, None),
        ),
        out_specs=(
            P("fsdp", "seq", None),
            P("fsdp", "seq", None),
            P(None, ("seq", "fsdp")),
            rows,
            rows,
            rows,
            P(("seq", "fsdp"), None, None),
            P(("seq", "fsdp"), None, None),
            P(),
        ),
        check_vma=False,
    )
```

```python
import functools

import jax
import jax.numpy as jnp
import numpy as np
from jax import lax
from jax.experimental import pallas as pl
from jax.experimental.pallas import tpu as pltpu
from jax.sharding import PartitionSpec as P

HEADS = 16
FF = 1024

epsilon = 1e-06
rope_base = 10000.0
MESH = pl.DeviceIdType.MESH
BF = jnp.bfloat16
F32 = jnp.float32


def dot(a, b, ca, cb):
    return lax.dot_general(a, b, (((ca,), (cb,)), ((), ())), preferred_element_type=F32)


def push_kernel(n_seq, n_fsdp, scope, gather, src, dst, send_sem, recv_sem, own_sem):
    me_s, me_f = lax.axis_index("seq"), lax.axis_index("fsdp")
    n = n_seq * n_fsdp if scope == "all" else n_seq
    me = me_s * n_fsdp + me_f if scope == "all" else me_s

    def where(index):
        if scope == "all":
            return (index // n_fsdp, index % n_fsdp)
        return (index, me_f)

    barrier = pltpu.get_barrier_semaphore()

    def greet(i, carry):
        pl.semaphore_signal(barrier, inc=1, device_id=where((me + i) % n), device_id_type=MESH)
        return carry

    lax.fori_loop(1, n, greet, 0)
    own = pltpu.make_async_copy(src if gather else src.at[me], dst.at[me], own_sem)
    own.start()
    pl.semaphore_wait(barrier, n - 1)

    def copy_to(other):
        return pltpu.make_async_remote_copy(
            src_ref=src if gather else src.at[other],
            dst_ref=dst.at[me],
            send_sem=send_sem.at[other],
            recv_sem=recv_sem.at[me],
            device_id=where(other),
            device_id_type=MESH,
        )

    def copy_from(other):
        return pltpu.make_async_remote_copy(
            src_ref=src if gather else src.at[other],
            dst_ref=dst.at[other],
            send_sem=send_sem.at[other],
            recv_sem=recv_sem.at[other],
            device_id=where(other),
            device_id_type=MESH,
        )

    def send(i, carry):
        copy_to((me + i) % n).start()
        return carry

    lax.fori_loop(1, n, send, 0)

    def finish(i, carry):
        other = (me + i) % n
        copy_from(other).wait_recv()
        copy_to(other).wait_send()
        return carry

    lax.fori_loop(1, n, finish, 0)
    own.wait()


def push(block, n_seq, n_fsdp, scope, gather, collective_id):
    n = n_seq * n_fsdp if scope == "all" else n_seq
    shape = (n,) + (block.shape if gather else block.shape[1:])
    return pl.pallas_call(
        functools.partial(push_kernel, n_seq, n_fsdp, scope, gather),
        out_shape=jax.ShapeDtypeStruct(shape, block.dtype),
        in_specs=[pl.BlockSpec(memory_space=pltpu.VMEM)],
        out_specs=pl.BlockSpec(memory_space=pltpu.VMEM),
        scratch_shapes=[
            pltpu.SemaphoreType.DMA((n,)),
            pltpu.SemaphoreType.DMA((n,)),
            pltpu.SemaphoreType.DMA,
        ],
        compiler_params=pltpu.CompilerParams(collective_id=collective_id, has_side_effects=True),
        name="push_" + scope,
    )(block)


def rows_of(flat, multiple):
    size = flat.shape[0]
    whole = -(-size // (multiple * 128)) * multiple * 128
    return jnp.pad(flat, (0, whole - size)).reshape(-1, 128)


def remote(src, dst, send_sem, recv_sem, device):
    return pltpu.make_async_remote_copy(
        src_ref=src,
        dst_ref=dst,
        send_sem=send_sem,
        recv_sem=recv_sem,
        device_id=device,
        device_id_type=MESH,
    )


def greet_all(n_seq, n_fsdp):
    me_s, me_f = lax.axis_index("seq"), lax.axis_index("fsdp")
    n = n_seq * n_fsdp
    me = me_s * n_fsdp + me_f
    barrier = pltpu.get_barrier_semaphore()

    def greet(i, carry):
        other = (me + i) % n
        pl.semaphore_signal(
            barrier, inc=1, device_id=(other // n_fsdp, other % n_fsdp), device_id_type=MESH
        )
        return carry

    lax.fori_loop(1, n, greet, 0)
    pl.semaphore_wait(barrier, n - 1)


def greet_lines(n_seq, n_fsdp):
    me_s, me_f = lax.axis_index("seq"), lax.axis_index("fsdp")
    barrier = pltpu.get_barrier_semaphore()
    for i in range(1, n_seq):
        pl.semaphore_signal(
            barrier, inc=1, device_id=((me_s + i) % n_seq, me_f), device_id_type=MESH
        )
    for i in range(1, n_fsdp):
        pl.semaphore_signal(
            barrier, inc=1, device_id=(me_s, (me_f + i) % n_fsdp), device_id_type=MESH
        )
    pl.semaphore_wait(barrier, n_seq + n_fsdp - 2)


def loading(body, greet, inputs):
    def kernel(*refs):
        held, sems = refs[-1 - inputs : -1], refs[-1]
        copies = [
            pltpu.make_async_copy(refs[i], held[i], sems.at[i]) for i in range(inputs)
        ]
        for copy in copies:
            copy.start()
        greet()
        for copy in copies:
            copy.wait()
        body(*held, *refs[inputs : -1 - inputs])

    return kernel


def load_scratch(arrays):
    held = [pltpu.VMEM(array.shape, array.dtype) for array in arrays]
    return held + [pltpu.SemaphoreType.DMA((len(arrays),))]


class Exchange:
    def __init__(self, n_seq, n_fsdp, src, dst, sems):
        self.n, self.n_fsdp, self.src, self.dst = n_seq * n_fsdp, n_fsdp, src, dst
        self.send_sem, self.recv_sem, self.own_sem = sems
        self.me = lax.axis_index("seq") * n_fsdp + lax.axis_index("fsdp")

    def copy(self, i, place):
        other = (self.me + i) % self.n
        return remote(
            self.src.at[other],
            self.dst.at[self.me if place is None else place],
            self.send_sem.at[i],
            self.recv_sem.at[self.me if place is None else place],
            (other // self.n_fsdp, other % self.n_fsdp),
        )

    def own(self):
        return pltpu.make_async_copy(
            self.src.at[self.me], self.dst.at[self.me], self.own_sem
        )

    def start(self):
        self.own().start()

        def one(i, carry):
            self.copy(i, None).start()
            return carry

        lax.fori_loop(1, self.n, one, 0)

    def finish(self):
        def one(i, carry):
            self.copy(i, None).wait_send()
            self.copy(i, (self.me + i) % self.n).wait_recv()
            return carry

        lax.fori_loop(1, self.n, one, 0)
        self.own().wait()


def exchange_sems(n):
    return [
        pltpu.SemaphoreType.DMA((n,)),
        pltpu.SemaphoreType.DMA((n,)),
        pltpu.SemaphoreType.DMA,
    ]


def line_step(n_fsdp, step, arrived, forward):
    me_f = lax.axis_index("fsdp")

    @pl.when(me_f - step >= 0)
    def _():
        arrived(me_f - step)

        @pl.when(me_f + 1 < n_fsdp)
        def _():
            forward(me_f - step, 0, me_f + 1)

    @pl.when(me_f + step < n_fsdp)
    def _():
        arrived(me_f + step)

        @pl.when(me_f >= 1)
        def _():
            forward(me_f + step, 1, me_f - 1)


def line_sent(n_fsdp, step, sent):
    me_f = lax.axis_index("fsdp")

    @pl.when((me_f - step >= 0) & (me_f + 1 < n_fsdp))
    def _():
        sent(me_f - step, 0, me_f + 1)

    @pl.when((me_f + step < n_fsdp) & (me_f >= 1))
    def _():
        sent(me_f + step, 1, me_f - 1)


def flipped(index, bit):
    return index + bit * (1 - 2 * ((index // bit) % 2))


class SeqGather:
    def __init__(self, order, own, block, send_sem, recv_sem):
        self.order, self.own, self.block = order, own, block
        self.send_sem, self.recv_sem = send_sem, recv_sem
        self.me_s, self.me_f = lax.axis_index("seq"), lax.axis_index("fsdp")

    def held(self, stage):
        indices = [self.me_s]
        for bit in self.order[:stage]:
            indices = indices + [flipped(i, bit) for i in indices]
        return indices

    def copies(self, stage):
        partner = flipped(self.me_s, self.order[stage])
        result = []
        for count, index in enumerate(self.held(stage)):
            src = self.own if count == 0 else self.block(index)
            sem = self.send_sem.at[(1 << stage) - 1 + count]
            result.append(
                remote(src, self.block(index), sem, self.recv_sem.at[index], (partner, self.me_f))
            )
        return result

    def start(self, stage):
        for copy in self.copies(stage):
            copy.start()

    def wait(self, stage):
        for index in self.held(stage):
            index = flipped(index, self.order[stage])
            remote(
                self.block(index),
                self.block(index),
                self.send_sem.at[0],
                self.recv_sem.at[index],
                (self.me_s, self.me_f),
            ).wait_recv()

    def sent(self):
        for stage in range(len(self.order)):
            for copy in self.copies(stage):
                copy.wait_send()


def gather_orders(n_seq):
    bits = [1 << b for b in range(n_seq.bit_length() - 1)]
    return bits[1:] + bits[:1], bits[:0:-1] + bits[:1]


def block_places(routes, ids, capacity):
    count = routes.shape[1]
    match = jnp.zeros((ids.shape[0], count), F32)
    for k in range(routes.shape[0]):
        match = match + (routes[k : k + 1, :] == ids).astype(F32)
    row = lax.broadcasted_iota(jnp.int32, (count, count), 0)
    column = lax.broadcasted_iota(jnp.int32, (count, count), 1)
    rank = dot(match.astype(BF), (row < column).astype(BF), 1, 0)
    place = lax.broadcasted_iota(jnp.int32, (ids.shape[0], capacity, count), 1).astype(F32)
    hot = match[:, None, :] * (rank[:, None, :] == place).astype(F32)
    return hot.reshape(ids.shape[0] * capacity, count)


def first_kernel(
    n_seq,
    n_fsdp,
    pieces,
    split,
    capacity,
    owned,
    top,
    small,
    tokens,
    qkv,
    masked,
    lengths,
    small_all,
    gains,
    slot,
    qkv_all,
    masked_all,
    to_places,
    to_rows,
    counts,
    own_gains,
    send,
    own_sem,
    small_send,
    small_recv,
    qkv_send,
    qkv_recv,
    line_send,
    line_recv,
    token_send,
    token_recv,
    row_send,
    row_recv,
    row_own,
):
    me_s, me_f = lax.axis_index("seq"), lax.axis_index("fsdp")
    n = n_seq * n_fsdp
    me = me_s * n_fsdp + me_f
    head_width = qkv_all.shape[3] // 3
    width = head_width * n_seq
    half = tokens.shape[0] // 2
    orders = gather_orders(n_seq)
    stages = len(orders[0])

    def columns(owner, part):
        start = pl.multiple_of(part * width + owner * head_width, 128)
        return qkv.at[:, pl.ds(start, head_width)]

    def column_place(source, part):
        return qkv_all.at[source, me_f, :, pl.ds(part * head_width, head_width)]

    own = [
        pltpu.make_async_copy(small, small_all.at[me], own_sem.at[0]),
        pltpu.make_async_copy(tokens, slot.at[me_s], own_sem.at[1]),
    ] + [
        pltpu.make_async_copy(columns(me_s, part), column_place(me_s, part), own_sem.at[2 + part])
        for part in range(3)
    ]
    for copy in own:
        copy.start()

    def small_copy(i):
        other = (me + i) % n
        return remote(
            small,
            small_all.at[me],
            small_send.at[i],
            small_recv.at[me],
            (other // n_fsdp, other % n_fsdp),
        )

    def small_arrived(other):
        return remote(
            small,
            small_all.at[other],
            small_send.at[0],
            small_recv.at[other],
            (other // n_fsdp, other % n_fsdp),
        )

    def small_start(i, carry):
        small_copy(i).start()
        return carry

    lax.fori_loop(1, n, small_start, 0)

    def column_copy(i, part):
        other = (me_s + i) % n_seq
        return remote(
            columns(other, part),
            column_place(me_s, part),
            qkv_send.at[i, part],
            qkv_recv.at[me_s, part],
            (other, me_f),
        )

    for i in range(1, n_seq):
        for part in range(3):
            column_copy(i, part).start()

    flows = []
    for side in range(2):
        rows = pl.ds(side * half, half)
        flows.append(
            SeqGather(
                orders[side],
                tokens.at[rows],
                lambda index, rows=rows: slot.at[index, rows],
                token_send.at[side],
                token_recv.at[side],
            )
        )

    def point(stage):
        for flow in flows:
            if 0 < stage <= stages:
                flow.wait(stage - 1)
            if stage < stages:
                flow.start(stage)

    point(0)
    for copy in own:
        copy.wait()

    piece = lax.broadcasted_iota(jnp.int32, (n_seq * pieces, 1), 0)
    piece = ((piece // pieces) * n_fsdp + me_f) * pieces + piece % pieces
    ids = piece // split

    def row_copy(i, place):
        other = (me_s + i) % n_seq
        return remote(
            send.at[other], masked_all.at[place, :, me_f], row_send.at[i], row_recv.at[place], (other, me_f)
        )

    def own_row():
        return pltpu.make_async_copy(send.at[me_s], masked_all.at[me_s, :, me_f], row_own)

    def table(block):
        routes = small_all[me_s * n_fsdp + block, 8 : 8 + top, :].astype(F32).astype(jnp.int32)
        hot = block_places(routes, ids, capacity)
        to_places[block] = hot.astype(BF)
        to_rows[block] = hot.T.astype(BF)

    def scatter():
        def some(lanes):
            picked = dot(to_places[me_f], masked[:, lanes], 1, 0).astype(BF)
            send[:, :, :, lanes] = picked.reshape(n_seq, pieces, capacity, -1)

        chunked(width, 512, some)
        for i in range(1, n_seq):
            row_copy(i, me_s).start()
        own_row().start()

    def line_copy(part, step, block, way, to):
        place = qkv_all.at[part, block]
        return remote(
            place, place, line_send.at[part, way, step], line_recv.at[part, block], (me_s, to)
        )

    def line_first(part):
        @pl.when(me_f + 1 < n_fsdp)
        def _():
            line_copy(part, 0, me_f, 0, me_f + 1).start()

        @pl.when(me_f >= 1)
        def _():
            line_copy(part, 0, me_f, 1, me_f - 1).start()

    def column_arrived(i, carry):
        source = (me_s + i) % n_seq

        @pl.when(i > 0)
        def _():
            for part in range(3):
                remote(
                    columns(source, part),
                    column_place(source, part),
                    qkv_send.at[i, part],
                    qkv_recv.at[source, part],
                    (source, me_f),
                ).wait_recv()

        line_first(source)
        return carry

    lax.fori_loop(0, n_seq, column_arrived, 0)

    def column_step(step):
        def column_next(i, carry):
            part = (me_s + i) % n_seq
            line_step(
                n_fsdp,
                step,
                lambda block: line_copy(part, 0, block, 0, me_f).wait_recv(),
                lambda block, way, to: line_copy(part, step, block, way, to).start(),
            )
            return carry

        lax.fori_loop(0, n_seq, column_next, 0)

    point(1)
    table(me_f)
    for stage in range(2, stages + 1):
        point(stage)
    scatter()
    column_step(1)
    for i in range(1, n_fsdp):
        block = (me_f + i) % n_fsdp
        small_arrived(me_s * n_fsdp + block).wait_recv()
        table(block)
    for flow in flows:
        flow.sent()

    def small_wait(i, carry):
        other = (me + i) % n
        small_copy(i).wait_send()

        @pl.when(other // n_fsdp != me_s)
        def _():
            small_arrived(other).wait_recv()

        return carry

    lax.fori_loop(1, n, small_wait, 0)

    lane = lax.broadcasted_iota(jnp.int32, (8, 128), 1)
    each = 128 // owned
    for j in range(width // 128):
        total = jnp.zeros((8, 128), F32)
        for k in range(each):
            some = jnp.where(lane < owned, small_all[j * each + k, :8, :].astype(F32), 0.0)
            total = total + (pltpu.roll(some, k * owned, 1) if k else some)
        gains[:, j * 128 : (j + 1) * 128] = total
    own_gains[...] = gains[:, pl.ds(pl.multiple_of(me_s * head_width, 128), head_width)]

    all_ids = lax.broadcasted_iota(jnp.int32, (counts.shape[1], 1), 0)
    position = lax.broadcasted_iota(jnp.int32, (1, tokens.shape[0]), 1)

    def seen(device, sums):
        routes = small_all[device, 8 : 8 + top, :].astype(F32).astype(jnp.int32)
        match = jnp.zeros(sums.shape, F32)
        for k in range(top):
            match = match + (routes[k : k + 1, :] == all_ids).astype(F32)
        first = (device // n_fsdp) * tokens.shape[0]
        live = (position + first < lengths[device % n_fsdp]).astype(F32)
        return sums + match * live

    sums = jnp.zeros((counts.shape[1], tokens.shape[0]), F32)
    sums = lax.fori_loop(0, n, seen, sums)
    counts[...] = jnp.broadcast_to(jnp.sum(sums.T, axis=0, keepdims=True), counts.shape)

    for step in range(2, n_fsdp):
        column_step(step)

    def column_sent(i, carry):
        for part in range(3):
            column_copy(i, part).wait_send()
        return carry

    lax.fori_loop(1, n_seq, column_sent, 0)

    def line_done(part, carry):
        for step in range(n_fsdp):
            line_sent(
                n_fsdp,
                step,
                lambda block, way, to: line_copy(part, step, block, way, to).wait_send(),
            )
        return carry

    lax.fori_loop(0, n_seq, line_done, 0)
    own_row().wait()
    for i in range(1, n_seq):
        row_copy(i, me_s).wait_send()
        row_copy(i, (me_s + i) % n_seq).wait_recv()


def first_gather(
    small,
    tokens,
    qkv,
    masked,
    lengths,
    n_seq,
    n_fsdp,
    pieces,
    split,
    capacity,
    top,
    experts,
    collective_id,
):
    owned = qkv.shape[0]
    rows, width = tokens.shape
    head_width = width // n_seq
    n = n_seq * n_fsdp
    places_all = n_seq * pieces * capacity
    vmem = pl.BlockSpec(memory_space=pltpu.VMEM)
    any_space = pl.BlockSpec(memory_space=pl.ANY)
    dma = pltpu.SemaphoreType.DMA
    return pl.pallas_call(
        loading(
            functools.partial(first_kernel, n_seq, n_fsdp, pieces, split, capacity, owned, top),
            functools.partial(greet_all, n_seq, n_fsdp),
            4,
        ),
        out_shape=[
            jax.ShapeDtypeStruct((n,) + small.shape, BF),
            jax.ShapeDtypeStruct((8, width), F32),
            jax.ShapeDtypeStruct((n_seq,) + tokens.shape, BF),
            jax.ShapeDtypeStruct((n_seq, n_fsdp, owned, 3 * head_width), BF),
            jax.ShapeDtypeStruct((n_seq, pieces, n_fsdp, capacity, width), BF),
            jax.ShapeDtypeStruct((n_fsdp, places_all, rows), BF),
            jax.ShapeDtypeStruct((n_fsdp, rows, places_all), BF),
            jax.ShapeDtypeStruct((8, experts), F32),
            jax.ShapeDtypeStruct((8, head_width), F32),
        ],
        in_specs=[pl.BlockSpec(memory_space=pltpu.HBM)] * 4 + [pl.BlockSpec(memory_space=pltpu.SMEM)],
        out_specs=[vmem, vmem, any_space, any_space, any_space, vmem, vmem, vmem, vmem],
        scratch_shapes=[
            pltpu.VMEM((n_seq, pieces, capacity, width), BF),
            dma((5,)),
            dma((n,)),
            dma((n,)),
            dma((n_seq, 3)),
            dma((n_seq, 3)),
            dma((n_seq, 2, n_fsdp)),
            dma((n_seq, n_fsdp)),
            dma((2, n_seq - 1)),
            dma((2, n_seq)),
            dma((n_seq,)),
            dma((n_seq,)),
            dma,
        ]
        + load_scratch([small, tokens, qkv, masked]),
        compiler_params=pltpu.CompilerParams(
            collective_id=collective_id, has_side_effects=True, vmem_limit_bytes=62 << 20
        ),
        name="first_gather",
    )(small, tokens, qkv, masked, lengths)


def greet_seq(n_seq):
    me_s, me_f = lax.axis_index("seq"), lax.axis_index("fsdp")
    barrier = pltpu.get_barrier_semaphore()
    for i in range(1, n_seq):
        pl.semaphore_signal(
            barrier, inc=1, device_id=((me_s + i) % n_seq, me_f), device_id_type=MESH
        )
    pl.semaphore_wait(barrier, n_seq - 1)


class TermSum:
    def __init__(
        self, n_seq, n_fsdp, terms, seq_terms, fsdp_terms, seq_send, seq_recv, fsdp_send, fsdp_recv
    ):
        self.n_seq, self.n_fsdp, self.terms = n_seq, n_fsdp, terms
        self.seq_terms, self.fsdp_terms = seq_terms, fsdp_terms
        self.seq_send, self.seq_recv = seq_send, seq_recv
        self.fsdp_send, self.fsdp_recv = fsdp_send, fsdp_recv
        self.me_s, self.me_f = lax.axis_index("seq"), lax.axis_index("fsdp")

    def part(self, owner):
        columns = self.seq_terms.shape[2]
        return self.terms.at[:, pl.ds(pl.multiple_of(owner * columns, 128), columns)]

    def seq_copy(self, i, place):
        other = (self.me_s + i) % self.n_seq
        return remote(
            self.part(other),
            self.seq_terms.at[place],
            self.seq_send.at[i],
            self.seq_recv.at[place],
            (other, self.me_f),
        )

    def fsdp_copy(self, i, place):
        other = (self.me_f + i) % self.n_fsdp
        return remote(
            self.seq_terms.at[self.me_s],
            self.fsdp_terms.at[place],
            self.fsdp_send.at[i],
            self.fsdp_recv.at[place],
            (self.me_s, other),
        )

    def start_seq(self):
        for i in range(1, self.n_seq):
            self.seq_copy(i, self.me_s).start()

    def over_seq(self):
        result = self.part(self.me_s)[...]
        for i in range(1, self.n_seq):
            place = (self.me_s + i) % self.n_seq
            self.seq_copy(i, place).wait_recv()
            result = result + self.seq_terms[place]
        for i in range(1, self.n_seq):
            self.seq_copy(i, self.me_s).wait_send()
        return result

    def start_fsdp(self, more):
        self.seq_terms[self.me_s] = more + (self.over_seq() if self.terms is not None else 0.0)
        for i in range(1, self.n_fsdp):
            self.fsdp_copy(i, self.me_f).start()

    def finish(self):
        result = self.seq_terms[self.me_s]
        for i in range(1, self.n_fsdp):
            place = (self.me_f + i) % self.n_fsdp
            self.fsdp_copy(i, place).wait_recv()
            result = result + self.fsdp_terms[place]
        for i in range(1, self.n_fsdp):
            self.fsdp_copy(i, self.me_f).wait_send()
        return result


def term_scratch(n_seq, n_fsdp, shape):
    dma = pltpu.SemaphoreType.DMA
    return [
        pltpu.VMEM((n_seq,) + shape, F32),
        pltpu.VMEM((n_fsdp,) + shape, F32),
        dma((n_seq,)),
        dma((n_seq,)),
        dma((n_fsdp,)),
        dma((n_fsdp,)),
    ]


def gather_kernel(n_seq, n_fsdp, x, terms, out, total, own_sem, send_sem, recv_sem, *scratch):
    me_s = lax.axis_index("seq")
    half = x.shape[0] // 2
    own = pltpu.make_async_copy(x, out.at[me_s], own_sem)
    own.start()
    term_sum = TermSum(n_seq, n_fsdp, terms, scratch[0], None, *scratch[1:], None, None)
    greet_seq(n_seq)
    flows = []
    for side, order in enumerate(gather_orders(n_seq)):
        rows = pl.ds(side * half, half)
        flows.append(
            SeqGather(
                order,
                x.at[rows],
                lambda index, rows=rows: out.at[index, rows],
                send_sem.at[side],
                recv_sem.at[side],
            )
        )
    for stage in range(len(flows[0].order)):
        for flow in flows:
            flow.start(stage)
        if stage == 0:
            term_sum.start_seq()
        if stage == 1:
            total[...] = term_sum.over_seq()
        for flow in flows:
            flow.wait(stage)
    for flow in flows:
        flow.sent()
    own.wait()


def gather_seq(x, terms, n_seq, n_fsdp, collective_id):
    vmem = pl.BlockSpec(memory_space=pltpu.VMEM)
    dma = pltpu.SemaphoreType.DMA
    part = (terms.shape[0], terms.shape[1] // n_seq)
    return pl.pallas_call(
        functools.partial(gather_kernel, n_seq, n_fsdp),
        out_shape=[
            jax.ShapeDtypeStruct((n_seq,) + x.shape, x.dtype),
            jax.ShapeDtypeStruct(part, terms.dtype),
        ],
        in_specs=[vmem] * 2,
        out_specs=[vmem] * 2,
        scratch_shapes=[
            dma,
            dma((2, n_seq - 1)),
            dma((2, n_seq)),
            pltpu.VMEM((n_seq,) + part, F32),
            dma((n_seq,)),
            dma((n_seq,)),
        ],
        compiler_params=pltpu.CompilerParams(collective_id=collective_id, has_side_effects=True),
        cost_estimate=pl.CostEstimate(flops=0, bytes_accessed=1 << 26, transcendentals=0),
        name="gather_seq",
    )(x, terms)


class SeqReduce:
    def __init__(self, n_seq, a, w, w_dim, sums, got, send_sem, recv_sem):
        self.a, self.w, self.w_dim, self.sums, self.got = a, w, w_dim, sums, got
        self.send_sem, self.recv_sem = send_sem, recv_sem
        self.me_s, self.me_f = lax.axis_index("seq"), lax.axis_index("fsdp")
        self.orders = [order[-1:] + order[-2::-1] for order in gather_orders(n_seq)]
        self.stages = len(self.orders[0])
        self.half = sums.shape[1] // 2
        self.width = sums.shape[2]

    def combined(self, index, bits):
        indices = [index]
        for bit in bits:
            indices = indices + [flipped(i, bit) for i in indices]
        return indices

    def product(self, index):
        def some(columns):
            w = self.w[:, columns] if self.w_dim == 0 else self.w[columns, :]
            self.sums[index, :, columns] = dot(self.a[index], w, 1, self.w_dim).astype(BF)

        chunked(self.width, 512, some)

    def copy(self, stage, side, count, index):
        order = self.orders[side]
        slot = sum(1 << (self.stages - 1 - s) for s in range(stage)) + count
        rows = pl.ds(side * self.half, self.half)
        return remote(
            self.sums.at[index, rows],
            self.got.at[slot, rows],
            self.send_sem.at[side, slot],
            self.recv_sem.at[side, slot],
            (flipped(self.me_s, order[stage]), self.me_f),
        )

    def leaving(self, stage, side):
        order = self.orders[side]
        return self.combined(flipped(self.me_s, order[stage]), order[stage + 1 :])

    def start(self, stage):
        if stage == 0:
            for count, index in enumerate(self.leaving(0, 0)):
                self.product(index)
                for side in range(2):
                    self.copy(0, side, self.twin(count) if side == 1 else count, index).start()
            for index in self.combined(self.me_s, self.orders[0][1:]):
                self.product(index)
        else:
            for side in range(2):
                for count, index in enumerate(self.leaving(stage, side)):
                    self.copy(stage, side, count, index).start()

    def twin(self, count):
        first, second = self.orders[0][1:], self.orders[1][1:]
        place = 0
        for position, bit in enumerate(first):
            if (count >> position) & 1:
                place += 1 << second.index(bit)
        return place

    def finish(self, stage, last=None):
        for side in range(2):
            order = self.orders[side]
            rows = pl.ds(side * self.half, self.half)
            for count, index in enumerate(self.combined(self.me_s, order[stage + 1 :])):
                copy = self.copy(stage, side, count, index)
                copy.wait_recv()
                slot = sum(1 << (self.stages - 1 - s) for s in range(stage)) + count

                def some(columns):
                    total = self.sums[index, rows, columns].astype(F32)
                    total = total + self.got[slot, rows, columns].astype(F32)
                    if last is None:
                        self.sums[index, rows, columns] = total.astype(BF)
                    else:
                        last[rows, columns] = total

                chunked(self.width, 1024, some)

    def events(self, last):
        def leave(count, index):
            self.product(index)
            for side in range(2):
                self.copy(0, side, self.twin(count) if side == 1 else count, index).start()

        result = [
            (1, functools.partial(leave, count, index))
            for count, index in enumerate(self.leaving(0, 0))
        ]
        for index in self.combined(self.me_s, self.orders[0][1:]):
            result.append((1, functools.partial(self.product, index)))
        result.append((1, functools.partial(self.finish, 0, last if self.stages == 1 else None)))
        for stage in range(1, self.stages):
            result.append((0, functools.partial(self.start, stage)))
            result.append(
                (7, functools.partial(self.finish, stage, last if stage == self.stages - 1 else None))
            )
        return result

    def sent(self):
        for stage in range(self.stages):
            for side in range(2):
                for count, index in enumerate(self.leaving(stage, side)):
                    self.copy(stage, side, count, index).wait_send()


def reduce_scratch(n_seq, rows, width):
    dma = pltpu.SemaphoreType.DMA
    return [
        pltpu.VMEM((n_seq, rows, width), BF),
        pltpu.VMEM((n_seq - 1, rows, width), BF),
        dma((2, n_seq - 1)),
        dma((2, n_seq - 1)),
    ]


def reduce_kernel(n_seq, w_dim, a, w, out, *scratch):
    reduce = SeqReduce(n_seq, a, w, w_dim, *scratch)
    for stage in range(reduce.stages):
        reduce.start(stage)
        reduce.finish(stage, out if stage == reduce.stages - 1 else None)
    reduce.sent()


def product_reduced(a, w, w_dim, n_seq, collective_id):
    rows = a.shape[0] // n_seq
    width = w.shape[1 - w_dim]
    a = a.reshape(n_seq, rows, -1)
    return pl.pallas_call(
        loading(
            functools.partial(reduce_kernel, n_seq, w_dim),
            functools.partial(greet_seq, n_seq),
            2,
        ),
        out_shape=jax.ShapeDtypeStruct((rows, width), F32),
        in_specs=[pl.BlockSpec(memory_space=pltpu.HBM)] * 2,
        out_specs=pl.BlockSpec(memory_space=pltpu.VMEM),
        scratch_shapes=reduce_scratch(n_seq, rows, width) + load_scratch([a, w]),
        compiler_params=pltpu.CompilerParams(
            collective_id=collective_id, has_side_effects=True, vmem_limit_bytes=62 << 20
        ),
        name="product_reduced",
    )(a, w)


def last_kernel(
    n_seq,
    n_fsdp,
    a,
    w,
    normed,
    x,
    mid,
    gains,
    terms_in,
    heads,
    resid,
    ready,
    input_out,
    qkv_out,
    total,
    layer_out,
    *scratch,
):
    up, down, done, got, up_send, up_recv, down_send, down_recv, done_send, done_recv = scratch[:10]
    one, part, terms, seq_terms, fsdp_terms, seq_send, seq_recv, fsdp_send, fsdp_recv = scratch[10:19]
    me_s, me_f = lax.axis_index("seq"), lax.axis_index("fsdp")
    head_width = a.shape[2] // 3
    width = n_seq * head_width
    greet_lines(n_seq, n_fsdp)
    reduce = SeqReduce(n_seq, a, w, 1, *scratch[19:])
    term_sum = TermSum(
        n_seq,
        n_fsdp,
        terms,
        seq_terms,
        fsdp_terms,
        seq_send,
        seq_recv,
        fsdp_send,
        fsdp_recv,
    )

    def input_rows():
        tile = 32
        terms[...] = terms_in[...]

        def some(i, carry):
            rows = pl.ds(pl.multiple_of(i * tile, tile), tile)
            values = x[rows, :].astype(F32)
            scale = lax.rsqrt(jnp.mean(values * values, axis=-1, keepdims=True) + epsilon)
            grad = one[rows, :]
            weighted = grad * gains[0:1, :]
            mean = jnp.mean(weighted * values, axis=-1, keepdims=True)
            result = scale * weighted - values * (scale * scale * scale * mean)
            input_out[rows, :] = (mid[rows, :] + result).astype(BF)
            terms[0:1, :] += jnp.sum(grad * values * scale, axis=0, keepdims=True)
            layer = resid[rows, :]
            for block in range(n_fsdp):
                layer = layer + ready[block, rows, :].astype(F32)
            layer_out[rows, :] = layer.astype(BF)
            return carry

        lax.fori_loop(0, x.shape[0] // tile, some, 0)
        term_sum.start_seq()

    def line_copy(src, way, s, block):
        buffer, send, recv = (up, up_send, up_recv) if way == 0 else (down, down_send, down_recv)
        to = me_f + 1 if way == 0 else me_f - 1
        place = buffer.at[block, s]
        return remote(
            place if src is None else src, place, send.at[block, s], recv.at[block, s], (me_s, to)
        )

    def done_copy(i):
        s = (me_s + i) % n_seq
        return remote(done.at[s], got.at[me_s], done_send.at[i], done_recv.at[me_s], (s, me_f))

    def stream(way, number):
        buffer = up if way == 0 else down
        behind = me_f if way == 0 else n_fsdp - 1 - me_f
        turn, i = number // n_seq, number % n_seq
        s = (me_s + i) % n_seq
        block = n_fsdp - 1 - turn if way == 0 else turn
        ahead = n_fsdp - 1 - behind
        on_time = (number >= 0) & (turn < ahead)
        finishes_up = (me_f == n_fsdp - 1) | ((n_fsdp - 1 > 2 * me_f) & (me_f > 0))

        @pl.when(on_time & (behind == 0))
        def _():
            line_copy(part.at[s, block], way, s, block).start()

        @pl.when(on_time & (behind > 0))
        def _():
            line_copy(None, way, s, block).wait_recv()
            total = buffer[block, s].astype(F32) + part[s, block].astype(F32)
            buffer[block, s] = total.astype(BF)
            line_copy(None, way, s, block).start()

        @pl.when((number >= 0) & (turn == ahead) & (behind > 0))
        def _():
            line_copy(None, way, s, me_f).wait_recv()
            done[s] = (done[s].astype(F32) + buffer[me_f, s].astype(F32)).astype(BF)

            @pl.when(finishes_up if way == 0 else jnp.logical_not(finishes_up))
            def _():
                @pl.when(i > 0)
                def _():
                    done_copy(i).start()

    lag = 2
    slots = n_seq * (n_fsdp - 1) + lag * (n_fsdp - 1)

    owned = part.shape[2]
    stripe = n_fsdp * owned

    def make(s):
        lanes = pl.ds(pl.multiple_of(s * stripe, 128), stripe)
        every = a[...].reshape(-1, a.shape[2])
        product = dot(normed[:, lanes], every, 0, 0).astype(BF)
        for block in range(n_fsdp):
            part[s, block] = product[block * owned : (block + 1) * owned]
        done[s] = part[s, me_f]

    def run(first, last):
        def slot(number, carry):
            @pl.when(number < n_seq)
            def _():
                make((me_s + number) % n_seq)

            stream(0, number - lag * me_f)
            stream(1, number - lag * (n_fsdp - 1 - me_f))
            return carry

        lax.fori_loop(first, last, slot, 0)

    reached = 0
    for number, event in enumerate(
        reduce.events(one)
        + [(0, input_rows), (3, functools.partial(term_sum.start_fsdp, heads[...]))]
    ):
        run(reached, min(slots, reached + event[0]))
        reached = min(slots, reached + event[0])
        event[1]()
    run(reached, slots)

    def place(s, rows):
        for third in range(3):
            columns = pl.ds(pl.multiple_of(third * width + s * head_width, 128), head_width)
            qkv_out[:, columns] = rows[:, third * head_width : (third + 1) * head_width].astype(F32)

    place(me_s, done[me_s])

    def arrived(i, carry):
        s = (me_s + i) % n_seq
        remote(done.at[s], got.at[s], done_send.at[i], done_recv.at[s], (s, me_f)).wait_recv()
        place(s, got[s])
        return carry

    lax.fori_loop(1, n_seq, arrived, 0)

    def all_sent(i, carry):
        s = (me_s + i) % n_seq

        @pl.when(i > 0)
        def _():
            done_copy(i).wait_send()

        for j in range(n_fsdp - 1):

            @pl.when(me_f + j < n_fsdp - 1)
            def _():
                line_copy(None, 0, s, n_fsdp - 1 - j).wait_send()

            @pl.when(j < me_f)
            def _():
                line_copy(None, 1, s, j).wait_send()

        return carry

    lax.fori_loop(0, n_seq, all_sent, 0)
    reduce.sent()
    total[...] = term_sum.finish()


def last_reduce(
    a, w, normed, x, mid, gains, terms, heads, resid, ready, n_seq, n_fsdp, collective_id
):
    rows, width = a.shape[0] // n_seq, w.shape[0]
    columns = a.shape[1]
    owned = width // (n_seq * n_fsdp)
    vmem = pl.BlockSpec(memory_space=pltpu.VMEM)
    dma = pltpu.SemaphoreType.DMA
    return pl.pallas_call(
        functools.partial(last_kernel, n_seq, n_fsdp),
        out_shape=[
            jax.ShapeDtypeStruct((rows, width), BF),
            jax.ShapeDtypeStruct((owned, n_seq * columns), F32),
            jax.ShapeDtypeStruct(heads.shape, F32),
            jax.ShapeDtypeStruct((rows, width), BF),
        ],
        in_specs=[vmem] * 10,
        out_specs=[vmem] * 4,
        scratch_shapes=[
            pltpu.VMEM((n_fsdp, n_seq, owned, columns), BF),
            pltpu.VMEM((n_fsdp, n_seq, owned, columns), BF),
            pltpu.VMEM((n_seq, owned, columns), BF),
            pltpu.VMEM((n_seq, owned, columns), BF),
            dma((n_fsdp, n_seq)),
            dma((n_fsdp, n_seq)),
            dma((n_fsdp, n_seq)),
            dma((n_fsdp, n_seq)),
            dma((n_seq,)),
            dma((n_seq,)),
            pltpu.VMEM((rows, width), F32),
            pltpu.VMEM((n_seq, n_fsdp, owned, columns), BF),
            pltpu.VMEM(terms.shape, F32),
        ]
        + term_scratch(n_seq, n_fsdp, heads.shape)
        + reduce_scratch(n_seq, rows, width),
        compiler_params=pltpu.CompilerParams(
            collective_id=collective_id, has_side_effects=True, vmem_limit_bytes=60 << 20
        ),
        cost_estimate=pl.CostEstimate(flops=0, bytes_accessed=1 << 27, transcendentals=0),
        name="last_reduce",
    )(a.reshape(n_seq, rows, -1), w, normed, x, mid, gains, terms, heads, resid, ready)


def chunked(total, size, body):
    def step(i, carry):
        body(pl.ds(pl.multiple_of(i * size, size), size))
        return carry

    lax.fori_loop(0, total // size, step, 0)


def dispatch_kernel(n_seq, n_fsdp, pieces, x, hot, gates, masked, before, w_up, w_down, *refs):
    masked_all, columns_out, scaled = refs[:3]
    outs, hiddens, acts, results = (refs[3 + k * pieces : 3 + (k + 1) * pieces] for k in range(4))
    rest = refs[3 + 4 * pieces :]
    gates_out, gathered, gathered_two, send, total = rest[:5]
    own_sem, line_send, line_recv, row_send, row_recv, own_two, send_two, recv_two = rest[5:13]
    line_send_two, line_recv_two = rest[13:15]
    gate_exchange = Exchange(n_seq, n_fsdp, gates, gates_out, rest[15:])
    me_s, me_f = lax.axis_index("seq"), lax.axis_index("fsdp")
    width = x.shape[1]
    capacity = outs[0].shape[2]
    greet_all(n_seq, n_fsdp)

    def line_copy(step, block, way, to):
        src = x if step == 0 else gathered.at[block]
        return remote(
            src, gathered.at[block], line_send.at[way, step], line_recv.at[block], (me_s, to)
        )

    def line_two(step, block, way, to):
        src = masked if step == 0 else gathered_two.at[block]
        return remote(
            src,
            gathered_two.at[block],
            line_send_two.at[way, step],
            line_recv_two.at[block],
            (me_s, to),
        )

    def row_copy(block, i, piece, place):
        other = (me_s + i) % n_seq
        return remote(
            send.at[block, other, piece],
            outs[piece].at[place, block],
            row_send.at[block, i, piece],
            row_recv.at[place, block, piece],
            (other, me_f),
        )

    def own_copy(block, piece):
        return pltpu.make_async_copy(
            send.at[block, me_s, piece], outs[piece].at[me_s, block], own_sem.at[block, piece]
        )

    def masked_copy(block, i, place):
        other = (me_s + i) % n_seq
        return remote(
            send.at[block, other],
            masked_all.at[place, :, block],
            send_two.at[block, i],
            recv_two.at[place, block],
            (other, me_f),
        )

    def own_masked(block):
        return pltpu.make_async_copy(
            send.at[block, me_s], masked_all.at[me_s, :, block], own_two.at[block]
        )

    def pick(block, rows):
        def some(columns):
            picked = dot(hot[block], rows[:, columns], 1, 0).astype(BF)
            send[block, :, :, :, columns] = picked.reshape(n_seq, pieces, capacity, -1)

        chunked(width, 512, some)

    def scatter(block, rows):
        pick(block, rows)
        for i in range(1, n_seq):
            for piece in range(pieces):
                row_copy(block, i, piece, me_s).start()
        for piece in range(pieces):
            own_copy(block, piece).start()

    def scatter_masked(block):
        for piece in range(pieces):
            own_copy(block, piece).wait()
            for i in range(1, n_seq):
                row_copy(block, i, piece, me_s).wait_send()
        pick(block, gathered_two.at[block])
        for i in range(1, n_seq):
            masked_copy(block, i, me_s).start()
        own_masked(block).start()

    def around(step, act):
        @pl.when(me_f - step >= 0)
        def _():
            act(me_f - step)

        @pl.when(me_f + step < n_fsdp)
        def _():
            act(me_f + step)

    @pl.when(me_f + 1 < n_fsdp)
    def _():
        line_copy(0, me_f, 0, me_f + 1).start()

    @pl.when(me_f >= 1)
    def _():
        line_copy(0, me_f, 1, me_f - 1).start()

    scatter(me_f, x)
    gate_exchange.start()
    for step in range(1, n_fsdp):
        line_step(
            n_fsdp,
            step,
            lambda block: line_copy(1, block, 0, me_f).wait_recv(),
            lambda block, way, to: line_copy(step, block, way, to).start(),
        )
        around(step, lambda block: scatter(block, gathered.at[block]))

    @pl.when(me_f + 1 < n_fsdp)
    def _():
        line_two(0, me_f, 0, me_f + 1).start()

    @pl.when(me_f >= 1)
    def _():
        line_two(0, me_f, 1, me_f - 1).start()

    for step in range(1, n_fsdp):
        line_step(
            n_fsdp,
            step,
            lambda block: line_two(1, block, 0, me_f).wait_recv(),
            lambda block, way, to: line_two(step, block, way, to).start(),
        )
        around(step, scatter_masked)
    for step in range(n_fsdp):
        line_sent(
            n_fsdp, step, lambda block, way, to: line_copy(step, block, way, to).wait_send()
        )
        line_sent(n_fsdp, step, lambda block, way, to: line_two(step, block, way, to).wait_send())

    gate_exchange.finish()
    n = n_seq * n_fsdp
    for piece in range(pieces):
        lanes = lax.broadcasted_iota(jnp.int32, (n, capacity, 128), 2)
        place = lax.broadcasted_iota(jnp.int32, (n, capacity, 128), 1)
        values = jnp.broadcast_to(gates_out[:, piece : piece + 1, :], (n, capacity, 128))
        column = jnp.sum(jnp.where(lanes == place, values, 0.0), axis=2, keepdims=True)
        columns_out[piece] = column.reshape(n * capacity, 1)

    for piece in range(pieces):
        own_copy(me_f, piece).wait()
        for i in range(1, n_seq):
            row_copy(me_f, i, piece, me_s).wait_send()
    for piece in range(pieces):
        for block in range(n_fsdp):
            for i in range(1, n_seq):
                row_copy(block, i, piece, (me_s + i) % n_seq).wait_recv()

    ff = w_down.shape[1]
    tile = min(256, ff)
    steps = ff // tile
    spans = seq_tile(n_seq, n_fsdp * capacity, 3072 // n_fsdp)
    count = spans * n_fsdp * capacity
    for piece in range(pieces):

        def body(rows, w_gate, w_value, w_back, hidden, act, result, scaled_rows):
            step = pl.program_id(1)
            low = rows[...].reshape(count, width)
            gate = dot(low, w_gate[0], 1, 0)
            up = dot(low, w_value[0], 1, 0)
            hidden[0] = gate
            hidden[1] = up
            act[...] = (gate * jax.nn.sigmoid(gate) * up).astype(BF)
            product = dot(act[...], w_back[0], 1, 0)

            @pl.when(step == 0)
            def _():
                total[...] = product

            @pl.when(step > 0)
            def _():
                total[...] += product

            @pl.when(step == steps - 1)
            def _():
                start = pl.multiple_of(pl.program_id(0) * count, 8)
                column = columns_out[piece, pl.ds(start, count), :]
                result[...] = total[...].astype(BF)
                gated = (result[...].astype(F32) * column).astype(BF)
                scaled_rows[...] = gated.reshape(scaled_rows.shape)

        pltpu.emit_pipeline(
            body,
            grid=(n * capacity // count, steps),
            in_specs=[
                pl.BlockSpec((spans, n_fsdp, capacity, width), lambda r, i: (r, 0, 0, 0)),
                pl.BlockSpec((1, width, tile), lambda r, i: (piece, 0, i)),
                pl.BlockSpec((1, width, tile), lambda r, i: (piece, 0, steps + i)),
                pl.BlockSpec((1, tile, width), lambda r, i: (piece, i, 0)),
            ],
            out_specs=[
                pl.BlockSpec((2, count, tile), lambda r, i: (0, r, i)),
                pl.BlockSpec((count, tile), lambda r, i: (r, i)),
                pl.BlockSpec((count, width), lambda r, i: (r, 0)),
                pl.BlockSpec((spans, 1, n_fsdp, capacity, width), lambda r, i: (r, piece, 0, 0, 0)),
            ],
        )(
            outs[piece],
            w_up,
            w_up,
            w_down,
            hiddens[piece],
            acts[piece],
            results[piece],
            scaled,
        )

    for step in range(1, n_fsdp):
        around(step, lambda block: own_masked(block).wait())
    for step in range(1, n_fsdp):
        for i in range(1, n_seq):

            def done(block):
                masked_copy(block, i, me_s).wait_send()
                masked_copy(block, i, (me_s + i) % n_seq).wait_recv()

            around(step, done)


def dispatch_rows(
    x, hot, gates, masked, before, w_up, w_down, n_seq, n_fsdp, capacity, collective_id
):
    count, width = x.shape
    pieces, ff = w_down.shape[:2]
    rows = n_seq * n_fsdp * capacity
    tile_rows = seq_tile(n_seq, n_fsdp * capacity, 3072 // n_fsdp) * n_fsdp * capacity
    vmem = pl.BlockSpec(memory_space=pltpu.VMEM)
    any_space = pl.BlockSpec(memory_space=pl.ANY)
    dma = pltpu.SemaphoreType.DMA
    return pl.pallas_call(
        functools.partial(dispatch_kernel, n_seq, n_fsdp, pieces),
        out_shape=[
            jax.ShapeDtypeStruct(before.shape, BF),
            jax.ShapeDtypeStruct((pieces, rows, 1), F32),
            jax.ShapeDtypeStruct(before.shape, BF),
        ]
        + [jax.ShapeDtypeStruct((n_seq, n_fsdp, capacity, width), BF)] * pieces
        + [jax.ShapeDtypeStruct((2, rows, ff), F32)] * pieces
        + [jax.ShapeDtypeStruct((rows, ff), BF)] * pieces
        + [jax.ShapeDtypeStruct((rows, width), BF)] * pieces,
        in_specs=[vmem] * 4 + [any_space] * 3,
        out_specs=[any_space, vmem] + [any_space] * (1 + 4 * pieces),
        scratch_shapes=[
            pltpu.VMEM(gates.shape, F32),
            pltpu.VMEM((n_fsdp, count, width), BF),
            pltpu.VMEM((n_fsdp, count, width), BF),
            pltpu.VMEM((n_fsdp, n_seq, pieces, capacity, width), BF),
            pltpu.VMEM((tile_rows, width), F32),
            dma((n_fsdp, pieces)),
            dma((2, n_fsdp)),
            dma((n_fsdp,)),
            dma((n_fsdp, n_seq, pieces)),
            dma((n_seq, n_fsdp, pieces)),
            dma((n_fsdp,)),
            dma((n_fsdp, n_seq)),
            dma((n_seq, n_fsdp)),
            dma((2, n_fsdp)),
            dma((n_fsdp,)),
        ]
        + exchange_sems(n_seq * n_fsdp),
        input_output_aliases={4: 0},
        compiler_params=pltpu.CompilerParams(
            collective_id=collective_id, has_side_effects=True, vmem_limit_bytes=60 << 20
        ),
        name="dispatch_rows",
    )(x, hot, gates, masked, before, w_up, w_down)


def return_kernel(n_seq, n_fsdp, pieces, hot, gates, ready, w_up, *refs):
    grads = refs[:pieces]
    out, gates_out, ready_sums = refs[pieces : pieces + 3]
    rest = refs[pieces + 3 :]
    weights, hidden, rows, got, parts, sums, some_ready = rest[:7]
    w_sem, h_sem, ready_sem, own_sem, row_send, row_recv, part_send, part_recv = rest[7:15]
    gate_exchange = Exchange(n_seq, n_fsdp, gates, gates_out, rest[15:])
    me_s, me_f = lax.axis_index("seq"), lax.axis_index("fsdp")
    width = out.shape[1]
    capacity = rows.shape[3]
    ff = hidden.shape[5]
    tile = min(256, width)
    chunks = width // tile

    def weight_copy(piece, chunk):
        lines = pl.ds(pl.multiple_of(chunk * tile, tile), tile)
        return pltpu.make_async_copy(
            w_up.at[piece, lines], weights.at[piece, lines], w_sem.at[piece, chunk]
        )

    def hidden_copy(piece):
        return pltpu.make_async_copy(grads[piece], hidden.at[piece], h_sem.at[piece])

    def ready_copy(block):
        return pltpu.make_async_copy(
            ready.at[:, :, block], some_ready.at[block % 2], ready_sem.at[block % 2]
        )

    def row_copy(block, i, piece, place):
        other = (me_s + i) % n_seq
        return remote(
            rows.at[block, other, piece],
            got.at[block, place, piece],
            row_send.at[block, i, piece],
            row_recv.at[block, place, piece],
            (other, me_f),
        )

    def own_copy(block, piece):
        return pltpu.make_async_copy(
            rows.at[block, me_s, piece], got.at[block, me_s, piece], own_sem.at[block, piece]
        )

    def part_copy(j):
        block = (me_f + j) % n_fsdp
        return remote(
            parts.at[block], sums.at[me_f], part_send.at[j], part_recv.at[me_f], (me_s, block)
        )

    for piece in range(pieces):
        hidden_copy(piece).start()

        def begin(chunk, carry):
            weight_copy(piece, chunk).start()
            return carry

        lax.fori_loop(0, chunks, begin, 0)
    for block in range(min(2, n_fsdp)):
        ready_copy(block).start()
    greet_all(n_seq, n_fsdp)
    gate_exchange.start()

    def compute(j):
        block = (me_f + j) % n_fsdp
        for piece in range(pieces):
            if j == 1:
                hidden_copy(piece).wait()
            gate_grad = hidden[piece, 0, :, block].reshape(-1, ff)
            up_grad = hidden[piece, 1, :, block].reshape(-1, ff)

            def some(chunk, carry):
                if j == 1:
                    weight_copy(piece, chunk).wait()
                lines = pl.ds(pl.multiple_of(chunk * tile, tile), tile)
                total = dot(gate_grad, weights[piece, lines, :ff], 1, 1)
                total = total + dot(up_grad, weights[piece, lines, ff:], 1, 1)
                rows[block, :, piece, :, lines] = total.astype(BF).reshape(n_seq, capacity, -1)
                return carry

            lax.fori_loop(0, chunks, some, 0)
            for i in range(1, n_seq):
                row_copy(block, i, piece, me_s).start()
            own_copy(block, piece).start()

    def finish(j):
        block = (me_f + j) % n_fsdp
        for piece in range(pieces):
            own_copy(block, piece).wait()
            for i in range(1, n_seq):
                row_copy(block, i, piece, (me_s + i) % n_seq).wait_recv()

        def some(columns):
            arrived = got[block, :, :, :, columns].reshape(n_seq * pieces * capacity, -1)
            total = dot(hot[block], arrived, 1, 0)
            if j < n_fsdp:
                parts[block, :, columns] = total.astype(BF)
            else:
                out[:, columns] = total

        chunked(width, 512, some)
        if j < n_fsdp:
            part_copy(j).start()

    def sum_ready(block):
        ready_copy(block).wait()

        def some(columns):
            arrived = some_ready[block % 2, :, :, :, columns]
            arrived = arrived.reshape(n_seq * pieces * capacity, -1)
            ready_sums[block, :, columns] = dot(hot[block], arrived, 1, 0).astype(BF)

        chunked(width, 512, some)
        if block + 2 < n_fsdp:
            ready_copy(block + 2).start()

    for j in range(1, n_fsdp + 1):
        compute(j)
        if j >= 3:
            finish(j - 2)
    for block in range(n_fsdp):
        sum_ready(block)
    for j in range(max(1, n_fsdp - 1), n_fsdp + 1):
        finish(j)
    for j in range(1, n_fsdp):
        source = (me_f + n_fsdp - j) % n_fsdp
        remote(
            parts.at[source], sums.at[source], part_send.at[j], part_recv.at[source], (me_s, source)
        ).wait_recv()

    def add(columns):
        total = out[:, columns]
        for j in range(1, n_fsdp):
            total = total + sums[(me_f + j) % n_fsdp, :, columns].astype(F32)
        out[:, columns] = total

    chunked(width, 512, add)
    for j in range(1, n_fsdp):
        part_copy(j).wait_send()
    for block in range(n_fsdp):
        for piece in range(pieces):
            for i in range(1, n_seq):
                row_copy(block, i, piece, me_s).wait_send()
    gate_exchange.finish()


def return_rows(grads, w_up, hot, gates, ready, n_seq, n_fsdp, collective_id):
    pieces, width = w_up.shape[:2]
    ff = w_up.shape[2] // 2
    count = hot.shape[1]
    capacity = ready.shape[3]
    vmem = pl.BlockSpec(memory_space=pltpu.VMEM)
    any_space = pl.BlockSpec(memory_space=pl.ANY)
    dma = pltpu.SemaphoreType.DMA
    return pl.pallas_call(
        functools.partial(return_kernel, n_seq, n_fsdp, pieces),
        out_shape=[
            jax.ShapeDtypeStruct((count, width), F32),
            jax.ShapeDtypeStruct(gates.shape, F32),
            jax.ShapeDtypeStruct((n_fsdp, count, width), BF),
        ],
        in_specs=[vmem, vmem, any_space, any_space] + [any_space] * pieces,
        out_specs=[vmem] * 3,
        scratch_shapes=[
            pltpu.VMEM(w_up.shape, BF),
            pltpu.VMEM((pieces, 2, n_seq, n_fsdp, capacity, ff), BF),
            pltpu.VMEM((n_fsdp, n_seq, pieces, capacity, width), BF),
            pltpu.VMEM((n_fsdp, n_seq, pieces, capacity, width), BF),
            pltpu.VMEM((n_fsdp, count, width), BF),
            pltpu.VMEM((n_fsdp, count, width), BF),
            pltpu.VMEM((2, n_seq, pieces, capacity, width), BF),
            dma((pieces, width // min(256, width))),
            dma((pieces,)),
            dma((2,)),
            dma((n_fsdp, pieces)),
            dma((n_fsdp, n_seq, pieces)),
            dma((n_fsdp, n_seq, pieces)),
            dma((n_fsdp,)),
            dma((n_fsdp,)),
        ]
        + exchange_sems(n_seq * n_fsdp),
        compiler_params=pltpu.CompilerParams(
            collective_id=collective_id, has_side_effects=True, vmem_limit_bytes=60 << 20
        ),
        name="return_rows",
    )(hot, gates, ready, w_up, *grads)


def weight_grad_kernel(a, b, *refs):
    parts, _, n = b.shape
    for part in range(parts):
        refs[-1][0, :, part * n : (part + 1) * n] = dot(a[...], b[part], 0, 0)


def weight_grad(a, b, whole, piece, pieces):
    rows, m = a.shape
    parts, _, n = b.shape
    tile = min(256, m)
    more = [] if whole is None else [whole]
    return pl.pallas_call(
        weight_grad_kernel,
        out_shape=jax.ShapeDtypeStruct((pieces, m, n * parts), F32),
        grid=(m // tile,),
        in_specs=[
            pl.BlockSpec((rows, tile), lambda i: (0, i)),
            pl.BlockSpec((parts, rows, n), lambda i: (0, 0, 0)),
        ]
        + [pl.BlockSpec(memory_space=pl.ANY)] * len(more),
        out_specs=pl.BlockSpec((1, tile, n * parts), lambda i: (piece, i, 0)),
        input_output_aliases={2: 0} if more else {},
        cost_estimate=pl.CostEstimate(
            flops=2 * rows * m * n * parts,
            bytes_accessed=4 * m * n * parts,
            transcendentals=0,
        ),
        name="weight_grad",
    )(a, b, *more)


def seq_tile(n_seq, rows_each, most=1024):
    tile = n_seq
    while tile > 1 and (tile * rows_each > most or n_seq % tile):
        tile -= 1
    return tile


def expert_backward_kernel(masked, gates, piece_out, hidden, w_down, out, grad, inner, partial):
    @pl.when(pl.program_id(1) == 0)
    def _():
        partial[...] = jnp.zeros_like(partial)

        def some(columns):
            low = masked[:, 0, :, :, columns].reshape(grad.shape[0], -1).astype(F32)
            grad[:, columns] = (low * gates[...]).astype(BF)
            product = low * piece_out[:, columns].astype(F32)
            for i in range(product.shape[1] // 128):
                partial[...] += product[:, i * 128 : (i + 1) * 128]

        chunked(grad.shape[1], 512, some)
        sums = jnp.sum(partial[...].T, axis=0, keepdims=True)
        inner[...] = jnp.broadcast_to(sums, inner.shape)

    act_grad = dot(grad[...], w_down[0], 1, 1)
    gate, up = hidden[0], hidden[1]
    sigmoid = jax.nn.sigmoid(gate)
    out[0] = (act_grad * up * sigmoid * (1.0 + gate * (1.0 - sigmoid))).astype(BF)
    out[1] = (act_grad * gate * sigmoid).astype(BF)


def expert_backward(masked, gates, piece_out, hidden, w_down, piece):
    rows, width = piece_out.shape
    ff = w_down.shape[1]
    n_seq, _, n_fsdp, capacity, _ = masked.shape
    tile = min(256, ff)
    spans = seq_tile(n_seq, n_fsdp * capacity)
    count = spans * n_fsdp * capacity
    part = pl.BlockSpec((2, count, tile), lambda r, i: (0, r, i))
    fixed = lambda r, i: (r, 0)
    return pl.pallas_call(
        expert_backward_kernel,
        out_shape=[
            jax.ShapeDtypeStruct((2, rows, ff), BF),
            jax.ShapeDtypeStruct((rows, width), BF),
            jax.ShapeDtypeStruct((8, rows), F32),
        ],
        grid=(rows // count, ff // tile),
        in_specs=[
            pl.BlockSpec((spans, 1, n_fsdp, capacity, width), lambda r, i: (r, piece, 0, 0, 0)),
            pl.BlockSpec((count, 1), fixed),
            pl.BlockSpec((count, width), fixed),
            part,
            pl.BlockSpec((1, tile, width), lambda r, i: (piece, i, 0)),
        ],
        out_specs=[
            part,
            pl.BlockSpec((count, width), fixed),
            pl.BlockSpec((8, count), lambda r, i: (0, r)),
        ],
        scratch_shapes=[pltpu.VMEM((count, 128), F32)],
        compiler_params=pltpu.CompilerParams(vmem_limit_bytes=62 << 20),
        cost_estimate=pl.CostEstimate(
            flops=2 * rows * width * ff, bytes_accessed=12 * rows * ff, transcendentals=rows * ff
        ),
        name="expert_backward",
    )(masked, gates, piece_out, hidden, w_down)


class SeqShare:
    def __init__(self, n_seq, own, every, send_sem, recv_sem):
        self.n_seq, self.own, self.every = n_seq, own, every
        self.send_sem, self.recv_sem = send_sem, recv_sem
        self.me_s, self.me_f = lax.axis_index("seq"), lax.axis_index("fsdp")

    def copy(self, i, place):
        other = (self.me_s + i) % self.n_seq
        return remote(
            self.own,
            self.every.at[place],
            self.send_sem.at[i],
            self.recv_sem.at[place],
            (other, self.me_f),
        )

    def total(self):
        for i in range(1, self.n_seq):
            self.copy(i, self.me_s).start()
        total = self.own[...]
        for i in range(1, self.n_seq):
            place = (self.me_s + i) % self.n_seq
            self.copy(i, place).wait_recv()
            total = total + self.every[place]
        for i in range(1, self.n_seq):
            self.copy(i, self.me_s).wait_send()
        return total


def share_scratch(n_seq, shape):
    dma = pltpu.SemaphoreType.DMA
    return [pltpu.VMEM(shape, F32), pltpu.VMEM((n_seq,) + shape, F32), dma((n_seq,)), dma((n_seq,))]


def row_sums(values):
    ones = jnp.ones((8, values.shape[1]), F32)
    return lax.dot_general(
        ones,
        values,
        (((1,), (1,)), ((), ())),
        preferred_element_type=F32,
        precision=lax.Precision.HIGHEST,
    )


def front_kernel(n_seq, x, gain, w, normed_out, raw_out, totals, normed, raw, sems, *scratch):
    share = SeqShare(n_seq, *scratch)
    head_width = w.shape[1] // 3
    tile = 256

    def some(i, carry):
        rows = pl.ds(pl.multiple_of(i * tile, tile), tile)
        values = x[rows, :].astype(F32)
        scale = lax.rsqrt(jnp.mean(values * values, axis=-1, keepdims=True) + epsilon)
        low = (values * scale * gain[0:1, :]).astype(BF)
        normed[rows, :] = low
        result = dot(low, w[...], 1, 0)
        raw[rows, :] = result
        for copy in away(i):
            copy.start()
        for part in range(2):
            piece = result[:, part * head_width : (part + 1) * head_width]
            share.own[part : part + 1, rows] = row_sums(piece * piece)[0:1]
        return carry

    def away(i):
        rows = pl.ds(pl.multiple_of(i * tile, tile), tile)
        return [
            pltpu.make_async_copy(normed.at[rows], normed_out.at[rows], sems.at[0, i]),
            pltpu.make_async_copy(raw.at[rows], raw_out.at[rows], sems.at[1, i]),
        ]

    def gone(i, carry):
        for copy in away(i):
            copy.wait()
        return carry

    share.own[...] = jnp.zeros_like(share.own)
    lax.fori_loop(0, x.shape[0] // tile, some, 0)
    totals[...] = share.total()
    lax.fori_loop(0, x.shape[0] // tile, gone, 0)


def front(x, gains, w, n_seq, collective_id):
    rows, width = x.shape
    vmem = pl.BlockSpec(memory_space=pltpu.VMEM)
    hbm = pl.BlockSpec(memory_space=pltpu.HBM)
    return pl.pallas_call(
        loading(functools.partial(front_kernel, n_seq), functools.partial(greet_seq, n_seq), 3),
        out_shape=[
            jax.ShapeDtypeStruct((rows, width), BF),
            jax.ShapeDtypeStruct((rows, w.shape[1]), F32),
            jax.ShapeDtypeStruct((8, rows), F32),
        ],
        in_specs=[hbm] * 3,
        out_specs=[hbm, hbm, vmem],
        scratch_shapes=[
            pltpu.VMEM((rows, width), BF),
            pltpu.VMEM((rows, w.shape[1]), F32),
            pltpu.SemaphoreType.DMA((2, rows // 256)),
        ]
        + share_scratch(n_seq, (8, rows))
        + load_scratch([x, gains, w]),
        compiler_params=pltpu.CompilerParams(
            collective_id=collective_id, has_side_effects=True, vmem_limit_bytes=62 << 20
        ),
        name="front",
    )(x, gains, w)


def column_rms(sums, part, width):
    return lax.rsqrt(sums.T[:, part : part + 1] / width + epsilon)


def turned(values, cosine, sine):
    return values * cosine + pltpu.roll(values, values.shape[1] // 2, 1) * sine


def softmax_columns(k, q, length, scaling):
    scores = dot(k, q, 1, 1) * scaling
    key = lax.broadcasted_iota(jnp.int32, scores.shape, 0)
    scores = jnp.where(key < length, scores, -1e30)
    weights = jnp.exp(scores - jnp.max(scores, axis=0, keepdims=True))
    return weights / jnp.sum(weights, axis=0, keepdims=True)


def attend_kernel(
    width,
    length,
    raw_q,
    raw_k,
    raw_v,
    q_sums,
    k_sums,
    gain,
    q_cos,
    q_sin,
    k_cos,
    k_sin,
    o_ref,
    q_ref,
    k_ref,
    v_ref,
):
    scaling = raw_q.shape[1] ** (-0.5)

    @pl.when(pl.program_id(1) == 0)
    def _():
        key = raw_k[...] * column_rms(k_sums[...], 1, width) * gain[2:3, :]
        k_ref[...] = turned(key, k_cos[...], k_sin[...]).astype(BF)
        v_ref[...] = raw_v[...].astype(BF)

    query = raw_q[...] * column_rms(q_sums[...], 0, width) * gain[1:2, :]
    query = turned(query, q_cos[...], q_sin[...]).astype(BF)
    q_ref[...] = query
    probs = softmax_columns(k_ref[...], query, length[0], scaling).astype(BF)
    o_ref[...] = dot(v_ref[...], probs, 0, 0).T.astype(BF)


def attend(raw, totals, gains, cosine, sine, length, block, width):
    slot_len, head_width = raw.shape[0], raw.shape[1] // 3
    hd = cosine.shape[1]
    heads = head_width // hd
    rows = lambda shift: pl.BlockSpec((block, hd), lambda h, i, n: (i, shift + h))
    full = lambda shift: pl.BlockSpec((slot_len, hd), lambda h, i, n: (0, shift + h))
    table = pl.BlockSpec((block, hd), lambda h, i, n: (i, 0))
    whole_table = pl.BlockSpec((slot_len, hd), lambda h, i, n: (0, 0))
    return pl.pallas_call(
        functools.partial(attend_kernel, width),
        out_shape=[jax.ShapeDtypeStruct((slot_len, head_width), BF)] * 4,
        grid_spec=pltpu.PrefetchScalarGridSpec(
            num_scalar_prefetch=1,
            grid=(heads, slot_len // block),
            in_specs=[
                rows(0),
                full(heads),
                full(2 * heads),
                pl.BlockSpec((8, block), lambda h, i, n: (0, i)),
                pl.BlockSpec((8, slot_len), lambda h, i, n: (0, 0)),
                pl.BlockSpec((8, hd), lambda h, i, n: (0, h)),
                table,
                table,
                whole_table,
                whole_table,
            ],
            out_specs=[rows(0), rows(0), full(0), full(0)],
        ),
        cost_estimate=pl.CostEstimate(
            flops=4 * heads * slot_len * slot_len * hd, bytes_accessed=1 << 23, transcendentals=0
        ),
        compiler_params=pltpu.CompilerParams(vmem_limit_bytes=62 << 20),
        name="attend",
    )(length, raw, raw, raw, totals, totals, gains, cosine, sine, cosine, sine)


def attend_back_kernel(
    width,
    length,
    q_ref,
    k_ref,
    v_ref,
    g_ref,
    raw_q,
    raw_k,
    q_sums,
    k_sums,
    gain,
    q_cos,
    q_sin,
    k_cos,
    k_sin,
    dq_ref,
    dk_ref,
    dv_ref,
    dots,
    gain_out,
    dk_sum,
    dv_sum,
):
    head, step = pl.program_id(0), pl.program_id(1)
    last = step == pl.num_programs(1) - 1
    block, hd = q_ref.shape
    scaling = hd ** (-0.5)

    @pl.when(step == 0)
    def _():
        dk_sum[...] = jnp.zeros_like(dk_sum)
        dv_sum[...] = jnp.zeros_like(dv_sum)
        gain_out[...] = jnp.zeros_like(gain_out)

        @pl.when(head == 0)
        def _():
            dots[...] = jnp.zeros_like(dots)

    q, k, v, g = q_ref[...], k_ref[...], v_ref[...], g_ref[...]
    probs = softmax_columns(k, q, length[0], scaling)
    dv_sum[...] += dot(probs.astype(BF), g, 1, 0)
    weights_grad = dot(v, g, 1, 1)
    inner = jnp.sum(probs * weights_grad, axis=0, keepdims=True)
    score_grad = (probs * (weights_grad - inner) * scaling).astype(BF)
    dk_sum[...] += dot(score_grad, q, 1, 0)
    query_grad = dot(k, score_grad, 0, 0).T.astype(BF).astype(F32)
    query_in = turned(query_grad, q_cos[...], -q_sin[...])
    dq_ref[...] = query_in
    product = query_in * raw_q[...]
    rows = pl.ds(pl.multiple_of(step * block, block), block)
    dots[0:1, rows] += row_sums(product * gain[1:2, :])[0:1]
    gain_out[0:1, :] += jnp.sum(
        product * column_rms(q_sums[...], 0, width), axis=0, keepdims=True
    )

    @pl.when(last)
    def _():
        key_in = turned(dk_sum[...].astype(BF).astype(F32), k_cos[...], -k_sin[...])
        dk_ref[...] = key_in
        dv_ref[...] = dv_sum[...].astype(BF)
        product = key_in * raw_k[...]
        dots[1:2, :] += row_sums(product * gain[2:3, :])[0:1]
        gain_out[1:2, :] = jnp.sum(
            product * column_rms(k_sums[...], 1, width), axis=0, keepdims=True
        )


def attend_back(query, key, value, grad, raw, totals, gains, cosine, sine, length, block, width):
    slot_len, head_width = query.shape
    hd = cosine.shape[1]
    heads = head_width // hd
    rows = pl.BlockSpec((block, hd), lambda h, i, n: (i, h))
    full = lambda shift: pl.BlockSpec((slot_len, hd), lambda h, i, n: (0, shift + h))
    table = pl.BlockSpec((block, hd), lambda h, i, n: (i, 0))
    whole_table = pl.BlockSpec((slot_len, hd), lambda h, i, n: (0, 0))
    return pl.pallas_call(
        functools.partial(attend_back_kernel, width),
        out_shape=[
            jax.ShapeDtypeStruct(query.shape, F32),
            jax.ShapeDtypeStruct(query.shape, F32),
            jax.ShapeDtypeStruct(query.shape, BF),
            jax.ShapeDtypeStruct((8, slot_len), F32),
            jax.ShapeDtypeStruct((8, head_width), F32),
        ],
        grid_spec=pltpu.PrefetchScalarGridSpec(
            num_scalar_prefetch=1,
            grid=(heads, slot_len // block),
            in_specs=[
                rows,
                full(0),
                full(0),
                rows,
                rows,
                full(heads),
                pl.BlockSpec((8, block), lambda h, i, n: (0, i)),
                pl.BlockSpec((8, slot_len), lambda h, i, n: (0, 0)),
                pl.BlockSpec((8, hd), lambda h, i, n: (0, h)),
                table,
                table,
                whole_table,
                whole_table,
            ],
            out_specs=[
                rows,
                full(0),
                full(0),
                pl.BlockSpec((8, slot_len), lambda h, i, n: (0, 0)),
                pl.BlockSpec((8, hd), lambda h, i, n: (0, h)),
            ],
            scratch_shapes=[pltpu.VMEM((slot_len, hd), F32), pltpu.VMEM((slot_len, hd), F32)],
        ),
        cost_estimate=pl.CostEstimate(
            flops=20 * heads * slot_len * slot_len * hd, bytes_accessed=1 << 24, transcendentals=0
        ),
        compiler_params=pltpu.CompilerParams(vmem_limit_bytes=62 << 20),
        name="attend_back",
    )(
        length,
        query,
        key,
        value,
        grad,
        raw,
        raw,
        totals,
        totals,
        gains,
        cosine,
        sine,
        cosine,
        sine,
    )


def raw_back_kernel(
    n_seq, n_fsdp, width, dq, dk, dv, raw, totals, gain, dots, terms, out, terms_out, *scratch
):
    share = SeqShare(n_seq, *scratch[:4])
    term_sum = TermSum(n_seq, n_fsdp, None, *scratch[4:6], None, None, *scratch[6:])
    term_sum.start_fsdp(terms[...])
    head_width = dq.shape[1]
    share.own[...] = dots[...]
    share.own[...] = share.total()
    tile = 256

    def some(i, carry):
        rows = pl.ds(pl.multiple_of(i * tile, tile), tile)
        inner = share.own[:, rows].T / width
        for part, grad in enumerate((dq, dk)):
            columns = slice(part * head_width, (part + 1) * head_width)
            scale = column_rms(totals[:, rows], part, width)
            weighted = grad[rows, :] * gain[part + 1 : part + 2, :]
            cube = scale * scale * scale
            result = scale * weighted - raw[rows, columns] * (cube * inner[:, part : part + 1])
            out[rows, columns] = result.astype(BF)
        out[rows, 2 * head_width :] = dv[rows, :]
        return carry

    lax.fori_loop(0, dq.shape[0] // tile, some, 0)
    terms_out[...] = term_sum.finish()


def raw_back(dq, dk, dv, raw, totals, gains, dots, terms, n_seq, n_fsdp, width, collective_id):
    vmem = pl.BlockSpec(memory_space=pltpu.VMEM)
    dma = pltpu.SemaphoreType.DMA
    return pl.pallas_call(
        loading(
            functools.partial(raw_back_kernel, n_seq, n_fsdp, width),
            functools.partial(greet_lines, n_seq, n_fsdp),
            8,
        ),
        out_shape=[
            jax.ShapeDtypeStruct(raw.shape, BF),
            jax.ShapeDtypeStruct(terms.shape, F32),
        ],
        in_specs=[pl.BlockSpec(memory_space=pltpu.HBM)] * 8,
        out_specs=[vmem] * 2,
        scratch_shapes=share_scratch(n_seq, dots.shape)
        + [
            pltpu.VMEM((n_seq,) + terms.shape, F32),
            pltpu.VMEM((n_fsdp,) + terms.shape, F32),
            dma((n_fsdp,)),
            dma((n_fsdp,)),
        ]
        + load_scratch([dq, dk, dv, raw, totals, gains, dots, terms]),
        compiler_params=pltpu.CompilerParams(
            collective_id=collective_id, has_side_effects=True, vmem_limit_bytes=62 << 20
        ),
        name="raw_back",
    )(dq, dk, dv, raw, totals, gains, dots, terms)


def rope_tables(count, head_dim):
    half = head_dim // 2
    frequency = rope_base ** (-np.arange(half, dtype=np.float64) * 2.0 / head_dim)
    angles = np.arange(count, dtype=np.float64)[:, None] * frequency[None, :]
    cosine, sine = np.cos(angles), np.sin(angles)
    both = np.concatenate([cosine, cosine], axis=1), np.concatenate([-sine, sine], axis=1)
    return tuple(jnp.asarray(table, F32) for table in both)


def places(block_routes, experts, capacity):
    count = block_routes.shape[0]
    match = (block_routes[:, :, None] == experts[None, None, :]).astype(F32).sum(axis=1)
    lower = jnp.tril(jnp.ones((count, count), BF), -1)
    rank = dot(lower, match.astype(BF), 1, 0)
    place = jnp.arange(capacity, dtype=F32)
    return match[:, :, None] * (rank[:, :, None] == place[None, None, :]).astype(F32)


def local(
    tokens,
    cotangent,
    lengths,
    routes,
    norm_gains,
    qkv_weight,
    proj_weight,
    router_weight,
    expert_up,
    expert_down,
):
    n_seq, n_fsdp = lax.axis_size("seq"), lax.axis_size("fsdp")
    n_dev = n_seq * n_fsdp
    me_s, me_f = lax.axis_index("seq"), lax.axis_index("fsdp")
    shard_len, width = tokens.shape[1], tokens.shape[2]
    slot_len = shard_len * n_seq
    experts = router_weight.shape[1]
    top_count = routes.shape[2]
    capacity = 3 * shard_len * top_count // (2 * experts)
    piece_ff = expert_down.shape[1]
    pieces_dev = expert_up.shape[0]
    split = FF // piece_ff
    head_dim = width // HEADS
    head_width = width // n_seq
    heads_dev = HEADS // n_seq
    owned = qkv_weight.shape[0]
    block = min(512, slot_len)
    length = lax.dynamic_slice_in_dim(lengths, me_f, 1)
    valid_total = jnp.sum(lengths).astype(F32).reshape(1)
    positions = me_s * shard_len + jnp.arange(shard_len, dtype=jnp.int32)
    row_valid = (positions < length[0]).astype(F32)
    local_routes = routes[0]
    push_all = functools.partial(push, n_seq=n_seq, n_fsdp=n_fsdp, scope="all")
    push_seq = functools.partial(push, n_seq=n_seq, n_fsdp=n_fsdp, scope="seq")

    masked_low = jnp.where(row_valid[:, None] > 0, cotangent[0], jnp.zeros((), BF))
    own_small = jnp.concatenate(
        [
            jnp.pad(norm_gains, ((0, 4), (0, 128 - owned))),
            local_routes.T.astype(BF),
            rows_of(router_weight.reshape(-1), 16),
        ]
    )
    small, gains, slot_tokens, qkv_local, cot_all, to_places, to_rows, *more = first_gather(
        own_small,
        tokens[0],
        qkv_weight,
        masked_low,
        lengths,
        n_seq,
        n_fsdp,
        pieces_dev,
        split,
        capacity,
        top_count,
        experts,
        collective_id=0,
    )
    counts, own_gains = more
    slot_tokens = slot_tokens.reshape(slot_len, width)
    qkv_local = qkv_local.reshape(width, 3 * head_width)
    router = small[:, 8 + top_count :].reshape(n_dev, -1)[:, : owned * experts]
    router = router.reshape(width, experts)
    proj_later = lax.optimization_barrier((proj_weight, slot_tokens))[0]
    proj_rows = lax.all_gather(proj_later, "fsdp", axis=0, tiled=True)

    def exchange(rows):
        return lax.all_to_all(rows, "seq", split_axis=0, concat_axis=0, tiled=True)

    normed_one, raw, totals = front(slot_tokens, gains, qkv_local, n_seq, collective_id=1)


    def rms(values):
        return lax.rsqrt(jnp.mean(values * values, axis=-1, keepdims=True) + epsilon)

    cosine, sine = rope_tables(slot_len, head_dim)
    attended, query, key, value = attend(
        raw, totals, own_gains, cosine, sine, length, block, width
    )

    resid_in = tokens[0].astype(F32)
    resid_mid = resid_in + product_reduced(attended, proj_rows, 0, n_seq, collective_id=8)
    mid_rms = rms(resid_mid)
    normed_two = (resid_mid * mid_rms * gains[3]).astype(BF)
    router_probs = jax.nn.softmax(jnp.dot(normed_two, router, preferred_element_type=F32), axis=-1)

    own_hot = places(local_routes, jnp.arange(experts, dtype=jnp.int32), capacity)
    gate_slot = jnp.sum(own_hot * router_probs[:, :, None], axis=0)
    gate_send = jnp.broadcast_to(gate_slot[:, None], (experts, split, capacity))
    gate_send = gate_send.reshape(n_dev, pieces_dev, capacity)
    gate_send = jnp.pad(gate_send, ((0, 0), (0, -pieces_dev % 8), (0, 128 - capacity)))
    cot_all, gate_columns, outs, *experts_forward = dispatch_rows(
        normed_two,
        to_places,
        gate_send,
        masked_low,
        cot_all,
        expert_up,
        expert_down,
        n_seq,
        n_fsdp,
        capacity,
        collective_id=6,
    )
    outs_back = exchange(outs)
    backs, gate_backs = [], []
    up_grad = down_grad = None
    for piece in range(pieces_dev):
        rows, hidden, activation, piece_out = experts_forward[piece::pieces_dev]
        rows = rows.reshape(-1, width)
        hidden_grad, out_grad, gate_back = expert_backward(
            cot_all, gate_columns[piece], piece_out, hidden, expert_down, piece
        )
        gate_backs.append(gate_back[0].reshape(n_dev, capacity))
        backs.append(hidden_grad.reshape(2, n_seq, n_fsdp, capacity, piece_ff))
        down_grad = weight_grad(activation, out_grad[None], down_grad, piece, pieces_dev)
        up_grad = weight_grad(rows, hidden_grad, up_grad, piece, pieces_dev)
    back_send = jnp.stack(gate_backs, axis=1).reshape(n_dev, pieces_dev * capacity)
    gate_pad = -pieces_dev * capacity % 1024
    back_send = jnp.pad(back_send, ((0, 0), (0, gate_pad))).reshape(n_dev, -1, 128)
    backs, outs_back, up_grad, down_grad = lax.optimization_barrier(
        (backs, outs_back, up_grad, down_grad)
    )
    backs, outs_back, up_grad, down_grad = lax.optimization_barrier(
        (backs, outs_back, up_grad, down_grad)
    )
    normed_two_grad, back_recv, outs_sums = return_rows(
        backs, expert_up, to_rows, back_send, outs_back, n_seq, n_fsdp, collective_id=7
    )

    fraction = counts[0] / (top_count * valid_total)
    back_recv = back_recv.reshape(n_dev, -1)
    slot_gates_grad = back_recv[:, : pieces_dev * capacity].reshape(experts, split, capacity).sum(axis=1)
    probs_grad = (
        jnp.sum(own_hot * slot_gates_grad[None], axis=2)
        + (experts * fraction / valid_total)[None, :] * row_valid[:, None]
    )
    logits_grad = router_probs * (
        probs_grad - jnp.sum(router_probs * probs_grad, axis=-1, keepdims=True)
    )
    router_term = lax.dot_general(
        logits_grad, normed_two.astype(F32), (((0,), (0,)), ((), ())), precision=lax.Precision.HIGHEST
    )
    normed_two_grad = normed_two_grad + lax.dot_general(
        logits_grad, router.astype(F32), (((1,), (1,)), ((), ())), precision=lax.Precision.HIGHEST
    )

    def rms_back(values, scale, gain, grad):
        weighted = gain * grad
        mean = jnp.mean(weighted * values, axis=-1, keepdims=True)
        return scale * weighted - values * (scale * scale * scale) * mean, jnp.sum(
            grad * values * scale, axis=0
        )

    mid_part, gain_three = rms_back(resid_mid, mid_rms, gains[3], normed_two_grad)
    mid_grad = masked_low.astype(F32) + mid_part
    branch_grad = mid_grad.astype(BF)
    outs_parts = lax.all_to_all(outs_sums, "fsdp", split_axis=0, concat_axis=0, tiled=True)
    slot_branch, router_parts = gather_seq(
        branch_grad, router_term, n_seq, n_fsdp, collective_id=9
    )
    slot_branch = slot_branch.reshape(slot_len, width)
    heads_grad = dot(slot_branch, proj_rows, 1, 1).astype(BF)
    query_in, key_in, value_grad, dots, heads_gain = attend_back(
        query,
        key,
        value,
        heads_grad,
        raw,
        totals,
        own_gains,
        cosine,
        sine,
        length,
        block,
        width,
    )
    raw_grad, router_parts = raw_back(
        query_in,
        key_in,
        value_grad,
        raw,
        totals,
        own_gains,
        dots,
        router_parts,
        n_seq,
        n_fsdp,
        width,
        collective_id=4,
    )
    raw_grad, outs_parts = lax.optimization_barrier((raw_grad, outs_parts))

    prob_part = jnp.sum(router_probs * row_valid[:, None], axis=0)
    prob_row = jnp.tile(jnp.pad(prob_part, (0, head_width - experts)), n_seq)
    terms = jnp.pad(jnp.stack([gain_three, prob_row]), ((1, 5), (0, 0)))
    heads_terms = jnp.pad(heads_gain[:2], ((3, 3), (0, 0)))
    input_grad, qkv_grad, last, layer_out = last_reduce(
        raw_grad,
        qkv_local,
        normed_one,
        tokens[0],
        mid_grad,
        gains,
        terms,
        heads_terms,
        resid_mid,
        outs_parts,
        n_seq,
        n_fsdp,
        collective_id=10,
    )
    input_grad = input_grad[None]
    layer_out = layer_out[None]

    proj_part = dot(attended, slot_branch, 0, 0).astype(BF)
    proj_grad = lax.psum_scatter(proj_part, "fsdp", scatter_dimension=0, tiled=True).astype(F32)

    router_grad = lax.dynamic_slice_in_dim(router_parts, me_f * owned, owned, 1).T
    prob_total = last[2, :experts]
    last = lax.dynamic_slice_in_dim(last, me_f * owned, owned, 1)
    gains_grad = jnp.stack([last[0], last[3], last[4], last[1]])
    loss_value = (experts * jnp.sum(fraction * prob_total / valid_total)).reshape(1)
    return (
        layer_out,
        input_grad,
        gains_grad,
        qkv_grad,
        proj_grad,
        router_grad,
        up_grad,
        down_grad,
        loss_value,
    )


def solution(mesh):
    rows = P(("seq", "fsdp"), None)
    return jax.shard_map(
        local,
        mesh=mesh,
        in_specs=(
            P("fsdp", "seq", None),
            P("fsdp", "seq", None),
            P(),
            P("fsdp", "seq", None),
            P(None, ("seq", "fsdp")),
            rows,
            rows,
            rows,
            P(("seq", "fsdp"), None, None),
            P(("seq", "fsdp"), None, None),
        ),
        out_specs=(
            P("fsdp", "seq", None),
            P("fsdp", "seq", None),
            P(None, ("seq", "fsdp")),
            rows,
            rows,
            rows,
            P(("seq", "fsdp"), None, None),
            P(("seq", "fsdp"), None, None),
            P(),
        ),
        check_vma=False,
    )
```

```python
import functools

import jax
import jax.numpy as jnp
import numpy as np
from jax import lax
from jax.experimental import pallas as pl
from jax.experimental.pallas import tpu as pltpu
from jax.sharding import PartitionSpec as P

HEADS = 16
FF = 1024

epsilon = 1e-06
rope_base = 10000.0
MESH = pl.DeviceIdType.MESH
BF = jnp.bfloat16
F32 = jnp.float32


def dot(a, b, ca, cb):
    return lax.dot_general(a, b, (((ca,), (cb,)), ((), ())), preferred_element_type=F32)


def push_kernel(n_seq, n_fsdp, scope, gather, src, dst, send_sem, recv_sem, own_sem):
    me_s, me_f = lax.axis_index("seq"), lax.axis_index("fsdp")
    n = n_seq * n_fsdp if scope == "all" else n_seq
    me = me_s * n_fsdp + me_f if scope == "all" else me_s

    def where(index):
        if scope == "all":
            return (index // n_fsdp, index % n_fsdp)
        return (index, me_f)

    barrier = pltpu.get_barrier_semaphore()

    def greet(i, carry):
        pl.semaphore_signal(barrier, inc=1, device_id=where((me + i) % n), device_id_type=MESH)
        return carry

    lax.fori_loop(1, n, greet, 0)
    own = pltpu.make_async_copy(src if gather else src.at[me], dst.at[me], own_sem)
    own.start()
    pl.semaphore_wait(barrier, n - 1)

    def copy_to(other):
        return pltpu.make_async_remote_copy(
            src_ref=src if gather else src.at[other],
            dst_ref=dst.at[me],
            send_sem=send_sem.at[other],
            recv_sem=recv_sem.at[me],
            device_id=where(other),
            device_id_type=MESH,
        )

    def copy_from(other):
        return pltpu.make_async_remote_copy(
            src_ref=src if gather else src.at[other],
            dst_ref=dst.at[other],
            send_sem=send_sem.at[other],
            recv_sem=recv_sem.at[other],
            device_id=where(other),
            device_id_type=MESH,
        )

    def send(i, carry):
        copy_to((me + i) % n).start()
        return carry

    lax.fori_loop(1, n, send, 0)

    def finish(i, carry):
        other = (me + i) % n
        copy_from(other).wait_recv()
        copy_to(other).wait_send()
        return carry

    lax.fori_loop(1, n, finish, 0)
    own.wait()


def push(block, n_seq, n_fsdp, scope, gather, collective_id):
    n = n_seq * n_fsdp if scope == "all" else n_seq
    shape = (n,) + (block.shape if gather else block.shape[1:])
    return pl.pallas_call(
        functools.partial(push_kernel, n_seq, n_fsdp, scope, gather),
        out_shape=jax.ShapeDtypeStruct(shape, block.dtype),
        in_specs=[pl.BlockSpec(memory_space=pltpu.VMEM)],
        out_specs=pl.BlockSpec(memory_space=pltpu.VMEM),
        scratch_shapes=[
            pltpu.SemaphoreType.DMA((n,)),
            pltpu.SemaphoreType.DMA((n,)),
            pltpu.SemaphoreType.DMA,
        ],
        compiler_params=pltpu.CompilerParams(collective_id=collective_id, has_side_effects=True),
        name="push_" + scope,
    )(block)


def rows_of(flat, multiple):
    size = flat.shape[0]
    whole = -(-size // (multiple * 128)) * multiple * 128
    return jnp.pad(flat, (0, whole - size)).reshape(-1, 128)


def remote(src, dst, send_sem, recv_sem, device):
    return pltpu.make_async_remote_copy(
        src_ref=src,
        dst_ref=dst,
        send_sem=send_sem,
        recv_sem=recv_sem,
        device_id=device,
        device_id_type=MESH,
    )


def greet_all(n_seq, n_fsdp):
    me_s, me_f = lax.axis_index("seq"), lax.axis_index("fsdp")
    n = n_seq * n_fsdp
    me = me_s * n_fsdp + me_f
    barrier = pltpu.get_barrier_semaphore()

    def greet(i, carry):
        other = (me + i) % n
        pl.semaphore_signal(
            barrier, inc=1, device_id=(other // n_fsdp, other % n_fsdp), device_id_type=MESH
        )
        return carry

    lax.fori_loop(1, n, greet, 0)
    pl.semaphore_wait(barrier, n - 1)


def greet_lines(n_seq, n_fsdp):
    me_s, me_f = lax.axis_index("seq"), lax.axis_index("fsdp")
    barrier = pltpu.get_barrier_semaphore()
    for i in range(1, n_seq):
        pl.semaphore_signal(
            barrier, inc=1, device_id=((me_s + i) % n_seq, me_f), device_id_type=MESH
        )
    for i in range(1, n_fsdp):
        pl.semaphore_signal(
            barrier, inc=1, device_id=(me_s, (me_f + i) % n_fsdp), device_id_type=MESH
        )
    pl.semaphore_wait(barrier, n_seq + n_fsdp - 2)


def loading(body, greet, inputs):
    def kernel(*refs):
        held, sems = refs[-1 - inputs : -1], refs[-1]
        copies = [
            pltpu.make_async_copy(refs[i], held[i], sems.at[i]) for i in range(inputs)
        ]
        for copy in copies:
            copy.start()
        greet()
        for copy in copies:
            copy.wait()
        body(*held, *refs[inputs : -1 - inputs])

    return kernel


def load_scratch(arrays):
    held = [pltpu.VMEM(array.shape, array.dtype) for array in arrays]
    return held + [pltpu.SemaphoreType.DMA((len(arrays),))]


class Exchange:
    def __init__(self, n_seq, n_fsdp, src, dst, sems):
        self.n, self.n_fsdp, self.src, self.dst = n_seq * n_fsdp, n_fsdp, src, dst
        self.send_sem, self.recv_sem, self.own_sem = sems
        self.me = lax.axis_index("seq") * n_fsdp + lax.axis_index("fsdp")

    def copy(self, i, place):
        other = (self.me + i) % self.n
        return remote(
            self.src.at[other],
            self.dst.at[self.me if place is None else place],
            self.send_sem.at[i],
            self.recv_sem.at[self.me if place is None else place],
            (other // self.n_fsdp, other % self.n_fsdp),
        )

    def own(self):
        return pltpu.make_async_copy(
            self.src.at[self.me], self.dst.at[self.me], self.own_sem
        )

    def start(self):
        self.own().start()

        def one(i, carry):
            self.copy(i, None).start()
            return carry

        lax.fori_loop(1, self.n, one, 0)

    def finish(self):
        def one(i, carry):
            self.copy(i, None).wait_send()
            self.copy(i, (self.me + i) % self.n).wait_recv()
            return carry

        lax.fori_loop(1, self.n, one, 0)
        self.own().wait()


def exchange_sems(n):
    return [
        pltpu.SemaphoreType.DMA((n,)),
        pltpu.SemaphoreType.DMA((n,)),
        pltpu.SemaphoreType.DMA,
    ]


def line_step(n_fsdp, step, arrived, forward):
    me_f = lax.axis_index("fsdp")

    @pl.when(me_f - step >= 0)
    def _():
        arrived(me_f - step)

        @pl.when(me_f + 1 < n_fsdp)
        def _():
            forward(me_f - step, 0, me_f + 1)

    @pl.when(me_f + step < n_fsdp)
    def _():
        arrived(me_f + step)

        @pl.when(me_f >= 1)
        def _():
            forward(me_f + step, 1, me_f - 1)


def line_sent(n_fsdp, step, sent):
    me_f = lax.axis_index("fsdp")

    @pl.when((me_f - step >= 0) & (me_f + 1 < n_fsdp))
    def _():
        sent(me_f - step, 0, me_f + 1)

    @pl.when((me_f + step < n_fsdp) & (me_f >= 1))
    def _():
        sent(me_f + step, 1, me_f - 1)


def flipped(index, bit):
    return index + bit * (1 - 2 * ((index // bit) % 2))


class SeqGather:
    def __init__(self, order, own, block, send_sem, recv_sem):
        self.order, self.own, self.block = order, own, block
        self.send_sem, self.recv_sem = send_sem, recv_sem
        self.me_s, self.me_f = lax.axis_index("seq"), lax.axis_index("fsdp")

    def held(self, stage):
        indices = [self.me_s]
        for bit in self.order[:stage]:
            indices = indices + [flipped(i, bit) for i in indices]
        return indices

    def copies(self, stage):
        partner = flipped(self.me_s, self.order[stage])
        result = []
        for count, index in enumerate(self.held(stage)):
            src = self.own if count == 0 else self.block(index)
            sem = self.send_sem.at[(1 << stage) - 1 + count]
            result.append(
                remote(src, self.block(index), sem, self.recv_sem.at[index], (partner, self.me_f))
            )
        return result

    def start(self, stage):
        for copy in self.copies(stage):
            copy.start()

    def wait(self, stage):
        for index in self.held(stage):
            index = flipped(index, self.order[stage])
            remote(
                self.block(index),
                self.block(index),
                self.send_sem.at[0],
                self.recv_sem.at[index],
                (self.me_s, self.me_f),
            ).wait_recv()

    def sent(self):
        for stage in range(len(self.order)):
            for copy in self.copies(stage):
                copy.wait_send()


def gather_orders(n_seq):
    bits = [1 << b for b in range(n_seq.bit_length() - 1)]
    return bits[1:] + bits[:1], bits[:0:-1] + bits[:1]


def block_places(routes, ids, capacity):
    count = routes.shape[1]
    match = jnp.zeros((ids.shape[0], count), F32)
    for k in range(routes.shape[0]):
        match = match + (routes[k : k + 1, :] == ids).astype(F32)
    row = lax.broadcasted_iota(jnp.int32, (count, count), 0)
    column = lax.broadcasted_iota(jnp.int32, (count, count), 1)
    rank = dot(match.astype(BF), (row < column).astype(BF), 1, 0)
    place = lax.broadcasted_iota(jnp.int32, (ids.shape[0], capacity, count), 1).astype(F32)
    hot = match[:, None, :] * (rank[:, None, :] == place).astype(F32)
    return hot.reshape(ids.shape[0] * capacity, count)


def first_kernel(
    n_seq,
    n_fsdp,
    pieces,
    split,
    capacity,
    owned,
    top,
    small,
    tokens,
    qkv,
    cotangent,
    lengths,
    small_all,
    gains,
    slot,
    qkv_all,
    masked_all,
    to_places,
    to_rows,
    counts,
    own_gains,
    masked,
    send,
    own_sem,
    small_send,
    small_recv,
    qkv_send,
    qkv_recv,
    line_send,
    line_recv,
    token_send,
    token_recv,
    row_send,
    row_recv,
    row_own,
):
    me_s, me_f = lax.axis_index("seq"), lax.axis_index("fsdp")
    n = n_seq * n_fsdp
    me = me_s * n_fsdp + me_f
    head_width = qkv_all.shape[3] // 3
    width = head_width * n_seq
    half = tokens.shape[0] // 2
    orders = gather_orders(n_seq)
    stages = len(orders[0])

    def columns(owner, part):
        start = pl.multiple_of(part * width + owner * head_width, 128)
        return qkv.at[:, pl.ds(start, head_width)]

    def column_place(source, part):
        return qkv_all.at[source, me_f, :, pl.ds(part * head_width, head_width)]

    own = [
        pltpu.make_async_copy(small, small_all.at[me], own_sem.at[0]),
        pltpu.make_async_copy(tokens, slot.at[me_s], own_sem.at[1]),
    ] + [
        pltpu.make_async_copy(columns(me_s, part), column_place(me_s, part), own_sem.at[2 + part])
        for part in range(3)
    ]
    for copy in own:
        copy.start()

    def small_copy(i):
        other = (me + i) % n
        return remote(
            small,
            small_all.at[me],
            small_send.at[i],
            small_recv.at[me],
            (other // n_fsdp, other % n_fsdp),
        )

    def small_arrived(other):
        return remote(
            small,
            small_all.at[other],
            small_send.at[0],
            small_recv.at[other],
            (other // n_fsdp, other % n_fsdp),
        )

    def small_start(i, carry):
        small_copy(i).start()
        return carry

    lax.fori_loop(1, n, small_start, 0)

    def column_copy(i, part):
        other = (me_s + i) % n_seq
        return remote(
            columns(other, part),
            column_place(me_s, part),
            qkv_send.at[i, part],
            qkv_recv.at[me_s, part],
            (other, me_f),
        )

    for i in range(1, n_seq):
        for part in range(3):
            column_copy(i, part).start()

    flows = []
    for side in range(2):
        rows = pl.ds(side * half, half)
        flows.append(
            SeqGather(
                orders[side],
                tokens.at[rows],
                lambda index, rows=rows: slot.at[index, rows],
                token_send.at[side],
                token_recv.at[side],
            )
        )

    def point(stage):
        for flow in flows:
            if 0 < stage <= stages:
                flow.wait(stage - 1)
            if stage < stages:
                flow.start(stage)

    point(0)
    for copy in own:
        copy.wait()

    piece = lax.broadcasted_iota(jnp.int32, (n_seq * pieces, 1), 0)
    piece = ((piece // pieces) * n_fsdp + me_f) * pieces + piece % pieces
    ids = piece // split

    def row_copy(i, place):
        other = (me_s + i) % n_seq
        return remote(
            send.at[other], masked_all.at[place, :, me_f], row_send.at[i], row_recv.at[place], (other, me_f)
        )

    def own_row():
        return pltpu.make_async_copy(send.at[me_s], masked_all.at[me_s, :, me_f], row_own)

    def table(block):
        routes = small_all[me_s * n_fsdp + block, 8 : 8 + top, :].astype(F32).astype(jnp.int32)
        hot = block_places(routes, ids, capacity)
        to_places[block] = hot.astype(BF)
        to_rows[block] = hot.T.astype(BF)

    row = lax.broadcasted_iota(jnp.int32, (tokens.shape[0], 1), 0) + me_s * tokens.shape[0]
    valid = row < lengths[me_f]

    def mask(lanes):
        values = cotangent[:, lanes].astype(F32)
        masked[:, lanes] = jnp.where(valid, values, 0.0).astype(BF)

    chunked(width, 512, mask)

    def scatter():
        def some(lanes):
            picked = dot(to_places[me_f], masked[:, lanes], 1, 0).astype(BF)
            send[:, :, :, lanes] = picked.reshape(n_seq, pieces, capacity, -1)

        chunked(width, 512, some)
        for i in range(1, n_seq):
            row_copy(i, me_s).start()
        own_row().start()

    def line_copy(part, step, block, way, to):
        place = qkv_all.at[part, block]
        return remote(
            place, place, line_send.at[part, way, step], line_recv.at[part, block], (me_s, to)
        )

    def line_first(part):
        @pl.when(me_f + 1 < n_fsdp)
        def _():
            line_copy(part, 0, me_f, 0, me_f + 1).start()

        @pl.when(me_f >= 1)
        def _():
            line_copy(part, 0, me_f, 1, me_f - 1).start()

    def column_arrived(i, carry):
        source = (me_s + i) % n_seq

        @pl.when(i > 0)
        def _():
            for part in range(3):
                remote(
                    columns(source, part),
                    column_place(source, part),
                    qkv_send.at[i, part],
                    qkv_recv.at[source, part],
                    (source, me_f),
                ).wait_recv()

        line_first(source)
        return carry

    lax.fori_loop(0, n_seq, column_arrived, 0)

    def column_step(step):
        def column_next(i, carry):
            part = (me_s + i) % n_seq
            line_step(
                n_fsdp,
                step,
                lambda block: line_copy(part, 0, block, 0, me_f).wait_recv(),
                lambda block, way, to: line_copy(part, step, block, way, to).start(),
            )
            return carry

        lax.fori_loop(0, n_seq, column_next, 0)

    point(1)
    table(me_f)
    for stage in range(2, stages + 1):
        point(stage)
    scatter()
    column_step(1)
    for i in range(1, n_fsdp):
        block = (me_f + i) % n_fsdp
        small_arrived(me_s * n_fsdp + block).wait_recv()
        table(block)
    for flow in flows:
        flow.sent()

    def small_wait(i, carry):
        other = (me + i) % n
        small_copy(i).wait_send()

        @pl.when(other // n_fsdp != me_s)
        def _():
            small_arrived(other).wait_recv()

        return carry

    lax.fori_loop(1, n, small_wait, 0)

    lane = lax.broadcasted_iota(jnp.int32, (8, 128), 1)
    each = 128 // owned
    for j in range(width // 128):
        total = jnp.zeros((8, 128), F32)
        for k in range(each):
            some = jnp.where(lane < owned, small_all[j * each + k, :8, :].astype(F32), 0.0)
            total = total + (pltpu.roll(some, k * owned, 1) if k else some)
        gains[:, j * 128 : (j + 1) * 128] = total
    own_gains[...] = gains[:, pl.ds(pl.multiple_of(me_s * head_width, 128), head_width)]

    all_ids = lax.broadcasted_iota(jnp.int32, (counts.shape[1], 1), 0)
    position = lax.broadcasted_iota(jnp.int32, (1, tokens.shape[0]), 1)

    def seen(device, sums):
        routes = small_all[device, 8 : 8 + top, :].astype(F32).astype(jnp.int32)
        match = jnp.zeros(sums.shape, F32)
        for k in range(top):
            match = match + (routes[k : k + 1, :] == all_ids).astype(F32)
        first = (device // n_fsdp) * tokens.shape[0]
        live = (position + first < lengths[device % n_fsdp]).astype(F32)
        return sums + match * live

    sums = jnp.zeros((counts.shape[1], tokens.shape[0]), F32)
    sums = lax.fori_loop(0, n, seen, sums)
    counts[...] = jnp.broadcast_to(jnp.sum(sums.T, axis=0, keepdims=True), counts.shape)

    for step in range(2, n_fsdp):
        column_step(step)

    def column_sent(i, carry):
        for part in range(3):
            column_copy(i, part).wait_send()
        return carry

    lax.fori_loop(1, n_seq, column_sent, 0)

    def line_done(part, carry):
        for step in range(n_fsdp):
            line_sent(
                n_fsdp,
                step,
                lambda block, way, to: line_copy(part, step, block, way, to).wait_send(),
            )
        return carry

    lax.fori_loop(0, n_seq, line_done, 0)
    own_row().wait()
    for i in range(1, n_seq):
        row_copy(i, me_s).wait_send()
        row_copy(i, (me_s + i) % n_seq).wait_recv()


def first_gather(
    small,
    tokens,
    qkv,
    masked,
    lengths,
    n_seq,
    n_fsdp,
    pieces,
    split,
    capacity,
    top,
    experts,
    collective_id,
):
    owned = qkv.shape[0]
    rows, width = tokens.shape
    head_width = width // n_seq
    n = n_seq * n_fsdp
    places_all = n_seq * pieces * capacity
    vmem = pl.BlockSpec(memory_space=pltpu.VMEM)
    any_space = pl.BlockSpec(memory_space=pl.ANY)
    dma = pltpu.SemaphoreType.DMA
    return pl.pallas_call(
        loading(
            functools.partial(first_kernel, n_seq, n_fsdp, pieces, split, capacity, owned, top),
            functools.partial(greet_all, n_seq, n_fsdp),
            4,
        ),
        out_shape=[
            jax.ShapeDtypeStruct((n,) + small.shape, BF),
            jax.ShapeDtypeStruct((8, width), F32),
            jax.ShapeDtypeStruct((n_seq,) + tokens.shape, BF),
            jax.ShapeDtypeStruct((n_seq, n_fsdp, owned, 3 * head_width), BF),
            jax.ShapeDtypeStruct((n_seq, pieces, n_fsdp, capacity, width), BF),
            jax.ShapeDtypeStruct((n_fsdp, places_all, rows), BF),
            jax.ShapeDtypeStruct((n_fsdp, rows, places_all), BF),
            jax.ShapeDtypeStruct((8, experts), F32),
            jax.ShapeDtypeStruct((8, head_width), F32),
            jax.ShapeDtypeStruct((rows, width), BF),
        ],
        in_specs=[pl.BlockSpec(memory_space=pltpu.HBM)] * 4 + [pl.BlockSpec(memory_space=pltpu.SMEM)],
        out_specs=[vmem, vmem, any_space, any_space, any_space] + [vmem] * 5,
        scratch_shapes=[
            pltpu.VMEM((n_seq, pieces, capacity, width), BF),
            dma((5,)),
            dma((n,)),
            dma((n,)),
            dma((n_seq, 3)),
            dma((n_seq, 3)),
            dma((n_seq, 2, n_fsdp)),
            dma((n_seq, n_fsdp)),
            dma((2, n_seq - 1)),
            dma((2, n_seq)),
            dma((n_seq,)),
            dma((n_seq,)),
            dma,
        ]
        + load_scratch([small, tokens, qkv, masked]),
        compiler_params=pltpu.CompilerParams(
            collective_id=collective_id, has_side_effects=True, vmem_limit_bytes=62 << 20
        ),
        name="first_gather",
    )(small, tokens, qkv, masked, lengths)


def greet_seq(n_seq):
    me_s, me_f = lax.axis_index("seq"), lax.axis_index("fsdp")
    barrier = pltpu.get_barrier_semaphore()
    for i in range(1, n_seq):
        pl.semaphore_signal(
            barrier, inc=1, device_id=((me_s + i) % n_seq, me_f), device_id_type=MESH
        )
    pl.semaphore_wait(barrier, n_seq - 1)


class TermSum:
    def __init__(
        self, n_seq, n_fsdp, terms, seq_terms, fsdp_terms, seq_send, seq_recv, fsdp_send, fsdp_recv
    ):
        self.n_seq, self.n_fsdp, self.terms = n_seq, n_fsdp, terms
        self.seq_terms, self.fsdp_terms = seq_terms, fsdp_terms
        self.seq_send, self.seq_recv = seq_send, seq_recv
        self.fsdp_send, self.fsdp_recv = fsdp_send, fsdp_recv
        self.me_s, self.me_f = lax.axis_index("seq"), lax.axis_index("fsdp")

    def part(self, owner):
        columns = self.seq_terms.shape[2]
        return self.terms.at[:, pl.ds(pl.multiple_of(owner * columns, 128), columns)]

    def seq_copy(self, i, place):
        other = (self.me_s + i) % self.n_seq
        return remote(
            self.part(other),
            self.seq_terms.at[place],
            self.seq_send.at[i],
            self.seq_recv.at[place],
            (other, self.me_f),
        )

    def fsdp_copy(self, i, place):
        other = (self.me_f + i) % self.n_fsdp
        return remote(
            self.seq_terms.at[self.me_s],
            self.fsdp_terms.at[place],
            self.fsdp_send.at[i],
            self.fsdp_recv.at[place],
            (self.me_s, other),
        )

    def start_seq(self):
        for i in range(1, self.n_seq):
            self.seq_copy(i, self.me_s).start()

    def over_seq(self):
        result = self.part(self.me_s)[...]
        for i in range(1, self.n_seq):
            place = (self.me_s + i) % self.n_seq
            self.seq_copy(i, place).wait_recv()
            result = result + self.seq_terms[place]
        for i in range(1, self.n_seq):
            self.seq_copy(i, self.me_s).wait_send()
        return result

    def start_fsdp(self, more):
        self.seq_terms[self.me_s] = more + (self.over_seq() if self.terms is not None else 0.0)
        for i in range(1, self.n_fsdp):
            self.fsdp_copy(i, self.me_f).start()

    def finish(self):
        result = self.seq_terms[self.me_s]
        for i in range(1, self.n_fsdp):
            place = (self.me_f + i) % self.n_fsdp
            self.fsdp_copy(i, place).wait_recv()
            result = result + self.fsdp_terms[place]
        for i in range(1, self.n_fsdp):
            self.fsdp_copy(i, self.me_f).wait_send()
        return result


def term_scratch(n_seq, n_fsdp, shape):
    dma = pltpu.SemaphoreType.DMA
    return [
        pltpu.VMEM((n_seq,) + shape, F32),
        pltpu.VMEM((n_fsdp,) + shape, F32),
        dma((n_seq,)),
        dma((n_seq,)),
        dma((n_fsdp,)),
        dma((n_fsdp,)),
    ]


def gather_kernel(n_seq, n_fsdp, x, terms, out, total, own_sem, send_sem, recv_sem, *scratch):
    me_s = lax.axis_index("seq")
    half = x.shape[0] // 2
    own = pltpu.make_async_copy(x, out.at[me_s], own_sem)
    own.start()
    term_sum = TermSum(n_seq, n_fsdp, terms, scratch[0], None, *scratch[1:], None, None)
    greet_seq(n_seq)
    flows = []
    for side, order in enumerate(gather_orders(n_seq)):
        rows = pl.ds(side * half, half)
        flows.append(
            SeqGather(
                order,
                x.at[rows],
                lambda index, rows=rows: out.at[index, rows],
                send_sem.at[side],
                recv_sem.at[side],
            )
        )
    for stage in range(len(flows[0].order)):
        for flow in flows:
            flow.start(stage)
        if stage == 0:
            term_sum.start_seq()
        if stage == 1:
            total[...] = term_sum.over_seq()
        for flow in flows:
            flow.wait(stage)
    for flow in flows:
        flow.sent()
    own.wait()


def gather_seq(x, terms, n_seq, n_fsdp, collective_id):
    vmem = pl.BlockSpec(memory_space=pltpu.VMEM)
    dma = pltpu.SemaphoreType.DMA
    part = (terms.shape[0], terms.shape[1] // n_seq)
    return pl.pallas_call(
        functools.partial(gather_kernel, n_seq, n_fsdp),
        out_shape=[
            jax.ShapeDtypeStruct((n_seq,) + x.shape, x.dtype),
            jax.ShapeDtypeStruct(part, terms.dtype),
        ],
        in_specs=[vmem] * 2,
        out_specs=[vmem] * 2,
        scratch_shapes=[
            dma,
            dma((2, n_seq - 1)),
            dma((2, n_seq)),
            pltpu.VMEM((n_seq,) + part, F32),
            dma((n_seq,)),
            dma((n_seq,)),
        ],
        compiler_params=pltpu.CompilerParams(collective_id=collective_id, has_side_effects=True),
        cost_estimate=pl.CostEstimate(flops=0, bytes_accessed=1 << 26, transcendentals=0),
        name="gather_seq",
    )(x, terms)


class SeqReduce:
    def __init__(self, n_seq, a, w, w_dim, sums, got, send_sem, recv_sem):
        self.a, self.w, self.w_dim, self.sums, self.got = a, w, w_dim, sums, got
        self.send_sem, self.recv_sem = send_sem, recv_sem
        self.me_s, self.me_f = lax.axis_index("seq"), lax.axis_index("fsdp")
        self.orders = [order[-1:] + order[-2::-1] for order in gather_orders(n_seq)]
        self.stages = len(self.orders[0])
        self.half = sums.shape[1] // 2
        self.width = sums.shape[2]

    def combined(self, index, bits):
        indices = [index]
        for bit in bits:
            indices = indices + [flipped(i, bit) for i in indices]
        return indices

    def product(self, index):
        def some(columns):
            w = self.w[:, columns] if self.w_dim == 0 else self.w[columns, :]
            self.sums[index, :, columns] = dot(self.a[index], w, 1, self.w_dim).astype(BF)

        chunked(self.width, 512, some)

    def copy(self, stage, side, count, index):
        order = self.orders[side]
        slot = sum(1 << (self.stages - 1 - s) for s in range(stage)) + count
        rows = pl.ds(side * self.half, self.half)
        return remote(
            self.sums.at[index, rows],
            self.got.at[slot, rows],
            self.send_sem.at[side, slot],
            self.recv_sem.at[side, slot],
            (flipped(self.me_s, order[stage]), self.me_f),
        )

    def leaving(self, stage, side):
        order = self.orders[side]
        return self.combined(flipped(self.me_s, order[stage]), order[stage + 1 :])

    def start(self, stage):
        if stage == 0:
            for count, index in enumerate(self.leaving(0, 0)):
                self.product(index)
                for side in range(2):
                    self.copy(0, side, self.twin(count) if side == 1 else count, index).start()
            for index in self.combined(self.me_s, self.orders[0][1:]):
                self.product(index)
        else:
            for side in range(2):
                for count, index in enumerate(self.leaving(stage, side)):
                    self.copy(stage, side, count, index).start()

    def twin(self, count):
        first, second = self.orders[0][1:], self.orders[1][1:]
        place = 0
        for position, bit in enumerate(first):
            if (count >> position) & 1:
                place += 1 << second.index(bit)
        return place

    def finish(self, stage, last=None):
        for side in range(2):
            order = self.orders[side]
            rows = pl.ds(side * self.half, self.half)
            for count, index in enumerate(self.combined(self.me_s, order[stage + 1 :])):
                copy = self.copy(stage, side, count, index)
                copy.wait_recv()
                slot = sum(1 << (self.stages - 1 - s) for s in range(stage)) + count

                def some(columns):
                    total = self.sums[index, rows, columns].astype(F32)
                    total = total + self.got[slot, rows, columns].astype(F32)
                    if last is None:
                        self.sums[index, rows, columns] = total.astype(BF)
                    else:
                        last[rows, columns] = total

                chunked(self.width, 1024, some)

    def events(self, last):
        def leave(count, index):
            self.product(index)
            for side in range(2):
                self.copy(0, side, self.twin(count) if side == 1 else count, index).start()

        result = [
            (1, functools.partial(leave, count, index))
            for count, index in enumerate(self.leaving(0, 0))
        ]
        for index in self.combined(self.me_s, self.orders[0][1:]):
            result.append((1, functools.partial(self.product, index)))
        result.append((1, functools.partial(self.finish, 0, last if self.stages == 1 else None)))
        for stage in range(1, self.stages):
            result.append((0, functools.partial(self.start, stage)))
            result.append(
                (7, functools.partial(self.finish, stage, last if stage == self.stages - 1 else None))
            )
        return result

    def sent(self):
        for stage in range(self.stages):
            for side in range(2):
                for count, index in enumerate(self.leaving(stage, side)):
                    self.copy(stage, side, count, index).wait_send()


def reduce_scratch(n_seq, rows, width):
    dma = pltpu.SemaphoreType.DMA
    return [
        pltpu.VMEM((n_seq, rows, width), BF),
        pltpu.VMEM((n_seq - 1, rows, width), BF),
        dma((2, n_seq - 1)),
        dma((2, n_seq - 1)),
    ]


def reduce_kernel(n_seq, w_dim, a, w, out, *scratch):
    reduce = SeqReduce(n_seq, a, w, w_dim, *scratch)
    for stage in range(reduce.stages):
        reduce.start(stage)
        reduce.finish(stage, out if stage == reduce.stages - 1 else None)
    reduce.sent()


def product_reduced(a, w, w_dim, n_seq, collective_id):
    rows = a.shape[0] // n_seq
    width = w.shape[1 - w_dim]
    a = a.reshape(n_seq, rows, -1)
    return pl.pallas_call(
        loading(
            functools.partial(reduce_kernel, n_seq, w_dim),
            functools.partial(greet_seq, n_seq),
            2,
        ),
        out_shape=jax.ShapeDtypeStruct((rows, width), F32),
        in_specs=[pl.BlockSpec(memory_space=pltpu.HBM)] * 2,
        out_specs=pl.BlockSpec(memory_space=pltpu.VMEM),
        scratch_shapes=reduce_scratch(n_seq, rows, width) + load_scratch([a, w]),
        compiler_params=pltpu.CompilerParams(
            collective_id=collective_id, has_side_effects=True, vmem_limit_bytes=62 << 20
        ),
        name="product_reduced",
    )(a, w)


def last_kernel(
    n_seq,
    n_fsdp,
    a,
    w,
    normed,
    x,
    mid,
    gains,
    terms_in,
    heads,
    resid,
    ready,
    input_out,
    qkv_out,
    total,
    layer_out,
    *scratch,
):
    up, down, done, got, up_send, up_recv, down_send, down_recv, done_send, done_recv = scratch[:10]
    one, part, terms, seq_terms, fsdp_terms, seq_send, seq_recv, fsdp_send, fsdp_recv = scratch[10:19]
    me_s, me_f = lax.axis_index("seq"), lax.axis_index("fsdp")
    head_width = a.shape[2] // 3
    width = n_seq * head_width
    greet_lines(n_seq, n_fsdp)
    reduce = SeqReduce(n_seq, a, w, 1, *scratch[19:])
    term_sum = TermSum(
        n_seq,
        n_fsdp,
        terms,
        seq_terms,
        fsdp_terms,
        seq_send,
        seq_recv,
        fsdp_send,
        fsdp_recv,
    )

    def input_rows():
        tile = 32
        terms[...] = terms_in[...]

        def some(i, carry):
            rows = pl.ds(pl.multiple_of(i * tile, tile), tile)
            values = x[rows, :].astype(F32)
            scale = lax.rsqrt(jnp.mean(values * values, axis=-1, keepdims=True) + epsilon)
            grad = one[rows, :]
            weighted = grad * gains[0:1, :]
            mean = jnp.mean(weighted * values, axis=-1, keepdims=True)
            result = scale * weighted - values * (scale * scale * scale * mean)
            input_out[rows, :] = (mid[rows, :] + result).astype(BF)
            terms[0:1, :] += jnp.sum(grad * values * scale, axis=0, keepdims=True)
            layer = resid[rows, :]
            for block in range(n_fsdp):
                layer = layer + ready[block, rows, :].astype(F32)
            layer_out[rows, :] = layer.astype(BF)
            return carry

        lax.fori_loop(0, x.shape[0] // tile, some, 0)
        term_sum.start_seq()

    def line_copy(src, way, s, block):
        buffer, send, recv = (up, up_send, up_recv) if way == 0 else (down, down_send, down_recv)
        to = me_f + 1 if way == 0 else me_f - 1
        place = buffer.at[block, s]
        return remote(
            place if src is None else src, place, send.at[block, s], recv.at[block, s], (me_s, to)
        )

    def done_copy(i):
        s = (me_s + i) % n_seq
        return remote(done.at[s], got.at[me_s], done_send.at[i], done_recv.at[me_s], (s, me_f))

    def stream(way, number):
        buffer = up if way == 0 else down
        behind = me_f if way == 0 else n_fsdp - 1 - me_f
        turn, i = number // n_seq, number % n_seq
        s = (me_s + i) % n_seq
        block = n_fsdp - 1 - turn if way == 0 else turn
        ahead = n_fsdp - 1 - behind
        on_time = (number >= 0) & (turn < ahead)
        finishes_up = (me_f == n_fsdp - 1) | ((n_fsdp - 1 > 2 * me_f) & (me_f > 0))

        @pl.when(on_time & (behind == 0))
        def _():
            line_copy(part.at[s, block], way, s, block).start()

        @pl.when(on_time & (behind > 0))
        def _():
            line_copy(None, way, s, block).wait_recv()
            total = buffer[block, s].astype(F32) + part[s, block].astype(F32)
            buffer[block, s] = total.astype(BF)
            line_copy(None, way, s, block).start()

        @pl.when((number >= 0) & (turn == ahead) & (behind > 0))
        def _():
            line_copy(None, way, s, me_f).wait_recv()
            done[s] = (done[s].astype(F32) + buffer[me_f, s].astype(F32)).astype(BF)

            @pl.when(finishes_up if way == 0 else jnp.logical_not(finishes_up))
            def _():
                @pl.when(i > 0)
                def _():
                    done_copy(i).start()

    lag = 2
    slots = n_seq * (n_fsdp - 1) + lag * (n_fsdp - 1)

    owned = part.shape[2]
    stripe = n_fsdp * owned

    def make(s):
        lanes = pl.ds(pl.multiple_of(s * stripe, 128), stripe)
        every = a[...].reshape(-1, a.shape[2])
        product = dot(normed[:, lanes], every, 0, 0).astype(BF)
        for block in range(n_fsdp):
            part[s, block] = product[block * owned : (block + 1) * owned]
        done[s] = part[s, me_f]

    def run(first, last):
        def slot(number, carry):
            @pl.when(number < n_seq)
            def _():
                make((me_s + number) % n_seq)

            stream(0, number - lag * me_f)
            stream(1, number - lag * (n_fsdp - 1 - me_f))
            return carry

        lax.fori_loop(first, last, slot, 0)

    reached = 0
    for number, event in enumerate(
        reduce.events(one)
        + [(0, input_rows), (3, functools.partial(term_sum.start_fsdp, heads[...]))]
    ):
        run(reached, min(slots, reached + event[0]))
        reached = min(slots, reached + event[0])
        event[1]()
    run(reached, slots)

    def place(s, rows):
        for third in range(3):
            columns = pl.ds(pl.multiple_of(third * width + s * head_width, 128), head_width)
            qkv_out[:, columns] = rows[:, third * head_width : (third + 1) * head_width].astype(F32)

    place(me_s, done[me_s])

    def arrived(i, carry):
        s = (me_s + i) % n_seq
        remote(done.at[s], got.at[s], done_send.at[i], done_recv.at[s], (s, me_f)).wait_recv()
        place(s, got[s])
        return carry

    lax.fori_loop(1, n_seq, arrived, 0)

    def all_sent(i, carry):
        s = (me_s + i) % n_seq

        @pl.when(i > 0)
        def _():
            done_copy(i).wait_send()

        for j in range(n_fsdp - 1):

            @pl.when(me_f + j < n_fsdp - 1)
            def _():
                line_copy(None, 0, s, n_fsdp - 1 - j).wait_send()

            @pl.when(j < me_f)
            def _():
                line_copy(None, 1, s, j).wait_send()

        return carry

    lax.fori_loop(0, n_seq, all_sent, 0)
    reduce.sent()
    total[...] = term_sum.finish()


def last_reduce(
    a, w, normed, x, mid, gains, terms, heads, resid, ready, n_seq, n_fsdp, collective_id
):
    rows, width = a.shape[0] // n_seq, w.shape[0]
    columns = a.shape[1]
    owned = width // (n_seq * n_fsdp)
    vmem = pl.BlockSpec(memory_space=pltpu.VMEM)
    dma = pltpu.SemaphoreType.DMA
    return pl.pallas_call(
        functools.partial(last_kernel, n_seq, n_fsdp),
        out_shape=[
            jax.ShapeDtypeStruct((rows, width), BF),
            jax.ShapeDtypeStruct((owned, n_seq * columns), F32),
            jax.ShapeDtypeStruct(heads.shape, F32),
            jax.ShapeDtypeStruct((rows, width), BF),
        ],
        in_specs=[vmem] * 10,
        out_specs=[vmem] * 4,
        scratch_shapes=[
            pltpu.VMEM((n_fsdp, n_seq, owned, columns), BF),
            pltpu.VMEM((n_fsdp, n_seq, owned, columns), BF),
            pltpu.VMEM((n_seq, owned, columns), BF),
            pltpu.VMEM((n_seq, owned, columns), BF),
            dma((n_fsdp, n_seq)),
            dma((n_fsdp, n_seq)),
            dma((n_fsdp, n_seq)),
            dma((n_fsdp, n_seq)),
            dma((n_seq,)),
            dma((n_seq,)),
            pltpu.VMEM((rows, width), F32),
            pltpu.VMEM((n_seq, n_fsdp, owned, columns), BF),
            pltpu.VMEM(terms.shape, F32),
        ]
        + term_scratch(n_seq, n_fsdp, heads.shape)
        + reduce_scratch(n_seq, rows, width),
        compiler_params=pltpu.CompilerParams(
            collective_id=collective_id, has_side_effects=True, vmem_limit_bytes=60 << 20
        ),
        cost_estimate=pl.CostEstimate(flops=0, bytes_accessed=1 << 27, transcendentals=0),
        name="last_reduce",
    )(a.reshape(n_seq, rows, -1), w, normed, x, mid, gains, terms, heads, resid, ready)


def chunked(total, size, body):
    def step(i, carry):
        body(pl.ds(pl.multiple_of(i * size, size), size))
        return carry

    lax.fori_loop(0, total // size, step, 0)


def dispatch_kernel(n_seq, n_fsdp, pieces, x, hot, gates, masked, before, w_up, w_down, *refs):
    masked_all, columns_out, scaled = refs[:3]
    outs, hiddens, acts, results = (refs[3 + k * pieces : 3 + (k + 1) * pieces] for k in range(4))
    rest = refs[3 + 4 * pieces :]
    gates_out, gathered, gathered_two, send, total = rest[:5]
    own_sem, line_send, line_recv, row_send, row_recv, own_two, send_two, recv_two = rest[5:13]
    line_send_two, line_recv_two = rest[13:15]
    gate_exchange = Exchange(n_seq, n_fsdp, gates, gates_out, rest[15:])
    me_s, me_f = lax.axis_index("seq"), lax.axis_index("fsdp")
    width = x.shape[1]
    capacity = outs[0].shape[2]
    greet_all(n_seq, n_fsdp)

    def line_copy(step, block, way, to):
        src = x if step == 0 else gathered.at[block]
        return remote(
            src, gathered.at[block], line_send.at[way, step], line_recv.at[block], (me_s, to)
        )

    def line_two(step, block, way, to):
        src = masked if step == 0 else gathered_two.at[block]
        return remote(
            src,
            gathered_two.at[block],
            line_send_two.at[way, step],
            line_recv_two.at[block],
            (me_s, to),
        )

    def row_copy(block, i, piece, place):
        other = (me_s + i) % n_seq
        return remote(
            send.at[block, other, piece],
            outs[piece].at[place, block],
            row_send.at[block, i, piece],
            row_recv.at[place, block, piece],
            (other, me_f),
        )

    def own_copy(block, piece):
        return pltpu.make_async_copy(
            send.at[block, me_s, piece], outs[piece].at[me_s, block], own_sem.at[block, piece]
        )

    def masked_copy(block, i, place):
        other = (me_s + i) % n_seq
        return remote(
            send.at[block, other],
            masked_all.at[place, :, block],
            send_two.at[block, i],
            recv_two.at[place, block],
            (other, me_f),
        )

    def own_masked(block):
        return pltpu.make_async_copy(
            send.at[block, me_s], masked_all.at[me_s, :, block], own_two.at[block]
        )

    def pick(block, rows):
        def some(columns):
            picked = dot(hot[block], rows[:, columns], 1, 0).astype(BF)
            send[block, :, :, :, columns] = picked.reshape(n_seq, pieces, capacity, -1)

        chunked(width, 512, some)

    def scatter(block, rows):
        pick(block, rows)
        for i in range(1, n_seq):
            for piece in range(pieces):
                row_copy(block, i, piece, me_s).start()
        for piece in range(pieces):
            own_copy(block, piece).start()

    def scatter_masked(block):
        for piece in range(pieces):
            own_copy(block, piece).wait()
            for i in range(1, n_seq):
                row_copy(block, i, piece, me_s).wait_send()
        pick(block, gathered_two.at[block])
        for i in range(1, n_seq):
            masked_copy(block, i, me_s).start()
        own_masked(block).start()

    def around(step, act):
        @pl.when(me_f - step >= 0)
        def _():
            act(me_f - step)

        @pl.when(me_f + step < n_fsdp)
        def _():
            act(me_f + step)

    @pl.when(me_f + 1 < n_fsdp)
    def _():
        line_copy(0, me_f, 0, me_f + 1).start()

    @pl.when(me_f >= 1)
    def _():
        line_copy(0, me_f, 1, me_f - 1).start()

    scatter(me_f, x)
    gate_exchange.start()
    for step in range(1, n_fsdp):
        line_step(
            n_fsdp,
            step,
            lambda block: line_copy(1, block, 0, me_f).wait_recv(),
            lambda block, way, to: line_copy(step, block, way, to).start(),
        )
        around(step, lambda block: scatter(block, gathered.at[block]))

    @pl.when(me_f + 1 < n_fsdp)
    def _():
        line_two(0, me_f, 0, me_f + 1).start()

    @pl.when(me_f >= 1)
    def _():
        line_two(0, me_f, 1, me_f - 1).start()

    for step in range(1, n_fsdp):
        line_step(
            n_fsdp,
            step,
            lambda block: line_two(1, block, 0, me_f).wait_recv(),
            lambda block, way, to: line_two(step, block, way, to).start(),
        )
        around(step, scatter_masked)
    for step in range(n_fsdp):
        line_sent(
            n_fsdp, step, lambda block, way, to: line_copy(step, block, way, to).wait_send()
        )
        line_sent(n_fsdp, step, lambda block, way, to: line_two(step, block, way, to).wait_send())

    gate_exchange.finish()
    n = n_seq * n_fsdp
    for piece in range(pieces):
        lanes = lax.broadcasted_iota(jnp.int32, (n, capacity, 128), 2)
        place = lax.broadcasted_iota(jnp.int32, (n, capacity, 128), 1)
        values = jnp.broadcast_to(gates_out[:, piece : piece + 1, :], (n, capacity, 128))
        column = jnp.sum(jnp.where(lanes == place, values, 0.0), axis=2, keepdims=True)
        columns_out[piece] = column.reshape(n * capacity, 1)

    for piece in range(pieces):
        own_copy(me_f, piece).wait()
        for i in range(1, n_seq):
            row_copy(me_f, i, piece, me_s).wait_send()
    for piece in range(pieces):
        for block in range(n_fsdp):
            for i in range(1, n_seq):
                row_copy(block, i, piece, (me_s + i) % n_seq).wait_recv()

    ff = w_down.shape[1]
    tile = min(256, ff)
    steps = ff // tile
    spans = seq_tile(n_seq, n_fsdp * capacity, 3072 // n_fsdp)
    count = spans * n_fsdp * capacity
    for piece in range(pieces):

        def body(rows, w_gate, w_value, w_back, hidden, act, result, scaled_rows):
            step = pl.program_id(1)
            low = rows[...].reshape(count, width)
            gate = dot(low, w_gate[0], 1, 0)
            up = dot(low, w_value[0], 1, 0)
            hidden[0] = gate
            hidden[1] = up
            act[...] = (gate * jax.nn.sigmoid(gate) * up).astype(BF)
            product = dot(act[...], w_back[0], 1, 0)

            @pl.when(step == 0)
            def _():
                total[...] = product

            @pl.when(step > 0)
            def _():
                total[...] += product

            @pl.when(step == steps - 1)
            def _():
                start = pl.multiple_of(pl.program_id(0) * count, 8)
                column = columns_out[piece, pl.ds(start, count), :]
                result[...] = total[...].astype(BF)
                gated = (result[...].astype(F32) * column).astype(BF)
                scaled_rows[...] = gated.reshape(scaled_rows.shape)

        pltpu.emit_pipeline(
            body,
            grid=(n * capacity // count, steps),
            in_specs=[
                pl.BlockSpec((spans, n_fsdp, capacity, width), lambda r, i: (r, 0, 0, 0)),
                pl.BlockSpec((1, width, tile), lambda r, i: (piece, 0, i)),
                pl.BlockSpec((1, width, tile), lambda r, i: (piece, 0, steps + i)),
                pl.BlockSpec((1, tile, width), lambda r, i: (piece, i, 0)),
            ],
            out_specs=[
                pl.BlockSpec((2, count, tile), lambda r, i: (0, r, i)),
                pl.BlockSpec((count, tile), lambda r, i: (r, i)),
                pl.BlockSpec((count, width), lambda r, i: (r, 0)),
                pl.BlockSpec((spans, 1, n_fsdp, capacity, width), lambda r, i: (r, piece, 0, 0, 0)),
            ],
        )(
            outs[piece],
            w_up,
            w_up,
            w_down,
            hiddens[piece],
            acts[piece],
            results[piece],
            scaled,
        )

    for step in range(1, n_fsdp):
        around(step, lambda block: own_masked(block).wait())
    for step in range(1, n_fsdp):
        for i in range(1, n_seq):

            def done(block):
                masked_copy(block, i, me_s).wait_send()
                masked_copy(block, i, (me_s + i) % n_seq).wait_recv()

            around(step, done)


def dispatch_rows(
    x, hot, gates, masked, before, w_up, w_down, n_seq, n_fsdp, capacity, collective_id
):
    count, width = x.shape
    pieces, ff = w_down.shape[:2]
    rows = n_seq * n_fsdp * capacity
    tile_rows = seq_tile(n_seq, n_fsdp * capacity, 3072 // n_fsdp) * n_fsdp * capacity
    vmem = pl.BlockSpec(memory_space=pltpu.VMEM)
    any_space = pl.BlockSpec(memory_space=pl.ANY)
    dma = pltpu.SemaphoreType.DMA
    return pl.pallas_call(
        functools.partial(dispatch_kernel, n_seq, n_fsdp, pieces),
        out_shape=[
            jax.ShapeDtypeStruct(before.shape, BF),
            jax.ShapeDtypeStruct((pieces, rows, 1), F32),
            jax.ShapeDtypeStruct(before.shape, BF),
        ]
        + [jax.ShapeDtypeStruct((n_seq, n_fsdp, capacity, width), BF)] * pieces
        + [jax.ShapeDtypeStruct((2, rows, ff), F32)] * pieces
        + [jax.ShapeDtypeStruct((rows, ff), BF)] * pieces
        + [jax.ShapeDtypeStruct((rows, width), BF)] * pieces,
        in_specs=[vmem] * 4 + [any_space] * 3,
        out_specs=[any_space, vmem] + [any_space] * (1 + 4 * pieces),
        scratch_shapes=[
            pltpu.VMEM(gates.shape, F32),
            pltpu.VMEM((n_fsdp, count, width), BF),
            pltpu.VMEM((n_fsdp, count, width), BF),
            pltpu.VMEM((n_fsdp, n_seq, pieces, capacity, width), BF),
            pltpu.VMEM((tile_rows, width), F32),
            dma((n_fsdp, pieces)),
            dma((2, n_fsdp)),
            dma((n_fsdp,)),
            dma((n_fsdp, n_seq, pieces)),
            dma((n_seq, n_fsdp, pieces)),
            dma((n_fsdp,)),
            dma((n_fsdp, n_seq)),
            dma((n_seq, n_fsdp)),
            dma((2, n_fsdp)),
            dma((n_fsdp,)),
        ]
        + exchange_sems(n_seq * n_fsdp),
        input_output_aliases={4: 0},
        compiler_params=pltpu.CompilerParams(
            collective_id=collective_id, has_side_effects=True, vmem_limit_bytes=60 << 20
        ),
        name="dispatch_rows",
    )(x, hot, gates, masked, before, w_up, w_down)


def return_kernel(n_seq, n_fsdp, pieces, hot, gates, ready, w_up, *refs):
    grads = refs[:pieces]
    out, gates_out, ready_sums = refs[pieces : pieces + 3]
    rest = refs[pieces + 3 :]
    weights, hidden, rows, got, parts, sums, some_ready = rest[:7]
    w_sem, h_sem, ready_sem, own_sem, row_send, row_recv, part_send, part_recv = rest[7:15]
    gate_exchange = Exchange(n_seq, n_fsdp, gates, gates_out, rest[15:])
    me_s, me_f = lax.axis_index("seq"), lax.axis_index("fsdp")
    width = out.shape[1]
    capacity = rows.shape[3]
    ff = hidden.shape[5]
    tile = min(256, width)
    chunks = width // tile

    def weight_copy(piece, chunk):
        lines = pl.ds(pl.multiple_of(chunk * tile, tile), tile)
        return pltpu.make_async_copy(
            w_up.at[piece, lines], weights.at[piece, lines], w_sem.at[piece, chunk]
        )

    def hidden_copy(piece):
        return pltpu.make_async_copy(grads[piece], hidden.at[piece], h_sem.at[piece])

    def ready_copy(block):
        return pltpu.make_async_copy(
            ready.at[:, :, block], some_ready.at[block % 2], ready_sem.at[block % 2]
        )

    def row_copy(block, i, piece, place):
        other = (me_s + i) % n_seq
        return remote(
            rows.at[block, other, piece],
            got.at[block, place, piece],
            row_send.at[block, i, piece],
            row_recv.at[block, place, piece],
            (other, me_f),
        )

    def own_copy(block, piece):
        return pltpu.make_async_copy(
            rows.at[block, me_s, piece], got.at[block, me_s, piece], own_sem.at[block, piece]
        )

    def part_copy(j):
        block = (me_f + j) % n_fsdp
        return remote(
            parts.at[block], sums.at[me_f], part_send.at[j], part_recv.at[me_f], (me_s, block)
        )

    for piece in range(pieces):
        hidden_copy(piece).start()

        def begin(chunk, carry):
            weight_copy(piece, chunk).start()
            return carry

        lax.fori_loop(0, chunks, begin, 0)
    for block in range(min(2, n_fsdp)):
        ready_copy(block).start()
    greet_all(n_seq, n_fsdp)
    gate_exchange.start()

    def compute(j):
        block = (me_f + j) % n_fsdp
        for piece in range(pieces):
            if j == 1:
                hidden_copy(piece).wait()
            gate_grad = hidden[piece, 0, :, block].reshape(-1, ff)
            up_grad = hidden[piece, 1, :, block].reshape(-1, ff)

            def some(chunk, carry):
                if j == 1:
                    weight_copy(piece, chunk).wait()
                lines = pl.ds(pl.multiple_of(chunk * tile, tile), tile)
                total = dot(gate_grad, weights[piece, lines, :ff], 1, 1)
                total = total + dot(up_grad, weights[piece, lines, ff:], 1, 1)
                rows[block, :, piece, :, lines] = total.astype(BF).reshape(n_seq, capacity, -1)
                return carry

            lax.fori_loop(0, chunks, some, 0)
            for i in range(1, n_seq):
                row_copy(block, i, piece, me_s).start()
            own_copy(block, piece).start()

    def finish(j):
        block = (me_f + j) % n_fsdp
        for piece in range(pieces):
            own_copy(block, piece).wait()
            for i in range(1, n_seq):
                row_copy(block, i, piece, (me_s + i) % n_seq).wait_recv()

        def some(columns):
            arrived = got[block, :, :, :, columns].reshape(n_seq * pieces * capacity, -1)
            total = dot(hot[block], arrived, 1, 0)
            if j < n_fsdp:
                parts[block, :, columns] = total.astype(BF)
            else:
                out[:, columns] = total

        chunked(width, 512, some)
        if j < n_fsdp:
            part_copy(j).start()

    def sum_ready(block):
        ready_copy(block).wait()

        def some(columns):
            arrived = some_ready[block % 2, :, :, :, columns]
            arrived = arrived.reshape(n_seq * pieces * capacity, -1)
            ready_sums[block, :, columns] = dot(hot[block], arrived, 1, 0).astype(BF)

        chunked(width, 512, some)
        if block + 2 < n_fsdp:
            ready_copy(block + 2).start()

    for j in range(1, n_fsdp + 1):
        compute(j)
        if j >= 3:
            finish(j - 2)
    for block in range(n_fsdp):
        sum_ready(block)
    for j in range(max(1, n_fsdp - 1), n_fsdp + 1):
        finish(j)
    for j in range(1, n_fsdp):
        source = (me_f + n_fsdp - j) % n_fsdp
        remote(
            parts.at[source], sums.at[source], part_send.at[j], part_recv.at[source], (me_s, source)
        ).wait_recv()

    def add(columns):
        total = out[:, columns]
        for j in range(1, n_fsdp):
            total = total + sums[(me_f + j) % n_fsdp, :, columns].astype(F32)
        out[:, columns] = total

    chunked(width, 512, add)
    for j in range(1, n_fsdp):
        part_copy(j).wait_send()
    for block in range(n_fsdp):
        for piece in range(pieces):
            for i in range(1, n_seq):
                row_copy(block, i, piece, me_s).wait_send()
    gate_exchange.finish()


def return_rows(grads, w_up, hot, gates, ready, n_seq, n_fsdp, collective_id):
    pieces, width = w_up.shape[:2]
    ff = w_up.shape[2] // 2
    count = hot.shape[1]
    capacity = ready.shape[3]
    vmem = pl.BlockSpec(memory_space=pltpu.VMEM)
    any_space = pl.BlockSpec(memory_space=pl.ANY)
    dma = pltpu.SemaphoreType.DMA
    return pl.pallas_call(
        functools.partial(return_kernel, n_seq, n_fsdp, pieces),
        out_shape=[
            jax.ShapeDtypeStruct((count, width), F32),
            jax.ShapeDtypeStruct(gates.shape, F32),
            jax.ShapeDtypeStruct((n_fsdp, count, width), BF),
        ],
        in_specs=[vmem, vmem, any_space, any_space] + [any_space] * pieces,
        out_specs=[vmem] * 3,
        scratch_shapes=[
            pltpu.VMEM(w_up.shape, BF),
            pltpu.VMEM((pieces, 2, n_seq, n_fsdp, capacity, ff), BF),
            pltpu.VMEM((n_fsdp, n_seq, pieces, capacity, width), BF),
            pltpu.VMEM((n_fsdp, n_seq, pieces, capacity, width), BF),
            pltpu.VMEM((n_fsdp, count, width), BF),
            pltpu.VMEM((n_fsdp, count, width), BF),
            pltpu.VMEM((2, n_seq, pieces, capacity, width), BF),
            dma((pieces, width // min(256, width))),
            dma((pieces,)),
            dma((2,)),
            dma((n_fsdp, pieces)),
            dma((n_fsdp, n_seq, pieces)),
            dma((n_fsdp, n_seq, pieces)),
            dma((n_fsdp,)),
            dma((n_fsdp,)),
        ]
        + exchange_sems(n_seq * n_fsdp),
        compiler_params=pltpu.CompilerParams(
            collective_id=collective_id, has_side_effects=True, vmem_limit_bytes=60 << 20
        ),
        name="return_rows",
    )(hot, gates, ready, w_up, *grads)


def weight_grad_kernel(a, b, *refs):
    parts, _, n = b.shape
    for part in range(parts):
        refs[-1][0, :, part * n : (part + 1) * n] = dot(a[...], b[part], 0, 0)


def weight_grad(a, b, whole, piece, pieces):
    rows, m = a.shape
    parts, _, n = b.shape
    tile = min(256, m)
    more = [] if whole is None else [whole]
    return pl.pallas_call(
        weight_grad_kernel,
        out_shape=jax.ShapeDtypeStruct((pieces, m, n * parts), F32),
        grid=(m // tile,),
        in_specs=[
            pl.BlockSpec((rows, tile), lambda i: (0, i)),
            pl.BlockSpec((parts, rows, n), lambda i: (0, 0, 0)),
        ]
        + [pl.BlockSpec(memory_space=pl.ANY)] * len(more),
        out_specs=pl.BlockSpec((1, tile, n * parts), lambda i: (piece, i, 0)),
        input_output_aliases={2: 0} if more else {},
        cost_estimate=pl.CostEstimate(
            flops=2 * rows * m * n * parts,
            bytes_accessed=4 * m * n * parts,
            transcendentals=0,
        ),
        name="weight_grad",
    )(a, b, *more)


def seq_tile(n_seq, rows_each, most=1024):
    tile = n_seq
    while tile > 1 and (tile * rows_each > most or n_seq % tile):
        tile -= 1
    return tile


def expert_backward_kernel(masked, gates, piece_out, hidden, w_down, out, grad, inner, partial):
    @pl.when(pl.program_id(1) == 0)
    def _():
        partial[...] = jnp.zeros_like(partial)

        def some(columns):
            low = masked[:, 0, :, :, columns].reshape(grad.shape[0], -1).astype(F32)
            grad[:, columns] = (low * gates[...]).astype(BF)
            product = low * piece_out[:, columns].astype(F32)
            for i in range(product.shape[1] // 128):
                partial[...] += product[:, i * 128 : (i + 1) * 128]

        chunked(grad.shape[1], 512, some)
        sums = jnp.sum(partial[...].T, axis=0, keepdims=True)
        inner[...] = jnp.broadcast_to(sums, inner.shape)

    act_grad = dot(grad[...], w_down[0], 1, 1)
    gate, up = hidden[0], hidden[1]
    sigmoid = jax.nn.sigmoid(gate)
    out[0] = (act_grad * up * sigmoid * (1.0 + gate * (1.0 - sigmoid))).astype(BF)
    out[1] = (act_grad * gate * sigmoid).astype(BF)


def expert_backward(masked, gates, piece_out, hidden, w_down, piece):
    rows, width = piece_out.shape
    ff = w_down.shape[1]
    n_seq, _, n_fsdp, capacity, _ = masked.shape
    tile = min(256, ff)
    spans = seq_tile(n_seq, n_fsdp * capacity)
    count = spans * n_fsdp * capacity
    part = pl.BlockSpec((2, count, tile), lambda r, i: (0, r, i))
    fixed = lambda r, i: (r, 0)
    return pl.pallas_call(
        expert_backward_kernel,
        out_shape=[
            jax.ShapeDtypeStruct((2, rows, ff), BF),
            jax.ShapeDtypeStruct((rows, width), BF),
            jax.ShapeDtypeStruct((8, rows), F32),
        ],
        grid=(rows // count, ff // tile),
        in_specs=[
            pl.BlockSpec((spans, 1, n_fsdp, capacity, width), lambda r, i: (r, piece, 0, 0, 0)),
            pl.BlockSpec((count, 1), fixed),
            pl.BlockSpec((count, width), fixed),
            part,
            pl.BlockSpec((1, tile, width), lambda r, i: (piece, i, 0)),
        ],
        out_specs=[
            part,
            pl.BlockSpec((count, width), fixed),
            pl.BlockSpec((8, count), lambda r, i: (0, r)),
        ],
        scratch_shapes=[pltpu.VMEM((count, 128), F32)],
        compiler_params=pltpu.CompilerParams(vmem_limit_bytes=62 << 20),
        cost_estimate=pl.CostEstimate(
            flops=2 * rows * width * ff, bytes_accessed=12 * rows * ff, transcendentals=rows * ff
        ),
        name="expert_backward",
    )(masked, gates, piece_out, hidden, w_down)


class SeqShare:
    def __init__(self, n_seq, own, every, send_sem, recv_sem):
        self.n_seq, self.own, self.every = n_seq, own, every
        self.send_sem, self.recv_sem = send_sem, recv_sem
        self.me_s, self.me_f = lax.axis_index("seq"), lax.axis_index("fsdp")

    def copy(self, i, place):
        other = (self.me_s + i) % self.n_seq
        return remote(
            self.own,
            self.every.at[place],
            self.send_sem.at[i],
            self.recv_sem.at[place],
            (other, self.me_f),
        )

    def total(self):
        for i in range(1, self.n_seq):
            self.copy(i, self.me_s).start()
        total = self.own[...]
        for i in range(1, self.n_seq):
            place = (self.me_s + i) % self.n_seq
            self.copy(i, place).wait_recv()
            total = total + self.every[place]
        for i in range(1, self.n_seq):
            self.copy(i, self.me_s).wait_send()
        return total


def share_scratch(n_seq, shape):
    dma = pltpu.SemaphoreType.DMA
    return [pltpu.VMEM(shape, F32), pltpu.VMEM((n_seq,) + shape, F32), dma((n_seq,)), dma((n_seq,))]


def row_sums(values):
    ones = jnp.ones((8, values.shape[1]), F32)
    return lax.dot_general(
        ones,
        values,
        (((1,), (1,)), ((), ())),
        preferred_element_type=F32,
        precision=lax.Precision.HIGHEST,
    )


def front_kernel(n_seq, x, gain, w, normed_out, raw_out, totals, normed, raw, sems, *scratch):
    share = SeqShare(n_seq, *scratch)
    head_width = w.shape[1] // 3
    tile = 256

    def some(i, carry):
        rows = pl.ds(pl.multiple_of(i * tile, tile), tile)
        values = x[rows, :].astype(F32)
        scale = lax.rsqrt(jnp.mean(values * values, axis=-1, keepdims=True) + epsilon)
        low = (values * scale * gain[0:1, :]).astype(BF)
        normed[rows, :] = low
        result = dot(low, w[...], 1, 0)
        raw[rows, :] = result
        for copy in away(i):
            copy.start()
        for part in range(2):
            piece = result[:, part * head_width : (part + 1) * head_width]
            share.own[part : part + 1, rows] = row_sums(piece * piece)[0:1]
        return carry

    def away(i):
        rows = pl.ds(pl.multiple_of(i * tile, tile), tile)
        return [
            pltpu.make_async_copy(normed.at[rows], normed_out.at[rows], sems.at[0, i]),
            pltpu.make_async_copy(raw.at[rows], raw_out.at[rows], sems.at[1, i]),
        ]

    def gone(i, carry):
        for copy in away(i):
            copy.wait()
        return carry

    share.own[...] = jnp.zeros_like(share.own)
    lax.fori_loop(0, x.shape[0] // tile, some, 0)
    totals[...] = share.total()
    lax.fori_loop(0, x.shape[0] // tile, gone, 0)


def front(x, gains, w, n_seq, collective_id):
    rows, width = x.shape
    vmem = pl.BlockSpec(memory_space=pltpu.VMEM)
    hbm = pl.BlockSpec(memory_space=pltpu.HBM)
    return pl.pallas_call(
        loading(functools.partial(front_kernel, n_seq), functools.partial(greet_seq, n_seq), 3),
        out_shape=[
            jax.ShapeDtypeStruct((rows, width), BF),
            jax.ShapeDtypeStruct((rows, w.shape[1]), F32),
            jax.ShapeDtypeStruct((8, rows), F32),
        ],
        in_specs=[hbm] * 3,
        out_specs=[hbm, hbm, vmem],
        scratch_shapes=[
            pltpu.VMEM((rows, width), BF),
            pltpu.VMEM((rows, w.shape[1]), F32),
            pltpu.SemaphoreType.DMA((2, rows // 256)),
        ]
        + share_scratch(n_seq, (8, rows))
        + load_scratch([x, gains, w]),
        compiler_params=pltpu.CompilerParams(
            collective_id=collective_id, has_side_effects=True, vmem_limit_bytes=62 << 20
        ),
        name="front",
    )(x, gains, w)


def column_rms(sums, part, width):
    return lax.rsqrt(sums.T[:, part : part + 1] / width + epsilon)


def turned(values, cosine, sine):
    return values * cosine + pltpu.roll(values, values.shape[1] // 2, 1) * sine


def softmax_columns(k, q, length, scaling):
    scores = dot(k, q, 1, 1) * scaling
    key = lax.broadcasted_iota(jnp.int32, scores.shape, 0)
    scores = jnp.where(key < length, scores, -1e30)
    weights = jnp.exp(scores - jnp.max(scores, axis=0, keepdims=True))
    return weights / jnp.sum(weights, axis=0, keepdims=True)


def attend_kernel(
    width,
    length,
    raw_q,
    raw_k,
    raw_v,
    q_sums,
    k_sums,
    gain,
    q_cos,
    q_sin,
    k_cos,
    k_sin,
    o_ref,
    q_ref,
    k_ref,
    v_ref,
):
    scaling = raw_q.shape[1] ** (-0.5)

    @pl.when(pl.program_id(1) == 0)
    def _():
        key = raw_k[...] * column_rms(k_sums[...], 1, width) * gain[2:3, :]
        k_ref[...] = turned(key, k_cos[...], k_sin[...]).astype(BF)
        v_ref[...] = raw_v[...].astype(BF)

    query = raw_q[...] * column_rms(q_sums[...], 0, width) * gain[1:2, :]
    query = turned(query, q_cos[...], q_sin[...]).astype(BF)
    q_ref[...] = query
    probs = softmax_columns(k_ref[...], query, length[0], scaling).astype(BF)
    o_ref[...] = dot(v_ref[...], probs, 0, 0).T.astype(BF)


def attend(raw, totals, gains, cosine, sine, length, block, width):
    slot_len, head_width = raw.shape[0], raw.shape[1] // 3
    hd = cosine.shape[1]
    heads = head_width // hd
    rows = lambda shift: pl.BlockSpec((block, hd), lambda h, i, n: (i, shift + h))
    full = lambda shift: pl.BlockSpec((slot_len, hd), lambda h, i, n: (0, shift + h))
    table = pl.BlockSpec((block, hd), lambda h, i, n: (i, 0))
    whole_table = pl.BlockSpec((slot_len, hd), lambda h, i, n: (0, 0))
    return pl.pallas_call(
        functools.partial(attend_kernel, width),
        out_shape=[jax.ShapeDtypeStruct((slot_len, head_width), BF)] * 4,
        grid_spec=pltpu.PrefetchScalarGridSpec(
            num_scalar_prefetch=1,
            grid=(heads, slot_len // block),
            in_specs=[
                rows(0),
                full(heads),
                full(2 * heads),
                pl.BlockSpec((8, block), lambda h, i, n: (0, i)),
                pl.BlockSpec((8, slot_len), lambda h, i, n: (0, 0)),
                pl.BlockSpec((8, hd), lambda h, i, n: (0, h)),
                table,
                table,
                whole_table,
                whole_table,
            ],
            out_specs=[rows(0), rows(0), full(0), full(0)],
        ),
        cost_estimate=pl.CostEstimate(
            flops=4 * heads * slot_len * slot_len * hd, bytes_accessed=1 << 23, transcendentals=0
        ),
        compiler_params=pltpu.CompilerParams(vmem_limit_bytes=62 << 20),
        name="attend",
    )(length, raw, raw, raw, totals, totals, gains, cosine, sine, cosine, sine)


def attend_back_kernel(
    width,
    length,
    q_ref,
    k_ref,
    v_ref,
    g_ref,
    raw_q,
    raw_k,
    q_sums,
    k_sums,
    gain,
    q_cos,
    q_sin,
    k_cos,
    k_sin,
    dq_ref,
    dk_ref,
    dv_ref,
    dots,
    gain_out,
    dk_sum,
    dv_sum,
):
    head, step = pl.program_id(0), pl.program_id(1)
    last = step == pl.num_programs(1) - 1
    block, hd = q_ref.shape
    scaling = hd ** (-0.5)

    @pl.when(step == 0)
    def _():
        dk_sum[...] = jnp.zeros_like(dk_sum)
        dv_sum[...] = jnp.zeros_like(dv_sum)
        gain_out[...] = jnp.zeros_like(gain_out)

        @pl.when(head == 0)
        def _():
            dots[...] = jnp.zeros_like(dots)

    q, k, v, g = q_ref[...], k_ref[...], v_ref[...], g_ref[...]
    probs = softmax_columns(k, q, length[0], scaling)
    dv_sum[...] += dot(probs.astype(BF), g, 1, 0)
    weights_grad = dot(v, g, 1, 1)
    inner = jnp.sum(probs * weights_grad, axis=0, keepdims=True)
    score_grad = (probs * (weights_grad - inner) * scaling).astype(BF)
    dk_sum[...] += dot(score_grad, q, 1, 0)
    query_grad = dot(k, score_grad, 0, 0).T.astype(BF).astype(F32)
    query_in = turned(query_grad, q_cos[...], -q_sin[...])
    dq_ref[...] = query_in
    product = query_in * raw_q[...]
    rows = pl.ds(pl.multiple_of(step * block, block), block)
    dots[0:1, rows] += row_sums(product * gain[1:2, :])[0:1]
    gain_out[0:1, :] += jnp.sum(
        product * column_rms(q_sums[...], 0, width), axis=0, keepdims=True
    )

    @pl.when(last)
    def _():
        key_in = turned(dk_sum[...].astype(BF).astype(F32), k_cos[...], -k_sin[...])
        dk_ref[...] = key_in
        dv_ref[...] = dv_sum[...].astype(BF)
        product = key_in * raw_k[...]
        dots[1:2, :] += row_sums(product * gain[2:3, :])[0:1]
        gain_out[1:2, :] = jnp.sum(
            product * column_rms(k_sums[...], 1, width), axis=0, keepdims=True
        )


def attend_back(query, key, value, grad, raw, totals, gains, cosine, sine, length, block, width):
    slot_len, head_width = query.shape
    hd = cosine.shape[1]
    heads = head_width // hd
    rows = pl.BlockSpec((block, hd), lambda h, i, n: (i, h))
    full = lambda shift: pl.BlockSpec((slot_len, hd), lambda h, i, n: (0, shift + h))
    table = pl.BlockSpec((block, hd), lambda h, i, n: (i, 0))
    whole_table = pl.BlockSpec((slot_len, hd), lambda h, i, n: (0, 0))
    return pl.pallas_call(
        functools.partial(attend_back_kernel, width),
        out_shape=[
            jax.ShapeDtypeStruct(query.shape, F32),
            jax.ShapeDtypeStruct(query.shape, F32),
            jax.ShapeDtypeStruct(query.shape, BF),
            jax.ShapeDtypeStruct((8, slot_len), F32),
            jax.ShapeDtypeStruct((8, head_width), F32),
        ],
        grid_spec=pltpu.PrefetchScalarGridSpec(
            num_scalar_prefetch=1,
            grid=(heads, slot_len // block),
            in_specs=[
                rows,
                full(0),
                full(0),
                rows,
                rows,
                full(heads),
                pl.BlockSpec((8, block), lambda h, i, n: (0, i)),
                pl.BlockSpec((8, slot_len), lambda h, i, n: (0, 0)),
                pl.BlockSpec((8, hd), lambda h, i, n: (0, h)),
                table,
                table,
                whole_table,
                whole_table,
            ],
            out_specs=[
                rows,
                full(0),
                full(0),
                pl.BlockSpec((8, slot_len), lambda h, i, n: (0, 0)),
                pl.BlockSpec((8, hd), lambda h, i, n: (0, h)),
            ],
            scratch_shapes=[pltpu.VMEM((slot_len, hd), F32), pltpu.VMEM((slot_len, hd), F32)],
        ),
        cost_estimate=pl.CostEstimate(
            flops=20 * heads * slot_len * slot_len * hd, bytes_accessed=1 << 24, transcendentals=0
        ),
        compiler_params=pltpu.CompilerParams(vmem_limit_bytes=62 << 20),
        name="attend_back",
    )(
        length,
        query,
        key,
        value,
        grad,
        raw,
        raw,
        totals,
        totals,
        gains,
        cosine,
        sine,
        cosine,
        sine,
    )


def raw_back_kernel(
    n_seq, n_fsdp, width, dq, dk, dv, raw, totals, gain, dots, terms, out, terms_out, *scratch
):
    share = SeqShare(n_seq, *scratch[:4])
    term_sum = TermSum(n_seq, n_fsdp, None, *scratch[4:6], None, None, *scratch[6:])
    term_sum.start_fsdp(terms[...])
    head_width = dq.shape[1]
    share.own[...] = dots[...]
    share.own[...] = share.total()
    tile = 256

    def some(i, carry):
        rows = pl.ds(pl.multiple_of(i * tile, tile), tile)
        inner = share.own[:, rows].T / width
        for part, grad in enumerate((dq, dk)):
            columns = slice(part * head_width, (part + 1) * head_width)
            scale = column_rms(totals[:, rows], part, width)
            weighted = grad[rows, :] * gain[part + 1 : part + 2, :]
            cube = scale * scale * scale
            result = scale * weighted - raw[rows, columns] * (cube * inner[:, part : part + 1])
            out[rows, columns] = result.astype(BF)
        out[rows, 2 * head_width :] = dv[rows, :]
        return carry

    lax.fori_loop(0, dq.shape[0] // tile, some, 0)
    terms_out[...] = term_sum.finish()


def raw_back(dq, dk, dv, raw, totals, gains, dots, terms, n_seq, n_fsdp, width, collective_id):
    vmem = pl.BlockSpec(memory_space=pltpu.VMEM)
    dma = pltpu.SemaphoreType.DMA
    return pl.pallas_call(
        loading(
            functools.partial(raw_back_kernel, n_seq, n_fsdp, width),
            functools.partial(greet_lines, n_seq, n_fsdp),
            8,
        ),
        out_shape=[
            jax.ShapeDtypeStruct(raw.shape, BF),
            jax.ShapeDtypeStruct(terms.shape, F32),
        ],
        in_specs=[pl.BlockSpec(memory_space=pltpu.HBM)] * 8,
        out_specs=[vmem] * 2,
        scratch_shapes=share_scratch(n_seq, dots.shape)
        + [
            pltpu.VMEM((n_seq,) + terms.shape, F32),
            pltpu.VMEM((n_fsdp,) + terms.shape, F32),
            dma((n_fsdp,)),
            dma((n_fsdp,)),
        ]
        + load_scratch([dq, dk, dv, raw, totals, gains, dots, terms]),
        compiler_params=pltpu.CompilerParams(
            collective_id=collective_id, has_side_effects=True, vmem_limit_bytes=62 << 20
        ),
        name="raw_back",
    )(dq, dk, dv, raw, totals, gains, dots, terms)


def rope_tables(count, head_dim):
    half = head_dim // 2
    frequency = rope_base ** (-np.arange(half, dtype=np.float64) * 2.0 / head_dim)
    angles = np.arange(count, dtype=np.float64)[:, None] * frequency[None, :]
    cosine, sine = np.cos(angles), np.sin(angles)
    both = np.concatenate([cosine, cosine], axis=1), np.concatenate([-sine, sine], axis=1)
    return tuple(jnp.asarray(table, F32) for table in both)


def places(block_routes, experts, capacity):
    count = block_routes.shape[0]
    match = (block_routes[:, :, None] == experts[None, None, :]).astype(F32).sum(axis=1)
    lower = jnp.tril(jnp.ones((count, count), BF), -1)
    rank = dot(lower, match.astype(BF), 1, 0)
    place = jnp.arange(capacity, dtype=F32)
    return match[:, :, None] * (rank[:, :, None] == place[None, None, :]).astype(F32)


def local(
    tokens,
    cotangent,
    lengths,
    routes,
    norm_gains,
    qkv_weight,
    proj_weight,
    router_weight,
    expert_up,
    expert_down,
):
    n_seq, n_fsdp = lax.axis_size("seq"), lax.axis_size("fsdp")
    n_dev = n_seq * n_fsdp
    me_s, me_f = lax.axis_index("seq"), lax.axis_index("fsdp")
    shard_len, width = tokens.shape[1], tokens.shape[2]
    slot_len = shard_len * n_seq
    experts = router_weight.shape[1]
    top_count = routes.shape[2]
    capacity = 3 * shard_len * top_count // (2 * experts)
    piece_ff = expert_down.shape[1]
    pieces_dev = expert_up.shape[0]
    split = FF // piece_ff
    head_dim = width // HEADS
    head_width = width // n_seq
    heads_dev = HEADS // n_seq
    owned = qkv_weight.shape[0]
    block = min(512, slot_len)
    length = lax.dynamic_slice_in_dim(lengths, me_f, 1)
    valid_total = jnp.sum(lengths).astype(F32).reshape(1)
    positions = me_s * shard_len + jnp.arange(shard_len, dtype=jnp.int32)
    row_valid = (positions < length[0]).astype(F32)
    local_routes = routes[0]
    push_all = functools.partial(push, n_seq=n_seq, n_fsdp=n_fsdp, scope="all")
    push_seq = functools.partial(push, n_seq=n_seq, n_fsdp=n_fsdp, scope="seq")

    own_small = jnp.concatenate(
        [
            jnp.pad(norm_gains, ((0, 4), (0, 128 - owned))),
            local_routes.T.astype(BF),
            rows_of(router_weight.reshape(-1), 16),
        ]
    )
    small, gains, slot_tokens, qkv_local, cot_all, to_places, to_rows, *more = first_gather(
        own_small,
        tokens[0],
        qkv_weight,
        cotangent[0],
        lengths,
        n_seq,
        n_fsdp,
        pieces_dev,
        split,
        capacity,
        top_count,
        experts,
        collective_id=0,
    )
    counts, own_gains, masked_low = more
    slot_tokens = slot_tokens.reshape(slot_len, width)
    qkv_local = qkv_local.reshape(width, 3 * head_width)
    router = small[:, 8 + top_count :].reshape(n_dev, -1)[:, : owned * experts]
    router = router.reshape(width, experts)
    proj_later = lax.optimization_barrier((proj_weight, slot_tokens))[0]
    proj_rows = lax.all_gather(proj_later, "fsdp", axis=0, tiled=True)

    def exchange(rows):
        return lax.all_to_all(rows, "seq", split_axis=0, concat_axis=0, tiled=True)

    normed_one, raw, totals = front(slot_tokens, gains, qkv_local, n_seq, collective_id=1)


    def rms(values):
        return lax.rsqrt(jnp.mean(values * values, axis=-1, keepdims=True) + epsilon)

    cosine, sine = rope_tables(slot_len, head_dim)
    attended, query, key, value = attend(
        raw, totals, own_gains, cosine, sine, length, block, width
    )

    resid_in = tokens[0].astype(F32)
    resid_mid = resid_in + product_reduced(attended, proj_rows, 0, n_seq, collective_id=8)
    mid_rms = rms(resid_mid)
    normed_two = (resid_mid * mid_rms * gains[3]).astype(BF)
    router_probs = jax.nn.softmax(jnp.dot(normed_two, router, preferred_element_type=F32), axis=-1)

    own_hot = places(local_routes, jnp.arange(experts, dtype=jnp.int32), capacity)
    gate_slot = jnp.sum(own_hot * router_probs[:, :, None], axis=0)
    gate_send = jnp.broadcast_to(gate_slot[:, None], (experts, split, capacity))
    gate_send = gate_send.reshape(n_dev, pieces_dev, capacity)
    gate_send = jnp.pad(gate_send, ((0, 0), (0, -pieces_dev % 8), (0, 128 - capacity)))
    cot_all, gate_columns, outs, *experts_forward = dispatch_rows(
        normed_two,
        to_places,
        gate_send,
        masked_low,
        cot_all,
        expert_up,
        expert_down,
        n_seq,
        n_fsdp,
        capacity,
        collective_id=6,
    )
    outs_back = exchange(outs)
    backs, gate_backs = [], []
    up_grad = down_grad = None
    for piece in range(pieces_dev):
        rows, hidden, activation, piece_out = experts_forward[piece::pieces_dev]
        rows = rows.reshape(-1, width)
        hidden_grad, out_grad, gate_back = expert_backward(
            cot_all, gate_columns[piece], piece_out, hidden, expert_down, piece
        )
        gate_backs.append(gate_back[0].reshape(n_dev, capacity))
        backs.append(hidden_grad.reshape(2, n_seq, n_fsdp, capacity, piece_ff))
        down_grad = weight_grad(activation, out_grad[None], down_grad, piece, pieces_dev)
        up_grad = weight_grad(rows, hidden_grad, up_grad, piece, pieces_dev)
    back_send = jnp.stack(gate_backs, axis=1).reshape(n_dev, pieces_dev * capacity)
    gate_pad = -pieces_dev * capacity % 1024
    back_send = jnp.pad(back_send, ((0, 0), (0, gate_pad))).reshape(n_dev, -1, 128)
    backs, outs_back, up_grad, down_grad = lax.optimization_barrier(
        (backs, outs_back, up_grad, down_grad)
    )
    backs, outs_back, up_grad, down_grad = lax.optimization_barrier(
        (backs, outs_back, up_grad, down_grad)
    )
    normed_two_grad, back_recv, outs_sums = return_rows(
        backs, expert_up, to_rows, back_send, outs_back, n_seq, n_fsdp, collective_id=7
    )

    fraction = counts[0] / (top_count * valid_total)
    back_recv = back_recv.reshape(n_dev, -1)
    slot_gates_grad = back_recv[:, : pieces_dev * capacity].reshape(experts, split, capacity).sum(axis=1)
    probs_grad = (
        jnp.sum(own_hot * slot_gates_grad[None], axis=2)
        + (experts * fraction / valid_total)[None, :] * row_valid[:, None]
    )
    logits_grad = router_probs * (
        probs_grad - jnp.sum(router_probs * probs_grad, axis=-1, keepdims=True)
    )
    router_term = lax.dot_general(
        logits_grad, normed_two.astype(F32), (((0,), (0,)), ((), ())), precision=lax.Precision.HIGHEST
    )
    normed_two_grad = normed_two_grad + lax.dot_general(
        logits_grad, router.astype(F32), (((1,), (1,)), ((), ())), precision=lax.Precision.HIGHEST
    )

    def rms_back(values, scale, gain, grad):
        weighted = gain * grad
        mean = jnp.mean(weighted * values, axis=-1, keepdims=True)
        return scale * weighted - values * (scale * scale * scale) * mean, jnp.sum(
            grad * values * scale, axis=0
        )

    mid_part, gain_three = rms_back(resid_mid, mid_rms, gains[3], normed_two_grad)
    mid_grad = masked_low.astype(F32) + mid_part
    branch_grad = mid_grad.astype(BF)
    outs_parts = lax.all_to_all(outs_sums, "fsdp", split_axis=0, concat_axis=0, tiled=True)
    slot_branch, router_parts = gather_seq(
        branch_grad, router_term, n_seq, n_fsdp, collective_id=9
    )
    slot_branch = slot_branch.reshape(slot_len, width)
    heads_grad = dot(slot_branch, proj_rows, 1, 1).astype(BF)
    query_in, key_in, value_grad, dots, heads_gain = attend_back(
        query,
        key,
        value,
        heads_grad,
        raw,
        totals,
        own_gains,
        cosine,
        sine,
        length,
        block,
        width,
    )
    raw_grad, router_parts = raw_back(
        query_in,
        key_in,
        value_grad,
        raw,
        totals,
        own_gains,
        dots,
        router_parts,
        n_seq,
        n_fsdp,
        width,
        collective_id=4,
    )
    raw_grad, outs_parts = lax.optimization_barrier((raw_grad, outs_parts))

    prob_part = jnp.sum(router_probs * row_valid[:, None], axis=0)
    prob_row = jnp.tile(jnp.pad(prob_part, (0, head_width - experts)), n_seq)
    terms = jnp.pad(jnp.stack([gain_three, prob_row]), ((1, 5), (0, 0)))
    heads_terms = jnp.pad(heads_gain[:2], ((3, 3), (0, 0)))
    input_grad, qkv_grad, last, layer_out = last_reduce(
        raw_grad,
        qkv_local,
        normed_one,
        tokens[0],
        mid_grad,
        gains,
        terms,
        heads_terms,
        resid_mid,
        outs_parts,
        n_seq,
        n_fsdp,
        collective_id=10,
    )
    input_grad = input_grad[None]
    layer_out = layer_out[None]

    proj_part = dot(attended, slot_branch, 0, 0).astype(BF)
    proj_grad = lax.psum_scatter(proj_part, "fsdp", scatter_dimension=0, tiled=True).astype(F32)

    router_grad = lax.dynamic_slice_in_dim(router_parts, me_f * owned, owned, 1).T
    prob_total = last[2, :experts]
    last = lax.dynamic_slice_in_dim(last, me_f * owned, owned, 1)
    gains_grad = jnp.stack([last[0], last[3], last[4], last[1]])
    loss_value = (experts * jnp.sum(fraction * prob_total / valid_total)).reshape(1)
    return (
        layer_out,
        input_grad,
        gains_grad,
        qkv_grad,
        proj_grad,
        router_grad,
        up_grad,
        down_grad,
        loss_value,
    )


def solution(mesh):
    rows = P(("seq", "fsdp"), None)
    return jax.shard_map(
        local,
        mesh=mesh,
        in_specs=(
            P("fsdp", "seq", None),
            P("fsdp", "seq", None),
            P(),
            P("fsdp", "seq", None),
            P(None, ("seq", "fsdp")),
            rows,
            rows,
            rows,
            P(("seq", "fsdp"), None, None),
            P(("seq", "fsdp"), None, None),
        ),
        out_specs=(
            P("fsdp", "seq", None),
            P("fsdp", "seq", None),
            P(None, ("seq", "fsdp")),
            rows,
            rows,
            rows,
            P(("seq", "fsdp"), None, None),
            P(("seq", "fsdp"), None, None),
            P(),
        ),
        check_vma=False,
    )
```
